32 devices in a mesh: seq: 8 (over z, y), own: 4 (over x, core).
Axes of the slice: x: 2, y: 2, z: 4, core: 2. Of those that a mesh axis runs over, the one named last changes fastest.
Arguments:
- tokens: bfloat16 [4, 8192, 768], P('own', 'seq')
- cotangent: bfloat16 [4, 8192, 768], P('own', 'seq'), may hold values from -6 to 6
- lengths: int32 [4, 10], P('own'), may hold values from 512 to 2048, as said below
- offsets: int32 [4, 10], P('own'), may hold values from 0 to 1536, as said below
- valid_count: int32 [4, 10], P('own'), may hold values from 257 to 2048, as said below
- weights: float32 [768, 96, 96], P(('seq', 'own'))
- stat_left: float32 [768, 96, 96], P(('seq', 'own')), as said below
- stat_right: float32 [768, 96, 96], P(('seq', 'own')), as said below
- root_left: float32 [768, 96, 96], P(('seq', 'own')), as said below
- root_right: float32 [768, 96, 96], P(('seq', 'own')), as said below
- projection: float32 [2048, 256], P('own'), may hold values from -0.125 to 0.125
- projection_left: float32 [8, 256, 256], P('own'), as said below
- projection_right: float32 [8, 256, 256], P('own'), as said below
- projection_root_left: float32 [8, 256, 256], P('own'), as said below
- projection_root_right: float32 [8, 256, 256], P('own'), as said below
- norm_params: float32 [4, 768], replicated
- norm_stat: float32 [4, 768], replicated, as said below
Outputs:
- output: bfloat16 [4, 8192, 768], P('own', 'seq')
- grad_input: float32 [4, 8192, 768], P('own', 'seq')
- weight_grad: float32 [768, 96, 96], P(('seq', 'own'))
- stat_left_new: float32 [768, 96, 96], P(('seq', 'own'))
- stat_right_new: float32 [768, 96, 96], P(('seq', 'own'))
- weights_new: float32 [768, 96, 96], P(('seq', 'own'))
- projection_grad: float32 [2048, 256], P('own')
- projection_left_new: float32 [8, 256, 256], P('own')
- projection_right_new: float32 [8, 256, 256], P('own')
- projection_new: float32 [2048, 256], P('own')
- norm_grad: float32 [4, 768], replicated
- norm_stat_new: float32 [4, 768], replicated
- norm_new: float32 [4, 768], replicated
- residual_rms: float32 [2], replicated
The draws below stay inside these ranges and needn't reach their ends.
Inputs may be any that keep to these rules, and one draw needn't show every extreme that they name: `lengths`: each pack holds exactly 2 items of 2048 tokens and 8 of 512, in a drawn order, filling the pack. `offsets`: offset plus length is at most 2048; items of 2048 tokens have offset 0; in each pack some item of 512 tokens ends at position 2048. `valid_count`: an item's valid count is more than half of its length and at most its length; in each pack some item of 2048 tokens is wholly valid, and some item of 512 tokens has 257 valid tokens. `stat_left`: Symmetric. `stat_right`: Symmetric. `root_left`: Symmetric. `root_right`: Symmetric. `projection_left`: Symmetric. `projection_right`: Symmetric. `projection_root_left`: Symmetric. `projection_root_right`: Symmetric. `norm_stat`: Positive.
All inputs are finite; a program needn't handle non-finite values.
Results may differ from the reference program's by a relative error of at most 0.015.
The reference program's roundings to bfloat16 on the way count: a program that leaves them out, or rounds other values in their place, can miss the bound.
Values may be sent and summed in bfloat16 or wider, within the bound.
A program may use at most 448 MiB of HBM per device.

```python
import math
import jax
import jax.numpy as jnp
from jax import lax

D = 768
HEADS = 12
HD = 64
FF = 3072
KP = 256
LONG = 2048
SHORT = 512
TILE = 96
PACKS = 4
PACK_TOK = 8192
NLONG = 2
ITEMS = 10
ATT_TILES = 256
FFN_TILES = 512
TILES = 768
TPD = 24
ATT_DEV = 8
FFN_DEV = 16
EBLK = 8
DEVICES = 32


def item_table(key):
    keys = jax.random.split(jax.random.fold_in(key, 7), PACKS)

    def one_pack(pack_key):
        key_order, key_offset, key_cut = jax.random.split(pack_key, 3)
        order = jax.random.permutation(key_order, ITEMS)
        lengths = jnp.where(order < NLONG, LONG, SHORT).astype(jnp.int32)
        offsets = jax.random.randint(key_offset, (ITEMS,), 0, LONG - lengths + 1).astype(jnp.int32)
        offsets = jnp.where(order == NLONG, LONG - lengths, offsets).astype(jnp.int32)
        cut = jax.random.randint(key_cut, (ITEMS,), 0, lengths // 2).astype(jnp.int32)
        counts = jnp.where(order == 0, lengths, jnp.where(order == NLONG + 1, lengths // 2 + 1, lengths - cut)).astype(jnp.int32)
        return (lengths, offsets, counts)
    return jax.vmap(one_pack)(keys)


def draw_lengths(key, part):
    return item_table(key)[0]


def draw_offsets(key, part):
    return item_table(key)[1]


def draw_valid_count(key, part):
    return item_table(key)[2]


def rough(key, shape):
    return jnp.clip(jax.random.normal(key, shape, jnp.float32), -6.0, 6.0)


def square_stack(key, count, size, scale, low_end, high_end):
    key_diag, key_rest = jax.random.split(key)
    factor = jnp.exp(jax.random.uniform(key_diag, (count, 1, 1), jnp.float32, math.log(low_end), math.log(high_end)))
    raw = rough(key_rest, (count, size, size))
    mixed = 0.5 * (raw + jnp.swapaxes(raw, 1, 2))
    return scale * factor * (jnp.eye(size, dtype=jnp.float32) + 0.04 * mixed)


def draw_tokens(key, part):
    base = rough(jax.random.fold_in(key, 3), (PACKS, PACK_TOK, D))
    ramp = 1.0 + 2.0 * jnp.arange(PACK_TOK, dtype=jnp.float32) / PACK_TOK
    return (base * ramp[None, :, None]).astype(jnp.bfloat16)


def draw_weights(key, part):
    index = jnp.arange(TILES, dtype=jnp.int32)
    owner = index // TPD
    within = index % TPD
    att_index = owner * ATT_DEV + within
    ffn_index = owner * FFN_DEV + within - ATT_DEV
    kind = att_index // (ATT_TILES // 4)
    att_scale = jnp.where(kind == 0, 0.8, jnp.where(kind == 3, 8.0, 1.0)) / math.sqrt(D)
    ffn_scale = jnp.where(ffn_index < FFN_TILES // 2, 1.0 / math.sqrt(D), 1.5 / math.sqrt(FF))
    scale = jnp.where(within < ATT_DEV, att_scale, ffn_scale)
    return rough(jax.random.fold_in(key, 5), (TILES, TILE, TILE)) * scale[:, None, None]


def draw_stat_left(key, part):
    return square_stack(jax.random.fold_in(key, 21), TILES, TILE, float(TILE * PACKS * PACK_TOK), 1.0, 4.0)


def draw_stat_right(key, part):
    return square_stack(jax.random.fold_in(key, 22), TILES, TILE, float(TILE * PACKS * PACK_TOK), 1.0, 4.0)


def draw_root_left(key, part):
    return square_stack(jax.random.fold_in(key, 23), TILES, TILE, float(TILE * PACKS * PACK_TOK) ** (-0.25), 0.7, 1.4)


def draw_root_right(key, part):
    return square_stack(jax.random.fold_in(key, 24), TILES, TILE, float(TILE * PACKS * PACK_TOK) ** (-0.25), 0.7, 1.4)


def draw_projection_left(key, part):
    return square_stack(jax.random.fold_in(key, 31), EBLK, KP, float(KP * PACKS * PACK_TOK), 1.0, 4.0)


def draw_projection_right(key, part):
    return square_stack(jax.random.fold_in(key, 32), EBLK, KP, float(KP * PACKS * PACK_TOK), 1.0, 4.0)


def draw_projection_root_left(key, part):
    return square_stack(jax.random.fold_in(key, 33), EBLK, KP, float(KP * PACKS * PACK_TOK) ** (-0.25), 0.7, 1.4)


def draw_projection_root_right(key, part):
    return square_stack(jax.random.fold_in(key, 34), EBLK, KP, float(KP * PACKS * PACK_TOK) ** (-0.25), 0.7, 1.4)


def draw_norm_params(key, part):
    raw = rough(jax.random.fold_in(key, 41), (4, D))
    center = jnp.array([1.0, 0.0, 1.0, 0.0], jnp.float32)[:, None]
    spread = jnp.array([0.1, 0.3, 0.1, 0.3], jnp.float32)[:, None]
    return center + spread * raw


def draw_norm_stat(key, part):
    factor = jnp.exp(jax.random.uniform(jax.random.fold_in(key, 43), (4, D), jnp.float32, 0.0, math.log(4.0)))
    return float(PACKS * PACK_TOK) * factor


def levels(rng, dims, shards, smallest, largest):
    factor_of = 1.0
    for dim, blocks in shards:
        draws = jax.random.uniform(jax.random.fold_in(jax.random.fold_in(rng, 6), dim), (blocks,), jnp.float32, smallest / len(shards), largest / len(shards))
        factor_of = factor_of * jnp.repeat(jnp.exp(draws), dims[dim] // blocks).reshape((-1,) + (1,) * (len(dims) - 1 - dim))
    return factor_of


def noise(key, shape, deviation, most, cuts=(), kind=jnp.bfloat16):
    drawn = jax.random.normal(key, shape, jnp.float32) * deviation
    if len(cuts) > 0:
        drawn = levels(key, shape, cuts, -0.22, 0.18) * drawn
    return jnp.clip(drawn, min=-most, max=most).astype(kind)


def setup_inputs(seed: int = 0) -> dict:
    seeds = jax.random.split(jax.random.key(seed), 18)
    return {
        "tokens": draw_tokens(jax.random.fold_in(seeds[17], 71), 0),
        "cotangent": noise(seeds[1], (PACKS, PACK_TOK, D), 1.0, 6.0, ((0, 4), (1, 8))),
        "lengths": draw_lengths(jax.random.fold_in(seeds[17], 71), 0),
        "offsets": draw_offsets(jax.random.fold_in(seeds[17], 71), 0),
        "valid_count": draw_valid_count(jax.random.fold_in(seeds[17], 71), 0),
        "weights": draw_weights(jax.random.fold_in(seeds[17], 71), 0),
        "stat_left": draw_stat_left(jax.random.fold_in(seeds[17], 71), 0),
        "stat_right": draw_stat_right(jax.random.fold_in(seeds[17], 71), 0),
        "root_left": draw_root_left(jax.random.fold_in(seeds[17], 71), 0),
        "root_right": draw_root_right(jax.random.fold_in(seeds[17], 71), 0),
        "projection": noise(seeds[10], (LONG, KP), LONG ** -0.5, 0.125, ((0, 4),), jnp.float32),
        "projection_left": draw_projection_left(jax.random.fold_in(seeds[17], 71), 0),
        "projection_right": draw_projection_right(jax.random.fold_in(seeds[17], 71), 0),
        "projection_root_left": draw_projection_root_left(jax.random.fold_in(seeds[17], 71), 0),
        "projection_root_right": draw_projection_root_right(jax.random.fold_in(seeds[17], 71), 0),
        "norm_params": draw_norm_params(jax.random.fold_in(seeds[17], 71), 0),
        "norm_stat": draw_norm_stat(jax.random.fold_in(seeds[17], 71), 0),
    }


@jax.custom_vjp
def low(v):
    return lax.optimization_barrier(v.astype(jnp.bfloat16)).astype(jnp.float32)

@jax.custom_vjp
def low_back(v):
    return v

def low_keep(v):
    return (low(v), None)

def low_pass(kept, grad):
    return (grad,)

def back_keep(v):
    return (v, None)

def back_low(kept, grad):
    return (low(grad),)
low.defvjp(low_keep, low_pass)
low_back.defvjp(back_keep, back_low)
highest = lax.Precision.HIGHEST
eps_norm = 1e-05
decay = 0.5
rate_matrix = 0.2
rate_norm = 0.2

def to_matrix(tiles, rows, cols):
    size = tiles.shape[-1]
    return tiles.reshape(rows // size, cols // size, size, size).transpose(0, 2, 1, 3).reshape(rows, cols)

def to_tiles(matrix, size):
    rows, cols = matrix.shape
    return matrix.reshape(rows // size, size, cols // size, size).transpose(0, 2, 1, 3).reshape(-1, size, size)

def layer_norm(values, gain, shift):
    mean = lax.optimization_barrier(jnp.mean(values, axis=-1, keepdims=True))
    centered = values - mean
    normed = centered * lax.rsqrt(lax.optimization_barrier(jnp.mean(centered * centered, axis=-1, keepdims=True)) + eps_norm)
    return normed * gain + shift

def shampoo(grad, left, right, root_left, root_right, weight):
    new_left = decay * left + (1.0 - decay) * jnp.einsum('tij,tkj->tik', grad, grad, precision=highest)
    new_right = decay * right + (1.0 - decay) * jnp.einsum('tji,tjk->tik', grad, grad, precision=highest)
    inner = jnp.einsum('tij,tjk->tik', grad, root_right, precision=highest)
    step = jnp.einsum('tij,tjk->tik', root_left, inner, precision=highest)
    return (new_left, new_right, weight - rate_matrix * step)

def pack_forward(inputs, lens, offs, counts, w_qkv, w_out, w_up, w_down, proj_rows, norm_p):
    qkv = jnp.dot(inputs, w_qkv, precision=highest)
    query = low_back(low(qkv[:, :D]))
    keyval = low_back(low(qkv[:, D:]))
    starts = jnp.cumsum(lens) - lens
    place_all = jnp.arange(LONG, dtype=jnp.int32)
    keyval_pad = jnp.concatenate([keyval, jnp.zeros((LONG, 2 * D), jnp.float32)], axis=0)
    proj_pad = jnp.concatenate([proj_rows, jnp.zeros((LONG, KP), jnp.float32)], axis=0)

    def summary_of(item):
        block = lax.dynamic_slice_in_dim(keyval_pad, starts[item], LONG, 0)
        columns = lax.dynamic_slice_in_dim(proj_pad, offs[item], LONG, 0)
        columns = jnp.where((place_all < counts[item])[:, None], columns, 0.0)
        return jnp.dot(columns.T, block, precision=highest)
    summary = lax.map(jax.checkpoint(summary_of), jnp.arange(ITEMS, dtype=jnp.int32))
    summary = low_back(low(summary))
    query_pad = jnp.concatenate([query, jnp.zeros((LONG, D), jnp.float32)], axis=0)

    def attend(item):
        rows = lax.dynamic_slice_in_dim(query_pad, starts[item], LONG, 0).reshape(LONG, HEADS, HD)
        keys = summary[item, :, :D].reshape(KP, HEADS, HD)
        values = summary[item, :, D:].reshape(KP, HEADS, HD)
        scores = low_back(jnp.einsum('rhd,jhd->rhj', rows, keys, precision=highest) * HD ** (-0.5))
        prob = low(jax.nn.softmax(scores, axis=-1))
        return jnp.einsum('rhj,jhd->rhd', prob, values, precision=highest).reshape(LONG, D)
    per_item = lax.map(jax.checkpoint(attend), jnp.arange(ITEMS, dtype=jnp.int32))
    rows_all = jnp.arange(PACK_TOK, dtype=jnp.int32)
    item_of = lax.optimization_barrier(jnp.sum((starts[None, :] <= rows_all[:, None]).astype(jnp.int32), axis=1)) - 1
    place = rows_all - starts[item_of]
    attended = jnp.take(per_item.reshape(ITEMS * LONG, D), (item_of * LONG + place).astype(jnp.int32), axis=0)
    attended = low_back(low(attended))
    branch = low_back(jnp.dot(attended, w_out, precision=highest))
    first_sum = inputs + branch
    first_norm = layer_norm(first_sum, norm_p[0], norm_p[1])
    up_value = low_back(jnp.dot(low(first_norm), w_up, precision=highest))
    hidden = low(jax.nn.gelu(up_value, approximate=False))
    down_value = low_back(jnp.dot(hidden, w_down, precision=highest))
    result = layer_norm(first_norm + down_value, norm_p[2], norm_p[3])
    keep = (place < counts[item_of]).astype(jnp.float32)
    sums = jnp.stack([jnp.sum(keep[:, None] * first_sum * first_sum), jnp.sum(keep[:, None] * branch * branch), jnp.sum(keep)])
    return (result, sums)

def reference(tokens, cotangent, lengths, offsets, valid_count, weights, stat_left, stat_right, root_left, root_right, projection, projection_left, projection_right, projection_root_left, projection_root_right, norm_params, norm_stat):
    weights_low = lax.optimization_barrier(weights.astype(jnp.bfloat16)).astype(jnp.float32)
    grid = weights_low.reshape(DEVICES, TPD, TILE, TILE)
    attention = grid[:, :ATT_DEV].reshape(ATT_TILES, TILE, TILE)
    forward_tiles = grid[:, ATT_DEV:].reshape(FFN_TILES, TILE, TILE)
    count_sq = (D // TILE) ** 2
    count_ff = D // TILE * (FF // TILE)
    w_query = to_matrix(attention[0:count_sq], D, D)
    w_key = to_matrix(attention[count_sq:2 * count_sq], D, D)
    w_value = to_matrix(attention[2 * count_sq:3 * count_sq], D, D)
    w_out = to_matrix(attention[3 * count_sq:], D, D)
    w_up = to_matrix(forward_tiles[0:count_ff], D, FF)
    w_down = to_matrix(forward_tiles[count_ff:], FF, D)
    proj_low = lax.optimization_barrier(projection.astype(jnp.bfloat16)).astype(jnp.float32)
    inputs = tokens.astype(jnp.float32)

    def forward(wq, wk, wv, wo, wu, wd, proj_rows, norm_p, inputs_all):
        w_qkv = jnp.concatenate([wq, wk, wv], axis=1)
        results = []
        totals = jnp.zeros((3,), jnp.float32)
        for pack in range(PACKS):
            result, sums = pack_forward(inputs_all[pack], lengths[pack], offsets[pack], valid_count[pack], w_qkv, wo, wu, wd, proj_rows, norm_p)
            results.append(result)
            totals = totals + sums
        return (jnp.stack(results), totals)
    result, pull, totals = jax.vjp(forward, w_query, w_key, w_value, w_out, w_up, w_down, proj_low, norm_params, inputs, has_aux=True)
    grads = pull(cotangent.astype(jnp.float32))
    g_query, g_key, g_value, g_out, g_up, g_down, g_proj, g_norm, g_input = grads
    att_grad = jnp.concatenate([to_tiles(g_query, TILE), to_tiles(g_key, TILE), to_tiles(g_value, TILE), to_tiles(g_out, TILE)], axis=0)
    ffn_grad = jnp.concatenate([to_tiles(g_up, TILE), to_tiles(g_down, TILE)], axis=0)
    weight_grad = jnp.concatenate([att_grad.reshape(DEVICES, ATT_DEV, TILE, TILE), ffn_grad.reshape(DEVICES, FFN_DEV, TILE, TILE)], axis=1).reshape(TILES, TILE, TILE)
    left_new, right_new, weights_new = shampoo(weight_grad, stat_left, stat_right, root_left, root_right, weights)
    proj_blocks = g_proj.reshape(EBLK, KP, KP)
    p_left, p_right, p_new = shampoo(proj_blocks, projection_left, projection_right, projection_root_left, projection_root_right, projection.reshape(EBLK, KP, KP))
    stat_new = decay * norm_stat + (1.0 - decay) * g_norm * g_norm
    norm_new = norm_params - rate_norm * g_norm * lax.rsqrt(stat_new)
    rms = jnp.sqrt(totals[:2] / (totals[2] * D))
    return (result.astype(jnp.bfloat16), g_input, weight_grad, left_new, right_new, weights_new, g_proj, p_left, p_right, p_new.reshape(LONG, KP), g_norm, stat_new, norm_new, rms)
```

```python
import functools
import math

import jax
import jax.numpy as jnp
from jax import lax
from jax.experimental import pallas as pl
from jax.experimental.pallas import tpu as pltpu
from jax.sharding import PartitionSpec as P

HEADS = 12
FF = 3072
SHORT = 512
BF = jnp.bfloat16
F32 = jnp.float32

eps_norm = 1e-05
decay = 0.5
rate_matrix = 0.2
rate_norm = 0.2
highest = lax.Precision.HIGHEST
VMEM_LIMIT = 60 * 1024 * 1024


def dot(a, b):
    return lax.dot_general(a, b, (((1,), (0,)), ((), ())), preferred_element_type=F32)


def dot_t(a, b):
    return lax.dot_general(a, b, (((1,), (1,)), ((), ())), preferred_element_type=F32)


def dot_l(a, b):
    return lax.dot_general(a, b, (((0,), (0,)), ((), ())), preferred_element_type=F32)


def vspec(shape, index_map, once=False):
    if once:
        return pl.BlockSpec(shape, index_map, pipeline_mode=pl.Buffered(1))
    return pl.BlockSpec(shape, index_map)


def params():
    return pltpu.CompilerParams(
        dimension_semantics=("arbitrary",), vmem_limit_bytes=VMEM_LIMIT
    )


def cost(flops, nbytes, trans=0):
    return pl.CostEstimate(flops=int(flops), bytes_accessed=int(nbytes), transcendentals=int(trans))


def project_body(width, with_query, x_ref, w_ref, e_ref, *outs):
    x = x_ref[...]
    if with_query:
        q_ref, kv_ref, p_ref = outs
        q_ref[...] = dot(x, w_ref[pl.ds(0, width), :]).astype(BF)
    else:
        (p_ref,) = outs
    e = e_ref[0]
    for part in range(2):
        kv = dot(x, w_ref[pl.ds((1 + part) * width, width), :]).astype(BF)
        if with_query:
            kv_ref[:, pl.ds(part * width, width)] = kv
        p_ref[0, :, pl.ds(part * width, width)] = dot(e, kv)


def project(x, w_att, e_t, with_query):
    rows, width = x.shape
    blocks, kp, short = e_t.shape
    out_shape = [jax.ShapeDtypeStruct((blocks, kp, 2 * width), F32)]
    out_specs = [vspec((1, kp, 2 * width), lambda i: (i, 0, 0))]
    if with_query:
        out_shape = [
            jax.ShapeDtypeStruct((rows, width), BF),
            jax.ShapeDtypeStruct((rows, 2 * width), BF),
        ] + out_shape
        out_specs = [
            vspec((short, width), lambda i: (i, 0)),
            vspec((short, 2 * width), lambda i: (i, 0)),
        ] + out_specs
    return pl.pallas_call(
        functools.partial(project_body, width, with_query),
        grid=(blocks,),
        in_specs=[
            vspec((short, width), lambda i: (i, 0)),
            vspec((3 * width, width), lambda i: (0, 0), True),
            vspec((1, kp, short), lambda i: (i, 0, 0)),
        ],
        out_specs=out_specs,
        out_shape=out_shape,
        compiler_params=params(),
        cost_estimate=cost(2 * rows * width * width * 3, 12e6),
        name="project" if with_query else "project_peer",
    )(x, w_att, e_t)


def head_pair(ref_slice, low_lane):
    zero = jnp.zeros_like(ref_slice)
    return jnp.concatenate(
        [jnp.where(low_lane, ref_slice, zero), jnp.where(low_lane, zero, ref_slice)], axis=0
    )


def softmax_pair(scores, kp):
    parts = []
    for half in range(2):
        s = scores[:, half * kp : (half + 1) * kp]
        top = jnp.max(s, axis=-1, keepdims=True)
        e = jnp.exp(s - top)
        parts.append(e * (1.0 / jnp.sum(e, axis=-1, keepdims=True)))
    return parts


def attend_body(width, head, kp, n_ref, q_ref, s_ref, w_ref, x_ref, mix_ref, sum_ref, stat_ref):
    pairs = width // (2 * head)
    step = pl.program_id(0)
    scale = head ** (-0.5)
    low_lane = lax.broadcasted_iota(jnp.int32, (kp, 2 * head), 1) < head
    for j in range(pairs):
        cols = pl.ds(j * 2 * head, 2 * head)
        keys = head_pair(s_ref[0, :, cols], low_lane)
        values = head_pair(s_ref[0, :, pl.ds(width + j * 2 * head, 2 * head)], low_lane)
        scores = dot_t(q_ref[:, cols], keys) * scale
        prob = jnp.concatenate(softmax_pair(scores, kp), axis=1).astype(BF)
        mix_ref[:, cols] = dot(prob, values).astype(BF)
    branch = dot(mix_ref[...], w_ref[...])
    first = x_ref[...].astype(F32) + branch
    sum_ref[...] = first
    rows = q_ref.shape[0]
    keep = (lax.broadcasted_iota(jnp.int32, (rows, 1), 0) < n_ref[step]).astype(F32)
    sums = jnp.concatenate(
        [
            jnp.sum(keep * first * first, axis=0, keepdims=True),
            jnp.sum(keep * branch * branch, axis=0, keepdims=True),
        ],
        axis=0,
    )

    @pl.when(step == 0)
    def _():
        stat_ref[...] = sums

    @pl.when(step > 0)
    def _():
        stat_ref[...] += sums


def attend(n_valid, q, summary, w_att, x, head):
    rows, width = q.shape
    blocks, kp, _ = summary.shape
    short = rows // blocks
    return pl.pallas_call(
        functools.partial(attend_body, width, head, kp),
        grid_spec=pltpu.PrefetchScalarGridSpec(
            num_scalar_prefetch=1,
            grid=(blocks,),
            in_specs=[
                vspec((short, width), lambda i, n: (i, 0)),
                vspec((1, kp, 2 * width), lambda i, n: (i, 0, 0)),
                vspec((width, width), lambda i, n: (3, 0), True),
                vspec((short, width), lambda i, n: (i, 0)),
            ],
            out_specs=[
                vspec((short, width), lambda i, n: (i, 0)),
                vspec((short, width), lambda i, n: (i, 0)),
                vspec((2, width), lambda i, n: (0, 0)),
            ],
        ),
        out_shape=[
            jax.ShapeDtypeStruct((rows, width), BF),
            jax.ShapeDtypeStruct((rows, width), F32),
            jax.ShapeDtypeStruct((2, width), F32),
        ],
        compiler_params=params(),
        cost_estimate=cost(2 * rows * width * (width + 4 * kp), 10e6, rows * kp * 12),
        name="attend",
    )(n_valid, q, summary, w_att, x)


def normalize(values):
    mean = jnp.mean(values, axis=-1, keepdims=True)
    centered = values - mean
    inverse = lax.rsqrt(jnp.mean(centered * centered, axis=-1, keepdims=True) + eps_norm)
    return centered * inverse, inverse


def norm_back(grad_out, normed, inverse, gain):
    scaled = grad_out * gain
    return inverse * (
        scaled
        - jnp.mean(scaled, axis=-1, keepdims=True)
        - normed * jnp.mean(scaled * normed, axis=-1, keepdims=True)
    )


def feed_body(
    chunks,
    first_ref,
    w1_ref,
    w2_ref,
    wo_ref,
    cot_ref,
    np_ref,
    out_ref,
    hid_ref,
    up_ref,
    down_ref,
    flow_ref,
    dfirst_ref,
    dbranch_ref,
    dmix_ref,
    ng_ref,
    slope_ref,
):
    step = pl.program_id(0)
    rows, width = first_ref.shape
    normed_one, inverse_one = normalize(first_ref[...])
    first_norm = normed_one * np_ref[0:1, :] + np_ref[1:2, :]
    first_low = first_norm.astype(BF)
    flow_ref[...] = first_low
    second = first_norm
    for c in range(chunks):
        cols = pl.ds(c * width, width)
        u = dot(first_low, w1_ref[:, c].reshape(width, width))
        cumulative = 0.5 * (1.0 + lax.erf(u * (1.0 / math.sqrt(2.0))))
        density = jnp.exp(-0.5 * u * u) * (1.0 / math.sqrt(2.0 * math.pi))
        slope_ref[:, cols] = cumulative + u * density
        hidden = (u * cumulative).astype(BF)
        hid_ref[:, cols] = hidden
        second = second + dot(hidden, w2_ref[pl.ds(c * width, width), :])
    normed_two, inverse_two = normalize(second)
    out_ref[...] = (normed_two * np_ref[2:3, :] + np_ref[3:4, :]).astype(BF)
    grad_out = cot_ref[...].astype(F32)
    gain_two = jnp.sum(grad_out * normed_two, axis=0, keepdims=True)
    shift_two = jnp.sum(grad_out, axis=0, keepdims=True)
    grad_second = norm_back(grad_out, normed_two, inverse_two, np_ref[2:3, :])
    down = grad_second.astype(BF)
    down_ref[...] = down
    grad_first_norm = grad_second
    for c in range(chunks):
        cols = pl.ds(c * width, width)
        grad_hidden = dot_t(down, w2_ref[pl.ds(c * width, width), :])
        up = (grad_hidden * slope_ref[:, cols]).astype(BF)
        up_ref[:, cols] = up
        grad_first_norm = grad_first_norm + dot_t(up, w1_ref[:, c].reshape(width, width))
    gain_one = jnp.sum(grad_first_norm * normed_one, axis=0, keepdims=True)
    shift_one = jnp.sum(grad_first_norm, axis=0, keepdims=True)
    grad_first = norm_back(grad_first_norm, normed_one, inverse_one, np_ref[0:1, :])
    dfirst_ref[...] = grad_first
    grad_branch = grad_first.astype(BF)
    dbranch_ref[...] = grad_branch
    dmix_ref[...] = dot_t(grad_branch, wo_ref[...]).astype(BF)
    sums = jnp.concatenate([gain_one, shift_one, gain_two, shift_two], axis=0)

    @pl.when(step == 0)
    def _():
        ng_ref[...] = sums

    @pl.when(step > 0)
    def _():
        ng_ref[...] += sums


def feed(first_sum, w_up, w_down, w_att, cotangent, norm_params, tile):
    rows, width = first_sum.shape
    chunks = w_up.shape[1]
    ff = chunks * width
    row = lambda i: (i, 0)
    return pl.pallas_call(
        functools.partial(feed_body, chunks),
        grid=(rows // tile,),
        in_specs=[
            vspec((tile, width), row),
            vspec(w_up.shape, lambda i: (0, 0, 0, 0), True),
            vspec((ff, width), lambda i: (0, 0), True),
            vspec((width, width), lambda i: (3, 0), True),
            vspec((tile, width), row),
            vspec(norm_params.shape, lambda i: (0, 0)),
        ],
        out_specs=[
            vspec((tile, width), row),
            vspec((tile, ff), row),
            vspec((tile, ff), row),
            vspec((tile, width), row),
            vspec((tile, width), row),
            vspec((tile, width), row),
            vspec((tile, width), row),
            vspec((tile, width), row),
            vspec((4, width), lambda i: (0, 0)),
        ],
        out_shape=[
            jax.ShapeDtypeStruct((rows, width), BF),
            jax.ShapeDtypeStruct((rows, ff), BF),
            jax.ShapeDtypeStruct((rows, ff), BF),
            jax.ShapeDtypeStruct((rows, width), BF),
            jax.ShapeDtypeStruct((rows, width), BF),
            jax.ShapeDtypeStruct((rows, width), F32),
            jax.ShapeDtypeStruct((rows, width), BF),
            jax.ShapeDtypeStruct((rows, width), BF),
            jax.ShapeDtypeStruct((4, width), F32),
        ],
        scratch_shapes=[pltpu.VMEM((tile, ff), F32)],
        compiler_params=params(),
        cost_estimate=cost(2 * rows * width * ff * 4, 30e6, rows * ff * 2),
        name="feed",
    )(first_sum, w_up, w_down, w_att, cotangent, norm_params)


def attend_back_body(width, head, kp, q_ref, s_ref, g_ref, dq_ref, ds_ref):
    pairs = width // (2 * head)
    scale = head ** (-0.5)
    low_lane = lax.broadcasted_iota(jnp.int32, (kp, 2 * head), 1) < head
    for j in range(pairs):
        cols = pl.ds(j * 2 * head, 2 * head)
        vcols = pl.ds(width + j * 2 * head, 2 * head)
        keys = head_pair(s_ref[0, :, cols], low_lane)
        values = head_pair(s_ref[0, :, vcols], low_lane)
        q = q_ref[:, cols]
        g = g_ref[:, cols]
        prob = softmax_pair(dot_t(q, keys) * scale, kp)
        grad_prob = dot_t(g, values)
        low_parts = []
        for half in range(2):
            p = prob[half]
            d = grad_prob[:, half * kp : (half + 1) * kp]
            low_parts.append((p * (d - jnp.sum(p * d, axis=-1, keepdims=True))).astype(BF))
        grad_scores = jnp.concatenate(low_parts, axis=1)
        prob_low = jnp.concatenate(prob, axis=1).astype(BF)
        dq_ref[:, cols] = (dot(grad_scores, keys) * scale).astype(BF)
        dk = dot_l(grad_scores, q) * scale
        dv = dot_l(prob_low, g)
        ds_ref[0, :, cols] = jnp.where(low_lane, dk[:kp], dk[kp:])
        ds_ref[0, :, vcols] = jnp.where(low_lane, dv[:kp], dv[kp:])


def attend_back(q, summary, grad_mix, head):
    rows, width = q.shape
    blocks, kp, _ = summary.shape
    short = rows // blocks
    return pl.pallas_call(
        functools.partial(attend_back_body, width, head, kp),
        grid=(blocks,),
        in_specs=[
            vspec((short, width), lambda i: (i, 0)),
            vspec((1, kp, 2 * width), lambda i: (i, 0, 0)),
            vspec((short, width), lambda i: (i, 0)),
        ],
        out_specs=[
            vspec((short, width), lambda i: (i, 0)),
            vspec((1, kp, 2 * width), lambda i: (i, 0, 0)),
        ],
        out_shape=[
            jax.ShapeDtypeStruct((rows, width), BF),
            jax.ShapeDtypeStruct((blocks, kp, 2 * width), F32),
        ],
        compiler_params=params(),
        cost_estimate=cost(2 * rows * width * 8 * kp, 10e6, rows * kp * 12),
        name="attend_back",
    )(q, summary, grad_mix)


def outer_body(split, l_ref, r_ref, o_ref):
    value = dot_l(l_ref[...], r_ref[...])
    o_ref[...] = value.reshape(o_ref.shape).astype(o_ref.dtype)


def outer_up(first_low, grad_up, size, dtype):
    rows, width = first_low.shape
    chunks = grad_up.shape[1] // width
    groups = width // size
    return pl.pallas_call(
        functools.partial(outer_body, True),
        grid=(chunks,),
        in_specs=[
            vspec((rows, width), lambda i: (0, 0), True),
            vspec((rows, width), lambda i: (0, i)),
        ],
        out_specs=vspec((groups, 1, size, width), lambda i: (0, i, 0, 0)),
        out_shape=jax.ShapeDtypeStruct((groups, chunks, size, width), dtype),
        compiler_params=params(),
        cost_estimate=cost(2 * rows * width * width * chunks, 20e6),
        name="outer_up",
    )(first_low, grad_up)


def outer_rows(left, right, dtype, name):
    rows, width = right.shape
    chunks = left.shape[1] // width
    return pl.pallas_call(
        functools.partial(outer_body, False),
        grid=(chunks,),
        in_specs=[
            vspec((rows, width), lambda i: (0, i)),
            vspec((rows, width), lambda i: (0, 0), True),
        ],
        out_specs=vspec((width, width), lambda i: (i, 0)),
        out_shape=jax.ShapeDtypeStruct((chunks * width, width), dtype),
        compiler_params=params(),
        cost_estimate=cost(2 * rows * width * width * chunks, 20e6),
        name=name,
    )(left, right)


def back_body(width, e_ref, kv_ref, s_ref, dq_ref, w_ref, df_ref, dkv_ref, ge_ref, gi_ref):
    summary = s_ref[0]
    dkv = dot(e_ref[0], summary).astype(BF)
    dkv_ref[...] = dkv
    ge_ref[0] = dot_t(kv_ref[...], summary)
    gi_ref[...] = (
        df_ref[...]
        + dot_t(dq_ref[...], w_ref[pl.ds(0, width), :])
        + dot_t(dkv[:, :width], w_ref[pl.ds(width, width), :])
        + dot_t(dkv[:, width:], w_ref[pl.ds(2 * width, width), :])
    )


def back(e_rows, kv, grad_summary, dq, w_att, grad_first):
    rows, width = dq.shape
    blocks, short, kp = e_rows.shape
    row = lambda i: (i, 0)
    lead = lambda i: (i, 0, 0)
    return pl.pallas_call(
        functools.partial(back_body, width),
        grid=(blocks,),
        in_specs=[
            vspec((1, short, kp), lead),
            vspec((short, 2 * width), row),
            vspec((1, kp, 2 * width), lead),
            vspec((short, width), row),
            vspec((3 * width, width), lambda i: (0, 0), True),
            vspec((short, width), row),
        ],
        out_specs=[
            vspec((short, 2 * width), row),
            vspec((1, short, kp), lead),
            vspec((short, width), row),
        ],
        out_shape=[
            jax.ShapeDtypeStruct((rows, 2 * width), BF),
            jax.ShapeDtypeStruct((blocks, short, kp), F32),
            jax.ShapeDtypeStruct((rows, width), F32),
        ],
        compiler_params=params(),
        cost_estimate=cost(2 * rows * width * (3 * width + 4 * kp), 20e6),
        name="back",
    )(e_rows, kv, grad_summary, dq, w_att, grad_first)


MESH_ID = pl.DeviceIdType.MESH


def reduce_body(depth, half, n_src, extra_keep, *refs):
    sources = refs[:n_src]
    outs = refs[n_src : n_src + 5]
    (own, got_c, sum_c, got_a, got_b, sum_a, sum_b, got_a2, got_b2, sum_z, got_z) = refs[
        n_src + 5 : n_src + 16
    ]
    (e_own, e_got, e_sum, e_got1, e_sum1, e_got2, e_sum2, e_gotz, e_all, e_rows) = refs[
        n_src + 16 : n_src + 26
    ]
    send, recv, local = refs[n_src + 26 :]
    seq, mine = lax.axis_index("seq"), lax.axis_index("own")
    z, y, x, c = seq // 2, seq % 2, mine // 2, mine % 2
    core = (seq, 2 * x + (1 - c))
    along_x = (seq, 2 * (1 - x) + c)
    along_y = (2 * z + (1 - y), mine)
    along_z = [(2 * lax.rem(z + d, depth) + y, mine) for d in range(1, depth)]
    barrier = pltpu.get_barrier_semaphore()
    partners = [core, along_x, along_y] + along_z
    for partner in partners:
        pl.semaphore_signal(barrier, inc=1, device_id=partner, device_id_type=MESH_ID)
    pl.semaphore_wait(barrier, len(partners))

    sent = []

    def push(src, dst, partner):
        at = len(sent)
        copy = pltpu.make_async_remote_copy(
            src_ref=src,
            dst_ref=dst,
            send_sem=send.at[at],
            recv_sem=recv.at[at],
            device_id=partner,
            device_id_type=MESH_ID,
        )
        copy.start()
        sent.append(copy)
        return copy

    pieces = 3
    up, down, extra = sources[0], sources[1], sources[6]
    half_z = depth // 2
    loads, firsts = [], []

    def load(src, dst):
        copy = pltpu.make_async_copy(src, dst, local.at[len(loads)])
        copy.start()
        loads.append(copy)
        return copy

    e_first = [push(extra.at[:, :, 1 - c], e_got, core)]
    e_load = [load(extra.at[:, :, c], e_own)]
    piece_first, piece_load = [], []
    for p in range(2):
        piece_first.append(
            [
                push(up.at[:, :, 1 - c, p], got_c.at[p, pl.ds(0, half_z)], core),
                push(down.at[:, :, 1 - c, p], got_c.at[p, pl.ds(half_z, half_z)], core),
            ]
        )
        piece_load.append(
            [
                load(up.at[:, :, c, p], own.at[p, pl.ds(0, half_z)]),
                load(down.at[:, :, c, p], own.at[p, pl.ds(half_z, half_z)]),
            ]
        )
    piece_first.append(
        [push(sources[2 + m].at[:, 1 - c], got_c.at[2, m], core) for m in range(depth)]
    )
    piece_load.append([load(sources[2 + m].at[:, c], own.at[2, m]) for m in range(depth)])

    state = {}

    def wait_recv(copies):
        for copy in copies:
            copy.wait_recv()

    def add(a, b):
        return (a.astype(F32) + b.astype(F32)).astype(BF)

    def piece_c(p):
        for copy in piece_load[p]:
            copy.wait()
        wait_recv(piece_first[p])

        def body(i, carry):
            zz, yx = i // 4, i % 4
            sum_c[p, zz, yx // 2, yx % 2] = add(own[p, zz, yx], got_c[p, zz, yx])
            return carry

        lax.fori_loop(0, depth * 4, body, 0)
        state["1", p] = [
            push(sum_c.at[p, :, :, 1 - x, pl.ds(0, half), :], got_a.at[p], along_x),
            push(sum_c.at[p, :, 1 - y, :, pl.ds(half, half), :], got_b.at[p], along_y),
        ]

    def piece_1(p):
        wait_recv(state["1", p])

        def body(i, carry):
            zz, w = i // 2, i % 2
            sum_a[p, zz, w] = add(sum_c[p, zz, w, x, pl.ds(0, half), :], got_a[p, zz, w])
            sum_b[p, zz, w] = add(sum_c[p, zz, y, w, pl.ds(half, half), :], got_b[p, zz, w])
            return carry

        lax.fori_loop(0, depth * 2, body, 0)
        state["2", p] = [
            push(sum_a.at[p, :, 1 - y], got_a2.at[p], along_y),
            push(sum_b.at[p, :, 1 - x], got_b2.at[p], along_x),
        ]

    def piece_2(p):
        wait_recv(state["2", p])

        def body(zz, carry):
            sum_z[p, zz, pl.ds(0, half), :] = add(sum_a[p, zz, y], got_a2[p, zz])
            sum_z[p, zz, pl.ds(half, half), :] = add(sum_b[p, zz, x], got_b2[p, zz])
            return carry

        lax.fori_loop(0, depth, body, 0)
        state["z", p] = [
            push(sum_z.at[p, lax.rem(z + d, depth)], got_z.at[p, d - 1], along_z[d - 1])
            for d in range(1, depth)
        ]

    def piece_z(p):
        wait_recv(state["z", p])
        total = sum_z[p, z].astype(F32)
        for d in range(depth - 1):
            total = total + got_z[p, d].astype(F32)
        outs[p][...] = total

    def extra_c():
        e_load[0].wait()
        wait_recv(e_first)

        def body(i, carry):
            zz, yx = i // 4, i % 4
            e_sum[zz, yx // 2, yx % 2] = e_own[zz, yx] + e_got[zz, yx]
            return carry

        lax.fori_loop(0, depth * 4, body, 0)
        state["e1"] = [push(e_sum.at[:, :, 1 - x], e_got1, along_x)]

    def extra_1():
        wait_recv(state["e1"])

        def body(i, carry):
            zz, yy = i // 2, i % 2
            e_sum1[zz, yy] = e_sum[zz, yy, x] + e_got1[zz, yy]
            return carry

        lax.fori_loop(0, depth * 2, body, 0)
        state["e2"] = [push(e_sum1.at[:, 1 - y], e_got2, along_y)]

    def extra_2():
        wait_recv(state["e2"])

        def body(zz, carry):
            e_sum2[zz] = e_sum1[zz, y] + e_got2[zz]
            return carry

        lax.fori_loop(0, depth, body, 0)
        state["ez"] = [
            push(e_sum2.at[lax.rem(z + d, depth)], e_gotz.at[d - 1], along_z[d - 1])
            for d in range(1, depth)
        ]

    def extra_z():
        wait_recv(state["ez"])
        total = e_sum2[z]
        for d in range(depth - 1):
            total = total + e_gotz[d]
        e_all[z, y] = total
        state["gz"] = [push(e_all.at[z, y], e_all.at[z, y], there) for there in along_z]

    def extra_gather_y():
        wait_recv(state["gz"])
        state["gy"] = [push(e_all.at[:, y], e_all.at[:, y], along_y)]

    def extra_gather_x():
        wait_recv(state["gy"])
        e_rows[x, c] = e_all[:, :, pl.ds(extra_keep, e_rows.shape[4]), :]
        state["gx"] = [push(e_rows.at[x, c], e_rows.at[x, c], along_x)]

    def extra_gather_c():
        wait_recv(state["gx"])
        state["gc"] = [push(e_rows.at[:, c], e_rows.at[:, c], core)]

    extra_c()
    piece_c(0)
    extra_1()
    piece_c(1)
    extra_2()
    piece_1(0)
    piece_c(2)
    extra_z()
    piece_2(0)
    piece_1(1)
    extra_gather_y()
    piece_1(2)
    piece_2(1)
    extra_gather_x()
    piece_z(0)
    piece_2(2)
    extra_gather_c()
    piece_z(1)
    piece_z(2)
    outs[3][...] = e_all[:, :, pl.ds(0, extra_keep), :]
    wait_recv(state["gc"])
    outs[4][...] = e_rows[...]
    for copy in sent:
        copy.wait_send()


def reduce_all(g_att, g_up, g_down, extra, peers):
    depth = peers // 2
    size, width = g_up.shape[2], g_up.shape[3]
    half = size // 2
    e_rows_all, kp = extra.shape[1], extra.shape[2]
    keep = e_rows_all - 8
    sources = (
        [
            g_up.reshape(depth // 2, 4, 2, 2, size, width),
            g_down.reshape(depth // 2, 4, 2, 2, size, width),
        ]
        + [g.reshape(4, 2, size, width) for g in g_att]
        + [extra.reshape(depth, 4, 2, e_rows_all, kp)]
    )
    n_src = len(sources)
    messages = 1 + 4 + depth + 3 * (4 + depth - 1) + 2 + 2 * (depth - 1) + 3
    loads = 1 + 4 + depth
    any_spec = pl.BlockSpec(memory_space=pl.ANY)
    vmem = pl.BlockSpec(memory_space=pltpu.VMEM)
    scratch = [
        pltpu.VMEM((3, depth, 4, size, width), BF),
        pltpu.VMEM((3, depth, 4, size, width), BF),
        pltpu.VMEM((3, depth, 2, 2, size, width), BF),
        pltpu.VMEM((3, depth, 2, half, width), BF),
        pltpu.VMEM((3, depth, 2, half, width), BF),
        pltpu.VMEM((3, depth, 2, half, width), BF),
        pltpu.VMEM((3, depth, 2, half, width), BF),
        pltpu.VMEM((3, depth, half, width), BF),
        pltpu.VMEM((3, depth, half, width), BF),
        pltpu.VMEM((3, depth, size, width), BF),
        pltpu.VMEM((3, depth - 1, size, width), BF),
        pltpu.VMEM((depth, 4, e_rows_all, kp), F32),
        pltpu.VMEM((depth, 4, e_rows_all, kp), F32),
        pltpu.VMEM((depth, 2, 2, e_rows_all, kp), F32),
        pltpu.VMEM((depth, 2, e_rows_all, kp), F32),
        pltpu.VMEM((depth, 2, e_rows_all, kp), F32),
        pltpu.VMEM((depth, e_rows_all, kp), F32),
        pltpu.VMEM((depth, e_rows_all, kp), F32),
        pltpu.VMEM((depth - 1, e_rows_all, kp), F32),
        pltpu.VMEM((depth, 2, e_rows_all, kp), F32),
        pltpu.VMEM((2, 2, depth, 2, 8, kp), F32),
        pltpu.SemaphoreType.DMA((messages,)),
        pltpu.SemaphoreType.DMA((messages,)),
        pltpu.SemaphoreType.DMA((loads,)),
    ]
    return pl.pallas_call(
        functools.partial(reduce_body, depth, half, n_src, keep),
        in_specs=[any_spec] * n_src,
        out_specs=[vmem] * 5,
        out_shape=[jax.ShapeDtypeStruct((size, width), F32)] * 3
        + [
            jax.ShapeDtypeStruct((depth, 2, keep, kp), F32),
            jax.ShapeDtypeStruct((2, 2, depth, 2, 8, kp), F32),
        ],
        scratch_shapes=scratch,
        compiler_params=pltpu.CompilerParams(
            collective_id=1, has_side_effects=True, vmem_limit_bytes=VMEM_LIMIT
        ),
        name="reduce_all",
    )(*sources)


def shampoo(grad, left, right, root_left, root_right, weight):
    new_left = decay * left + (1.0 - decay) * jnp.einsum(
        "tij,tkj->tik", grad, grad, precision=highest
    )
    new_right = decay * right + (1.0 - decay) * jnp.einsum(
        "tji,tjk->tik", grad, grad, precision=highest
    )
    inner = jnp.einsum("tij,tjk->tik", grad, root_right, precision=highest)
    step = jnp.einsum("tij,tjk->tik", root_left, inner, precision=highest)
    return (new_left, new_right, weight - rate_matrix * step)


def to_matrix(tiles, rows, cols):
    size = tiles.shape[-1]
    return (
        tiles.reshape(rows // size, cols // size, size, size)
        .transpose(0, 2, 1, 3)
        .reshape(rows, cols)
    )


def to_bands(tiles, cols):
    count, size, _ = tiles.shape
    return to_matrix(tiles, count * size * size // cols, cols)


def from_bands(bands, size):
    rows, cols = bands.shape
    return (
        bands.reshape(rows // size, size, cols // size, size)
        .transpose(0, 2, 1, 3)
        .reshape(-1, size, size)
    )


def gather_weights(weights, att_dev, width, both):
    size = weights.shape[-1]
    low = weights.astype(BF)
    groups, chunks = width // size, FF // width
    if banded(weights.shape[0], att_dev, width, size):
        att = lax.all_gather(to_bands(low[:att_dev], width), both, axis=0, tiled=True)
        ffn = lax.all_gather(to_bands(low[att_dev:], width), both, axis=0, tiled=True)
        half = ffn.shape[0] // 2
        return att, ffn[:half].reshape(groups, chunks, size, width), ffn[half:]
    per_dev = weights.shape[0]
    grid = lax.all_gather(low, both, axis=0, tiled=True).reshape(-1, per_dev, size, size)
    att = to_bands(grid[:, :att_dev].reshape(-1, size, size), width)
    tiles = grid[:, att_dev:].reshape(-1, size, size)
    half = tiles.shape[0] // 2
    w_up = to_matrix(tiles[:half], width, FF).reshape(groups, size, chunks, width)
    return att, w_up.transpose(0, 2, 1, 3), to_matrix(tiles[half:], FF, width)


def banded(per_dev, att_dev, width, size):
    wide = width // size
    return att_dev % wide == 0 and (per_dev - att_dev) % wide == 0


def scatter_weight_grads(g_att, g_up, g_down, per_dev, att_dev, both):
    size, width = g_up.shape[2], g_up.shape[3]
    if banded(per_dev, att_dev, width, size):
        ffn = jnp.concatenate([g_up.reshape(-1, width), g_down], axis=0)
        ffn = lax.psum_scatter(ffn, both, scatter_dimension=0, tiled=True)
        att = lax.psum_scatter(g_att, both, scatter_dimension=0, tiled=True)
        return jnp.concatenate([from_bands(att, size), from_bands(ffn, size)], axis=0)
    up = g_up.transpose(0, 2, 1, 3).reshape(width, -1)
    att = from_bands(g_att, size)
    ffn = jnp.concatenate([from_bands(up, size), from_bands(g_down, size)], axis=0)
    stacked = jnp.concatenate(
        [
            att.reshape(-1, att_dev, size, size),
            ffn.reshape(-1, per_dev - att_dev, size, size),
        ],
        axis=1,
    ).reshape(-1, size, size)
    return lax.psum_scatter(stacked, both, scatter_dimension=0, tiled=True)


def per_device(
    tokens,
    cotangent,
    lengths,
    offsets,
    valid_count,
    weights,
    stat_left,
    stat_right,
    root_left,
    root_right,
    projection,
    projection_left,
    projection_right,
    projection_root_left,
    projection_root_right,
    norm_params,
    norm_stat,
):
    both = ("seq", "own")
    size = weights.shape[-1]
    width = tokens.shape[-1]
    rows_here = tokens.shape[1]
    head = width // HEADS
    kp = projection.shape[1]
    blocks = rows_here // SHORT
    peers = lax.axis_size("seq")
    devices = peers * lax.axis_size("own")
    per_dev = weights.shape[0]
    att_dev = 4 * (width // size) ** 2 // devices
    x = tokens[0]
    seq = lax.axis_index("seq")
    side = seq % 2

    swap = [(i, i ^ 1) for i in range(peers)]
    peer_x = lax.ppermute(x, "seq", swap)
    proj_all = lax.all_gather(projection.astype(BF), "own", axis=0, tiled=True)
    w_att, w_up, w_down = gather_weights(weights, att_dev, width, both)

    lens, offs, counts = lengths[0], offsets[0], valid_count[0]
    ends = jnp.cumsum(lens)
    starts = ends - lens
    unit_rows = 2 * rows_here
    unit_start = (seq - side) * rows_here
    unit_end = unit_start + unit_rows
    block_row = unit_start + SHORT * jnp.arange(2 * blocks, dtype=jnp.int32)
    hot = ((starts[None, :] <= block_row[:, None]) & (block_row[:, None] < ends[None, :])).astype(
        jnp.int32
    )
    b_start = jnp.sum(hot * starts[None, :], axis=1)
    b_end = jnp.sum(hot * ends[None, :], axis=1)
    place = block_row - b_start
    column = jnp.sum(hot * offs[None, :], axis=1) + place
    n_valid = jnp.clip(jnp.sum(hot * counts[None, :], axis=1) - place, 0, SHORT)
    is_head = b_start == b_start[0]
    is_tail = b_start == b_start[-1]
    own_at = side * blocks
    peer_at = (1 - side) * blocks
    take = lambda v, at: lax.dynamic_slice_in_dim(v, at, blocks, 0)

    def proj_rows(at):
        col, n = take(column, at), take(n_valid, at)
        rows = jnp.stack(
            [lax.dynamic_slice_in_dim(proj_all, col[b], SHORT, 0) for b in range(blocks)]
        )
        keep = lax.broadcasted_iota(jnp.int32, (blocks, SHORT, 1), 1) < n[:, None, None]
        return jnp.where(keep, rows, jnp.zeros((), BF))

    e_own = proj_rows(own_at)
    e_own_t = e_own.transpose(0, 2, 1)
    e_peer_t = proj_rows(peer_at).transpose(0, 2, 1)
    n_own = take(n_valid, own_at)

    query, keyval, part_own = project(x, w_att, e_own_t, True)
    (part_peer,) = project(peer_x, w_att, e_peer_t, False)
    coef = lambda flag, at: take(flag, at).astype(F32)

    def unit_sum(flag):
        mine = coef(flag, own_at)
        theirs = coef(flag, peer_at)
        total = mine[0] * part_own[0]
        for b in range(1, blocks):
            total = total + mine[b] * part_own[b]
        for b in range(blocks):
            total = total + theirs[b] * part_peer[b]
        return total

    head_sum, tail_sum = unit_sum(is_head), unit_sum(is_tail)
    from_left = lax.ppermute(tail_sum, "seq", [(i, i + 2) for i in range(peers - 2)])
    from_right = lax.ppermute(head_sum, "seq", [(i + 2, i) for i in range(peers - 2)])
    head_cross = (b_start[0] < unit_start).astype(F32)
    tail_cross = (b_end[-1] > unit_end).astype(F32)
    own_head, own_tail = coef(is_head, own_at), coef(is_tail, own_at)
    summary = jnp.stack(
        [
            jnp.where(
                own_head[b] > 0,
                head_sum + head_cross * from_left,
                jnp.where(own_tail[b] > 0, tail_sum + tail_cross * from_right, part_own[b]),
            ).astype(BF)
            for b in range(blocks)
        ]
    )
    mixed, first_sum, row_sums = attend(n_own, query, summary, w_att, x, head)
    (
        result,
        hidden,
        grad_up,
        grad_down,
        first_low,
        grad_first,
        grad_branch,
        grad_mix,
        norm_terms,
    ) = feed(first_sum, w_up, w_down, w_att, cotangent[0], norm_params, 256)
    grad_query, grad_parts = attend_back(query, summary, grad_mix, head)

    row_start = seq * rows_here
    row_end = row_start + rows_here
    o_start, o_end = take(b_start, own_at), take(b_end, own_at)
    same = (o_start[0] == o_start[-1]).astype(F32)
    g_head = grad_parts[0]
    g_tail = grad_parts[-1]
    for b in range(1, blocks):
        g_head = g_head + (o_start[b] == o_start[0]).astype(F32) * grad_parts[b]
    for b in range(blocks - 1):
        g_tail = g_tail + (o_start[b] == o_start[-1]).astype(F32) * grad_parts[b]
    low_head, low_tail = g_head.astype(BF), g_tail.astype(BF)
    left_sum = jnp.zeros_like(g_head)
    right_sum = jnp.zeros_like(g_head)
    for far in (1, 2):
        tail_far = lax.ppermute(low_tail, "seq", [(i, i + far) for i in range(peers - far)])
        head_far = lax.ppermute(low_head, "seq", [(i + far, i) for i in range(peers - far)])
        reach = (far - 1) * rows_here
        left_sum = left_sum + (o_start[0] < row_start - reach).astype(F32) * tail_far.astype(F32)
        right_sum = right_sum + (o_end[-1] > row_end + reach).astype(F32) * head_far.astype(F32)
    at_head = (o_start == o_start[0]).astype(F32)
    grad_summary = jnp.stack(
        [
            jnp.where(
                at_head[b] > 0, g_head + left_sum + same * right_sum, g_tail + right_sum
            ).astype(BF)
            for b in range(blocks)
        ]
    )
    own_size = lax.axis_size("own")
    fused = own_size == 4 and peers == 8 and banded(per_dev, att_dev, width, size)
    gtype = BF if fused else F32
    g_up = outer_up(first_low, grad_up, size, gtype)
    g_down = outer_rows(hidden, grad_down, gtype, "outer_down")
    g_out = outer_rows(mixed, grad_branch, gtype, "outer_out")
    g_query = outer_rows(x, grad_query, gtype, "outer_query")
    grad_keyval, grad_e, grad_input = back(e_own, keyval, grad_summary, grad_query, w_att, grad_first)
    g_key = outer_rows(x, grad_keyval[:, :width], gtype, "outer_key")
    g_value = outer_rows(x, grad_keyval[:, width:], gtype, "outer_value")
    g_att = [g_query, g_key, g_value, g_out]

    part_rows = projection.shape[0]
    grad_proj = jnp.zeros((proj_all.shape[0], kp), F32)
    keep_e = lax.broadcasted_iota(jnp.int32, (blocks, SHORT, 1), 1) < n_own[:, None, None]
    grad_e = jnp.where(keep_e, grad_e, 0.0)
    own_col = take(column, own_at)
    for b in range(blocks):
        current = lax.dynamic_slice_in_dim(grad_proj, own_col[b], SHORT, 0)
        grad_proj = lax.dynamic_update_slice_in_dim(grad_proj, current + grad_e[b], own_col[b], 0)
    valid_here = jnp.sum(n_own).astype(F32)
    extra = jnp.concatenate(
        [
            norm_terms.reshape(-1, kp),
            row_sums.reshape(-1, kp),
            jnp.full((1, kp), 1.0 / kp, F32) * valid_here,
        ],
        axis=0,
    )
    n_norm = 4 * width // kp
    n_row = 2 * width // kp
    if fused:
        extra = jnp.pad(extra, ((0, devices - extra.shape[0]), (0, 0)))[:, None, :]
        extra = jnp.pad(extra, ((0, 0), (0, 7), (0, 0)))
        shares = grad_proj.reshape(own_size, peers, part_rows // peers, kp).swapaxes(0, 1)
        shares = shares.reshape(devices, part_rows // peers, kp)
        ffn_a, ffn_b, att, proj_parts, rows = reduce_all(
            g_att, g_up, g_down, jnp.concatenate([shares, extra], axis=1), peers
        )
        owned = jnp.concatenate(
            [from_bands(att, size), from_bands(ffn_a, size), from_bands(ffn_b, size)], axis=0
        )
        proj_grad = proj_parts.reshape(part_rows, kp)
        totals = rows[..., 0, :].transpose(2, 3, 0, 1, 4).reshape(devices, kp)
    else:
        owned = scatter_weight_grads(
            jnp.concatenate(g_att, axis=0), g_up, g_down, per_dev, att_dev, both
        )
        packed = jnp.concatenate([grad_proj, extra], axis=0)
        packed = lax.psum(jnp.pad(packed, ((0, -packed.shape[0] % 16), (0, 0))), both)
        proj_grad = lax.dynamic_slice_in_dim(
            packed, lax.axis_index("own") * part_rows, part_rows, 0
        )
        totals = packed[grad_proj.shape[0] :]
    norm_grad = totals[:n_norm].reshape(4, width)
    row_total = totals[n_norm : n_norm + n_row].reshape(2, width).sum(axis=1)
    valid_total = totals[n_norm + n_row].sum()
    residual_rms = jnp.sqrt(row_total / (valid_total * width))
    left_new, right_new, weights_new = shampoo(
        owned, stat_left, stat_right, root_left, root_right, weights
    )
    proj_left_new, proj_right_new, proj_blocks = shampoo(
        proj_grad.reshape(-1, kp, kp),
        projection_left,
        projection_right,
        projection_root_left,
        projection_root_right,
        projection.reshape(-1, kp, kp),
    )
    stat_new = decay * norm_stat + (1.0 - decay) * norm_grad * norm_grad
    norm_new = norm_params - rate_norm * norm_grad * lax.rsqrt(stat_new)
    return (
        result[None],
        grad_input[None],
        owned,
        left_new,
        right_new,
        weights_new,
        proj_grad,
        proj_left_new,
        proj_right_new,
        proj_blocks.reshape(part_rows, kp),
        norm_grad,
        stat_new,
        norm_new,
        residual_rms,
    )


def solution(mesh):
    pack = P("own", "seq", None)
    table = P("own", None)
    tile = P(("seq", "own"), None, None)
    proj = P("own", None, None)
    return jax.shard_map(
        per_device,
        mesh=mesh,
        in_specs=(pack, pack, table, table, table)
        + (tile,) * 5
        + (table, proj, proj, proj, proj, P(), P()),
        out_specs=(pack, pack) + (tile,) * 4 + (table, proj, proj, table, P(), P(), P(), P()),
        check_vma=False,
    )
```

```python
import functools
import math

import jax
import jax.numpy as jnp
from jax import lax
from jax.experimental import pallas as pl
from jax.experimental.pallas import tpu as pltpu
from jax.sharding import PartitionSpec as P

HEADS = 12
FF = 3072
SHORT = 512
BF = jnp.bfloat16
F32 = jnp.float32

eps_norm = 1e-05
decay = 0.5
rate_matrix = 0.2
rate_norm = 0.2
highest = lax.Precision.HIGHEST
VMEM_LIMIT = 60 * 1024 * 1024


def dot(a, b):
    return lax.dot_general(a, b, (((1,), (0,)), ((), ())), preferred_element_type=F32)


def dot_t(a, b):
    return lax.dot_general(a, b, (((1,), (1,)), ((), ())), preferred_element_type=F32)


def dot_l(a, b):
    return lax.dot_general(a, b, (((0,), (0,)), ((), ())), preferred_element_type=F32)


def vspec(shape, index_map, once=False):
    if once:
        return pl.BlockSpec(shape, index_map, pipeline_mode=pl.Buffered(1))
    return pl.BlockSpec(shape, index_map)


def params():
    return pltpu.CompilerParams(
        dimension_semantics=("arbitrary",), vmem_limit_bytes=VMEM_LIMIT
    )


def cost(flops, nbytes, trans=0):
    return pl.CostEstimate(flops=int(flops), bytes_accessed=int(nbytes), transcendentals=int(trans))


def project_body(width, with_query, x_ref, w_ref, e_ref, *outs):
    x = x_ref[...]
    if with_query:
        q_ref, kv_ref, p_ref = outs
        q_ref[...] = dot(x, w_ref[pl.ds(0, width), :]).astype(BF)
    else:
        (p_ref,) = outs
    e = e_ref[0]
    for part in range(2):
        kv = dot(x, w_ref[pl.ds((1 + part) * width, width), :]).astype(BF)
        if with_query:
            kv_ref[:, pl.ds(part * width, width)] = kv
        p_ref[0, :, pl.ds(part * width, width)] = dot(e, kv)


def project(x, w_att, e_t, with_query):
    rows, width = x.shape
    blocks, kp, short = e_t.shape
    out_shape = [jax.ShapeDtypeStruct((blocks, kp, 2 * width), F32)]
    out_specs = [vspec((1, kp, 2 * width), lambda i: (i, 0, 0))]
    if with_query:
        out_shape = [
            jax.ShapeDtypeStruct((rows, width), BF),
            jax.ShapeDtypeStruct((rows, 2 * width), BF),
        ] + out_shape
        out_specs = [
            vspec((short, width), lambda i: (i, 0)),
            vspec((short, 2 * width), lambda i: (i, 0)),
        ] + out_specs
    return pl.pallas_call(
        functools.partial(project_body, width, with_query),
        grid=(blocks,),
        in_specs=[
            vspec((short, width), lambda i: (i, 0)),
            vspec((3 * width, width), lambda i: (0, 0), True),
            vspec((1, kp, short), lambda i: (i, 0, 0)),
        ],
        out_specs=out_specs,
        out_shape=out_shape,
        compiler_params=params(),
        cost_estimate=cost(2 * rows * width * width * 3, 12e6),
        name="project" if with_query else "project_peer",
    )(x, w_att, e_t)


def head_pair(ref_slice, low_lane):
    zero = jnp.zeros_like(ref_slice)
    return jnp.concatenate(
        [jnp.where(low_lane, ref_slice, zero), jnp.where(low_lane, zero, ref_slice)], axis=0
    )


def softmax_pair(scores, kp):
    parts = []
    for half in range(2):
        s = scores[:, half * kp : (half + 1) * kp]
        top = jnp.max(s, axis=-1, keepdims=True)
        e = jnp.exp(s - top)
        parts.append(e * (1.0 / jnp.sum(e, axis=-1, keepdims=True)))
    return parts


def attend_body(width, head, kp, n_ref, q_ref, s_ref, w_ref, x_ref, mix_ref, sum_ref, stat_ref):
    pairs = width // (2 * head)
    step = pl.program_id(0)
    scale = head ** (-0.5)
    low_lane = lax.broadcasted_iota(jnp.int32, (kp, 2 * head), 1) < head
    for j in range(pairs):
        cols = pl.ds(j * 2 * head, 2 * head)
        keys = head_pair(s_ref[0, :, cols], low_lane)
        values = head_pair(s_ref[0, :, pl.ds(width + j * 2 * head, 2 * head)], low_lane)
        scores = dot_t(q_ref[:, cols], keys) * scale
        prob = jnp.concatenate(softmax_pair(scores, kp), axis=1).astype(BF)
        mix_ref[:, cols] = dot(prob, values).astype(BF)
    branch = dot(mix_ref[...], w_ref[...])
    first = x_ref[...].astype(F32) + branch
    sum_ref[...] = first
    rows = q_ref.shape[0]
    keep = (lax.broadcasted_iota(jnp.int32, (rows, 1), 0) < n_ref[step]).astype(F32)
    sums = jnp.concatenate(
        [
            jnp.sum(keep * first * first, axis=0, keepdims=True),
            jnp.sum(keep * branch * branch, axis=0, keepdims=True),
        ],
        axis=0,
    )

    @pl.when(step == 0)
    def _():
        stat_ref[...] = sums

    @pl.when(step > 0)
    def _():
        stat_ref[...] += sums


def attend(n_valid, q, summary, w_att, x, head):
    rows, width = q.shape
    blocks, kp, _ = summary.shape
    short = rows // blocks
    return pl.pallas_call(
        functools.partial(attend_body, width, head, kp),
        grid_spec=pltpu.PrefetchScalarGridSpec(
            num_scalar_prefetch=1,
            grid=(blocks,),
            in_specs=[
                vspec((short, width), lambda i, n: (i, 0)),
                vspec((1, kp, 2 * width), lambda i, n: (i, 0, 0)),
                vspec((width, width), lambda i, n: (3, 0), True),
                vspec((short, width), lambda i, n: (i, 0)),
            ],
            out_specs=[
                vspec((short, width), lambda i, n: (i, 0)),
                vspec((short, width), lambda i, n: (i, 0)),
                vspec((2, width), lambda i, n: (0, 0)),
            ],
        ),
        out_shape=[
            jax.ShapeDtypeStruct((rows, width), BF),
            jax.ShapeDtypeStruct((rows, width), F32),
            jax.ShapeDtypeStruct((2, width), F32),
        ],
        compiler_params=params(),
        cost_estimate=cost(2 * rows * width * (width + 4 * kp), 10e6, rows * kp * 12),
        name="attend",
    )(n_valid, q, summary, w_att, x)


def normalize(values):
    mean = jnp.mean(values, axis=-1, keepdims=True)
    centered = values - mean
    inverse = lax.rsqrt(jnp.mean(centered * centered, axis=-1, keepdims=True) + eps_norm)
    return centered * inverse, inverse


def norm_back(grad_out, normed, inverse, gain):
    scaled = grad_out * gain
    return inverse * (
        scaled
        - jnp.mean(scaled, axis=-1, keepdims=True)
        - normed * jnp.mean(scaled * normed, axis=-1, keepdims=True)
    )


def feed_body(
    chunks,
    first_ref,
    w1_ref,
    w2_ref,
    wo_ref,
    cot_ref,
    np_ref,
    out_ref,
    hid_ref,
    up_ref,
    down_ref,
    flow_ref,
    dfirst_ref,
    dbranch_ref,
    dmix_ref,
    ng_ref,
    slope_ref,
):
    step = pl.program_id(0)
    rows, width = first_ref.shape
    deep = w2_ref.shape[0] // chunks
    down_rows = lambda c: w2_ref[pl.ds(c * deep, deep)].reshape(width, width)
    normed_one, inverse_one = normalize(first_ref[...])
    first_norm = normed_one * np_ref[0:1, :] + np_ref[1:2, :]
    first_low = first_norm.astype(BF)
    flow_ref[...] = first_low
    second = first_norm
    for c in range(chunks):
        cols = pl.ds(c * width, width)
        u = dot(first_low, w1_ref[:, c].reshape(width, width))
        cumulative = 0.5 * (1.0 + lax.erf(u * (1.0 / math.sqrt(2.0))))
        density = jnp.exp(-0.5 * u * u) * (1.0 / math.sqrt(2.0 * math.pi))
        slope_ref[:, cols] = cumulative + u * density
        hidden = (u * cumulative).astype(BF)
        hid_ref[:, cols] = hidden
        second = second + dot(hidden, down_rows(c))
    normed_two, inverse_two = normalize(second)
    out_ref[...] = (normed_two * np_ref[2:3, :] + np_ref[3:4, :]).astype(BF)
    grad_out = cot_ref[...].astype(F32)
    gain_two = jnp.sum(grad_out * normed_two, axis=0, keepdims=True)
    shift_two = jnp.sum(grad_out, axis=0, keepdims=True)
    grad_second = norm_back(grad_out, normed_two, inverse_two, np_ref[2:3, :])
    down = grad_second.astype(BF)
    down_ref[...] = down
    grad_first_norm = grad_second
    for c in range(chunks):
        cols = pl.ds(c * width, width)
        grad_hidden = dot_t(down, down_rows(c))
        up = (grad_hidden * slope_ref[:, cols]).astype(BF)
        up_ref[:, cols] = up
        grad_first_norm = grad_first_norm + dot_t(up, w1_ref[:, c].reshape(width, width))
    gain_one = jnp.sum(grad_first_norm * normed_one, axis=0, keepdims=True)
    shift_one = jnp.sum(grad_first_norm, axis=0, keepdims=True)
    grad_first = norm_back(grad_first_norm, normed_one, inverse_one, np_ref[0:1, :])
    dfirst_ref[...] = grad_first
    grad_branch = grad_first.astype(BF)
    dbranch_ref[...] = grad_branch
    dmix_ref[...] = dot_t(grad_branch, wo_ref[...]).astype(BF)
    sums = jnp.concatenate([gain_one, shift_one, gain_two, shift_two], axis=0)

    @pl.when(step == 0)
    def _():
        ng_ref[...] = sums

    @pl.when(step > 0)
    def _():
        ng_ref[...] += sums


def feed(first_sum, w_ffn, w_att, cotangent, norm_params, tile):
    rows, width = first_sum.shape
    groups, chunks, size, _ = w_ffn.shape
    groups = groups // 2
    ff = chunks * width
    row = lambda i: (i, 0)
    return pl.pallas_call(
        functools.partial(feed_body, chunks),
        grid=(rows // tile,),
        in_specs=[
            vspec((tile, width), row),
            vspec((groups, chunks, size, width), lambda i: (0, 0, 0, 0), True),
            vspec((groups, chunks, size, width), lambda i: (1, 0, 0, 0), True),
            vspec((width, width), lambda i: (3, 0), True),
            vspec((tile, width), row),
            vspec(norm_params.shape, lambda i: (0, 0)),
        ],
        out_specs=[
            vspec((tile, width), row),
            vspec((tile, ff), row),
            vspec((tile, ff), row),
            vspec((tile, width), row),
            vspec((tile, width), row),
            vspec((tile, width), row),
            vspec((tile, width), row),
            vspec((tile, width), row),
            vspec((4, width), lambda i: (0, 0)),
        ],
        out_shape=[
            jax.ShapeDtypeStruct((rows, width), BF),
            jax.ShapeDtypeStruct((rows, ff), BF),
            jax.ShapeDtypeStruct((rows, ff), BF),
            jax.ShapeDtypeStruct((rows, width), BF),
            jax.ShapeDtypeStruct((rows, width), BF),
            jax.ShapeDtypeStruct((rows, width), F32),
            jax.ShapeDtypeStruct((rows, width), BF),
            jax.ShapeDtypeStruct((rows, width), BF),
            jax.ShapeDtypeStruct((4, width), F32),
        ],
        scratch_shapes=[pltpu.VMEM((tile, ff), F32)],
        compiler_params=params(),
        cost_estimate=cost(2 * rows * width * ff * 4, 30e6, rows * ff * 2),
        name="feed",
    )(first_sum, w_ffn, w_ffn, w_att, cotangent, norm_params)


def attend_back_body(width, head, kp, q_ref, s_ref, g_ref, dq_ref, ds_ref):
    pairs = width // (2 * head)
    scale = head ** (-0.5)
    low_lane = lax.broadcasted_iota(jnp.int32, (kp, 2 * head), 1) < head
    for j in range(pairs):
        cols = pl.ds(j * 2 * head, 2 * head)
        vcols = pl.ds(width + j * 2 * head, 2 * head)
        keys = head_pair(s_ref[0, :, cols], low_lane)
        values = head_pair(s_ref[0, :, vcols], low_lane)
        q = q_ref[:, cols]
        g = g_ref[:, cols]
        prob = softmax_pair(dot_t(q, keys) * scale, kp)
        grad_prob = dot_t(g, values)
        low_parts = []
        for half in range(2):
            p = prob[half]
            d = grad_prob[:, half * kp : (half + 1) * kp]
            low_parts.append((p * (d - jnp.sum(p * d, axis=-1, keepdims=True))).astype(BF))
        grad_scores = jnp.concatenate(low_parts, axis=1)
        prob_low = jnp.concatenate(prob, axis=1).astype(BF)
        dq_ref[:, cols] = (dot(grad_scores, keys) * scale).astype(BF)
        dk = dot_l(grad_scores, q) * scale
        dv = dot_l(prob_low, g)
        ds_ref[0, :, cols] = jnp.where(low_lane, dk[:kp], dk[kp:])
        ds_ref[0, :, vcols] = jnp.where(low_lane, dv[:kp], dv[kp:])


def attend_back(q, summary, grad_mix, head):
    rows, width = q.shape
    blocks, kp, _ = summary.shape
    short = rows // blocks
    return pl.pallas_call(
        functools.partial(attend_back_body, width, head, kp),
        grid=(blocks,),
        in_specs=[
            vspec((short, width), lambda i: (i, 0)),
            vspec((1, kp, 2 * width), lambda i: (i, 0, 0)),
            vspec((short, width), lambda i: (i, 0)),
        ],
        out_specs=[
            vspec((short, width), lambda i: (i, 0)),
            vspec((1, kp, 2 * width), lambda i: (i, 0, 0)),
        ],
        out_shape=[
            jax.ShapeDtypeStruct((rows, width), BF),
            jax.ShapeDtypeStruct((blocks, kp, 2 * width), F32),
        ],
        compiler_params=params(),
        cost_estimate=cost(2 * rows * width * 8 * kp, 10e6, rows * kp * 12),
        name="attend_back",
    )(q, summary, grad_mix)


def outer_body(split, l_ref, r_ref, o_ref):
    value = dot_l(l_ref[...], r_ref[...])
    o_ref[...] = value.reshape(o_ref.shape).astype(o_ref.dtype)


def outer_up(first_low, grad_up, size, dtype):
    rows, width = first_low.shape
    chunks = grad_up.shape[1] // width
    groups = width // size
    return pl.pallas_call(
        functools.partial(outer_body, True),
        grid=(chunks,),
        in_specs=[
            vspec((rows, width), lambda i: (0, 0), True),
            vspec((rows, width), lambda i: (0, i)),
        ],
        out_specs=vspec((groups, 1, size, width), lambda i: (0, i, 0, 0)),
        out_shape=jax.ShapeDtypeStruct((groups, chunks, size, width), dtype),
        compiler_params=params(),
        cost_estimate=cost(2 * rows * width * width * chunks, 20e6),
        name="outer_up",
    )(first_low, grad_up)


def outer_rows(left, right, dtype, name):
    rows, width = right.shape
    chunks = left.shape[1] // width
    return pl.pallas_call(
        functools.partial(outer_body, False),
        grid=(chunks,),
        in_specs=[
            vspec((rows, width), lambda i: (0, i)),
            vspec((rows, width), lambda i: (0, 0), True),
        ],
        out_specs=vspec((width, width), lambda i: (i, 0)),
        out_shape=jax.ShapeDtypeStruct((chunks * width, width), dtype),
        compiler_params=params(),
        cost_estimate=cost(2 * rows * width * width * chunks, 20e6),
        name=name,
    )(left, right)


def back_body(width, e_ref, kv_ref, s_ref, dq_ref, w_ref, df_ref, dkv_ref, ge_ref, gi_ref):
    summary = s_ref[0]
    dkv = dot(e_ref[0], summary).astype(BF)
    dkv_ref[...] = dkv
    ge_ref[0] = dot_t(kv_ref[...], summary)
    gi_ref[...] = (
        df_ref[...]
        + dot_t(dq_ref[...], w_ref[pl.ds(0, width), :])
        + dot_t(dkv[:, :width], w_ref[pl.ds(width, width), :])
        + dot_t(dkv[:, width:], w_ref[pl.ds(2 * width, width), :])
    )


def back(e_rows, kv, grad_summary, dq, w_att, grad_first):
    rows, width = dq.shape
    blocks, short, kp = e_rows.shape
    row = lambda i: (i, 0)
    lead = lambda i: (i, 0, 0)
    return pl.pallas_call(
        functools.partial(back_body, width),
        grid=(blocks,),
        in_specs=[
            vspec((1, short, kp), lead),
            vspec((short, 2 * width), row),
            vspec((1, kp, 2 * width), lead),
            vspec((short, width), row),
            vspec((3 * width, width), lambda i: (0, 0), True),
            vspec((short, width), row),
        ],
        out_specs=[
            vspec((short, 2 * width), row),
            vspec((1, short, kp), lead),
            vspec((short, width), row),
        ],
        out_shape=[
            jax.ShapeDtypeStruct((rows, 2 * width), BF),
            jax.ShapeDtypeStruct((blocks, short, kp), F32),
            jax.ShapeDtypeStruct((rows, width), F32),
        ],
        compiler_params=params(),
        cost_estimate=cost(2 * rows * width * (3 * width + 4 * kp), 20e6),
        name="back",
    )(e_rows, kv, grad_summary, dq, w_att, grad_first)


MESH_ID = pl.DeviceIdType.MESH


def reduce_body(depth, half, n_src, extra_keep, *refs):
    sources = refs[:n_src]
    outs = refs[n_src : n_src + 5]
    (own, got_c, sum_c, got_a, got_b, sum_a, sum_b, got_a2, got_b2, sum_z, got_z) = refs[
        n_src + 5 : n_src + 16
    ]
    (e_own, e_got, e_sum, e_got1, e_sum1, e_got2, e_sum2, e_gotz, e_all, e_rows) = refs[
        n_src + 16 : n_src + 26
    ]
    send, recv, local = refs[n_src + 26 :]
    seq, mine = lax.axis_index("seq"), lax.axis_index("own")
    z, y, x, c = seq // 2, seq % 2, mine // 2, mine % 2
    core = (seq, 2 * x + (1 - c))
    along_x = (seq, 2 * (1 - x) + c)
    along_y = (2 * z + (1 - y), mine)
    along_z = [(2 * lax.rem(z + d, depth) + y, mine) for d in range(1, depth)]
    barrier = pltpu.get_barrier_semaphore()
    partners = [core, along_x, along_y] + along_z
    for partner in partners:
        pl.semaphore_signal(barrier, inc=1, device_id=partner, device_id_type=MESH_ID)
    pl.semaphore_wait(barrier, len(partners))

    sent = []

    def push(src, dst, partner):
        at = len(sent)
        copy = pltpu.make_async_remote_copy(
            src_ref=src,
            dst_ref=dst,
            send_sem=send.at[at],
            recv_sem=recv.at[at],
            device_id=partner,
            device_id_type=MESH_ID,
        )
        copy.start()
        sent.append(copy)
        return copy

    pieces = 3
    up, down, extra = sources[0], sources[1], sources[6]
    half_z = depth // 2
    loads, firsts = [], []

    def load(src, dst):
        copy = pltpu.make_async_copy(src, dst, local.at[len(loads)])
        copy.start()
        loads.append(copy)
        return copy

    e_first = [push(extra.at[:, :, 1 - c], e_got, core)]
    e_load = [load(extra.at[:, :, c], e_own)]
    piece_first, piece_load = [], []
    for p in range(2):
        piece_first.append(
            [
                push(up.at[:, :, 1 - c, p], got_c.at[p, pl.ds(0, half_z)], core),
                push(down.at[:, :, 1 - c, p], got_c.at[p, pl.ds(half_z, half_z)], core),
            ]
        )
        piece_load.append(
            [
                load(up.at[:, :, c, p], own.at[p, pl.ds(0, half_z)]),
                load(down.at[:, :, c, p], own.at[p, pl.ds(half_z, half_z)]),
            ]
        )
    piece_first.append(
        [push(sources[2 + m].at[:, 1 - c], got_c.at[2, m], core) for m in range(depth)]
    )
    piece_load.append([load(sources[2 + m].at[:, c], own.at[2, m]) for m in range(depth)])

    state = {}

    def wait_recv(copies):
        for copy in copies:
            copy.wait_recv()

    def add(a, b):
        return (a.astype(F32) + b.astype(F32)).astype(BF)

    def piece_c(p):
        for copy in piece_load[p]:
            copy.wait()
        wait_recv(piece_first[p])

        def body(i, carry):
            zz, yx = i // 4, i % 4
            sum_c[p, zz, yx // 2, yx % 2] = add(own[p, zz, yx], got_c[p, zz, yx])
            return carry

        lax.fori_loop(0, depth * 4, body, 0)
        state["1", p] = [
            push(sum_c.at[p, :, :, 1 - x, pl.ds(0, half), :], got_a.at[p], along_x),
            push(sum_c.at[p, :, 1 - y, :, pl.ds(half, half), :], got_b.at[p], along_y),
        ]

    def piece_1(p):
        wait_recv(state["1", p])

        def body(i, carry):
            zz, w = i // 2, i % 2
            sum_a[p, zz, w] = add(sum_c[p, zz, w, x, pl.ds(0, half), :], got_a[p, zz, w])
            sum_b[p, zz, w] = add(sum_c[p, zz, y, w, pl.ds(half, half), :], got_b[p, zz, w])
            return carry

        lax.fori_loop(0, depth * 2, body, 0)
        state["2", p] = [
            push(sum_a.at[p, :, 1 - y], got_a2.at[p], along_y),
            push(sum_b.at[p, :, 1 - x], got_b2.at[p], along_x),
        ]

    def piece_2(p):
        wait_recv(state["2", p])

        def body(zz, carry):
            sum_z[p, zz, pl.ds(0, half), :] = add(sum_a[p, zz, y], got_a2[p, zz])
            sum_z[p, zz, pl.ds(half, half), :] = add(sum_b[p, zz, x], got_b2[p, zz])
            return carry

        lax.fori_loop(0, depth, body, 0)
        state["z", p] = [
            push(sum_z.at[p, lax.rem(z + d, depth)], got_z.at[p, d - 1], along_z[d - 1])
            for d in range(1, depth)
        ]

    def piece_z(p):
        wait_recv(state["z", p])
        total = sum_z[p, z].astype(F32)
        for d in range(depth - 1):
            total = total + got_z[p, d].astype(F32)
        outs[p][...] = total

    def extra_c():
        e_load[0].wait()
        wait_recv(e_first)

        def body(i, carry):
            zz, yx = i // 4, i % 4
            e_sum[zz, yx // 2, yx % 2] = e_own[zz, yx] + e_got[zz, yx]
            return carry

        lax.fori_loop(0, depth * 4, body, 0)
        state["e1"] = [push(e_sum.at[:, :, 1 - x], e_got1, along_x)]

    def extra_1():
        wait_recv(state["e1"])

        def body(i, carry):
            zz, yy = i // 2, i % 2
            e_sum1[zz, yy] = e_sum[zz, yy, x] + e_got1[zz, yy]
            return carry

        lax.fori_loop(0, depth * 2, body, 0)
        state["e2"] = [push(e_sum1.at[:, 1 - y], e_got2, along_y)]

    def extra_2():
        wait_recv(state["e2"])

        def body(zz, carry):
            e_sum2[zz] = e_sum1[zz, y] + e_got2[zz]
            return carry

        lax.fori_loop(0, depth, body, 0)
        state["ez"] = [
            push(e_sum2.at[lax.rem(z + d, depth)], e_gotz.at[d - 1], along_z[d - 1])
            for d in range(1, depth)
        ]

    def extra_z():
        wait_recv(state["ez"])
        total = e_sum2[z]
        for d in range(depth - 1):
            total = total + e_gotz[d]
        e_all[z, y] = total
        state["gz"] = [push(e_all.at[z, y], e_all.at[z, y], there) for there in along_z]

    def extra_gather_y():
        wait_recv(state["gz"])
        state["gy"] = [push(e_all.at[:, y], e_all.at[:, y], along_y)]

    def extra_gather_x():
        wait_recv(state["gy"])
        e_rows[x, c] = e_all[:, :, pl.ds(extra_keep, e_rows.shape[4]), :]
        state["gx"] = [push(e_rows.at[x, c], e_rows.at[x, c], along_x)]

    def extra_gather_c():
        wait_recv(state["gx"])
        state["gc"] = [push(e_rows.at[:, c], e_rows.at[:, c], core)]

    extra_c()
    piece_c(0)
    extra_1()
    piece_c(1)
    extra_2()
    piece_1(0)
    piece_c(2)
    extra_z()
    piece_2(0)
    piece_1(1)
    extra_gather_y()
    piece_1(2)
    piece_2(1)
    extra_gather_x()
    piece_z(0)
    piece_2(2)
    extra_gather_c()
    piece_z(1)
    piece_z(2)
    outs[3][...] = e_all[:, :, pl.ds(0, extra_keep), :]
    wait_recv(state["gc"])
    outs[4][...] = e_rows[...]
    for copy in sent:
        copy.wait_send()


def reduce_all(g_att, g_up, g_down, extra, peers):
    depth = peers // 2
    size, width = g_up.shape[2], g_up.shape[3]
    half = size // 2
    e_rows_all, kp = extra.shape[1], extra.shape[2]
    keep = e_rows_all - 8
    sources = (
        [
            g_up.reshape(depth // 2, 4, 2, 2, size, width),
            g_down.reshape(depth // 2, 4, 2, 2, size, width),
        ]
        + [g.reshape(4, 2, size, width) for g in g_att]
        + [extra.reshape(depth, 4, 2, e_rows_all, kp)]
    )
    n_src = len(sources)
    messages = 1 + 4 + depth + 3 * (4 + depth - 1) + 2 + 2 * (depth - 1) + 3
    loads = 1 + 4 + depth
    any_spec = pl.BlockSpec(memory_space=pl.ANY)
    vmem = pl.BlockSpec(memory_space=pltpu.VMEM)
    scratch = [
        pltpu.VMEM((3, depth, 4, size, width), BF),
        pltpu.VMEM((3, depth, 4, size, width), BF),
        pltpu.VMEM((3, depth, 2, 2, size, width), BF),
        pltpu.VMEM((3, depth, 2, half, width), BF),
        pltpu.VMEM((3, depth, 2, half, width), BF),
        pltpu.VMEM((3, depth, 2, half, width), BF),
        pltpu.VMEM((3, depth, 2, half, width), BF),
        pltpu.VMEM((3, depth, half, width), BF),
        pltpu.VMEM((3, depth, half, width), BF),
        pltpu.VMEM((3, depth, size, width), BF),
        pltpu.VMEM((3, depth - 1, size, width), BF),
        pltpu.VMEM((depth, 4, e_rows_all, kp), F32),
        pltpu.VMEM((depth, 4, e_rows_all, kp), F32),
        pltpu.VMEM((depth, 2, 2, e_rows_all, kp), F32),
        pltpu.VMEM((depth, 2, e_rows_all, kp), F32),
        pltpu.VMEM((depth, 2, e_rows_all, kp), F32),
        pltpu.VMEM((depth, e_rows_all, kp), F32),
        pltpu.VMEM((depth, e_rows_all, kp), F32),
        pltpu.VMEM((depth - 1, e_rows_all, kp), F32),
        pltpu.VMEM((depth, 2, e_rows_all, kp), F32),
        pltpu.VMEM((2, 2, depth, 2, 8, kp), F32),
        pltpu.SemaphoreType.DMA((messages,)),
        pltpu.SemaphoreType.DMA((messages,)),
        pltpu.SemaphoreType.DMA((loads,)),
    ]
    return pl.pallas_call(
        functools.partial(reduce_body, depth, half, n_src, keep),
        in_specs=[any_spec] * n_src,
        out_specs=[vmem] * 5,
        out_shape=[jax.ShapeDtypeStruct((size, width), F32)] * 3
        + [
            jax.ShapeDtypeStruct((depth, 2, keep, kp), F32),
            jax.ShapeDtypeStruct((2, 2, depth, 2, 8, kp), F32),
        ],
        scratch_shapes=scratch,
        compiler_params=pltpu.CompilerParams(
            collective_id=1, has_side_effects=True, vmem_limit_bytes=VMEM_LIMIT
        ),
        name="reduce_all",
    )(*sources)


def gather_body(depth, half, band_ref, proj_ref, out_ref, pout_ref, send, recv, local):
    seq, mine = lax.axis_index("seq"), lax.axis_index("own")
    z, y, x, c = seq // 2, seq % 2, mine // 2, mine % 2
    core = (seq, 2 * x + (1 - c))
    along_x = (seq, 2 * (1 - x) + c)
    along_y = (2 * z + (1 - y), mine)
    order = [1, 3, 2]
    along_z = [(2 * lax.rem(z + d, depth) + y, mine) for d in order]
    barrier = pltpu.get_barrier_semaphore()
    partners = [core, along_x, along_y] + along_z
    for partner in partners:
        pl.semaphore_signal(barrier, inc=1, device_id=partner, device_id_type=MESH_ID)
    pl.semaphore_wait(barrier, len(partners))

    sent = []

    def push(src, dst, partner):
        at = len(sent)
        copy = pltpu.make_async_remote_copy(
            src_ref=src,
            dst_ref=dst,
            send_sem=send.at[at],
            recv_sem=recv.at[at],
            device_id=partner,
            device_id_type=MESH_ID,
        )
        copy.start()
        sent.append(copy)
        return copy

    keep = pltpu.make_async_copy(band_ref, out_ref.at[z, y, x, c], local.at[0])
    keep.start()
    keep_p = pltpu.make_async_copy(proj_ref, pout_ref.at[x, c], local.at[1])
    keep_p.start()
    mine_at = out_ref.at[z, y, x, c]
    from_z = [push(band_ref, mine_at, there) for there in along_z]
    from_x = [push(band_ref, mine_at, along_x)]
    from_y = [push(band_ref, mine_at, along_y)]
    proj_x = push(proj_ref, pout_ref.at[x, c], along_x)
    last = [push(band_ref, mine_at, core), push(proj_ref, pout_ref.at[x, c], core)]
    planes = [z]
    for k in range(depth - 1):
        from_z[k].wait_recv()
        plane = lax.rem(z + depth - order[k], depth)
        planes.append(plane)
        slab = out_ref.at[plane, y, x, c]
        from_x.append(push(slab, slab, along_x))
        from_y.append(push(slab, slab, along_y))
        last.append(push(slab, slab, core))
    low, high = pl.ds(0, half), pl.ds(half, half)
    cross = []
    for k in range(depth):
        plane = planes[k]
        from_x[k].wait_recv()
        slab = out_ref.at[plane, y, 1 - x, c]
        part = out_ref.at[plane, y, 1 - x, c, low, :]
        cross_y = push(part, part, along_y)
        last.append(push(slab, slab, core))
        from_y[k].wait_recv()
        slab = out_ref.at[plane, 1 - y, x, c]
        part = out_ref.at[plane, 1 - y, x, c, high, :]
        cross.append((cross_y, push(part, part, along_x)))
        last.append(push(slab, slab, core))
        if k == 0:
            proj_x.wait_recv()
            slab = pout_ref.at[1 - x, c]
            last.append(push(slab, slab, core))
    for k in range(depth):
        for copy in cross[k]:
            copy.wait_recv()
        slab = out_ref.at[planes[k], 1 - y, 1 - x, c]
        last.append(push(slab, slab, core))
    for copy in last:
        copy.wait_recv()
    keep.wait()
    keep_p.wait()
    for copy in sent:
        copy.wait_send()


def gather_bands(band, proj, peers):
    depth = peers // 2
    size, width = band.shape
    messages = (depth - 1) + 3 + 2 + 3 * (depth - 1) + 4 * depth + 1 + depth
    vmem = pl.BlockSpec(memory_space=pltpu.VMEM)
    return pl.pallas_call(
        functools.partial(gather_body, depth, size // 2),
        in_specs=[vmem] * 2,
        out_specs=[vmem] * 2,
        out_shape=[
            jax.ShapeDtypeStruct((depth, 2, 2, 2, size, width), BF),
            jax.ShapeDtypeStruct((2, 2) + proj.shape, BF),
        ],
        scratch_shapes=[
            pltpu.SemaphoreType.DMA((messages,)),
            pltpu.SemaphoreType.DMA((messages,)),
            pltpu.SemaphoreType.DMA((2,)),
        ],
        compiler_params=pltpu.CompilerParams(
            collective_id=2, has_side_effects=True, vmem_limit_bytes=VMEM_LIMIT
        ),
        cost_estimate=cost(1e9, 90e6),
        name="gather_bands",
    )(band, proj)


def shampoo(grad, left, right, root_left, root_right, weight):
    new_left = decay * left + (1.0 - decay) * jnp.einsum(
        "tij,tkj->tik", grad, grad, precision=highest
    )
    new_right = decay * right + (1.0 - decay) * jnp.einsum(
        "tji,tjk->tik", grad, grad, precision=highest
    )
    inner = jnp.einsum("tij,tjk->tik", grad, root_right, precision=highest)
    step = jnp.einsum("tij,tjk->tik", root_left, inner, precision=highest)
    return (new_left, new_right, weight - rate_matrix * step)


def to_matrix(tiles, rows, cols):
    size = tiles.shape[-1]
    return (
        tiles.reshape(rows // size, cols // size, size, size)
        .transpose(0, 2, 1, 3)
        .reshape(rows, cols)
    )


def to_bands(tiles, cols):
    count, size, _ = tiles.shape
    return to_matrix(tiles, count * size * size // cols, cols)


def from_bands(bands, size):
    rows, cols = bands.shape
    return (
        bands.reshape(rows // size, size, cols // size, size)
        .transpose(0, 2, 1, 3)
        .reshape(-1, size, size)
    )


def gather_weights(weights, projection, att_dev, width, both, fused, peers):
    size = weights.shape[-1]
    low = weights.astype(BF)
    groups, chunks = width // size, FF // width
    if banded(weights.shape[0], att_dev, width, size):
        ffn = lax.all_gather(to_bands(low[att_dev:], width), both, axis=0, tiled=True)
        band = to_bands(low[:att_dev], width)
        if fused:
            att, proj = gather_bands(band, projection.astype(BF), peers)
            att, proj = att.reshape(-1, width), proj.reshape(-1, projection.shape[1])
        else:
            att = lax.all_gather(band, both, axis=0, tiled=True)
            proj = lax.all_gather(projection.astype(BF), "own", axis=0, tiled=True)
        return att, ffn.reshape(2 * groups, chunks, size, width), proj
    per_dev = weights.shape[0]
    proj = lax.all_gather(projection.astype(BF), "own", axis=0, tiled=True)
    grid = lax.all_gather(low, both, axis=0, tiled=True).reshape(-1, per_dev, size, size)
    att = to_bands(grid[:, :att_dev].reshape(-1, size, size), width)
    tiles = grid[:, att_dev:].reshape(-1, size, size)
    half = tiles.shape[0] // 2
    w_up = to_matrix(tiles[:half], width, FF).reshape(groups, size, chunks, width)
    w_down = to_matrix(tiles[half:], FF, width).reshape(groups, chunks, size, width)
    return att, jnp.concatenate([w_up.transpose(0, 2, 1, 3), w_down], axis=0), proj


def banded(per_dev, att_dev, width, size):
    wide = width // size
    return att_dev % wide == 0 and (per_dev - att_dev) % wide == 0


def scatter_weight_grads(g_att, g_up, g_down, per_dev, att_dev, both):
    size, width = g_up.shape[2], g_up.shape[3]
    if banded(per_dev, att_dev, width, size):
        ffn = jnp.concatenate([g_up.reshape(-1, width), g_down], axis=0)
        ffn = lax.psum_scatter(ffn, both, scatter_dimension=0, tiled=True)
        att = lax.psum_scatter(g_att, both, scatter_dimension=0, tiled=True)
        return jnp.concatenate([from_bands(att, size), from_bands(ffn, size)], axis=0)
    up = g_up.transpose(0, 2, 1, 3).reshape(width, -1)
    att = from_bands(g_att, size)
    ffn = jnp.concatenate([from_bands(up, size), from_bands(g_down, size)], axis=0)
    stacked = jnp.concatenate(
        [
            att.reshape(-1, att_dev, size, size),
            ffn.reshape(-1, per_dev - att_dev, size, size),
        ],
        axis=1,
    ).reshape(-1, size, size)
    return lax.psum_scatter(stacked, both, scatter_dimension=0, tiled=True)


def per_device(
    tokens,
    cotangent,
    lengths,
    offsets,
    valid_count,
    weights,
    stat_left,
    stat_right,
    root_left,
    root_right,
    projection,
    projection_left,
    projection_right,
    projection_root_left,
    projection_root_right,
    norm_params,
    norm_stat,
):
    both = ("seq", "own")
    size = weights.shape[-1]
    width = tokens.shape[-1]
    rows_here = tokens.shape[1]
    head = width // HEADS
    kp = projection.shape[1]
    blocks = rows_here // SHORT
    peers = lax.axis_size("seq")
    devices = peers * lax.axis_size("own")
    per_dev = weights.shape[0]
    att_dev = 4 * (width // size) ** 2 // devices
    x = tokens[0]
    seq = lax.axis_index("seq")
    side = seq % 2

    swap = [(i, i ^ 1) for i in range(peers)]
    peer_x = lax.ppermute(x, "seq", swap)
    own_size = lax.axis_size("own")
    fused = own_size == 4 and peers == 8 and banded(per_dev, att_dev, width, size)
    w_att, w_ffn, proj_all = gather_weights(
        weights, projection, att_dev, width, both, fused, peers
    )

    lens, offs, counts = lengths[0], offsets[0], valid_count[0]
    ends = jnp.cumsum(lens)
    starts = ends - lens
    unit_rows = 2 * rows_here
    unit_start = (seq - side) * rows_here
    unit_end = unit_start + unit_rows
    block_row = unit_start + SHORT * jnp.arange(2 * blocks, dtype=jnp.int32)
    hot = ((starts[None, :] <= block_row[:, None]) & (block_row[:, None] < ends[None, :])).astype(
        jnp.int32
    )
    b_start = jnp.sum(hot * starts[None, :], axis=1)
    b_end = jnp.sum(hot * ends[None, :], axis=1)
    place = block_row - b_start
    column = jnp.sum(hot * offs[None, :], axis=1) + place
    n_valid = jnp.clip(jnp.sum(hot * counts[None, :], axis=1) - place, 0, SHORT)
    is_head = b_start == b_start[0]
    is_tail = b_start == b_start[-1]
    own_at = side * blocks
    peer_at = (1 - side) * blocks
    take = lambda v, at: lax.dynamic_slice_in_dim(v, at, blocks, 0)

    def proj_rows(at):
        col, n = take(column, at), take(n_valid, at)
        rows = jnp.stack(
            [lax.dynamic_slice_in_dim(proj_all, col[b], SHORT, 0) for b in range(blocks)]
        )
        keep = lax.broadcasted_iota(jnp.int32, (blocks, SHORT, 1), 1) < n[:, None, None]
        return jnp.where(keep, rows, jnp.zeros((), BF))

    e_own = proj_rows(own_at)
    e_own_t = e_own.transpose(0, 2, 1)
    e_peer_t = proj_rows(peer_at).transpose(0, 2, 1)
    n_own = take(n_valid, own_at)

    query, keyval, part_own = project(x, w_att, e_own_t, True)
    (part_peer,) = project(peer_x, w_att, e_peer_t, False)
    coef = lambda flag, at: take(flag, at).astype(F32)

    def unit_sum(flag):
        mine = coef(flag, own_at)
        theirs = coef(flag, peer_at)
        total = mine[0] * part_own[0]
        for b in range(1, blocks):
            total = total + mine[b] * part_own[b]
        for b in range(blocks):
            total = total + theirs[b] * part_peer[b]
        return total

    head_sum, tail_sum = unit_sum(is_head), unit_sum(is_tail)
    from_left = lax.ppermute(tail_sum, "seq", [(i, i + 2) for i in range(peers - 2)])
    from_right = lax.ppermute(head_sum, "seq", [(i + 2, i) for i in range(peers - 2)])
    head_cross = (b_start[0] < unit_start).astype(F32)
    tail_cross = (b_end[-1] > unit_end).astype(F32)
    own_head, own_tail = coef(is_head, own_at), coef(is_tail, own_at)
    summary = jnp.stack(
        [
            jnp.where(
                own_head[b] > 0,
                head_sum + head_cross * from_left,
                jnp.where(own_tail[b] > 0, tail_sum + tail_cross * from_right, part_own[b]),
            ).astype(BF)
            for b in range(blocks)
        ]
    )
    mixed, first_sum, row_sums = attend(n_own, query, summary, w_att, x, head)
    (
        result,
        hidden,
        grad_up,
        grad_down,
        first_low,
        grad_first,
        grad_branch,
        grad_mix,
        norm_terms,
    ) = feed(first_sum, w_ffn, w_att, cotangent[0], norm_params, 256)
    grad_query, grad_parts = attend_back(query, summary, grad_mix, head)

    row_start = seq * rows_here
    row_end = row_start + rows_here
    o_start, o_end = take(b_start, own_at), take(b_end, own_at)
    same = (o_start[0] == o_start[-1]).astype(F32)
    g_head = grad_parts[0]
    g_tail = grad_parts[-1]
    for b in range(1, blocks):
        g_head = g_head + (o_start[b] == o_start[0]).astype(F32) * grad_parts[b]
    for b in range(blocks - 1):
        g_tail = g_tail + (o_start[b] == o_start[-1]).astype(F32) * grad_parts[b]
    low_head, low_tail = g_head.astype(BF), g_tail.astype(BF)
    left_sum = jnp.zeros_like(g_head)
    right_sum = jnp.zeros_like(g_head)
    for far in (1, 2):
        tail_far = lax.ppermute(low_tail, "seq", [(i, i + far) for i in range(peers - far)])
        head_far = lax.ppermute(low_head, "seq", [(i + far, i) for i in range(peers - far)])
        reach = (far - 1) * rows_here
        left_sum = left_sum + (o_start[0] < row_start - reach).astype(F32) * tail_far.astype(F32)
        right_sum = right_sum + (o_end[-1] > row_end + reach).astype(F32) * head_far.astype(F32)
    at_head = (o_start == o_start[0]).astype(F32)
    grad_summary = jnp.stack(
        [
            jnp.where(
                at_head[b] > 0, g_head + left_sum + same * right_sum, g_tail + right_sum
            ).astype(BF)
            for b in range(blocks)
        ]
    )
    gtype = BF if fused else F32
    g_up = outer_up(first_low, grad_up, size, gtype)
    g_down = outer_rows(hidden, grad_down, gtype, "outer_down")
    g_out = outer_rows(mixed, grad_branch, gtype, "outer_out")
    g_query = outer_rows(x, grad_query, gtype, "outer_query")
    grad_keyval, grad_e, grad_input = back(e_own, keyval, grad_summary, grad_query, w_att, grad_first)
    g_key = outer_rows(x, grad_keyval[:, :width], gtype, "outer_key")
    g_value = outer_rows(x, grad_keyval[:, width:], gtype, "outer_value")
    g_att = [g_query, g_key, g_value, g_out]

    part_rows = projection.shape[0]
    grad_proj = jnp.zeros((proj_all.shape[0], kp), F32)
    keep_e = lax.broadcasted_iota(jnp.int32, (blocks, SHORT, 1), 1) < n_own[:, None, None]
    grad_e = jnp.where(keep_e, grad_e, 0.0)
    own_col = take(column, own_at)
    for b in range(blocks):
        current = lax.dynamic_slice_in_dim(grad_proj, own_col[b], SHORT, 0)
        grad_proj = lax.dynamic_update_slice_in_dim(grad_proj, current + grad_e[b], own_col[b], 0)
    valid_here = jnp.sum(n_own).astype(F32)
    extra = jnp.concatenate(
        [
            norm_terms.reshape(-1, kp),
            row_sums.reshape(-1, kp),
            jnp.full((1, kp), 1.0 / kp, F32) * valid_here,
        ],
        axis=0,
    )
    n_norm = 4 * width // kp
    n_row = 2 * width // kp
    if fused:
        extra = jnp.pad(extra, ((0, devices - extra.shape[0]), (0, 0)))[:, None, :]
        extra = jnp.pad(extra, ((0, 0), (0, 7), (0, 0)))
        shares = grad_proj.reshape(own_size, peers, part_rows // peers, kp).swapaxes(0, 1)
        shares = shares.reshape(devices, part_rows // peers, kp)
        ffn_a, ffn_b, att, proj_parts, rows = reduce_all(
            g_att, g_up, g_down, jnp.concatenate([shares, extra], axis=1), peers
        )
        owned = jnp.concatenate(
            [from_bands(att, size), from_bands(ffn_a, size), from_bands(ffn_b, size)], axis=0
        )
        proj_grad = proj_parts.reshape(part_rows, kp)
        totals = rows[..., 0, :].transpose(2, 3, 0, 1, 4).reshape(devices, kp)
    else:
        owned = scatter_weight_grads(
            jnp.concatenate(g_att, axis=0), g_up, g_down, per_dev, att_dev, both
        )
        packed = jnp.concatenate([grad_proj, extra], axis=0)
        packed = lax.psum(jnp.pad(packed, ((0, -packed.shape[0] % 16), (0, 0))), both)
        proj_grad = lax.dynamic_slice_in_dim(
            packed, lax.axis_index("own") * part_rows, part_rows, 0
        )
        totals = packed[grad_proj.shape[0] :]
    norm_grad = totals[:n_norm].reshape(4, width)
    row_total = totals[n_norm : n_norm + n_row].reshape(2, width).sum(axis=1)
    valid_total = totals[n_norm + n_row].sum()
    residual_rms = jnp.sqrt(row_total / (valid_total * width))
    left_new, right_new, weights_new = shampoo(
        owned, stat_left, stat_right, root_left, root_right, weights
    )
    proj_left_new, proj_right_new, proj_blocks = shampoo(
        proj_grad.reshape(-1, kp, kp),
        projection_left,
        projection_right,
        projection_root_left,
        projection_root_right,
        projection.reshape(-1, kp, kp),
    )
    stat_new = decay * norm_stat + (1.0 - decay) * norm_grad * norm_grad
    norm_new = norm_params - rate_norm * norm_grad * lax.rsqrt(stat_new)
    return (
        result[None],
        grad_input[None],
        owned,
        left_new,
        right_new,
        weights_new,
        proj_grad,
        proj_left_new,
        proj_right_new,
        proj_blocks.reshape(part_rows, kp),
        norm_grad,
        stat_new,
        norm_new,
        residual_rms,
    )


def solution(mesh):
    pack = P("own", "seq", None)
    table = P("own", None)
    tile = P(("seq", "own"), None, None)
    proj = P("own", None, None)
    return jax.shard_map(
        per_device,
        mesh=mesh,
        in_specs=(pack, pack, table, table, table)
        + (tile,) * 5
        + (table, proj, proj, proj, proj, P(), P()),
        out_specs=(pack, pack) + (tile,) * 4 + (table, proj, proj, table, P(), P(), P(), P()),
        check_vma=False,
    )
```

```python
import functools
import math

import jax
import jax.numpy as jnp
from jax import lax
from jax.experimental import pallas as pl
from jax.experimental.pallas import tpu as pltpu
from jax.sharding import PartitionSpec as P

HEADS = 12
FF = 3072
SHORT = 512
BF = jnp.bfloat16
F32 = jnp.float32

eps_norm = 1e-05
decay = 0.5
rate_matrix = 0.2
rate_norm = 0.2
highest = lax.Precision.HIGHEST
VMEM_LIMIT = 60 * 1024 * 1024


def dot(a, b):
    return lax.dot_general(a, b, (((1,), (0,)), ((), ())), preferred_element_type=F32)


def dot_t(a, b):
    return lax.dot_general(a, b, (((1,), (1,)), ((), ())), preferred_element_type=F32)


def dot_l(a, b):
    return lax.dot_general(a, b, (((0,), (0,)), ((), ())), preferred_element_type=F32)


def vspec(shape, index_map, once=False):
    if once:
        return pl.BlockSpec(shape, index_map, pipeline_mode=pl.Buffered(1))
    return pl.BlockSpec(shape, index_map)


def params():
    return pltpu.CompilerParams(
        dimension_semantics=("arbitrary",), vmem_limit_bytes=VMEM_LIMIT
    )


def cost(flops, nbytes, trans=0):
    return pl.CostEstimate(flops=int(flops), bytes_accessed=int(nbytes), transcendentals=int(trans))


def project_body(width, with_query, x_ref, w_ref, e_ref, *outs):
    x = x_ref[...]
    if with_query:
        q_ref, kv_ref, p_ref = outs
        q_ref[...] = dot(x, w_ref[pl.ds(0, width), :]).astype(BF)
    else:
        (p_ref,) = outs
    e = e_ref[0]
    for part in range(2):
        kv = dot(x, w_ref[pl.ds((1 + part) * width, width), :]).astype(BF)
        if with_query:
            kv_ref[:, pl.ds(part * width, width)] = kv
        p_ref[0, :, pl.ds(part * width, width)] = dot(e, kv)


def project(x, w_att, e_t, with_query):
    rows, width = x.shape
    blocks, kp, short = e_t.shape
    out_shape = [jax.ShapeDtypeStruct((blocks, kp, 2 * width), F32)]
    out_specs = [vspec((1, kp, 2 * width), lambda i: (i, 0, 0))]
    if with_query:
        out_shape = [
            jax.ShapeDtypeStruct((rows, width), BF),
            jax.ShapeDtypeStruct((rows, 2 * width), BF),
        ] + out_shape
        out_specs = [
            vspec((short, width), lambda i: (i, 0)),
            vspec((short, 2 * width), lambda i: (i, 0)),
        ] + out_specs
    return pl.pallas_call(
        functools.partial(project_body, width, with_query),
        grid=(blocks,),
        in_specs=[
            vspec((short, width), lambda i: (i, 0)),
            vspec((3 * width, width), lambda i: (0, 0), True),
            vspec((1, kp, short), lambda i: (i, 0, 0)),
        ],
        out_specs=out_specs,
        out_shape=out_shape,
        compiler_params=params(),
        cost_estimate=cost(2 * rows * width * width * 3, 12e6),
        name="project" if with_query else "project_peer",
    )(x, w_att, e_t)


def head_pair(ref_slice, low_lane):
    zero = jnp.zeros_like(ref_slice)
    return jnp.concatenate(
        [jnp.where(low_lane, ref_slice, zero), jnp.where(low_lane, zero, ref_slice)], axis=0
    )


def softmax_pair(scores, kp):
    parts = []
    for half in range(2):
        s = scores[:, half * kp : (half + 1) * kp]
        top = jnp.max(s, axis=-1, keepdims=True)
        e = jnp.exp(s - top)
        parts.append(e * (1.0 / jnp.sum(e, axis=-1, keepdims=True)))
    return parts


def attend_body(width, head, kp, n_ref, q_ref, s_ref, w_ref, x_ref, mix_ref, sum_ref, stat_ref):
    pairs = width // (2 * head)
    step = pl.program_id(0)
    scale = head ** (-0.5)
    low_lane = lax.broadcasted_iota(jnp.int32, (kp, 2 * head), 1) < head
    for j in range(pairs):
        cols = pl.ds(j * 2 * head, 2 * head)
        keys = head_pair(s_ref[0, :, cols], low_lane)
        values = head_pair(s_ref[0, :, pl.ds(width + j * 2 * head, 2 * head)], low_lane)
        scores = dot_t(q_ref[:, cols], keys) * scale
        prob = jnp.concatenate(softmax_pair(scores, kp), axis=1).astype(BF)
        mix_ref[:, cols] = dot(prob, values).astype(BF)
    branch = dot(mix_ref[...], w_ref[...])
    first = x_ref[...].astype(F32) + branch
    sum_ref[...] = first
    rows = q_ref.shape[0]
    keep = (lax.broadcasted_iota(jnp.int32, (rows, 1), 0) < n_ref[step]).astype(F32)
    sums = jnp.concatenate(
        [
            jnp.sum(keep * first * first, axis=0, keepdims=True),
            jnp.sum(keep * branch * branch, axis=0, keepdims=True),
        ],
        axis=0,
    )

    @pl.when(step == 0)
    def _():
        stat_ref[...] = sums

    @pl.when(step > 0)
    def _():
        stat_ref[...] += sums


def attend(n_valid, q, summary, w_att, x, head):
    rows, width = q.shape
    blocks, kp, _ = summary.shape
    short = rows // blocks
    return pl.pallas_call(
        functools.partial(attend_body, width, head, kp),
        grid_spec=pltpu.PrefetchScalarGridSpec(
            num_scalar_prefetch=1,
            grid=(blocks,),
            in_specs=[
                vspec((short, width), lambda i, n: (i, 0)),
                vspec((1, kp, 2 * width), lambda i, n: (i, 0, 0)),
                vspec((width, width), lambda i, n: (3, 0), True),
                vspec((short, width), lambda i, n: (i, 0)),
            ],
            out_specs=[
                vspec((short, width), lambda i, n: (i, 0)),
                vspec((short, width), lambda i, n: (i, 0)),
                vspec((2, width), lambda i, n: (0, 0)),
            ],
        ),
        out_shape=[
            jax.ShapeDtypeStruct((rows, width), BF),
            jax.ShapeDtypeStruct((rows, width), F32),
            jax.ShapeDtypeStruct((2, width), F32),
        ],
        compiler_params=params(),
        cost_estimate=cost(2 * rows * width * (width + 4 * kp), 10e6, rows * kp * 12),
        name="attend",
    )(n_valid, q, summary, w_att, x)


def normalize(values):
    mean = jnp.mean(values, axis=-1, keepdims=True)
    centered = values - mean
    inverse = lax.rsqrt(jnp.mean(centered * centered, axis=-1, keepdims=True) + eps_norm)
    return centered * inverse, inverse


def norm_back(grad_out, normed, inverse, gain):
    scaled = grad_out * gain
    return inverse * (
        scaled
        - jnp.mean(scaled, axis=-1, keepdims=True)
        - normed * jnp.mean(scaled * normed, axis=-1, keepdims=True)
    )


def feed_body(
    chunks,
    first_ref,
    w1_ref,
    w2_ref,
    wo_ref,
    cot_ref,
    np_ref,
    out_ref,
    hid_ref,
    up_ref,
    down_ref,
    flow_ref,
    dfirst_ref,
    dbranch_ref,
    dmix_ref,
    ng_ref,
    slope_ref,
):
    step = pl.program_id(0)
    rows, width = first_ref.shape
    deep = w2_ref.shape[0] // chunks
    down_rows = lambda c: w2_ref[pl.ds(c * deep, deep)].reshape(width, width)
    normed_one, inverse_one = normalize(first_ref[...])
    first_norm = normed_one * np_ref[0:1, :] + np_ref[1:2, :]
    first_low = first_norm.astype(BF)
    flow_ref[...] = first_low
    second = first_norm
    for c in range(chunks):
        cols = pl.ds(c * width, width)
        u = dot(first_low, w1_ref[:, c].reshape(width, width))
        cumulative = 0.5 * (1.0 + lax.erf(u * (1.0 / math.sqrt(2.0))))
        density = jnp.exp(-0.5 * u * u) * (1.0 / math.sqrt(2.0 * math.pi))
        slope_ref[:, cols] = cumulative + u * density
        hidden = (u * cumulative).astype(BF)
        hid_ref[:, cols] = hidden
        second = second + dot(hidden, down_rows(c))
    normed_two, inverse_two = normalize(second)
    out_ref[...] = (normed_two * np_ref[2:3, :] + np_ref[3:4, :]).astype(BF)
    grad_out = cot_ref[...].astype(F32)
    gain_two = jnp.sum(grad_out * normed_two, axis=0, keepdims=True)
    shift_two = jnp.sum(grad_out, axis=0, keepdims=True)
    grad_second = norm_back(grad_out, normed_two, inverse_two, np_ref[2:3, :])
    down = grad_second.astype(BF)
    down_ref[...] = down
    grad_first_norm = grad_second
    for c in range(chunks):
        cols = pl.ds(c * width, width)
        grad_hidden = dot_t(down, down_rows(c))
        up = (grad_hidden * slope_ref[:, cols]).astype(BF)
        up_ref[:, cols] = up
        grad_first_norm = grad_first_norm + dot_t(up, w1_ref[:, c].reshape(width, width))
    gain_one = jnp.sum(grad_first_norm * normed_one, axis=0, keepdims=True)
    shift_one = jnp.sum(grad_first_norm, axis=0, keepdims=True)
    grad_first = norm_back(grad_first_norm, normed_one, inverse_one, np_ref[0:1, :])
    dfirst_ref[...] = grad_first
    grad_branch = grad_first.astype(BF)
    dbranch_ref[...] = grad_branch
    dmix_ref[...] = dot_t(grad_branch, wo_ref[...]).astype(BF)
    sums = jnp.concatenate([gain_one, shift_one, gain_two, shift_two], axis=0)

    @pl.when(step == 0)
    def _():
        ng_ref[...] = sums

    @pl.when(step > 0)
    def _():
        ng_ref[...] += sums


def feed(first_sum, w_ffn, w_att, cotangent, norm_params, tile):
    rows, width = first_sum.shape
    groups, chunks, size, _ = w_ffn.shape
    groups = groups // 2
    ff = chunks * width
    row = lambda i: (i, 0)
    return pl.pallas_call(
        functools.partial(feed_body, chunks),
        grid=(rows // tile,),
        in_specs=[
            vspec((tile, width), row),
            vspec((groups, chunks, size, width), lambda i: (0, 0, 0, 0), True),
            vspec((groups, chunks, size, width), lambda i: (1, 0, 0, 0), True),
            vspec((width, width), lambda i: (3, 0), True),
            vspec((tile, width), row),
            vspec(norm_params.shape, lambda i: (0, 0)),
        ],
        out_specs=[
            vspec((tile, width), row),
            vspec((tile, ff), row),
            vspec((tile, ff), row),
            vspec((tile, width), row),
            vspec((tile, width), row),
            vspec((tile, width), row),
            vspec((tile, width), row),
            vspec((tile, width), row),
            vspec((4, width), lambda i: (0, 0)),
        ],
        out_shape=[
            jax.ShapeDtypeStruct((rows, width), BF),
            jax.ShapeDtypeStruct((rows, ff), BF),
            jax.ShapeDtypeStruct((rows, ff), BF),
            jax.ShapeDtypeStruct((rows, width), BF),
            jax.ShapeDtypeStruct((rows, width), BF),
            jax.ShapeDtypeStruct((rows, width), F32),
            jax.ShapeDtypeStruct((rows, width), BF),
            jax.ShapeDtypeStruct((rows, width), BF),
            jax.ShapeDtypeStruct((4, width), F32),
        ],
        scratch_shapes=[pltpu.VMEM((tile, ff), F32)],
        compiler_params=params(),
        cost_estimate=cost(2 * rows * width * ff * 4, 30e6, rows * ff * 2),
        name="feed",
    )(first_sum, w_ffn, w_ffn, w_att, cotangent, norm_params)


def attend_back_body(width, head, kp, q_ref, s_ref, g_ref, dq_ref, ds_ref):
    pairs = width // (2 * head)
    scale = head ** (-0.5)
    low_lane = lax.broadcasted_iota(jnp.int32, (kp, 2 * head), 1) < head
    for j in range(pairs):
        cols = pl.ds(j * 2 * head, 2 * head)
        vcols = pl.ds(width + j * 2 * head, 2 * head)
        keys = head_pair(s_ref[0, :, cols], low_lane)
        values = head_pair(s_ref[0, :, vcols], low_lane)
        q = q_ref[:, cols]
        g = g_ref[:, cols]
        prob = softmax_pair(dot_t(q, keys) * scale, kp)
        grad_prob = dot_t(g, values)
        low_parts = []
        for half in range(2):
            p = prob[half]
            d = grad_prob[:, half * kp : (half + 1) * kp]
            low_parts.append((p * (d - jnp.sum(p * d, axis=-1, keepdims=True))).astype(BF))
        grad_scores = jnp.concatenate(low_parts, axis=1)
        prob_low = jnp.concatenate(prob, axis=1).astype(BF)
        dq_ref[:, cols] = (dot(grad_scores, keys) * scale).astype(BF)
        dk = dot_l(grad_scores, q) * scale
        dv = dot_l(prob_low, g)
        ds_ref[0, :, cols] = jnp.where(low_lane, dk[:kp], dk[kp:])
        ds_ref[0, :, vcols] = jnp.where(low_lane, dv[:kp], dv[kp:])


def attend_back(q, summary, grad_mix, head):
    rows, width = q.shape
    blocks, kp, _ = summary.shape
    short = rows // blocks
    return pl.pallas_call(
        functools.partial(attend_back_body, width, head, kp),
        grid=(blocks,),
        in_specs=[
            vspec((short, width), lambda i: (i, 0)),
            vspec((1, kp, 2 * width), lambda i: (i, 0, 0)),
            vspec((short, width), lambda i: (i, 0)),
        ],
        out_specs=[
            vspec((short, width), lambda i: (i, 0)),
            vspec((1, kp, 2 * width), lambda i: (i, 0, 0)),
        ],
        out_shape=[
            jax.ShapeDtypeStruct((rows, width), BF),
            jax.ShapeDtypeStruct((blocks, kp, 2 * width), F32),
        ],
        compiler_params=params(),
        cost_estimate=cost(2 * rows * width * 8 * kp, 10e6, rows * kp * 12),
        name="attend_back",
    )(q, summary, grad_mix)


def outer_body(split, l_ref, r_ref, o_ref):
    value = dot_l(l_ref[...], r_ref[...])
    o_ref[...] = value.reshape(o_ref.shape).astype(o_ref.dtype)


def outer_up(first_low, grad_up, size, dtype):
    rows, width = first_low.shape
    chunks = grad_up.shape[1] // width
    groups = width // size
    return pl.pallas_call(
        functools.partial(outer_body, True),
        grid=(chunks,),
        in_specs=[
            vspec((rows, width), lambda i: (0, 0), True),
            vspec((rows, width), lambda i: (0, i)),
        ],
        out_specs=vspec((groups, 1, size, width), lambda i: (0, i, 0, 0)),
        out_shape=jax.ShapeDtypeStruct((groups, chunks, size, width), dtype),
        compiler_params=params(),
        cost_estimate=cost(2 * rows * width * width * chunks, 20e6),
        name="outer_up",
    )(first_low, grad_up)


def outer_rows(left, right, dtype, name):
    rows, width = right.shape[0], min(left.shape[1], right.shape[1])
    tall, wide = left.shape[1] // width, right.shape[1] // width
    moving = lambda n: (lambda i: (0, i)) if n > 1 else (lambda i: (0, 0))
    return pl.pallas_call(
        functools.partial(outer_body, False),
        grid=(tall * wide,),
        in_specs=[
            vspec((rows, width), moving(tall), tall == 1),
            vspec((rows, width), moving(wide), wide == 1),
        ],
        out_specs=vspec((width, width), lambda i: (i, 0)),
        out_shape=jax.ShapeDtypeStruct((tall * wide * width, width), dtype),
        compiler_params=params(),
        cost_estimate=cost(2 * rows * width * width * tall * wide, 20e6),
        name=name,
    )(left, right)


def back_body(
    width, blocks, c_ref, n_ref, e_ref, kv_ref, p_ref, *refs
):
    far_refs = refs[:4]
    dq_ref, w_ref, df_ref, dkv_ref, gp_ref, gi_ref = refs[4:]
    step = pl.program_id(0)
    short, kp = e_ref.shape[1], e_ref.shape[2]
    total = c_ref[step, 0] * p_ref[0]
    for other in range(1, blocks):
        total = total + c_ref[step, other] * p_ref[other]
    for k in range(4):
        total = total + c_ref[step, blocks + k] * far_refs[k][...].astype(F32)
    summary = total.astype(BF)
    dkv = dot(e_ref[0], summary).astype(BF)
    dkv_ref[...] = dkv
    keep = lax.broadcasted_iota(jnp.int32, (short, 1), 0) < n_ref[1, step]
    grad_e = jnp.where(keep, dot_t(kv_ref[...], summary), 0.0)
    column = n_ref[0, step]
    at = pl.multiple_of(jnp.minimum((column // 8) * 8, gp_ref.shape[0] - short - 8), 8)
    moved = pltpu.roll(
        jnp.concatenate([grad_e, jnp.zeros((8, kp), F32)], axis=0), column - at, 0
    )

    @pl.when(step == 0)
    def _():
        gp_ref[...] = jnp.zeros_like(gp_ref)

    gp_ref[pl.ds(at, short + 8), :] += moved
    gi_ref[...] = (
        df_ref[...]
        + dot_t(dq_ref[...], w_ref[pl.ds(0, width), :])
        + dot_t(dkv[:, :width], w_ref[pl.ds(width, width), :])
        + dot_t(dkv[:, width:], w_ref[pl.ds(2 * width, width), :])
    )


def back(coef, places, e_rows, kv, grad_parts, far_parts, dq, w_att, grad_first, positions):
    rows, width = dq.shape
    blocks, short, kp = e_rows.shape
    row = lambda i, *_: (i, 0)
    lead = lambda i, *_: (i, 0, 0)
    fixed = lambda i, *_: (0, 0)
    return pl.pallas_call(
        functools.partial(back_body, width, blocks),
        grid_spec=pltpu.PrefetchScalarGridSpec(
            num_scalar_prefetch=2,
            grid=(blocks,),
            in_specs=[
                vspec((1, short, kp), lead),
                vspec((short, 2 * width), row),
                vspec(grad_parts.shape, lambda i, *_: (0, 0, 0), True),
            ]
            + [vspec((kp, 2 * width), fixed, True)] * 4
            + [
                vspec((short, width), row),
                vspec((3 * width, width), fixed, True),
                vspec((short, width), row),
            ],
            out_specs=[
                vspec((short, 2 * width), row),
                vspec((positions, kp), fixed),
                vspec((short, width), row),
            ],
        ),
        out_shape=[
            jax.ShapeDtypeStruct((rows, 2 * width), BF),
            jax.ShapeDtypeStruct((positions, kp), F32),
            jax.ShapeDtypeStruct((rows, width), F32),
        ],
        compiler_params=params(),
        cost_estimate=cost(2 * rows * width * (3 * width + 4 * kp), 20e6),
        name="back",
    )(coef, places, e_rows, kv, grad_parts, *far_parts, dq, w_att, grad_first)


MESH_ID = pl.DeviceIdType.MESH


def reduce_body(depth, half, n_src, extra_keep, *refs):
    sources = refs[:n_src]
    outs = refs[n_src : n_src + 5]
    (own, got_c, sum_c, got_a, got_b, sum_a, sum_b, got_a2, got_b2, sum_z, got_z) = refs[
        n_src + 5 : n_src + 16
    ]
    keep_a, keep_b, keep_z = refs[n_src + 16 : n_src + 19]
    (e_own, e_got, e_sum, e_got1, e_sum1, e_got2, e_sum2, e_gotz, e_all, e_rows) = refs[
        n_src + 19 : n_src + 29
    ]
    send, recv, local = refs[n_src + 29 :]
    seq, mine = lax.axis_index("seq"), lax.axis_index("own")
    z, y, x, c = seq // 2, seq % 2, mine // 2, mine % 2
    core = (seq, 2 * x + (1 - c))
    along_x = (seq, 2 * (1 - x) + c)
    along_y = (2 * z + (1 - y), mine)
    along_z = [(2 * lax.rem(z + d, depth) + y, mine) for d in range(1, depth)]
    barrier = pltpu.get_barrier_semaphore()
    partners = [core, along_x, along_y] + along_z
    for partner in partners:
        pl.semaphore_signal(barrier, inc=1, device_id=partner, device_id_type=MESH_ID)
    pl.semaphore_wait(barrier, len(partners))

    sent = []

    def push(src, dst, partner):
        at = len(sent)
        copy = pltpu.make_async_remote_copy(
            src_ref=src,
            dst_ref=dst,
            send_sem=send.at[at],
            recv_sem=recv.at[at],
            device_id=partner,
            device_id_type=MESH_ID,
        )
        copy.start()
        sent.append(copy)
        return copy

    up, down, g_query, g_keyval, g_out, extra = sources
    bands = [g_query, g_keyval.at[0], g_keyval.at[1], g_out]
    half_z = depth // 2
    cols = own.shape[-1]
    loads = []

    def load(src, dst):
        copy = pltpu.make_async_copy(src, dst, local.at[len(loads)])
        copy.start()
        loads.append(copy)
        return copy

    e_first = [push(extra.at[:, :, 1 - c], e_got, core)]
    e_load = [load(extra.at[:, :, c], e_own)]
    piece_first, piece_load = [], []
    for p in range(6):
        at, part = p // 2, pl.ds((p % 2) * cols, cols)
        if at < 2:
            first = [
                push(up.at[:, :, 1 - c, at, :, part], got_c.at[p, pl.ds(0, half_z)], core),
                push(down.at[:, :, 1 - c, at, :, part], got_c.at[p, pl.ds(half_z, half_z)], core),
            ]
            kept = [
                load(up.at[:, :, c, at, :, part], own.at[p, pl.ds(0, half_z)]),
                load(down.at[:, :, c, at, :, part], own.at[p, pl.ds(half_z, half_z)]),
            ]
        else:
            first = [
                push(bands[m].at[:, 1 - c, :, part], got_c.at[p, m], core) for m in range(depth)
            ]
            kept = [load(bands[m].at[:, c, :, part], own.at[p, m]) for m in range(depth)]
        piece_first.append(first)
        piece_load.append(kept)

    state = {}

    def wait_recv(copies):
        for copy in copies:
            copy.wait_recv()

    low, high = pl.ds(0, half), pl.ds(half, half)

    def add(a, b):
        return a.astype(F32) + b.astype(F32)

    def piece_c(p):
        for copy in piece_load[p]:
            copy.wait()
        wait_recv(piece_first[p])

        def body(i, carry):
            zz, w = i // 2, i % 2
            to_x, to_y = 2 * w + 1 - x, 2 * (1 - y) + w
            sum_c[p, 0, zz, w] = add(own[p, zz, to_x, low, :], got_c[p, zz, to_x, low, :]).astype(BF)
            sum_c[p, 1, zz, w] = add(own[p, zz, to_y, high, :], got_c[p, zz, to_y, high, :]).astype(BF)
            return carry

        lax.fori_loop(0, depth * 2, body, 0)
        state["1", p] = [
            push(sum_c.at[p, 0], got_a.at[p], along_x),
            push(sum_c.at[p, 1], got_b.at[p], along_y),
        ]

    def piece_1(p):
        wait_recv(state["1", p])

        def side_a(zz, w):
            at = 2 * w + x
            return add(own[p, zz, at, low, :], got_c[p, zz, at, low, :]) + got_a[p, zz, w].astype(F32)

        def side_b(zz, w):
            at = 2 * y + w
            return add(own[p, zz, at, high, :], got_c[p, zz, at, high, :]) + got_b[p, zz, w].astype(F32)

        def body(zz, carry):
            sum_a[p, zz] = side_a(zz, 1 - y).astype(BF)
            sum_b[p, zz] = side_b(zz, 1 - x).astype(BF)
            keep_a[p, zz] = side_a(zz, y)
            keep_b[p, zz] = side_b(zz, x)
            return carry

        lax.fori_loop(0, depth, body, 0)
        state["2", p] = [
            push(sum_a.at[p], got_a2.at[p], along_y),
            push(sum_b.at[p], got_b2.at[p], along_x),
        ]

    def piece_2(p):
        wait_recv(state["2", p])

        def body(zz, carry):
            total_a = keep_a[p, zz] + got_a2[p, zz].astype(F32)
            total_b = keep_b[p, zz] + got_b2[p, zz].astype(F32)
            sum_z[p, zz, low, :] = total_a.astype(BF)
            sum_z[p, zz, high, :] = total_b.astype(BF)
            return carry

        lax.fori_loop(0, depth, body, 0)
        keep_z[p, low, :] = keep_a[p, z] + got_a2[p, z].astype(F32)
        keep_z[p, high, :] = keep_b[p, z] + got_b2[p, z].astype(F32)
        state["z", p] = [
            push(sum_z.at[p, lax.rem(z + d, depth)], got_z.at[p, d - 1], along_z[d - 1])
            for d in range(1, depth)
        ]

    def piece_z(p):
        wait_recv(state["z", p])
        total = keep_z[p]
        for d in range(depth - 1):
            total = total + got_z[p, d].astype(F32)
        outs[p // 2][:, pl.ds((p % 2) * cols, cols)] = total

    def extra_c():
        e_load[0].wait()
        wait_recv(e_first)

        def body(i, carry):
            zz, yx = i // 4, i % 4
            e_sum[zz, yx // 2, yx % 2] = e_own[zz, yx] + e_got[zz, yx]
            return carry

        lax.fori_loop(0, depth * 4, body, 0)
        state["e1"] = [push(e_sum.at[:, :, 1 - x], e_got1, along_x)]

    def extra_1():
        wait_recv(state["e1"])

        def body(i, carry):
            zz, yy = i // 2, i % 2
            e_sum1[zz, yy] = e_sum[zz, yy, x] + e_got1[zz, yy]
            return carry

        lax.fori_loop(0, depth * 2, body, 0)
        state["e2"] = [push(e_sum1.at[:, 1 - y], e_got2, along_y)]

    def extra_2():
        wait_recv(state["e2"])

        def body(zz, carry):
            e_sum2[zz] = e_sum1[zz, y] + e_got2[zz]
            return carry

        lax.fori_loop(0, depth, body, 0)
        state["ez"] = [
            push(e_sum2.at[lax.rem(z + d, depth)], e_gotz.at[d - 1], along_z[d - 1])
            for d in range(1, depth)
        ]

    def extra_z():
        wait_recv(state["ez"])
        total = e_sum2[z]
        for d in range(depth - 1):
            total = total + e_gotz[d]
        e_all[z, y] = total
        state["gz"] = [push(e_all.at[z, y], e_all.at[z, y], there) for there in along_z]

    def extra_gather_y():
        wait_recv(state["gz"])
        state["gy"] = [push(e_all.at[:, y], e_all.at[:, y], along_y)]

    def extra_gather_x():
        wait_recv(state["gy"])
        e_rows[x, c] = e_all[:, :, pl.ds(extra_keep, e_rows.shape[4]), :]
        state["gx"] = [push(e_rows.at[x, c], e_rows.at[x, c], along_x)]

    def extra_gather_c():
        wait_recv(state["gx"])
        state["gc"] = [push(e_rows.at[:, c], e_rows.at[:, c], core)]

    stages = [piece_c, piece_1, piece_2, piece_z]
    small = [extra_c, extra_1, extra_2, extra_z, extra_gather_y, extra_gather_x, extra_gather_c]
    for turn in range(9):
        if turn < len(small):
            small[turn]()
        for stage in range(4):
            if 0 <= turn - stage < 6:
                stages[stage](turn - stage)
    outs[3][...] = e_all[:, :, pl.ds(0, extra_keep), :]
    wait_recv(state["gc"])
    outs[4][...] = e_rows[...]
    for copy in sent:
        copy.wait_send()


def reduce_all(g_query, g_keyval, g_out, g_up, g_down, extra, peers):
    depth = peers // 2
    size, width = g_up.shape[2], g_up.shape[3]
    half = size // 2
    e_rows_all, kp = extra.shape[1], extra.shape[2]
    keep = e_rows_all - 8
    sources = (
        [
            g_up.reshape(depth // 2, 4, 2, 2, size, width),
            g_down.reshape(depth // 2, 4, 2, 2, size, width),
        ]
        + [
            g_query.reshape(4, 2, size, width),
            g_keyval.reshape(2, 4, 2, size, width),
            g_out.reshape(4, 2, size, width),
        ]
        + [extra.reshape(depth, 4, 2, e_rows_all, kp)]
    )
    n_src = len(sources)
    cols = width // 2
    messages = 1 + 8 + 2 * depth + 6 * (4 + depth - 1) + 2 + 2 * (depth - 1) + 3
    loads = 1 + 8 + 2 * depth
    any_spec = pl.BlockSpec(memory_space=pl.ANY)
    vmem = pl.BlockSpec(memory_space=pltpu.VMEM)
    scratch = [
        pltpu.VMEM((6, depth, 4, size, cols), BF),
        pltpu.VMEM((6, depth, 4, size, cols), BF),
        pltpu.VMEM((6, 2, depth, 2, half, cols), BF),
        pltpu.VMEM((6, depth, 2, half, cols), BF),
        pltpu.VMEM((6, depth, 2, half, cols), BF),
        pltpu.VMEM((6, depth, half, cols), BF),
        pltpu.VMEM((6, depth, half, cols), BF),
        pltpu.VMEM((6, depth, half, cols), BF),
        pltpu.VMEM((6, depth, half, cols), BF),
        pltpu.VMEM((6, depth, size, cols), BF),
        pltpu.VMEM((6, depth - 1, size, cols), BF),
        pltpu.VMEM((6, depth, half, cols), F32),
        pltpu.VMEM((6, depth, half, cols), F32),
        pltpu.VMEM((6, size, cols), F32),
        pltpu.VMEM((depth, 4, e_rows_all, kp), F32),
        pltpu.VMEM((depth, 4, e_rows_all, kp), F32),
        pltpu.VMEM((depth, 2, 2, e_rows_all, kp), F32),
        pltpu.VMEM((depth, 2, e_rows_all, kp), F32),
        pltpu.VMEM((depth, 2, e_rows_all, kp), F32),
        pltpu.VMEM((depth, e_rows_all, kp), F32),
        pltpu.VMEM((depth, e_rows_all, kp), F32),
        pltpu.VMEM((depth - 1, e_rows_all, kp), F32),
        pltpu.VMEM((depth, 2, e_rows_all, kp), F32),
        pltpu.VMEM((2, 2, depth, 2, 8, kp), F32),
        pltpu.SemaphoreType.DMA((messages,)),
        pltpu.SemaphoreType.DMA((messages,)),
        pltpu.SemaphoreType.DMA((loads,)),
    ]
    return pl.pallas_call(
        functools.partial(reduce_body, depth, half, n_src, keep),
        in_specs=[any_spec] * n_src,
        out_specs=[vmem] * 5,
        out_shape=[jax.ShapeDtypeStruct((size, width), F32)] * 3
        + [
            jax.ShapeDtypeStruct((depth, 2, keep, kp), F32),
            jax.ShapeDtypeStruct((2, 2, depth, 2, 8, kp), F32),
        ],
        scratch_shapes=scratch,
        compiler_params=pltpu.CompilerParams(
            collective_id=1, has_side_effects=True, vmem_limit_bytes=VMEM_LIMIT
        ),
        name="reduce_all",
    )(*sources)


def gather_body(depth, half, band_ref, proj_ref, out_ref, pout_ref, send, recv, local):
    seq, mine = lax.axis_index("seq"), lax.axis_index("own")
    z, y, x, c = seq // 2, seq % 2, mine // 2, mine % 2
    core = (seq, 2 * x + (1 - c))
    along_x = (seq, 2 * (1 - x) + c)
    along_y = (2 * z + (1 - y), mine)
    order = [1, 3, 2]
    along_z = [(2 * lax.rem(z + d, depth) + y, mine) for d in order]
    barrier = pltpu.get_barrier_semaphore()
    partners = [core, along_x, along_y] + along_z
    for partner in partners:
        pl.semaphore_signal(barrier, inc=1, device_id=partner, device_id_type=MESH_ID)
    pl.semaphore_wait(barrier, len(partners))

    sent = []

    def push(src, dst, partner):
        at = len(sent)
        copy = pltpu.make_async_remote_copy(
            src_ref=src,
            dst_ref=dst,
            send_sem=send.at[at],
            recv_sem=recv.at[at],
            device_id=partner,
            device_id_type=MESH_ID,
        )
        copy.start()
        sent.append(copy)
        return copy

    keep = pltpu.make_async_copy(band_ref, out_ref.at[z, y, x, c], local.at[0])
    keep.start()
    keep_p = pltpu.make_async_copy(proj_ref, pout_ref.at[x, c], local.at[1])
    keep_p.start()
    mine_at = out_ref.at[z, y, x, c]
    from_z = [push(band_ref, mine_at, there) for there in along_z]
    from_x = [push(band_ref, mine_at, along_x)]
    from_y = [push(band_ref, mine_at, along_y)]
    proj_x = push(proj_ref, pout_ref.at[x, c], along_x)
    last = [push(band_ref, mine_at, core), push(proj_ref, pout_ref.at[x, c], core)]
    planes = [z]
    for k in range(depth - 1):
        from_z[k].wait_recv()
        plane = lax.rem(z + depth - order[k], depth)
        planes.append(plane)
        slab = out_ref.at[plane, y, x, c]
        from_x.append(push(slab, slab, along_x))
        from_y.append(push(slab, slab, along_y))
        last.append(push(slab, slab, core))
    low, high = pl.ds(0, half), pl.ds(half, half)
    cross = []
    for k in range(depth):
        plane = planes[k]
        from_x[k].wait_recv()
        slab = out_ref.at[plane, y, 1 - x, c]
        part = out_ref.at[plane, y, 1 - x, c, low, :]
        cross_y = push(part, part, along_y)
        last.append(push(slab, slab, core))
        from_y[k].wait_recv()
        slab = out_ref.at[plane, 1 - y, x, c]
        part = out_ref.at[plane, 1 - y, x, c, high, :]
        cross.append((cross_y, push(part, part, along_x)))
        last.append(push(slab, slab, core))
        if k == 0:
            proj_x.wait_recv()
            slab = pout_ref.at[1 - x, c]
            last.append(push(slab, slab, core))
    for k in range(depth):
        for copy in cross[k]:
            copy.wait_recv()
        slab = out_ref.at[planes[k], 1 - y, 1 - x, c]
        last.append(push(slab, slab, core))
    for copy in last:
        copy.wait_recv()
    keep.wait()
    keep_p.wait()
    for copy in sent:
        copy.wait_send()


def gather_bands(band, proj, peers):
    depth = peers // 2
    size, width = band.shape
    messages = (depth - 1) + 3 + 2 + 3 * (depth - 1) + 4 * depth + 1 + depth
    vmem = pl.BlockSpec(memory_space=pltpu.VMEM)
    return pl.pallas_call(
        functools.partial(gather_body, depth, size // 2),
        in_specs=[vmem] * 2,
        out_specs=[vmem] * 2,
        out_shape=[
            jax.ShapeDtypeStruct((depth, 2, 2, 2, size, width), BF),
            jax.ShapeDtypeStruct((2, 2) + proj.shape, BF),
        ],
        scratch_shapes=[
            pltpu.SemaphoreType.DMA((messages,)),
            pltpu.SemaphoreType.DMA((messages,)),
            pltpu.SemaphoreType.DMA((2,)),
        ],
        compiler_params=pltpu.CompilerParams(
            collective_id=2, has_side_effects=True, vmem_limit_bytes=VMEM_LIMIT
        ),
        cost_estimate=cost(1e9, 90e6),
        name="gather_bands",
    )(band, proj)


def shampoo(grad, left, right, root_left, root_right, weight):
    new_left = decay * left + (1.0 - decay) * jnp.einsum(
        "tij,tkj->tik", grad, grad, precision=highest
    )
    new_right = decay * right + (1.0 - decay) * jnp.einsum(
        "tji,tjk->tik", grad, grad, precision=highest
    )
    inner = jnp.einsum("tij,tjk->tik", grad, root_right, precision=highest)
    step = jnp.einsum("tij,tjk->tik", root_left, inner, precision=highest)
    return (new_left, new_right, weight - rate_matrix * step)


def to_matrix(tiles, rows, cols):
    size = tiles.shape[-1]
    return (
        tiles.reshape(rows // size, cols // size, size, size)
        .transpose(0, 2, 1, 3)
        .reshape(rows, cols)
    )


def to_bands(tiles, cols):
    count, size, _ = tiles.shape
    return to_matrix(tiles, count * size * size // cols, cols)


def from_bands(bands, size):
    rows, cols = bands.shape
    return (
        bands.reshape(rows // size, size, cols // size, size)
        .transpose(0, 2, 1, 3)
        .reshape(-1, size, size)
    )


def gather_weights(weights, projection, att_dev, width, both, fused, peers):
    size = weights.shape[-1]
    low = weights.astype(BF)
    groups, chunks = width // size, FF // width
    if banded(weights.shape[0], att_dev, width, size):
        ffn = lax.all_gather(to_bands(low[att_dev:], width), both, axis=0, tiled=True)
        band = to_bands(low[:att_dev], width)
        if fused:
            att, proj = gather_bands(band, projection.astype(BF), peers)
            att, proj = att.reshape(-1, width), proj.reshape(-1, projection.shape[1])
        else:
            att = lax.all_gather(band, both, axis=0, tiled=True)
            proj = lax.all_gather(projection.astype(BF), "own", axis=0, tiled=True)
        return att, ffn.reshape(2 * groups, chunks, size, width), proj
    per_dev = weights.shape[0]
    proj = lax.all_gather(projection.astype(BF), "own", axis=0, tiled=True)
    grid = lax.all_gather(low, both, axis=0, tiled=True).reshape(-1, per_dev, size, size)
    att = to_bands(grid[:, :att_dev].reshape(-1, size, size), width)
    tiles = grid[:, att_dev:].reshape(-1, size, size)
    half = tiles.shape[0] // 2
    w_up = to_matrix(tiles[:half], width, FF).reshape(groups, size, chunks, width)
    w_down = to_matrix(tiles[half:], FF, width).reshape(groups, chunks, size, width)
    return att, jnp.concatenate([w_up.transpose(0, 2, 1, 3), w_down], axis=0), proj


def banded(per_dev, att_dev, width, size):
    wide = width // size
    return att_dev % wide == 0 and (per_dev - att_dev) % wide == 0


def scatter_weight_grads(g_att, g_up, g_down, per_dev, att_dev, both):
    size, width = g_up.shape[2], g_up.shape[3]
    if banded(per_dev, att_dev, width, size):
        ffn = jnp.concatenate([g_up.reshape(-1, width), g_down], axis=0)
        ffn = lax.psum_scatter(ffn, both, scatter_dimension=0, tiled=True)
        att = lax.psum_scatter(g_att, both, scatter_dimension=0, tiled=True)
        return jnp.concatenate([from_bands(att, size), from_bands(ffn, size)], axis=0)
    up = g_up.transpose(0, 2, 1, 3).reshape(width, -1)
    att = from_bands(g_att, size)
    ffn = jnp.concatenate([from_bands(up, size), from_bands(g_down, size)], axis=0)
    stacked = jnp.concatenate(
        [
            att.reshape(-1, att_dev, size, size),
            ffn.reshape(-1, per_dev - att_dev, size, size),
        ],
        axis=1,
    ).reshape(-1, size, size)
    return lax.psum_scatter(stacked, both, scatter_dimension=0, tiled=True)


def per_device(
    tokens,
    cotangent,
    lengths,
    offsets,
    valid_count,
    weights,
    stat_left,
    stat_right,
    root_left,
    root_right,
    projection,
    projection_left,
    projection_right,
    projection_root_left,
    projection_root_right,
    norm_params,
    norm_stat,
):
    both = ("seq", "own")
    size = weights.shape[-1]
    width = tokens.shape[-1]
    rows_here = tokens.shape[1]
    head = width // HEADS
    kp = projection.shape[1]
    blocks = rows_here // SHORT
    peers = lax.axis_size("seq")
    devices = peers * lax.axis_size("own")
    per_dev = weights.shape[0]
    att_dev = 4 * (width // size) ** 2 // devices
    x = tokens[0]
    seq = lax.axis_index("seq")
    side = seq % 2

    swap = [(i, i ^ 1) for i in range(peers)]
    peer_x = lax.ppermute(x, "seq", swap)
    own_size = lax.axis_size("own")
    fused = own_size == 4 and peers == 8 and banded(per_dev, att_dev, width, size)
    w_att, w_ffn, proj_all = gather_weights(
        weights, projection, att_dev, width, both, fused, peers
    )

    lens, offs, counts = lengths[0], offsets[0], valid_count[0]
    ends = jnp.cumsum(lens)
    starts = ends - lens
    unit_rows = 2 * rows_here
    unit_start = (seq - side) * rows_here
    unit_end = unit_start + unit_rows
    block_row = unit_start + SHORT * jnp.arange(2 * blocks, dtype=jnp.int32)
    hot = ((starts[None, :] <= block_row[:, None]) & (block_row[:, None] < ends[None, :])).astype(
        jnp.int32
    )
    b_start = jnp.sum(hot * starts[None, :], axis=1)
    b_end = jnp.sum(hot * ends[None, :], axis=1)
    place = block_row - b_start
    column = jnp.sum(hot * offs[None, :], axis=1) + place
    n_valid = jnp.clip(jnp.sum(hot * counts[None, :], axis=1) - place, 0, SHORT)
    is_head = b_start == b_start[0]
    is_tail = b_start == b_start[-1]
    own_at = side * blocks
    peer_at = (1 - side) * blocks
    take = lambda v, at: lax.dynamic_slice_in_dim(v, at, blocks, 0)

    def proj_rows(at):
        col, n = take(column, at), take(n_valid, at)
        rows = jnp.stack(
            [lax.dynamic_slice_in_dim(proj_all, col[b], SHORT, 0) for b in range(blocks)]
        )
        keep = lax.broadcasted_iota(jnp.int32, (blocks, SHORT, 1), 1) < n[:, None, None]
        return jnp.where(keep, rows, jnp.zeros((), BF))

    e_own = proj_rows(own_at)
    e_own_t = e_own.transpose(0, 2, 1)
    e_peer_t = proj_rows(peer_at).transpose(0, 2, 1)
    n_own = take(n_valid, own_at)

    query, keyval, part_own = project(x, w_att, e_own_t, True)
    (part_peer,) = project(peer_x, w_att, e_peer_t, False)
    coef = lambda flag, at: take(flag, at).astype(F32)

    def unit_sum(flag):
        mine = coef(flag, own_at)
        theirs = coef(flag, peer_at)
        total = mine[0] * part_own[0]
        for b in range(1, blocks):
            total = total + mine[b] * part_own[b]
        for b in range(blocks):
            total = total + theirs[b] * part_peer[b]
        return total

    head_sum, tail_sum = unit_sum(is_head), unit_sum(is_tail)
    from_left = lax.ppermute(tail_sum, "seq", [(i, i + 2) for i in range(peers - 2)])
    from_right = lax.ppermute(head_sum, "seq", [(i + 2, i) for i in range(peers - 2)])
    head_cross = (b_start[0] < unit_start).astype(F32)
    tail_cross = (b_end[-1] > unit_end).astype(F32)
    own_head, own_tail = coef(is_head, own_at), coef(is_tail, own_at)
    summary = jnp.stack(
        [
            jnp.where(
                own_head[b] > 0,
                head_sum + head_cross * from_left,
                jnp.where(own_tail[b] > 0, tail_sum + tail_cross * from_right, part_own[b]),
            ).astype(BF)
            for b in range(blocks)
        ]
    )
    mixed, first_sum, row_sums = attend(n_own, query, summary, w_att, x, head)
    (
        result,
        hidden,
        grad_up,
        grad_down,
        first_low,
        grad_first,
        grad_branch,
        grad_mix,
        norm_terms,
    ) = feed(first_sum, w_ffn, w_att, cotangent[0], norm_params, 256)
    grad_query, grad_parts = attend_back(query, summary, grad_mix, head)

    row_start = seq * rows_here
    row_end = row_start + rows_here
    o_start, o_end = take(b_start, own_at), take(b_end, own_at)
    g_head = grad_parts[0]
    g_tail = grad_parts[-1]
    for b in range(1, blocks):
        g_head = g_head + (o_start[b] == o_start[0]).astype(F32) * grad_parts[b]
    for b in range(blocks - 1):
        g_tail = g_tail + (o_start[b] == o_start[-1]).astype(F32) * grad_parts[b]
    low_head, low_tail = g_head.astype(BF), g_tail.astype(BF)
    far_parts, far_flags = [], []
    at_head = (o_start == o_start[0]).astype(F32)
    at_tail = (o_start == o_start[-1]).astype(F32)
    for far in (1, 2):
        reach = (far - 1) * rows_here
        far_parts.append(lax.ppermute(low_tail, "seq", [(i, i + far) for i in range(peers - far)]))
        far_flags.append(at_head * (o_start[0] < row_start - reach).astype(F32))
        far_parts.append(lax.ppermute(low_head, "seq", [(i + far, i) for i in range(peers - far)]))
        far_flags.append(at_tail * (o_end[-1] > row_end + reach).astype(F32))
    together = (o_start[:, None] == o_start[None, :]).astype(F32)
    coef_back = jnp.concatenate([together, jnp.stack(far_flags, axis=1)], axis=1)
    own_col = take(column, own_at)
    gtype = BF if fused else F32
    g_up = outer_up(first_low, grad_up, size, gtype)
    g_down = outer_rows(hidden, grad_down, gtype, "outer_down")
    g_out = outer_rows(mixed, grad_branch, gtype, "outer_out")
    g_query = outer_rows(x, grad_query, gtype, "outer_query")
    grad_keyval, grad_proj, grad_input = back(
        coef_back,
        jnp.stack([own_col, n_own]),
        e_own,
        keyval,
        grad_parts,
        far_parts,
        grad_query,
        w_att,
        grad_first,
        proj_all.shape[0],
    )
    g_keyval = outer_rows(x, grad_keyval, gtype, "outer_keyval")
    part_rows = projection.shape[0]
    valid_here = jnp.sum(n_own).astype(F32)
    extra = jnp.concatenate(
        [
            norm_terms.reshape(-1, kp),
            row_sums.reshape(-1, kp),
            jnp.full((1, kp), 1.0 / kp, F32) * valid_here,
        ],
        axis=0,
    )
    n_norm = 4 * width // kp
    n_row = 2 * width // kp
    if fused:
        extra = jnp.pad(extra, ((0, devices - extra.shape[0]), (0, 0)))[:, None, :]
        extra = jnp.pad(extra, ((0, 0), (0, 7), (0, 0)))
        shares = grad_proj.reshape(own_size, peers, part_rows // peers, kp).swapaxes(0, 1)
        shares = shares.reshape(devices, part_rows // peers, kp)
        ffn_a, ffn_b, att, proj_parts, rows = reduce_all(
            g_query, g_keyval, g_out, g_up, g_down, jnp.concatenate([shares, extra], axis=1), peers
        )
        owned = jnp.concatenate(
            [from_bands(att, size), from_bands(ffn_a, size), from_bands(ffn_b, size)], axis=0
        )
        proj_grad = proj_parts.reshape(part_rows, kp)
        totals = rows[..., 0, :].transpose(2, 3, 0, 1, 4).reshape(devices, kp)
    else:
        owned = scatter_weight_grads(
            jnp.concatenate([g_query, g_keyval, g_out], axis=0), g_up, g_down, per_dev, att_dev, both
        )
        packed = jnp.concatenate([grad_proj, extra], axis=0)
        packed = lax.psum(jnp.pad(packed, ((0, -packed.shape[0] % 16), (0, 0))), both)
        proj_grad = lax.dynamic_slice_in_dim(
            packed, lax.axis_index("own") * part_rows, part_rows, 0
        )
        totals = packed[grad_proj.shape[0] :]
    norm_grad = totals[:n_norm].reshape(4, width)
    row_total = totals[n_norm : n_norm + n_row].reshape(2, width).sum(axis=1)
    valid_total = totals[n_norm + n_row].sum()
    residual_rms = jnp.sqrt(row_total / (valid_total * width))
    left_new, right_new, weights_new = shampoo(
        owned, stat_left, stat_right, root_left, root_right, weights
    )
    proj_left_new, proj_right_new, proj_blocks = shampoo(
        proj_grad.reshape(-1, kp, kp),
        projection_left,
        projection_right,
        projection_root_left,
        projection_root_right,
        projection.reshape(-1, kp, kp),
    )
    stat_new = decay * norm_stat + (1.0 - decay) * norm_grad * norm_grad
    norm_new = norm_params - rate_norm * norm_grad * lax.rsqrt(stat_new)
    return (
        result[None],
        grad_input[None],
        owned,
        left_new,
        right_new,
        weights_new,
        proj_grad,
        proj_left_new,
        proj_right_new,
        proj_blocks.reshape(part_rows, kp),
        norm_grad,
        stat_new,
        norm_new,
        residual_rms,
    )


def solution(mesh):
    pack = P("own", "seq", None)
    table = P("own", None)
    tile = P(("seq", "own"), None, None)
    proj = P("own", None, None)
    return jax.shard_map(
        per_device,
        mesh=mesh,
        in_specs=(pack, pack, table, table, table)
        + (tile,) * 5
        + (table, proj, proj, proj, proj, P(), P()),
        out_specs=(pack, pack) + (tile,) * 4 + (table, proj, proj, table, P(), P(), P(), P()),
        check_vma=False,
    )
```

```python
import functools
import math

import jax
import jax.numpy as jnp
from jax import lax
from jax.experimental import pallas as pl
from jax.experimental.pallas import tpu as pltpu
from jax.sharding import PartitionSpec as P

HEADS = 12
FF = 3072
SHORT = 512
BF = jnp.bfloat16
F32 = jnp.float32

eps_norm = 1e-05
decay = 0.5
rate_matrix = 0.2
rate_norm = 0.2
highest = lax.Precision.HIGHEST
VMEM_LIMIT = 60 * 1024 * 1024
MESH_ID = pl.DeviceIdType.MESH


def dot(a, b):
    return lax.dot_general(a, b, (((1,), (0,)), ((), ())), preferred_element_type=F32)


def dot_t(a, b):
    return lax.dot_general(a, b, (((1,), (1,)), ((), ())), preferred_element_type=F32)


def dot_l(a, b):
    return lax.dot_general(a, b, (((0,), (0,)), ((), ())), preferred_element_type=F32)


def vspec(shape, index_map, once=False):
    if once:
        return pl.BlockSpec(shape, index_map, pipeline_mode=pl.Buffered(1))
    return pl.BlockSpec(shape, index_map)


def params():
    return pltpu.CompilerParams(
        dimension_semantics=("arbitrary",), vmem_limit_bytes=VMEM_LIMIT
    )


def cost(flops, nbytes, trans=0):
    return pl.CostEstimate(flops=int(flops), bytes_accessed=int(nbytes), transcendentals=int(trans))


def project_body(width, with_query, x_ref, w_ref, e_ref, *outs):
    x = x_ref[...]
    if with_query:
        q_ref, kv_ref, p_ref = outs
        q_ref[...] = dot(x, w_ref[pl.ds(0, width), :]).astype(BF)
    else:
        (p_ref,) = outs
    e = e_ref[0]
    for part in range(2):
        kv = dot(x, w_ref[pl.ds((1 + part) * width, width), :]).astype(BF)
        if with_query:
            kv_ref[:, pl.ds(part * width, width)] = kv
        p_ref[0, :, pl.ds(part * width, width)] = dot(e, kv)


def project(x, w_att, e_t, with_query):
    rows, width = x.shape
    blocks, kp, short = e_t.shape
    out_shape = [jax.ShapeDtypeStruct((blocks, kp, 2 * width), F32)]
    out_specs = [vspec((1, kp, 2 * width), lambda i: (i, 0, 0))]
    if with_query:
        out_shape = [
            jax.ShapeDtypeStruct((rows, width), BF),
            jax.ShapeDtypeStruct((rows, 2 * width), BF),
        ] + out_shape
        out_specs = [
            vspec((short, width), lambda i: (i, 0)),
            vspec((short, 2 * width), lambda i: (i, 0)),
        ] + out_specs
    return pl.pallas_call(
        functools.partial(project_body, width, with_query),
        grid=(blocks,),
        in_specs=[
            vspec((short, width), lambda i: (i, 0)),
            vspec((3 * width, width), lambda i: (0, 0), True),
            vspec((1, kp, short), lambda i: (i, 0, 0)),
        ],
        out_specs=out_specs,
        out_shape=out_shape,
        compiler_params=params(),
        cost_estimate=cost(2 * rows * width * width * 3, 12e6),
        name="project" if with_query else "project_peer",
    )(x, w_att, e_t)


def head_pair(ref_slice, low_lane):
    zero = jnp.zeros_like(ref_slice)
    return jnp.concatenate(
        [jnp.where(low_lane, ref_slice, zero), jnp.where(low_lane, zero, ref_slice)], axis=0
    )


def softmax_pair(scores, kp):
    parts = []
    for half in range(2):
        s = scores[:, half * kp : (half + 1) * kp]
        top = jnp.max(s, axis=-1, keepdims=True)
        e = jnp.exp(s - top)
        parts.append(e * (1.0 / jnp.sum(e, axis=-1, keepdims=True)))
    return parts


def attend_body(width, head, kp, n_ref, q_ref, s_ref, w_ref, x_ref, mix_ref, sum_ref, stat_ref):
    pairs = width // (2 * head)
    step = pl.program_id(0)
    scale = head ** (-0.5)
    low_lane = lax.broadcasted_iota(jnp.int32, (kp, 2 * head), 1) < head
    for j in range(pairs):
        cols = pl.ds(j * 2 * head, 2 * head)
        keys = head_pair(s_ref[0, :, cols], low_lane)
        values = head_pair(s_ref[0, :, pl.ds(width + j * 2 * head, 2 * head)], low_lane)
        scores = dot_t(q_ref[:, cols], keys) * scale
        prob = jnp.concatenate(softmax_pair(scores, kp), axis=1).astype(BF)
        mix_ref[:, cols] = dot(prob, values).astype(BF)
    branch = dot(mix_ref[...], w_ref[...])
    first = x_ref[...].astype(F32) + branch
    sum_ref[...] = first
    rows = q_ref.shape[0]
    keep = (lax.broadcasted_iota(jnp.int32, (rows, 1), 0) < n_ref[step]).astype(F32)
    sums = jnp.concatenate(
        [
            jnp.sum(keep * first * first, axis=0, keepdims=True),
            jnp.sum(keep * branch * branch, axis=0, keepdims=True),
        ],
        axis=0,
    )

    @pl.when(step == 0)
    def _():
        stat_ref[...] = sums

    @pl.when(step > 0)
    def _():
        stat_ref[...] += sums


def attend(n_valid, q, summary, w_att, x, head):
    rows, width = q.shape
    blocks, kp, _ = summary.shape
    short = rows // blocks
    return pl.pallas_call(
        functools.partial(attend_body, width, head, kp),
        grid_spec=pltpu.PrefetchScalarGridSpec(
            num_scalar_prefetch=1,
            grid=(blocks,),
            in_specs=[
                vspec((short, width), lambda i, n: (i, 0)),
                vspec((1, kp, 2 * width), lambda i, n: (i, 0, 0)),
                vspec((width, width), lambda i, n: (3, 0), True),
                vspec((short, width), lambda i, n: (i, 0)),
            ],
            out_specs=[
                vspec((short, width), lambda i, n: (i, 0)),
                vspec((short, width), lambda i, n: (i, 0)),
                vspec((2, width), lambda i, n: (0, 0)),
            ],
        ),
        out_shape=[
            jax.ShapeDtypeStruct((rows, width), BF),
            jax.ShapeDtypeStruct((rows, width), F32),
            jax.ShapeDtypeStruct((2, width), F32),
        ],
        compiler_params=params(),
        cost_estimate=cost(2 * rows * width * (width + 4 * kp), 10e6, rows * kp * 12),
        name="attend",
    )(n_valid, q, summary, w_att, x)


def forward_body(
    depth, head, c_ref, n_ref, x_ref, px_ref, w_ref, e_ref, pe_ref, *refs
):
    q_ref, kv_ref, s_ref, mix_ref, sum_ref, stat_ref, part, unit, got, send, recv = refs
    blocks, short, kp = e_ref.shape
    width = x_ref.shape[1]
    seq, mine = lax.axis_index("seq"), lax.axis_index("own")
    z, y = seq // 2, seq % 2
    along_y = (2 * z + (1 - y), mine)
    after = (2 * lax.rem(z + 1, depth) + y, mine)
    before = (2 * lax.rem(z + depth - 1, depth) + y, mine)
    has_left, has_right = z > 0, z < depth - 1
    shared = kp * 5 // 16
    direct = kp - 2 * shared
    barrier = pltpu.get_barrier_semaphore()
    pl.semaphore_signal(barrier, inc=1, device_id=along_y, device_id_type=MESH_ID)

    @pl.when(has_left)
    def _():
        pl.semaphore_signal(barrier, inc=1, device_id=before, device_id_type=MESH_ID)

    @pl.when(has_right)
    def _():
        pl.semaphore_signal(barrier, inc=1, device_id=after, device_id_type=MESH_ID)

    pl.semaphore_wait(barrier, 1 + jnp.minimum(z, 1) + jnp.minimum(depth - 1 - z, 1))

    @pl.when(jnp.logical_not(has_left))
    def _():
        got[0] = jnp.zeros_like(got[0])

    @pl.when(jnp.logical_not(has_right))
    def _():
        got[1] = jnp.zeros_like(got[1])

    def copy(at, src, dst, there):
        return pltpu.make_async_remote_copy(
            src_ref=src,
            dst_ref=dst,
            send_sem=send.at[at],
            recv_sem=recv.at[at],
            device_id=there,
            device_id_type=MESH_ID,
        )

    every = pl.ds(0, direct)
    single = pl.ds(pl.multiple_of(direct + shared * y, 8), shared)
    moves, hands = {}, {}
    for kind in range(2):
        cols = pl.ds(kind * width, width)
        for side in range(2):
            there = (after, before)[side]
            at = (kind * 2 + side) * 3
            moves[kind, side] = [
                copy(at, unit.at[side, every, cols], got.at[side, every, cols], there),
                copy(at + 1, unit.at[side, single, cols], got.at[side, single, cols], there),
            ]
            hands[kind, side] = copy(
                at + 2, got.at[side, single, cols], got.at[side, single, cols], along_y
            )
    can_send = (has_right, has_left)
    can_get = (has_left, has_right)

    for kind in range(2):
        cols = pl.ds(kind * width, width)
        weight = pl.ds((1 + kind) * width, width)

        def own_block(b, carry):
            rows = pl.ds(pl.multiple_of(b * short, short), short)
            kv = dot(x_ref[rows, :], w_ref[weight, :]).astype(BF)
            kv_ref[rows, cols] = kv
            total = dot_l(e_ref[b], kv)
            part[b, :, cols] = total

            @pl.when(b == 0)
            def _():
                for side in range(2):
                    unit[side, :, cols] = c_ref[1 - side, b] * total

            @pl.when(b > 0)
            def _():
                for side in range(2):
                    unit[side, :, cols] += c_ref[1 - side, b] * total

            return carry

        def peer_block(b, carry):
            rows = pl.ds(pl.multiple_of(b * short, short), short)
            kv = dot(px_ref[rows, :], w_ref[weight, :]).astype(BF)
            total = dot_l(pe_ref[b], kv)
            for side in range(2):
                unit[side, :, cols] += c_ref[1 - side, blocks + b] * total
            return carry

        lax.fori_loop(0, blocks, own_block, 0)
        lax.fori_loop(0, blocks, peer_block, 0)
        for side in range(2):

            @pl.when(can_send[side])
            def _():
                for move in moves[kind, side]:
                    move.start()

    def query_block(b, carry):
        rows = pl.ds(pl.multiple_of(b * short, short), short)
        q_ref[rows, :] = dot(x_ref[rows, :], w_ref[pl.ds(0, width), :]).astype(BF)
        return carry

    lax.fori_loop(0, blocks, query_block, 0)
    for kind in range(2):
        for side in range(2):

            @pl.when(can_get[side])
            def _():
                moves[kind, side][1].wait_recv()
                hands[kind, side].start()

    for kind in range(2):
        for side in range(2):

            @pl.when(can_get[side])
            def _():
                moves[kind, side][0].wait_recv()
                hands[kind, side].wait_recv()

    slab = 64

    def combine(i, carry):
        b, at = i // (kp // slab), i % (kp // slab)
        rows = pl.ds(pl.multiple_of(at * slab, slab), slab)
        total = c_ref[2, b] * unit[1, rows, :] + c_ref[3, b] * got[0, rows, :]
        total = total + c_ref[4, b] * unit[0, rows, :] + c_ref[5, b] * got[1, rows, :]
        s_ref[b, rows, :] = (total + c_ref[6, b] * part[b, rows, :]).astype(BF)
        return carry

    lax.fori_loop(0, blocks * (kp // slab), combine, 0)
    pairs = width // (2 * head)
    scale = head ** (-0.5)
    low_lane = lax.broadcasted_iota(jnp.int32, (kp, 2 * head), 1) < head

    def attend_block(b, carry):
        rows = pl.ds(pl.multiple_of(b * short, short), short)
        for j in range(pairs):
            cols = pl.ds(j * 2 * head, 2 * head)
            keys = head_pair(s_ref[b, :, cols], low_lane)
            values = head_pair(s_ref[b, :, pl.ds(width + j * 2 * head, 2 * head)], low_lane)
            scores = dot_t(q_ref[rows, cols], keys) * scale
            prob = jnp.concatenate(softmax_pair(scores, kp), axis=1).astype(BF)
            mix_ref[rows, cols] = dot(prob, values).astype(BF)
        branch = dot(mix_ref[rows, :], w_ref[pl.ds(3 * width, width), :])
        first = x_ref[rows, :].astype(F32) + branch
        sum_ref[rows, :] = first
        keep = (lax.broadcasted_iota(jnp.int32, (short, 1), 0) < n_ref[b]).astype(F32)
        stat_ref[...] += jnp.concatenate(
            [
                jnp.sum(keep * first * first, axis=0, keepdims=True),
                jnp.sum(keep * branch * branch, axis=0, keepdims=True),
            ],
            axis=0,
        )
        return carry

    stat_ref[...] = jnp.zeros_like(stat_ref)
    lax.fori_loop(0, blocks, attend_block, 0)
    for kind in range(2):
        for side in range(2):

            @pl.when(can_send[side])
            def _():
                for move in moves[kind, side]:
                    move.wait_send()

            @pl.when(can_get[side])
            def _():
                hands[kind, side].wait_send()


def forward(coef, n_valid, x, peer_x, w_att, e_own, e_peer, head, peers):
    rows, width = x.shape
    blocks, short, kp = e_own.shape
    vmem = pl.BlockSpec(memory_space=pltpu.VMEM)
    smem = pl.BlockSpec(memory_space=pltpu.SMEM)
    return pl.pallas_call(
        functools.partial(forward_body, peers // 2, head),
        in_specs=[smem] * 2 + [vmem] * 5,
        out_specs=[vmem] * 6,
        out_shape=[
            jax.ShapeDtypeStruct((rows, width), BF),
            jax.ShapeDtypeStruct((rows, 2 * width), BF),
            jax.ShapeDtypeStruct((blocks, kp, 2 * width), BF),
            jax.ShapeDtypeStruct((rows, width), BF),
            jax.ShapeDtypeStruct((rows, width), F32),
            jax.ShapeDtypeStruct((2, width), F32),
        ],
        scratch_shapes=[
            pltpu.VMEM((blocks, kp, 2 * width), F32),
            pltpu.VMEM((2, kp, 2 * width), F32),
            pltpu.VMEM((2, kp, 2 * width), F32),
            pltpu.SemaphoreType.DMA((12,)),
            pltpu.SemaphoreType.DMA((12,)),
        ],
        compiler_params=pltpu.CompilerParams(
            collective_id=3, has_side_effects=True, vmem_limit_bytes=VMEM_LIMIT
        ),
        cost_estimate=cost(2 * rows * width * width * 8, 200e6, rows * kp * 12),
        name="forward",
    )(coef, n_valid, x, peer_x, w_att, e_own, e_peer)


def normalize(values):
    mean = jnp.mean(values, axis=-1, keepdims=True)
    centered = values - mean
    inverse = lax.rsqrt(jnp.mean(centered * centered, axis=-1, keepdims=True) + eps_norm)
    return centered * inverse, inverse


def norm_back(grad_out, normed, inverse, gain):
    scaled = grad_out * gain
    return inverse * (
        scaled
        - jnp.mean(scaled, axis=-1, keepdims=True)
        - normed * jnp.mean(scaled * normed, axis=-1, keepdims=True)
    )


def feed_body(
    chunks,
    first_ref,
    w1_ref,
    w2_ref,
    wo_ref,
    cot_ref,
    np_ref,
    out_ref,
    hid_ref,
    up_ref,
    down_ref,
    flow_ref,
    dfirst_ref,
    dbranch_ref,
    dmix_ref,
    ng_ref,
    slope_ref,
):
    step = pl.program_id(0)
    rows, width = first_ref.shape
    deep = w2_ref.shape[0] // chunks
    down_rows = lambda c: w2_ref[pl.ds(c * deep, deep)].reshape(width, width)
    normed_one, inverse_one = normalize(first_ref[...])
    first_norm = normed_one * np_ref[0:1, :] + np_ref[1:2, :]
    first_low = first_norm.astype(BF)
    flow_ref[...] = first_low
    second = first_norm
    for c in range(chunks):
        cols = pl.ds(c * width, width)
        u = dot(first_low, w1_ref[:, c].reshape(width, width))
        cumulative = 0.5 * (1.0 + lax.erf(u * (1.0 / math.sqrt(2.0))))
        density = jnp.exp(-0.5 * u * u) * (1.0 / math.sqrt(2.0 * math.pi))
        slope_ref[:, cols] = cumulative + u * density
        hidden = (u * cumulative).astype(BF)
        hid_ref[:, cols] = hidden
        second = second + dot(hidden, down_rows(c))
    normed_two, inverse_two = normalize(second)
    out_ref[...] = (normed_two * np_ref[2:3, :] + np_ref[3:4, :]).astype(BF)
    grad_out = cot_ref[...].astype(F32)
    gain_two = jnp.sum(grad_out * normed_two, axis=0, keepdims=True)
    shift_two = jnp.sum(grad_out, axis=0, keepdims=True)
    grad_second = norm_back(grad_out, normed_two, inverse_two, np_ref[2:3, :])
    down = grad_second.astype(BF)
    down_ref[...] = down
    grad_first_norm = grad_second
    for c in range(chunks):
        cols = pl.ds(c * width, width)
        grad_hidden = dot_t(down, down_rows(c))
        up = (grad_hidden * slope_ref[:, cols]).astype(BF)
        up_ref[:, cols] = up
        grad_first_norm = grad_first_norm + dot_t(up, w1_ref[:, c].reshape(width, width))
    gain_one = jnp.sum(grad_first_norm * normed_one, axis=0, keepdims=True)
    shift_one = jnp.sum(grad_first_norm, axis=0, keepdims=True)
    grad_first = norm_back(grad_first_norm, normed_one, inverse_one, np_ref[0:1, :])
    dfirst_ref[...] = grad_first
    grad_branch = grad_first.astype(BF)
    dbranch_ref[...] = grad_branch
    dmix_ref[...] = dot_t(grad_branch, wo_ref[...]).astype(BF)
    sums = jnp.concatenate([gain_one, shift_one, gain_two, shift_two], axis=0)

    @pl.when(step == 0)
    def _():
        ng_ref[...] = sums

    @pl.when(step > 0)
    def _():
        ng_ref[...] += sums


def feed(first_sum, w_ffn, w_att, cotangent, norm_params, tile):
    rows, width = first_sum.shape
    groups, chunks, size, _ = w_ffn.shape
    groups = groups // 2
    ff = chunks * width
    row = lambda i: (i, 0)
    return pl.pallas_call(
        functools.partial(feed_body, chunks),
        grid=(rows // tile,),
        in_specs=[
            vspec((tile, width), row),
            vspec((groups, chunks, size, width), lambda i: (0, 0, 0, 0), True),
            vspec((groups, chunks, size, width), lambda i: (1, 0, 0, 0), True),
            vspec((width, width), lambda i: (3, 0), True),
            vspec((tile, width), row),
            vspec(norm_params.shape, lambda i: (0, 0)),
        ],
        out_specs=[
            vspec((tile, width), row),
            vspec((tile, ff), row),
            vspec((tile, ff), row),
            vspec((tile, width), row),
            vspec((tile, width), row),
            vspec((tile, width), row),
            vspec((tile, width), row),
            vspec((tile, width), row),
            vspec((4, width), lambda i: (0, 0)),
        ],
        out_shape=[
            jax.ShapeDtypeStruct((rows, width), BF),
            jax.ShapeDtypeStruct((rows, ff), BF),
            jax.ShapeDtypeStruct((rows, ff), BF),
            jax.ShapeDtypeStruct((rows, width), BF),
            jax.ShapeDtypeStruct((rows, width), BF),
            jax.ShapeDtypeStruct((rows, width), F32),
            jax.ShapeDtypeStruct((rows, width), BF),
            jax.ShapeDtypeStruct((rows, width), BF),
            jax.ShapeDtypeStruct((4, width), F32),
        ],
        scratch_shapes=[pltpu.VMEM((tile, ff), F32)],
        compiler_params=params(),
        cost_estimate=cost(2 * rows * width * ff * 4, 30e6, rows * ff * 2),
        name="feed",
    )(first_sum, w_ffn, w_ffn, w_att, cotangent, norm_params)


def attend_back_body(width, head, kp, q_ref, s_ref, g_ref, dq_ref, ds_ref):
    pairs = width // (2 * head)
    scale = head ** (-0.5)
    low_lane = lax.broadcasted_iota(jnp.int32, (kp, 2 * head), 1) < head
    for j in range(pairs):
        cols = pl.ds(j * 2 * head, 2 * head)
        vcols = pl.ds(width + j * 2 * head, 2 * head)
        keys = head_pair(s_ref[0, :, cols], low_lane)
        values = head_pair(s_ref[0, :, vcols], low_lane)
        q = q_ref[:, cols]
        g = g_ref[:, cols]
        prob = softmax_pair(dot_t(q, keys) * scale, kp)
        grad_prob = dot_t(g, values)
        low_parts = []
        for half in range(2):
            p = prob[half]
            d = grad_prob[:, half * kp : (half + 1) * kp]
            low_parts.append((p * (d - jnp.sum(p * d, axis=-1, keepdims=True))).astype(BF))
        grad_scores = jnp.concatenate(low_parts, axis=1)
        prob_low = jnp.concatenate(prob, axis=1).astype(BF)
        dq_ref[:, cols] = (dot(grad_scores, keys) * scale).astype(BF)
        dk = dot_l(grad_scores, q) * scale
        dv = dot_l(prob_low, g)
        ds_ref[0, :, cols] = jnp.where(low_lane, dk[:kp], dk[kp:])
        ds_ref[0, :, vcols] = jnp.where(low_lane, dv[:kp], dv[kp:])


def attend_back(q, summary, grad_mix, head):
    rows, width = q.shape
    blocks, kp, _ = summary.shape
    short = rows // blocks
    return pl.pallas_call(
        functools.partial(attend_back_body, width, head, kp),
        grid=(blocks,),
        in_specs=[
            vspec((short, width), lambda i: (i, 0)),
            vspec((1, kp, 2 * width), lambda i: (i, 0, 0)),
            vspec((short, width), lambda i: (i, 0)),
        ],
        out_specs=[
            vspec((short, width), lambda i: (i, 0)),
            vspec((1, kp, 2 * width), lambda i: (i, 0, 0)),
        ],
        out_shape=[
            jax.ShapeDtypeStruct((rows, width), BF),
            jax.ShapeDtypeStruct((blocks, kp, 2 * width), F32),
        ],
        compiler_params=params(),
        cost_estimate=cost(2 * rows * width * 8 * kp, 10e6, rows * kp * 12),
        name="attend_back",
    )(q, summary, grad_mix)


def outer_body(split, l_ref, r_ref, o_ref):
    value = dot_l(l_ref[...], r_ref[...])
    o_ref[...] = value.reshape(o_ref.shape).astype(o_ref.dtype)


def outer_up(first_low, grad_up, size, dtype):
    rows, width = first_low.shape
    chunks = grad_up.shape[1] // width
    groups = width // size
    return pl.pallas_call(
        functools.partial(outer_body, True),
        grid=(chunks,),
        in_specs=[
            vspec((rows, width), lambda i: (0, 0), True),
            vspec((rows, width), lambda i: (0, i)),
        ],
        out_specs=vspec((groups, 1, size, width), lambda i: (0, i, 0, 0)),
        out_shape=jax.ShapeDtypeStruct((groups, chunks, size, width), dtype),
        compiler_params=params(),
        cost_estimate=cost(2 * rows * width * width * chunks, 20e6),
        name="outer_up",
    )(first_low, grad_up)


def outer_rows(left, right, dtype, name):
    rows, width = right.shape[0], min(left.shape[1], right.shape[1])
    tall, wide = left.shape[1] // width, right.shape[1] // width
    moving = lambda n: (lambda i: (0, i)) if n > 1 else (lambda i: (0, 0))
    return pl.pallas_call(
        functools.partial(outer_body, False),
        grid=(tall * wide,),
        in_specs=[
            vspec((rows, width), moving(tall), tall == 1),
            vspec((rows, width), moving(wide), wide == 1),
        ],
        out_specs=vspec((width, width), lambda i: (i, 0)),
        out_shape=jax.ShapeDtypeStruct((tall * wide * width, width), dtype),
        compiler_params=params(),
        cost_estimate=cost(2 * rows * width * width * tall * wide, 20e6),
        name=name,
    )(left, right)


def back_body(
    width, blocks, c_ref, n_ref, e_ref, kv_ref, p_ref, *refs
):
    far_refs = refs[:4]
    dq_ref, w_ref, df_ref, dkv_ref, gp_ref, gi_ref = refs[4:]
    step = pl.program_id(0)
    short, kp = e_ref.shape[1], e_ref.shape[2]
    total = c_ref[step, 0] * p_ref[0]
    for other in range(1, blocks):
        total = total + c_ref[step, other] * p_ref[other]
    for k in range(4):
        total = total + c_ref[step, blocks + k] * far_refs[k][...].astype(F32)
    summary = total.astype(BF)
    dkv = dot(e_ref[0], summary).astype(BF)
    dkv_ref[...] = dkv
    keep = lax.broadcasted_iota(jnp.int32, (short, 1), 0) < n_ref[1, step]
    grad_e = jnp.where(keep, dot_t(kv_ref[...], summary), 0.0)
    column = n_ref[0, step]
    at = pl.multiple_of(jnp.minimum((column // 8) * 8, gp_ref.shape[0] - short - 8), 8)
    moved = pltpu.roll(
        jnp.concatenate([grad_e, jnp.zeros((8, kp), F32)], axis=0), column - at, 0
    )

    @pl.when(step == 0)
    def _():
        gp_ref[...] = jnp.zeros_like(gp_ref)

    gp_ref[pl.ds(at, short + 8), :] += moved
    gi_ref[...] = (
        df_ref[...]
        + dot_t(dq_ref[...], w_ref[pl.ds(0, width), :])
        + dot_t(dkv[:, :width], w_ref[pl.ds(width, width), :])
        + dot_t(dkv[:, width:], w_ref[pl.ds(2 * width, width), :])
    )


def back(coef, places, e_rows, kv, grad_parts, far_parts, dq, w_att, grad_first, positions):
    rows, width = dq.shape
    blocks, short, kp = e_rows.shape
    row = lambda i, *_: (i, 0)
    lead = lambda i, *_: (i, 0, 0)
    fixed = lambda i, *_: (0, 0)
    return pl.pallas_call(
        functools.partial(back_body, width, blocks),
        grid_spec=pltpu.PrefetchScalarGridSpec(
            num_scalar_prefetch=2,
            grid=(blocks,),
            in_specs=[
                vspec((1, short, kp), lead),
                vspec((short, 2 * width), row),
                vspec(grad_parts.shape, lambda i, *_: (0, 0, 0), True),
            ]
            + [vspec((kp, 2 * width), fixed, True)] * 4
            + [
                vspec((short, width), row),
                vspec((3 * width, width), fixed, True),
                vspec((short, width), row),
            ],
            out_specs=[
                vspec((short, 2 * width), row),
                vspec((positions, kp), fixed),
                vspec((short, width), row),
            ],
        ),
        out_shape=[
            jax.ShapeDtypeStruct((rows, 2 * width), BF),
            jax.ShapeDtypeStruct((positions, kp), F32),
            jax.ShapeDtypeStruct((rows, width), F32),
        ],
        compiler_params=params(),
        cost_estimate=cost(2 * rows * width * (3 * width + 4 * kp), 20e6),
        name="back",
    )(coef, places, e_rows, kv, grad_parts, *far_parts, dq, w_att, grad_first)


def reduce_body(depth, half, n_src, extra_keep, *refs):
    sources = refs[:n_src]
    outs = refs[n_src : n_src + 5]
    (own, got_c, sum_c, got_a, got_b, sum_a, sum_b, got_a2, got_b2, sum_z, got_z) = refs[
        n_src + 5 : n_src + 16
    ]
    keep_a, keep_b, keep_z = refs[n_src + 16 : n_src + 19]
    (e_own, e_got, e_sum, e_got1, e_sum1, e_got2, e_sum2, e_gotz, e_all, e_rows) = refs[
        n_src + 19 : n_src + 29
    ]
    send, recv, local = refs[n_src + 29 :]
    seq, mine = lax.axis_index("seq"), lax.axis_index("own")
    z, y, x, c = seq // 2, seq % 2, mine // 2, mine % 2
    core = (seq, 2 * x + (1 - c))
    along_x = (seq, 2 * (1 - x) + c)
    along_y = (2 * z + (1 - y), mine)
    along_z = [(2 * lax.rem(z + d, depth) + y, mine) for d in range(1, depth)]
    barrier = pltpu.get_barrier_semaphore()
    partners = [core, along_x, along_y] + along_z
    for partner in partners:
        pl.semaphore_signal(barrier, inc=1, device_id=partner, device_id_type=MESH_ID)
    pl.semaphore_wait(barrier, len(partners))

    sent = []

    def push(src, dst, partner):
        at = len(sent)
        copy = pltpu.make_async_remote_copy(
            src_ref=src,
            dst_ref=dst,
            send_sem=send.at[at],
            recv_sem=recv.at[at],
            device_id=partner,
            device_id_type=MESH_ID,
        )
        copy.start()
        sent.append(copy)
        return copy

    up, down, g_query, g_keyval, g_out, extra = sources
    bands = [g_query, g_keyval.at[0], g_keyval.at[1], g_out]
    half_z = depth // 2
    cols = own.shape[-1]
    loads = []

    def load(src, dst):
        copy = pltpu.make_async_copy(src, dst, local.at[len(loads)])
        copy.start()
        loads.append(copy)
        return copy

    e_first = [push(extra.at[:, :, 1 - c], e_got, core)]
    e_load = [load(extra.at[:, :, c], e_own)]
    piece_first, piece_load = [], []
    for p in range(6):
        at, part = p // 2, pl.ds((p % 2) * cols, cols)
        if at < 2:
            first = [
                push(up.at[:, :, 1 - c, at, :, part], got_c.at[p, pl.ds(0, half_z)], core),
                push(down.at[:, :, 1 - c, at, :, part], got_c.at[p, pl.ds(half_z, half_z)], core),
            ]
            kept = [
                load(up.at[:, :, c, at, :, part], own.at[p, pl.ds(0, half_z)]),
                load(down.at[:, :, c, at, :, part], own.at[p, pl.ds(half_z, half_z)]),
            ]
        else:
            first = [
                push(bands[m].at[:, 1 - c, :, part], got_c.at[p, m], core) for m in range(depth)
            ]
            kept = [load(bands[m].at[:, c, :, part], own.at[p, m]) for m in range(depth)]
        piece_first.append(first)
        piece_load.append(kept)

    state = {}

    def wait_recv(copies):
        for copy in copies:
            copy.wait_recv()

    low, high = pl.ds(0, half), pl.ds(half, half)

    def add(a, b):
        return a.astype(F32) + b.astype(F32)

    def piece_c(p):
        for copy in piece_load[p]:
            copy.wait()
        wait_recv(piece_first[p])

        def body(i, carry):
            zz, w = i // 2, i % 2
            to_x, to_y = 2 * w + 1 - x, 2 * (1 - y) + w
            sum_c[p, 0, zz, w] = add(own[p, zz, to_x, low, :], got_c[p, zz, to_x, low, :]).astype(BF)
            sum_c[p, 1, zz, w] = add(own[p, zz, to_y, high, :], got_c[p, zz, to_y, high, :]).astype(BF)
            return carry

        lax.fori_loop(0, depth * 2, body, 0)
        state["1", p] = [
            push(sum_c.at[p, 0], got_a.at[p], along_x),
            push(sum_c.at[p, 1], got_b.at[p], along_y),
        ]

    def piece_1(p):
        wait_recv(state["1", p])

        def side_a(zz, w):
            at = 2 * w + x
            return add(own[p, zz, at, low, :], got_c[p, zz, at, low, :]) + got_a[p, zz, w].astype(F32)

        def side_b(zz, w):
            at = 2 * y + w
            return add(own[p, zz, at, high, :], got_c[p, zz, at, high, :]) + got_b[p, zz, w].astype(F32)

        def body(zz, carry):
            sum_a[p, zz] = side_a(zz, 1 - y).astype(BF)
            sum_b[p, zz] = side_b(zz, 1 - x).astype(BF)
            keep_a[p, zz] = side_a(zz, y)
            keep_b[p, zz] = side_b(zz, x)
            return carry

        lax.fori_loop(0, depth, body, 0)
        state["2", p] = [
            push(sum_a.at[p], got_a2.at[p], along_y),
            push(sum_b.at[p], got_b2.at[p], along_x),
        ]

    def piece_2(p):
        wait_recv(state["2", p])

        def body(zz, carry):
            total_a = keep_a[p, zz] + got_a2[p, zz].astype(F32)
            total_b = keep_b[p, zz] + got_b2[p, zz].astype(F32)
            sum_z[p, zz, low, :] = total_a.astype(BF)
            sum_z[p, zz, high, :] = total_b.astype(BF)
            return carry

        lax.fori_loop(0, depth, body, 0)
        keep_z[p, low, :] = keep_a[p, z] + got_a2[p, z].astype(F32)
        keep_z[p, high, :] = keep_b[p, z] + got_b2[p, z].astype(F32)
        state["z", p] = [
            push(sum_z.at[p, lax.rem(z + d, depth)], got_z.at[p, d - 1], along_z[d - 1])
            for d in range(1, depth)
        ]

    def piece_z(p):
        wait_recv(state["z", p])
        total = keep_z[p]
        for d in range(depth - 1):
            total = total + got_z[p, d].astype(F32)
        outs[p // 2][:, pl.ds((p % 2) * cols, cols)] = total

    def extra_c():
        e_load[0].wait()
        wait_recv(e_first)

        def body(i, carry):
            zz, yx = i // 4, i % 4
            e_sum[zz, yx // 2, yx % 2] = e_own[zz, yx] + e_got[zz, yx]
            return carry

        lax.fori_loop(0, depth * 4, body, 0)
        state["ez"] = [
            push(e_sum.at[lax.rem(z + d, depth)], e_gotz.at[d - 1], along_z[d - 1])
            for d in range(1, depth)
        ]

    def extra_1():
        wait_recv(state["ez"])

        def body(i, carry):
            yy, xx = i // 2, i % 2
            total = e_sum[z, yy, xx]
            for d in range(depth - 1):
                total = total + e_gotz[d, yy, xx]
            e_sum1[yy, xx] = total
            return carry

        lax.fori_loop(0, 4, body, 0)
        state["e1"] = [push(e_sum1.at[:, 1 - x], e_got1, along_x)]

    def extra_2():
        wait_recv(state["e1"])

        def body(yy, carry):
            e_sum2[yy] = e_sum1[yy, x] + e_got1[yy]
            return carry

        lax.fori_loop(0, 2, body, 0)
        state["e2"] = [push(e_sum2.at[1 - y], e_got2, along_y)]

    def extra_z():
        wait_recv(state["e2"])
        e_all[z, y] = e_sum2[y] + e_got2[...]
        state["gz"] = [push(e_all.at[z, y], e_all.at[z, y], there) for there in along_z]

    def extra_gather_y():
        wait_recv(state["gz"])
        state["gy"] = [push(e_all.at[:, y], e_all.at[:, y], along_y)]

    def extra_gather_x():
        wait_recv(state["gy"])
        e_rows[x, c] = e_all[:, :, pl.ds(extra_keep, e_rows.shape[4]), :]
        state["gx"] = [push(e_rows.at[x, c], e_rows.at[x, c], along_x)]

    def extra_gather_c():
        wait_recv(state["gx"])
        state["gc"] = [push(e_rows.at[:, c], e_rows.at[:, c], core)]

    stages = [piece_c, piece_1, piece_2, piece_z]
    small = [extra_c, extra_1, extra_2, extra_z, extra_gather_y, extra_gather_x, extra_gather_c]
    for turn in range(9):
        if turn < len(small):
            small[turn]()
        for stage in range(4):
            if 0 <= turn - stage < 6:
                stages[stage](turn - stage)
    outs[3][...] = e_all[:, :, pl.ds(0, extra_keep), :]
    wait_recv(state["gc"])
    outs[4][...] = e_rows[...]
    for copy in sent:
        copy.wait_send()


def reduce_all(g_query, g_keyval, g_out, g_up, g_down, extra, peers):
    depth = peers // 2
    size, width = g_up.shape[2], g_up.shape[3]
    half = size // 2
    e_rows_all, kp = extra.shape[1], extra.shape[2]
    keep = e_rows_all - 8
    sources = (
        [
            g_up.reshape(depth // 2, 4, 2, 2, size, width),
            g_down.reshape(depth // 2, 4, 2, 2, size, width),
        ]
        + [
            g_query.reshape(4, 2, size, width),
            g_keyval.reshape(2, 4, 2, size, width),
            g_out.reshape(4, 2, size, width),
        ]
        + [extra.reshape(depth, 4, 2, e_rows_all, kp)]
    )
    n_src = len(sources)
    cols = width // 2
    messages = 1 + 8 + 2 * depth + 6 * (4 + depth - 1) + 2 + 2 * (depth - 1) + 3
    loads = 1 + 8 + 2 * depth
    any_spec = pl.BlockSpec(memory_space=pl.ANY)
    vmem = pl.BlockSpec(memory_space=pltpu.VMEM)
    scratch = [
        pltpu.VMEM((6, depth, 4, size, cols), BF),
        pltpu.VMEM((6, depth, 4, size, cols), BF),
        pltpu.VMEM((6, 2, depth, 2, half, cols), BF),
        pltpu.VMEM((6, depth, 2, half, cols), BF),
        pltpu.VMEM((6, depth, 2, half, cols), BF),
        pltpu.VMEM((6, depth, half, cols), BF),
        pltpu.VMEM((6, depth, half, cols), BF),
        pltpu.VMEM((6, depth, half, cols), BF),
        pltpu.VMEM((6, depth, half, cols), BF),
        pltpu.VMEM((6, depth, size, cols), BF),
        pltpu.VMEM((6, depth - 1, size, cols), BF),
        pltpu.VMEM((6, depth, half, cols), F32),
        pltpu.VMEM((6, depth, half, cols), F32),
        pltpu.VMEM((6, size, cols), F32),
        pltpu.VMEM((depth, 4, e_rows_all, kp), F32),
        pltpu.VMEM((depth, 4, e_rows_all, kp), F32),
        pltpu.VMEM((depth, 2, 2, e_rows_all, kp), F32),
        pltpu.VMEM((2, e_rows_all, kp), F32),
        pltpu.VMEM((2, 2, e_rows_all, kp), F32),
        pltpu.VMEM((e_rows_all, kp), F32),
        pltpu.VMEM((2, e_rows_all, kp), F32),
        pltpu.VMEM((depth - 1, 2, 2, e_rows_all, kp), F32),
        pltpu.VMEM((depth, 2, e_rows_all, kp), F32),
        pltpu.VMEM((2, 2, depth, 2, 8, kp), F32),
        pltpu.SemaphoreType.DMA((messages,)),
        pltpu.SemaphoreType.DMA((messages,)),
        pltpu.SemaphoreType.DMA((loads,)),
    ]
    return pl.pallas_call(
        functools.partial(reduce_body, depth, half, n_src, keep),
        in_specs=[any_spec] * n_src,
        out_specs=[vmem] * 5,
        out_shape=[jax.ShapeDtypeStruct((size, width), F32)] * 3
        + [
            jax.ShapeDtypeStruct((depth, 2, keep, kp), F32),
            jax.ShapeDtypeStruct((2, 2, depth, 2, 8, kp), F32),
        ],
        scratch_shapes=scratch,
        compiler_params=pltpu.CompilerParams(
            collective_id=1, has_side_effects=True, vmem_limit_bytes=VMEM_LIMIT
        ),
        name="reduce_all",
    )(*sources)


def gather_body(depth, half, band_ref, proj_ref, out_ref, pout_ref, send, recv, local):
    seq, mine = lax.axis_index("seq"), lax.axis_index("own")
    z, y, x, c = seq // 2, seq % 2, mine // 2, mine % 2
    core = (seq, 2 * x + (1 - c))
    along_x = (seq, 2 * (1 - x) + c)
    along_y = (2 * z + (1 - y), mine)
    order = [1, 3, 2]
    along_z = [(2 * lax.rem(z + d, depth) + y, mine) for d in order]
    barrier = pltpu.get_barrier_semaphore()
    partners = [core, along_x, along_y] + along_z
    for partner in partners:
        pl.semaphore_signal(barrier, inc=1, device_id=partner, device_id_type=MESH_ID)
    pl.semaphore_wait(barrier, len(partners))

    sent = []

    def push(src, dst, partner):
        at = len(sent)
        copy = pltpu.make_async_remote_copy(
            src_ref=src,
            dst_ref=dst,
            send_sem=send.at[at],
            recv_sem=recv.at[at],
            device_id=partner,
            device_id_type=MESH_ID,
        )
        copy.start()
        sent.append(copy)
        return copy

    keep = pltpu.make_async_copy(band_ref, out_ref.at[z, y, x, c], local.at[0])
    keep.start()
    keep_p = pltpu.make_async_copy(proj_ref, pout_ref.at[x, c], local.at[1])
    keep_p.start()
    mine_at = out_ref.at[z, y, x, c]
    from_z = [push(band_ref, mine_at, there) for there in along_z]
    from_x = [push(band_ref, mine_at, along_x)]
    from_y = [push(band_ref, mine_at, along_y)]
    proj_x = push(proj_ref, pout_ref.at[x, c], along_x)
    last = [push(band_ref, mine_at, core), push(proj_ref, pout_ref.at[x, c], core)]
    planes = [z]
    for k in range(depth - 1):
        from_z[k].wait_recv()
        plane = lax.rem(z + depth - order[k], depth)
        planes.append(plane)
        slab = out_ref.at[plane, y, x, c]
        from_x.append(push(slab, slab, along_x))
        from_y.append(push(slab, slab, along_y))
        last.append(push(slab, slab, core))
    low, high = pl.ds(0, half), pl.ds(half, half)
    cross = []
    for k in range(depth):
        plane = planes[k]
        from_x[k].wait_recv()
        slab = out_ref.at[plane, y, 1 - x, c]
        part = out_ref.at[plane, y, 1 - x, c, low, :]
        cross_y = push(part, part, along_y)
        last.append(push(slab, slab, core))
        from_y[k].wait_recv()
        slab = out_ref.at[plane, 1 - y, x, c]
        part = out_ref.at[plane, 1 - y, x, c, high, :]
        cross.append((cross_y, push(part, part, along_x)))
        last.append(push(slab, slab, core))
        if k == 0:
            proj_x.wait_recv()
            slab = pout_ref.at[1 - x, c]
            last.append(push(slab, slab, core))
    for k in range(depth):
        for copy in cross[k]:
            copy.wait_recv()
        slab = out_ref.at[planes[k], 1 - y, 1 - x, c]
        last.append(push(slab, slab, core))
    for copy in last:
        copy.wait_recv()
    keep.wait()
    keep_p.wait()
    for copy in sent:
        copy.wait_send()


def gather_bands(band, proj, peers):
    depth = peers // 2
    size, width = band.shape
    messages = (depth - 1) + 3 + 2 + 3 * (depth - 1) + 4 * depth + 1 + depth
    vmem = pl.BlockSpec(memory_space=pltpu.VMEM)
    return pl.pallas_call(
        functools.partial(gather_body, depth, size // 2),
        in_specs=[vmem] * 2,
        out_specs=[vmem] * 2,
        out_shape=[
            jax.ShapeDtypeStruct((depth, 2, 2, 2, size, width), BF),
            jax.ShapeDtypeStruct((2, 2) + proj.shape, BF),
        ],
        scratch_shapes=[
            pltpu.SemaphoreType.DMA((messages,)),
            pltpu.SemaphoreType.DMA((messages,)),
            pltpu.SemaphoreType.DMA((2,)),
        ],
        compiler_params=pltpu.CompilerParams(
            collective_id=2, has_side_effects=True, vmem_limit_bytes=VMEM_LIMIT
        ),
        cost_estimate=cost(1e9, 90e6),
        name="gather_bands",
    )(band, proj)


def shampoo(grad, left, right, root_left, root_right, weight):
    new_left = decay * left + (1.0 - decay) * jnp.einsum(
        "tij,tkj->tik", grad, grad, precision=highest
    )
    new_right = decay * right + (1.0 - decay) * jnp.einsum(
        "tji,tjk->tik", grad, grad, precision=highest
    )
    inner = jnp.einsum("tij,tjk->tik", grad, root_right, precision=highest)
    step = jnp.einsum("tij,tjk->tik", root_left, inner, precision=highest)
    return (new_left, new_right, weight - rate_matrix * step)


def to_matrix(tiles, rows, cols):
    size = tiles.shape[-1]
    return (
        tiles.reshape(rows // size, cols // size, size, size)
        .transpose(0, 2, 1, 3)
        .reshape(rows, cols)
    )


def to_bands(tiles, cols):
    count, size, _ = tiles.shape
    return to_matrix(tiles, count * size * size // cols, cols)


def from_bands(bands, size):
    rows, cols = bands.shape
    return (
        bands.reshape(rows // size, size, cols // size, size)
        .transpose(0, 2, 1, 3)
        .reshape(-1, size, size)
    )


def gather_weights(weights, projection, att_dev, width, both, fused, peers):
    size = weights.shape[-1]
    low = weights.astype(BF)
    groups, chunks = width // size, FF // width
    if banded(weights.shape[0], att_dev, width, size):
        ffn = lax.all_gather(to_bands(low[att_dev:], width), both, axis=0, tiled=True)
        band = to_bands(low[:att_dev], width)
        if fused:
            att, proj = gather_bands(band, projection.astype(BF), peers)
            att, proj = att.reshape(-1, width), proj.reshape(-1, projection.shape[1])
        else:
            att = lax.all_gather(band, both, axis=0, tiled=True)
            proj = lax.all_gather(projection.astype(BF), "own", axis=0, tiled=True)
        return att, ffn.reshape(2 * groups, chunks, size, width), proj
    per_dev = weights.shape[0]
    proj = lax.all_gather(projection.astype(BF), "own", axis=0, tiled=True)
    grid = lax.all_gather(low, both, axis=0, tiled=True).reshape(-1, per_dev, size, size)
    att = to_bands(grid[:, :att_dev].reshape(-1, size, size), width)
    tiles = grid[:, att_dev:].reshape(-1, size, size)
    half = tiles.shape[0] // 2
    w_up = to_matrix(tiles[:half], width, FF).reshape(groups, size, chunks, width)
    w_down = to_matrix(tiles[half:], FF, width).reshape(groups, chunks, size, width)
    return att, jnp.concatenate([w_up.transpose(0, 2, 1, 3), w_down], axis=0), proj


def banded(per_dev, att_dev, width, size):
    wide = width // size
    return att_dev % wide == 0 and (per_dev - att_dev) % wide == 0


def scatter_weight_grads(g_att, g_up, g_down, per_dev, att_dev, both):
    size, width = g_up.shape[2], g_up.shape[3]
    if banded(per_dev, att_dev, width, size):
        ffn = jnp.concatenate([g_up.reshape(-1, width), g_down], axis=0)
        ffn = lax.psum_scatter(ffn, both, scatter_dimension=0, tiled=True)
        att = lax.psum_scatter(g_att, both, scatter_dimension=0, tiled=True)
        return jnp.concatenate([from_bands(att, size), from_bands(ffn, size)], axis=0)
    up = g_up.transpose(0, 2, 1, 3).reshape(width, -1)
    att = from_bands(g_att, size)
    ffn = jnp.concatenate([from_bands(up, size), from_bands(g_down, size)], axis=0)
    stacked = jnp.concatenate(
        [
            att.reshape(-1, att_dev, size, size),
            ffn.reshape(-1, per_dev - att_dev, size, size),
        ],
        axis=1,
    ).reshape(-1, size, size)
    return lax.psum_scatter(stacked, both, scatter_dimension=0, tiled=True)


def per_device(
    tokens,
    cotangent,
    lengths,
    offsets,
    valid_count,
    weights,
    stat_left,
    stat_right,
    root_left,
    root_right,
    projection,
    projection_left,
    projection_right,
    projection_root_left,
    projection_root_right,
    norm_params,
    norm_stat,
):
    both = ("seq", "own")
    size = weights.shape[-1]
    width = tokens.shape[-1]
    rows_here = tokens.shape[1]
    head = width // HEADS
    kp = projection.shape[1]
    blocks = rows_here // SHORT
    peers = lax.axis_size("seq")
    devices = peers * lax.axis_size("own")
    per_dev = weights.shape[0]
    att_dev = 4 * (width // size) ** 2 // devices
    x = tokens[0]
    seq = lax.axis_index("seq")
    side = seq % 2

    swap = [(i, i ^ 1) for i in range(peers)]
    peer_x = lax.ppermute(x, "seq", swap)
    own_size = lax.axis_size("own")
    fused = own_size == 4 and peers == 8 and banded(per_dev, att_dev, width, size)
    w_att, w_ffn, proj_all = gather_weights(
        weights, projection, att_dev, width, both, fused, peers
    )

    lens, offs, counts = lengths[0], offsets[0], valid_count[0]
    ends = jnp.cumsum(lens)
    starts = ends - lens
    unit_rows = 2 * rows_here
    unit_start = (seq - side) * rows_here
    unit_end = unit_start + unit_rows
    block_row = unit_start + SHORT * jnp.arange(2 * blocks, dtype=jnp.int32)
    hot = ((starts[None, :] <= block_row[:, None]) & (block_row[:, None] < ends[None, :])).astype(
        jnp.int32
    )
    b_start = jnp.sum(hot * starts[None, :], axis=1)
    b_end = jnp.sum(hot * ends[None, :], axis=1)
    place = block_row - b_start
    column = jnp.sum(hot * offs[None, :], axis=1) + place
    n_valid = jnp.clip(jnp.sum(hot * counts[None, :], axis=1) - place, 0, SHORT)
    is_head = b_start == b_start[0]
    is_tail = b_start == b_start[-1]
    own_at = side * blocks
    peer_at = (1 - side) * blocks
    take = lambda v, at: lax.dynamic_slice_in_dim(v, at, blocks, 0)

    def proj_rows(at):
        col, n = take(column, at), take(n_valid, at)
        rows = jnp.stack(
            [lax.dynamic_slice_in_dim(proj_all, col[b], SHORT, 0) for b in range(blocks)]
        )
        keep = lax.broadcasted_iota(jnp.int32, (blocks, SHORT, 1), 1) < n[:, None, None]
        return jnp.where(keep, rows, jnp.zeros((), BF))

    e_own = proj_rows(own_at)
    e_peer = proj_rows(peer_at)
    n_own = take(n_valid, own_at)

    coef = lambda flag, at: take(flag, at).astype(F32)
    head_cross = (b_start[0] < unit_start).astype(F32)
    tail_cross = (b_end[-1] > unit_end).astype(F32)
    own_head, own_tail = coef(is_head, own_at), coef(is_tail, own_at)
    if fused:
        pick_tail = (1.0 - own_head) * own_tail
        unit_coef = lambda flag: jnp.concatenate([coef(flag, own_at), coef(flag, peer_at)])
        pad = lambda v: jnp.concatenate([v, jnp.zeros((blocks,), F32)])
        table = jnp.stack(
            [
                unit_coef(is_head),
                unit_coef(is_tail),
                pad(own_head),
                pad(own_head * head_cross),
                pad(pick_tail),
                pad(pick_tail * tail_cross),
                pad((1.0 - own_head) * (1.0 - own_tail)),
            ]
        )
        query, keyval, summary, mixed, first_sum, row_sums = forward(
            table, n_own, x, peer_x, w_att, e_own, e_peer, head, peers
        )
    else:
        query, keyval, part_own = project(x, w_att, e_own.transpose(0, 2, 1), True)
        (part_peer,) = project(peer_x, w_att, e_peer.transpose(0, 2, 1), False)

        def unit_sum(flag):
            mine = coef(flag, own_at)
            theirs = coef(flag, peer_at)
            total = mine[0] * part_own[0]
            for b in range(1, blocks):
                total = total + mine[b] * part_own[b]
            for b in range(blocks):
                total = total + theirs[b] * part_peer[b]
            return total

        head_sum, tail_sum = unit_sum(is_head), unit_sum(is_tail)
        from_left = lax.ppermute(tail_sum, "seq", [(i, i + 2) for i in range(peers - 2)])
        from_right = lax.ppermute(head_sum, "seq", [(i + 2, i) for i in range(peers - 2)])
        summary = jnp.stack(
            [
                jnp.where(
                    own_head[b] > 0,
                    head_sum + head_cross * from_left,
                    jnp.where(own_tail[b] > 0, tail_sum + tail_cross * from_right, part_own[b]),
                ).astype(BF)
                for b in range(blocks)
            ]
        )
        mixed, first_sum, row_sums = attend(n_own, query, summary, w_att, x, head)
    (
        result,
        hidden,
        grad_up,
        grad_down,
        first_low,
        grad_first,
        grad_branch,
        grad_mix,
        norm_terms,
    ) = feed(first_sum, w_ffn, w_att, cotangent[0], norm_params, 256)
    grad_query, grad_parts = attend_back(query, summary, grad_mix, head)

    row_start = seq * rows_here
    row_end = row_start + rows_here
    o_start, o_end = take(b_start, own_at), take(b_end, own_at)
    g_head = grad_parts[0]
    g_tail = grad_parts[-1]
    for b in range(1, blocks):
        g_head = g_head + (o_start[b] == o_start[0]).astype(F32) * grad_parts[b]
    for b in range(blocks - 1):
        g_tail = g_tail + (o_start[b] == o_start[-1]).astype(F32) * grad_parts[b]
    low_head, low_tail = g_head.astype(BF), g_tail.astype(BF)
    far_parts, far_flags = [], []
    at_head = (o_start == o_start[0]).astype(F32)
    at_tail = (o_start == o_start[-1]).astype(F32)
    for far in (1, 2):
        reach = (far - 1) * rows_here
        far_parts.append(lax.ppermute(low_tail, "seq", [(i, i + far) for i in range(peers - far)]))
        far_flags.append(at_head * (o_start[0] < row_start - reach).astype(F32))
        far_parts.append(lax.ppermute(low_head, "seq", [(i + far, i) for i in range(peers - far)]))
        far_flags.append(at_tail * (o_end[-1] > row_end + reach).astype(F32))
    together = (o_start[:, None] == o_start[None, :]).astype(F32)
    coef_back = jnp.concatenate([together, jnp.stack(far_flags, axis=1)], axis=1)
    own_col = take(column, own_at)
    gtype = BF if fused else F32
    g_up = outer_up(first_low, grad_up, size, gtype)
    g_down = outer_rows(hidden, grad_down, gtype, "outer_down")
    g_out = outer_rows(mixed, grad_branch, gtype, "outer_out")
    g_query = outer_rows(x, grad_query, gtype, "outer_query")
    grad_keyval, grad_proj, grad_input = back(
        coef_back,
        jnp.stack([own_col, n_own]),
        e_own,
        keyval,
        grad_parts,
        far_parts,
        grad_query,
        w_att,
        grad_first,
        proj_all.shape[0],
    )
    g_keyval = outer_rows(x, grad_keyval, gtype, "outer_keyval")
    part_rows = projection.shape[0]
    valid_here = jnp.sum(n_own).astype(F32)
    extra = jnp.concatenate(
        [
            norm_terms.reshape(-1, kp),
            row_sums.reshape(-1, kp),
            jnp.full((1, kp), 1.0 / kp, F32) * valid_here,
        ],
        axis=0,
    )
    n_norm = 4 * width // kp
    n_row = 2 * width // kp
    if fused:
        extra = jnp.pad(extra, ((0, devices - extra.shape[0]), (0, 0)))[:, None, :]
        extra = jnp.pad(extra, ((0, 0), (0, 7), (0, 0)))
        shares = grad_proj.reshape(own_size, peers, part_rows // peers, kp).swapaxes(0, 1)
        shares = shares.reshape(devices, part_rows // peers, kp)
        ffn_a, ffn_b, att, proj_parts, rows = reduce_all(
            g_query, g_keyval, g_out, g_up, g_down, jnp.concatenate([shares, extra], axis=1), peers
        )
        owned = jnp.concatenate(
            [from_bands(att, size), from_bands(ffn_a, size), from_bands(ffn_b, size)], axis=0
        )
        proj_grad = proj_parts.reshape(part_rows, kp)
        totals = rows[..., 0, :].transpose(2, 3, 0, 1, 4).reshape(devices, kp)
    else:
        owned = scatter_weight_grads(
            jnp.concatenate([g_query, g_keyval, g_out], axis=0), g_up, g_down, per_dev, att_dev, both
        )
        packed = jnp.concatenate([grad_proj, extra], axis=0)
        packed = lax.psum(jnp.pad(packed, ((0, -packed.shape[0] % 16), (0, 0))), both)
        proj_grad = lax.dynamic_slice_in_dim(
            packed, lax.axis_index("own") * part_rows, part_rows, 0
        )
        totals = packed[grad_proj.shape[0] :]
    norm_grad = totals[:n_norm].reshape(4, width)
    row_total = totals[n_norm : n_norm + n_row].reshape(2, width).sum(axis=1)
    valid_total = totals[n_norm + n_row].sum()
    residual_rms = jnp.sqrt(row_total / (valid_total * width))
    left_new, right_new, weights_new = shampoo(
        owned, stat_left, stat_right, root_left, root_right, weights
    )
    proj_left_new, proj_right_new, proj_blocks = shampoo(
        proj_grad.reshape(-1, kp, kp),
        projection_left,
        projection_right,
        projection_root_left,
        projection_root_right,
        projection.reshape(-1, kp, kp),
    )
    stat_new = decay * norm_stat + (1.0 - decay) * norm_grad * norm_grad
    norm_new = norm_params - rate_norm * norm_grad * lax.rsqrt(stat_new)
    return (
        result[None],
        grad_input[None],
        owned,
        left_new,
        right_new,
        weights_new,
        proj_grad,
        proj_left_new,
        proj_right_new,
        proj_blocks.reshape(part_rows, kp),
        norm_grad,
        stat_new,
        norm_new,
        residual_rms,
    )


def solution(mesh):
    pack = P("own", "seq", None)
    table = P("own", None)
    tile = P(("seq", "own"), None, None)
    proj = P("own", None, None)
    return jax.shard_map(
        per_device,
        mesh=mesh,
        in_specs=(pack, pack, table, table, table)
        + (tile,) * 5
        + (table, proj, proj, proj, proj, P(), P()),
        out_specs=(pack, pack) + (tile,) * 4 + (table, proj, proj, table, P(), P(), P(), P()),
        check_vma=False,
    )
```

```python
import functools
import math

import jax
import jax.numpy as jnp
from jax import lax
from jax.experimental import pallas as pl
from jax.experimental.pallas import tpu as pltpu
from jax.sharding import PartitionSpec as P

HEADS = 12
FF = 3072
SHORT = 512
BF = jnp.bfloat16
F32 = jnp.float32

eps_norm = 1e-05
decay = 0.5
rate_matrix = 0.2
rate_norm = 0.2
highest = lax.Precision.HIGHEST
VMEM_LIMIT = 60 * 1024 * 1024
MESH_ID = pl.DeviceIdType.MESH


def dot(a, b):
    return lax.dot_general(a, b, (((1,), (0,)), ((), ())), preferred_element_type=F32)


def dot_t(a, b):
    return lax.dot_general(a, b, (((1,), (1,)), ((), ())), preferred_element_type=F32)


def dot_l(a, b):
    return lax.dot_general(a, b, (((0,), (0,)), ((), ())), preferred_element_type=F32)


def vspec(shape, index_map, once=False):
    if once:
        return pl.BlockSpec(shape, index_map, pipeline_mode=pl.Buffered(1))
    return pl.BlockSpec(shape, index_map)


def params():
    return pltpu.CompilerParams(
        dimension_semantics=("arbitrary",), vmem_limit_bytes=VMEM_LIMIT
    )


def cost(flops, nbytes, trans=0):
    return pl.CostEstimate(flops=int(flops), bytes_accessed=int(nbytes), transcendentals=int(trans))


def tables_body(blocks, rows_here, l_ref, o_ref, v_ref, i_ref, f_ref, b_ref):
    seq = lax.axis_index("seq")
    side = seq % 2
    row_start = seq * rows_here
    row_end = row_start + rows_here
    unit_start = (seq - side) * rows_here
    peer_start = (seq + 1 - 2 * side) * rows_here
    flag = lambda cond: jnp.where(cond, 1.0, 0.0).astype(F32)

    def locate(row):
        def body(i, carry):
            at, start, end, off, count = carry
            stop = at + l_ref[0, i]
            inside = jnp.logical_and(row >= at, row < stop)
            pick = lambda new, old: jnp.where(inside, new, old)
            return (
                stop,
                pick(at, start),
                pick(stop, end),
                pick(o_ref[0, i], off),
                pick(v_ref[0, i], count),
            )

        zero = jnp.int32(0)
        return lax.fori_loop(0, l_ref.shape[1], body, (zero,) * 5)[1:]

    starts, ends = [], []
    for k in range(2 * blocks):
        row = row_start + SHORT * k if k < blocks else peer_start + SHORT * (k - blocks)
        start, end, off, count = locate(row)
        starts.append(start)
        ends.append(end)
        i_ref[0, k] = off + row - start
        i_ref[1, k] = jnp.clip(count - (row - start), 0, SHORT)
    first = jnp.where(side == 0, starts[0], starts[blocks])
    last = jnp.where(side == 0, starts[-1], starts[blocks - 1])
    last_end = jnp.where(side == 0, ends[-1], ends[blocks - 1])
    head_cross = flag(first < unit_start)
    tail_cross = flag(last_end > unit_start + 2 * rows_here)
    for k in range(2 * blocks):
        is_head, is_tail = flag(starts[k] == first), flag(starts[k] == last)
        pick_tail = (1.0 - is_head) * is_tail
        f_ref[0, k] = is_head
        f_ref[1, k] = is_tail
        f_ref[2, k] = is_head
        f_ref[3, k] = is_head * head_cross
        f_ref[4, k] = pick_tail
        f_ref[5, k] = pick_tail * tail_cross
        f_ref[6, k] = (1.0 - is_head) * (1.0 - is_tail)
    own_last, own_end = starts[blocks - 1], ends[blocks - 1]
    for k in range(blocks):
        at_head, at_tail = flag(starts[k] == starts[0]), flag(starts[k] == own_last)
        for other in range(blocks):
            b_ref[k, other] = flag(starts[k] == starts[other])
        for far in range(2):
            reach = far * rows_here
            b_ref[k, blocks + 2 * far] = at_head * flag(starts[0] < row_start - reach)
            b_ref[k, blocks + 2 * far + 1] = at_tail * flag(own_end > row_end + reach)


def tables(lengths, offsets, valid_count, blocks, rows_here):
    smem = pl.BlockSpec(memory_space=pltpu.SMEM)
    return pl.pallas_call(
        functools.partial(tables_body, blocks, rows_here),
        in_specs=[smem] * 3,
        out_specs=[smem] * 3,
        out_shape=[
            jax.ShapeDtypeStruct((2, 2 * blocks), jnp.int32),
            jax.ShapeDtypeStruct((7, 2 * blocks), F32),
            jax.ShapeDtypeStruct((blocks, blocks + 4), F32),
        ],
        name="tables",
    )(lengths, offsets, valid_count)


def project_body(width, with_query, x_ref, w_ref, e_ref, *outs):
    x = x_ref[...]
    if with_query:
        q_ref, kv_ref, p_ref = outs
        q_ref[...] = dot(x, w_ref[pl.ds(0, width), :]).astype(BF)
    else:
        (p_ref,) = outs
    e = e_ref[0]
    for part in range(2):
        kv = dot(x, w_ref[pl.ds((1 + part) * width, width), :]).astype(BF)
        if with_query:
            kv_ref[:, pl.ds(part * width, width)] = kv
        p_ref[0, :, pl.ds(part * width, width)] = dot(e, kv)


def project(x, w_att, e_t, with_query):
    rows, width = x.shape
    blocks, kp, short = e_t.shape
    out_shape = [jax.ShapeDtypeStruct((blocks, kp, 2 * width), F32)]
    out_specs = [vspec((1, kp, 2 * width), lambda i: (i, 0, 0))]
    if with_query:
        out_shape = [
            jax.ShapeDtypeStruct((rows, width), BF),
            jax.ShapeDtypeStruct((rows, 2 * width), BF),
        ] + out_shape
        out_specs = [
            vspec((short, width), lambda i: (i, 0)),
            vspec((short, 2 * width), lambda i: (i, 0)),
        ] + out_specs
    return pl.pallas_call(
        functools.partial(project_body, width, with_query),
        grid=(blocks,),
        in_specs=[
            vspec((short, width), lambda i: (i, 0)),
            vspec((3 * width, width), lambda i: (0, 0), True),
            vspec((1, kp, short), lambda i: (i, 0, 0)),
        ],
        out_specs=out_specs,
        out_shape=out_shape,
        compiler_params=params(),
        cost_estimate=cost(2 * rows * width * width * 3, 12e6),
        name="project" if with_query else "project_peer",
    )(x, w_att, e_t)


def head_pair(ref_slice, low_lane):
    zero = jnp.zeros_like(ref_slice)
    return jnp.concatenate(
        [jnp.where(low_lane, ref_slice, zero), jnp.where(low_lane, zero, ref_slice)], axis=0
    )


def softmax_pair(scores, kp):
    parts = []
    for half in range(2):
        s = scores[:, half * kp : (half + 1) * kp]
        top = jnp.max(s, axis=-1, keepdims=True)
        e = jnp.exp(s - top)
        parts.append(e * (1.0 / jnp.sum(e, axis=-1, keepdims=True)))
    return parts


def attend_body(width, head, kp, n_ref, q_ref, s_ref, w_ref, x_ref, mix_ref, sum_ref, stat_ref):
    pairs = width // (2 * head)
    step = pl.program_id(0)
    scale = head ** (-0.5)
    low_lane = lax.broadcasted_iota(jnp.int32, (kp, 2 * head), 1) < head
    for j in range(pairs):
        cols = pl.ds(j * 2 * head, 2 * head)
        keys = head_pair(s_ref[0, :, cols], low_lane)
        values = head_pair(s_ref[0, :, pl.ds(width + j * 2 * head, 2 * head)], low_lane)
        scores = dot_t(q_ref[:, cols], keys) * scale
        prob = jnp.concatenate(softmax_pair(scores, kp), axis=1).astype(BF)
        mix_ref[:, cols] = dot(prob, values).astype(BF)
    branch = dot(mix_ref[...], w_ref[...])
    first = x_ref[...].astype(F32) + branch
    sum_ref[...] = first
    rows = q_ref.shape[0]
    keep = (lax.broadcasted_iota(jnp.int32, (rows, 1), 0) < n_ref[step]).astype(F32)
    sums = jnp.concatenate(
        [
            jnp.sum(keep * first * first, axis=0, keepdims=True),
            jnp.sum(keep * branch * branch, axis=0, keepdims=True),
        ],
        axis=0,
    )

    @pl.when(step == 0)
    def _():
        stat_ref[...] = sums

    @pl.when(step > 0)
    def _():
        stat_ref[...] += sums


def attend(n_valid, q, summary, w_att, x, head):
    rows, width = q.shape
    blocks, kp, _ = summary.shape
    short = rows // blocks
    return pl.pallas_call(
        functools.partial(attend_body, width, head, kp),
        grid_spec=pltpu.PrefetchScalarGridSpec(
            num_scalar_prefetch=1,
            grid=(blocks,),
            in_specs=[
                vspec((short, width), lambda i, n: (i, 0)),
                vspec((1, kp, 2 * width), lambda i, n: (i, 0, 0)),
                vspec((width, width), lambda i, n: (3, 0), True),
                vspec((short, width), lambda i, n: (i, 0)),
            ],
            out_specs=[
                vspec((short, width), lambda i, n: (i, 0)),
                vspec((short, width), lambda i, n: (i, 0)),
                vspec((2, width), lambda i, n: (0, 0)),
            ],
        ),
        out_shape=[
            jax.ShapeDtypeStruct((rows, width), BF),
            jax.ShapeDtypeStruct((rows, width), F32),
            jax.ShapeDtypeStruct((2, width), F32),
        ],
        compiler_params=params(),
        cost_estimate=cost(2 * rows * width * (width + 4 * kp), 10e6, rows * kp * 12),
        name="attend",
    )(n_valid, q, summary, w_att, x)


def forward_body(
    depth, head, c_ref, n_ref, x_ref, px_ref, w_ref, e_ref, pe_ref, *refs
):
    q_ref, kv_ref, s_ref, mix_ref, sum_ref, stat_ref, part, unit, got, send, recv = refs
    blocks, short, kp = e_ref.shape
    width = x_ref.shape[1]
    seq, mine = lax.axis_index("seq"), lax.axis_index("own")
    z, y = seq // 2, seq % 2
    along_y = (2 * z + (1 - y), mine)
    after = (2 * lax.rem(z + 1, depth) + y, mine)
    before = (2 * lax.rem(z + depth - 1, depth) + y, mine)
    has_left, has_right = z > 0, z < depth - 1
    shared = kp * 5 // 16
    direct = kp - 2 * shared
    barrier = pltpu.get_barrier_semaphore()
    pl.semaphore_signal(barrier, inc=1, device_id=along_y, device_id_type=MESH_ID)

    @pl.when(has_left)
    def _():
        pl.semaphore_signal(barrier, inc=1, device_id=before, device_id_type=MESH_ID)

    @pl.when(has_right)
    def _():
        pl.semaphore_signal(barrier, inc=1, device_id=after, device_id_type=MESH_ID)

    pl.semaphore_wait(barrier, 1 + jnp.minimum(z, 1) + jnp.minimum(depth - 1 - z, 1))

    @pl.when(jnp.logical_not(has_left))
    def _():
        got[0] = jnp.zeros_like(got[0])

    @pl.when(jnp.logical_not(has_right))
    def _():
        got[1] = jnp.zeros_like(got[1])

    def copy(at, src, dst, there):
        return pltpu.make_async_remote_copy(
            src_ref=src,
            dst_ref=dst,
            send_sem=send.at[at],
            recv_sem=recv.at[at],
            device_id=there,
            device_id_type=MESH_ID,
        )

    every = pl.ds(0, direct)
    single = pl.ds(pl.multiple_of(direct + shared * y, 8), shared)
    moves, hands = {}, {}
    for kind in range(2):
        cols = pl.ds(kind * width, width)
        for side in range(2):
            there = (after, before)[side]
            at = (kind * 2 + side) * 3
            moves[kind, side] = [
                copy(at, unit.at[side, every, cols], got.at[side, every, cols], there),
                copy(at + 1, unit.at[side, single, cols], got.at[side, single, cols], there),
            ]
            hands[kind, side] = copy(
                at + 2, got.at[side, single, cols], got.at[side, single, cols], along_y
            )
    can_send = (has_right, has_left)
    can_get = (has_left, has_right)

    for kind in range(2):
        cols = pl.ds(kind * width, width)
        weight = pl.ds((1 + kind) * width, width)

        def own_block(b, carry):
            rows = pl.ds(pl.multiple_of(b * short, short), short)
            kv = dot(x_ref[rows, :], w_ref[weight, :]).astype(BF)
            kv_ref[rows, cols] = kv
            total = dot_l(e_ref[b], kv)
            part[b, :, cols] = total

            @pl.when(b == 0)
            def _():
                for side in range(2):
                    unit[side, :, cols] = c_ref[1 - side, b] * total

            @pl.when(b > 0)
            def _():
                for side in range(2):
                    unit[side, :, cols] += c_ref[1 - side, b] * total

            return carry

        def peer_block(b, carry):
            rows = pl.ds(pl.multiple_of(b * short, short), short)
            kv = dot(px_ref[rows, :], w_ref[weight, :]).astype(BF)
            total = dot_l(pe_ref[b], kv)
            for side in range(2):
                unit[side, :, cols] += c_ref[1 - side, blocks + b] * total
            return carry

        lax.fori_loop(0, blocks, own_block, 0)
        lax.fori_loop(0, blocks, peer_block, 0)
        for side in range(2):

            @pl.when(can_send[side])
            def _():
                for move in moves[kind, side]:
                    move.start()

    def query_block(b, carry):
        rows = pl.ds(pl.multiple_of(b * short, short), short)
        q_ref[rows, :] = dot(x_ref[rows, :], w_ref[pl.ds(0, width), :]).astype(BF)
        return carry

    lax.fori_loop(0, blocks, query_block, 0)
    for kind in range(2):
        for side in range(2):

            @pl.when(can_get[side])
            def _():
                moves[kind, side][1].wait_recv()
                hands[kind, side].start()

    for kind in range(2):
        for side in range(2):

            @pl.when(can_get[side])
            def _():
                moves[kind, side][0].wait_recv()
                hands[kind, side].wait_recv()

    slab = 64

    def combine(i, carry):
        b, at = i // (kp // slab), i % (kp // slab)
        rows = pl.ds(pl.multiple_of(at * slab, slab), slab)
        total = c_ref[2, b] * unit[1, rows, :] + c_ref[3, b] * got[0, rows, :]
        total = total + c_ref[4, b] * unit[0, rows, :] + c_ref[5, b] * got[1, rows, :]
        s_ref[b, rows, :] = (total + c_ref[6, b] * part[b, rows, :]).astype(BF)
        return carry

    lax.fori_loop(0, blocks * (kp // slab), combine, 0)
    pairs = width // (2 * head)
    scale = head ** (-0.5)
    low_lane = lax.broadcasted_iota(jnp.int32, (kp, 2 * head), 1) < head

    def attend_block(b, carry):
        rows = pl.ds(pl.multiple_of(b * short, short), short)
        for j in range(pairs):
            cols = pl.ds(j * 2 * head, 2 * head)
            keys = head_pair(s_ref[b, :, cols], low_lane)
            values = head_pair(s_ref[b, :, pl.ds(width + j * 2 * head, 2 * head)], low_lane)
            scores = dot_t(q_ref[rows, cols], keys) * scale
            prob = jnp.concatenate(softmax_pair(scores, kp), axis=1).astype(BF)
            mix_ref[rows, cols] = dot(prob, values).astype(BF)
        branch = dot(mix_ref[rows, :], w_ref[pl.ds(3 * width, width), :])
        first = x_ref[rows, :].astype(F32) + branch
        sum_ref[rows, :] = first
        keep = (lax.broadcasted_iota(jnp.int32, (short, 1), 0) < n_ref[1, b]).astype(F32)
        stat_ref[...] += jnp.concatenate(
            [
                jnp.sum(keep * first * first, axis=0, keepdims=True),
                jnp.sum(keep * branch * branch, axis=0, keepdims=True),
            ],
            axis=0,
        )
        return carry

    stat_ref[...] = jnp.zeros_like(stat_ref)
    lax.fori_loop(0, blocks, attend_block, 0)
    for kind in range(2):
        for side in range(2):

            @pl.when(can_send[side])
            def _():
                for move in moves[kind, side]:
                    move.wait_send()

            @pl.when(can_get[side])
            def _():
                hands[kind, side].wait_send()


def forward(coef, n_valid, x, peer_x, w_att, e_own, e_peer, head, peers):
    rows, width = x.shape
    blocks, short, kp = e_own.shape
    vmem = pl.BlockSpec(memory_space=pltpu.VMEM)
    smem = pl.BlockSpec(memory_space=pltpu.SMEM)
    return pl.pallas_call(
        functools.partial(forward_body, peers // 2, head),
        in_specs=[smem] * 2 + [vmem] * 5,
        out_specs=[vmem] * 6,
        out_shape=[
            jax.ShapeDtypeStruct((rows, width), BF),
            jax.ShapeDtypeStruct((rows, 2 * width), BF),
            jax.ShapeDtypeStruct((blocks, kp, 2 * width), BF),
            jax.ShapeDtypeStruct((rows, width), BF),
            jax.ShapeDtypeStruct((rows, width), F32),
            jax.ShapeDtypeStruct((2, width), F32),
        ],
        scratch_shapes=[
            pltpu.VMEM((blocks, kp, 2 * width), F32),
            pltpu.VMEM((2, kp, 2 * width), F32),
            pltpu.VMEM((2, kp, 2 * width), F32),
            pltpu.SemaphoreType.DMA((12,)),
            pltpu.SemaphoreType.DMA((12,)),
        ],
        compiler_params=pltpu.CompilerParams(
            collective_id=3, has_side_effects=True, vmem_limit_bytes=VMEM_LIMIT
        ),
        cost_estimate=cost(2 * rows * width * width * 8, 200e6, rows * kp * 12),
        name="forward",
    )(coef, n_valid, x, peer_x, w_att, e_own, e_peer)


def normalize(values):
    mean = jnp.mean(values, axis=-1, keepdims=True)
    centered = values - mean
    inverse = lax.rsqrt(jnp.mean(centered * centered, axis=-1, keepdims=True) + eps_norm)
    return centered * inverse, inverse


def norm_back(grad_out, normed, inverse, gain):
    scaled = grad_out * gain
    return inverse * (
        scaled
        - jnp.mean(scaled, axis=-1, keepdims=True)
        - normed * jnp.mean(scaled * normed, axis=-1, keepdims=True)
    )


def feed_body(
    chunks,
    first_ref,
    w1_ref,
    w2_ref,
    wo_ref,
    cot_ref,
    np_ref,
    out_ref,
    hid_ref,
    up_ref,
    down_ref,
    flow_ref,
    dfirst_ref,
    dbranch_ref,
    dmix_ref,
    ng_ref,
    slope_ref,
):
    step = pl.program_id(0)
    rows, width = first_ref.shape
    deep = w2_ref.shape[0] // chunks
    down_rows = lambda c: w2_ref[pl.ds(c * deep, deep)].reshape(width, width)
    normed_one, inverse_one = normalize(first_ref[...])
    first_norm = normed_one * np_ref[0:1, :] + np_ref[1:2, :]
    first_low = first_norm.astype(BF)
    flow_ref[...] = first_low
    second = first_norm
    for c in range(chunks):
        cols = pl.ds(c * width, width)
        u = dot(first_low, w1_ref[:, c].reshape(width, width))
        cumulative = 0.5 * (1.0 + lax.erf(u * (1.0 / math.sqrt(2.0))))
        density = jnp.exp(-0.5 * u * u) * (1.0 / math.sqrt(2.0 * math.pi))
        slope_ref[:, cols] = cumulative + u * density
        hidden = (u * cumulative).astype(BF)
        hid_ref[:, cols] = hidden
        second = second + dot(hidden, down_rows(c))
    normed_two, inverse_two = normalize(second)
    out_ref[...] = (normed_two * np_ref[2:3, :] + np_ref[3:4, :]).astype(BF)
    grad_out = cot_ref[...].astype(F32)
    gain_two = jnp.sum(grad_out * normed_two, axis=0, keepdims=True)
    shift_two = jnp.sum(grad_out, axis=0, keepdims=True)
    grad_second = norm_back(grad_out, normed_two, inverse_two, np_ref[2:3, :])
    down = grad_second.astype(BF)
    down_ref[...] = down
    grad_first_norm = grad_second
    for c in range(chunks):
        cols = pl.ds(c * width, width)
        grad_hidden = dot_t(down, down_rows(c))
        up = (grad_hidden * slope_ref[:, cols]).astype(BF)
        up_ref[:, cols] = up
        grad_first_norm = grad_first_norm + dot_t(up, w1_ref[:, c].reshape(width, width))
    gain_one = jnp.sum(grad_first_norm * normed_one, axis=0, keepdims=True)
    shift_one = jnp.sum(grad_first_norm, axis=0, keepdims=True)
    grad_first = norm_back(grad_first_norm, normed_one, inverse_one, np_ref[0:1, :])
    dfirst_ref[...] = grad_first
    grad_branch = grad_first.astype(BF)
    dbranch_ref[...] = grad_branch
    dmix_ref[...] = dot_t(grad_branch, wo_ref[...]).astype(BF)
    sums = jnp.concatenate([gain_one, shift_one, gain_two, shift_two], axis=0)

    @pl.when(step == 0)
    def _():
        ng_ref[...] = sums

    @pl.when(step > 0)
    def _():
        ng_ref[...] += sums


def feed(first_sum, w_ffn, w_att, cotangent, norm_params, tile):
    rows, width = first_sum.shape
    groups, chunks, size, _ = w_ffn.shape
    groups = groups // 2
    ff = chunks * width
    row = lambda i: (i, 0)
    return pl.pallas_call(
        functools.partial(feed_body, chunks),
        grid=(rows // tile,),
        in_specs=[
            vspec((tile, width), row),
            vspec((groups, chunks, size, width), lambda i: (0, 0, 0, 0), True),
            vspec((groups, chunks, size, width), lambda i: (1, 0, 0, 0), True),
            vspec((width, width), lambda i: (3, 0), True),
            vspec((tile, width), row),
            vspec(norm_params.shape, lambda i: (0, 0)),
        ],
        out_specs=[
            vspec((tile, width), row),
            vspec((tile, ff), row),
            vspec((tile, ff), row),
            vspec((tile, width), row),
            vspec((tile, width), row),
            vspec((tile, width), row),
            vspec((tile, width), row),
            vspec((tile, width), row),
            vspec((4, width), lambda i: (0, 0)),
        ],
        out_shape=[
            jax.ShapeDtypeStruct((rows, width), BF),
            jax.ShapeDtypeStruct((rows, ff), BF),
            jax.ShapeDtypeStruct((rows, ff), BF),
            jax.ShapeDtypeStruct((rows, width), BF),
            jax.ShapeDtypeStruct((rows, width), BF),
            jax.ShapeDtypeStruct((rows, width), F32),
            jax.ShapeDtypeStruct((rows, width), BF),
            jax.ShapeDtypeStruct((rows, width), BF),
            jax.ShapeDtypeStruct((4, width), F32),
        ],
        scratch_shapes=[pltpu.VMEM((tile, ff), F32)],
        compiler_params=params(),
        cost_estimate=cost(2 * rows * width * ff * 4, 30e6, rows * ff * 2),
        name="feed",
    )(first_sum, w_ffn, w_ffn, w_att, cotangent, norm_params)


def attend_back_body(width, head, kp, q_ref, s_ref, g_ref, dq_ref, ds_ref):
    pairs = width // (2 * head)
    scale = head ** (-0.5)
    low_lane = lax.broadcasted_iota(jnp.int32, (kp, 2 * head), 1) < head
    for j in range(pairs):
        cols = pl.ds(j * 2 * head, 2 * head)
        vcols = pl.ds(width + j * 2 * head, 2 * head)
        keys = head_pair(s_ref[0, :, cols], low_lane)
        values = head_pair(s_ref[0, :, vcols], low_lane)
        q = q_ref[:, cols]
        g = g_ref[:, cols]
        prob = softmax_pair(dot_t(q, keys) * scale, kp)
        grad_prob = dot_t(g, values)
        low_parts = []
        for half in range(2):
            p = prob[half]
            d = grad_prob[:, half * kp : (half + 1) * kp]
            low_parts.append((p * (d - jnp.sum(p * d, axis=-1, keepdims=True))).astype(BF))
        grad_scores = jnp.concatenate(low_parts, axis=1)
        prob_low = jnp.concatenate(prob, axis=1).astype(BF)
        dq_ref[:, cols] = (dot(grad_scores, keys) * scale).astype(BF)
        dk = dot_l(grad_scores, q) * scale
        dv = dot_l(prob_low, g)
        ds_ref[0, :, cols] = jnp.where(low_lane, dk[:kp], dk[kp:])
        ds_ref[0, :, vcols] = jnp.where(low_lane, dv[:kp], dv[kp:])


def attend_back(q, summary, grad_mix, head):
    rows, width = q.shape
    blocks, kp, _ = summary.shape
    short = rows // blocks
    return pl.pallas_call(
        functools.partial(attend_back_body, width, head, kp),
        grid=(blocks,),
        in_specs=[
            vspec((short, width), lambda i: (i, 0)),
            vspec((1, kp, 2 * width), lambda i: (i, 0, 0)),
            vspec((short, width), lambda i: (i, 0)),
        ],
        out_specs=[
            vspec((short, width), lambda i: (i, 0)),
            vspec((1, kp, 2 * width), lambda i: (i, 0, 0)),
        ],
        out_shape=[
            jax.ShapeDtypeStruct((rows, width), BF),
            jax.ShapeDtypeStruct((blocks, kp, 2 * width), F32),
        ],
        compiler_params=params(),
        cost_estimate=cost(2 * rows * width * 8 * kp, 10e6, rows * kp * 12),
        name="attend_back",
    )(q, summary, grad_mix)


def outer_body(split, l_ref, r_ref, o_ref):
    value = dot_l(l_ref[...], r_ref[...])
    o_ref[...] = value.reshape(o_ref.shape).astype(o_ref.dtype)


def outer_up(first_low, grad_up, size, dtype):
    rows, width = first_low.shape
    chunks = grad_up.shape[1] // width
    groups = width // size
    return pl.pallas_call(
        functools.partial(outer_body, True),
        grid=(chunks,),
        in_specs=[
            vspec((rows, width), lambda i: (0, 0), True),
            vspec((rows, width), lambda i: (0, i)),
        ],
        out_specs=vspec((groups, 1, size, width), lambda i: (0, i, 0, 0)),
        out_shape=jax.ShapeDtypeStruct((groups, chunks, size, width), dtype),
        compiler_params=params(),
        cost_estimate=cost(2 * rows * width * width * chunks, 20e6),
        name="outer_up",
    )(first_low, grad_up)


def outer_rows(left, right, dtype, name):
    rows, width = right.shape[0], min(left.shape[1], right.shape[1])
    tall, wide = left.shape[1] // width, right.shape[1] // width
    moving = lambda n: (lambda i: (0, i)) if n > 1 else (lambda i: (0, 0))
    return pl.pallas_call(
        functools.partial(outer_body, False),
        grid=(tall * wide,),
        in_specs=[
            vspec((rows, width), moving(tall), tall == 1),
            vspec((rows, width), moving(wide), wide == 1),
        ],
        out_specs=vspec((width, width), lambda i: (i, 0)),
        out_shape=jax.ShapeDtypeStruct((tall * wide * width, width), dtype),
        compiler_params=params(),
        cost_estimate=cost(2 * rows * width * width * tall * wide, 20e6),
        name=name,
    )(left, right)


def back_body(
    width, blocks, c_ref, n_ref, e_ref, kv_ref, p_ref, *refs
):
    far_refs = refs[:4]
    dq_ref, w_ref, df_ref, dkv_ref, gp_ref, gi_ref = refs[4:]
    step = pl.program_id(0)
    short, kp = e_ref.shape[1], e_ref.shape[2]
    total = c_ref[step, 0] * p_ref[0]
    for other in range(1, blocks):
        total = total + c_ref[step, other] * p_ref[other]
    for k in range(4):
        total = total + c_ref[step, blocks + k] * far_refs[k][...].astype(F32)
    summary = total.astype(BF)
    dkv = dot(e_ref[0], summary).astype(BF)
    dkv_ref[...] = dkv
    keep = lax.broadcasted_iota(jnp.int32, (short, 1), 0) < n_ref[1, step]
    grad_e = jnp.where(keep, dot_t(kv_ref[...], summary), 0.0)
    column = n_ref[0, step]
    at = pl.multiple_of(jnp.minimum((column // 8) * 8, gp_ref.shape[0] - short - 8), 8)
    moved = pltpu.roll(
        jnp.concatenate([grad_e, jnp.zeros((8, kp), F32)], axis=0), column - at, 0
    )

    @pl.when(step == 0)
    def _():
        gp_ref[...] = jnp.zeros_like(gp_ref)

    gp_ref[pl.ds(at, short + 8), :] += moved
    gi_ref[...] = (
        df_ref[...]
        + dot_t(dq_ref[...], w_ref[pl.ds(0, width), :])
        + dot_t(dkv[:, :width], w_ref[pl.ds(width, width), :])
        + dot_t(dkv[:, width:], w_ref[pl.ds(2 * width, width), :])
    )


def back(coef, places, e_rows, kv, grad_parts, far_parts, dq, w_att, grad_first, positions):
    rows, width = dq.shape
    blocks, short, kp = e_rows.shape
    row = lambda i, *_: (i, 0)
    lead = lambda i, *_: (i, 0, 0)
    fixed = lambda i, *_: (0, 0)
    return pl.pallas_call(
        functools.partial(back_body, width, blocks),
        grid_spec=pltpu.PrefetchScalarGridSpec(
            num_scalar_prefetch=2,
            grid=(blocks,),
            in_specs=[
                vspec((1, short, kp), lead),
                vspec((short, 2 * width), row),
                vspec(grad_parts.shape, lambda i, *_: (0, 0, 0), True),
            ]
            + [vspec((kp, 2 * width), fixed, True)] * 4
            + [
                vspec((short, width), row),
                vspec((3 * width, width), fixed, True),
                vspec((short, width), row),
            ],
            out_specs=[
                vspec((short, 2 * width), row),
                vspec((positions, kp), fixed),
                vspec((short, width), row),
            ],
        ),
        out_shape=[
            jax.ShapeDtypeStruct((rows, 2 * width), BF),
            jax.ShapeDtypeStruct((positions, kp), F32),
            jax.ShapeDtypeStruct((rows, width), F32),
        ],
        compiler_params=params(),
        cost_estimate=cost(2 * rows * width * (3 * width + 4 * kp), 20e6),
        name="back",
    )(coef, places, e_rows, kv, grad_parts, *far_parts, dq, w_att, grad_first)


def reduce_body(depth, half, n_src, extra_keep, *refs):
    sources = refs[:n_src]
    grads, shares_out, rows_out = refs[n_src : n_src + 3]
    (own, got_c, sum_c, got_a, got_b, sum_a, sum_b, got_a2, got_b2, sum_z, got_z) = refs[
        n_src + 3 : n_src + 14
    ]
    keep_a, keep_b, keep_z = refs[n_src + 14 : n_src + 17]
    (e_own, e_got, e_sum, e_got1, e_sum1, e_got2, e_sum2, e_gotz, e_all, e_rows) = refs[
        n_src + 17 : n_src + 27
    ]
    send, recv, local = refs[n_src + 27 :]
    seq, mine = lax.axis_index("seq"), lax.axis_index("own")
    z, y, x, c = seq // 2, seq % 2, mine // 2, mine % 2
    core = (seq, 2 * x + (1 - c))
    along_x = (seq, 2 * (1 - x) + c)
    along_y = (2 * z + (1 - y), mine)
    along_z = [(2 * lax.rem(z + d, depth) + y, mine) for d in range(1, depth)]
    barrier = pltpu.get_barrier_semaphore()
    partners = [core, along_x, along_y] + along_z
    for partner in partners:
        pl.semaphore_signal(barrier, inc=1, device_id=partner, device_id_type=MESH_ID)
    pl.semaphore_wait(barrier, len(partners))

    sent = []

    def push(src, dst, partner):
        at = len(sent)
        copy = pltpu.make_async_remote_copy(
            src_ref=src,
            dst_ref=dst,
            send_sem=send.at[at],
            recv_sem=recv.at[at],
            device_id=partner,
            device_id_type=MESH_ID,
        )
        copy.start()
        sent.append(copy)
        return copy

    up, down, g_query, g_keyval, g_out, extra = sources
    bands = [g_query, g_keyval.at[0], g_keyval.at[1], g_out]
    half_z = depth // 2
    cols = own.shape[-1]
    loads = []

    def load(src, dst):
        copy = pltpu.make_async_copy(src, dst, local.at[len(loads)])
        copy.start()
        loads.append(copy)
        return copy

    e_first = [push(extra.at[:, :, 1 - c], e_got, core)]
    e_load = [load(extra.at[:, :, c], e_own)]
    piece_first, piece_load = [], []

    def piece_core(p):
        at, part = p // 2, pl.ds((p % 2) * cols, cols)
        if at < 2:
            first = [
                push(up.at[:, :, 1 - c, at, :, part], got_c.at[p, pl.ds(0, half_z)], core),
                push(down.at[:, :, 1 - c, at, :, part], got_c.at[p, pl.ds(half_z, half_z)], core),
            ]
            kept = [
                load(up.at[:, :, c, at, :, part], own.at[p, pl.ds(0, half_z)]),
                load(down.at[:, :, c, at, :, part], own.at[p, pl.ds(half_z, half_z)]),
            ]
        else:
            first = [
                push(bands[m].at[:, 1 - c, :, part], got_c.at[p, m], core) for m in range(depth)
            ]
            kept = [load(bands[m].at[:, c, :, part], own.at[p, m]) for m in range(depth)]
        piece_first.append(first)
        piece_load.append(kept)

    state = {}

    def wait_recv(copies):
        for copy in copies:
            copy.wait_recv()

    low, high = pl.ds(0, half), pl.ds(half, half)

    def add(a, b):
        return a.astype(F32) + b.astype(F32)

    def piece_c(p):
        for copy in piece_load[p]:
            copy.wait()
        wait_recv(piece_first[p])

        def body(i, carry):
            zz, w = i // 2, i % 2
            to_x, to_y = 2 * w + 1 - x, 2 * (1 - y) + w
            sum_c[p, 0, zz, w] = add(own[p, zz, to_x, low, :], got_c[p, zz, to_x, low, :]).astype(BF)
            sum_c[p, 1, zz, w] = add(own[p, zz, to_y, high, :], got_c[p, zz, to_y, high, :]).astype(BF)
            return carry

        lax.fori_loop(0, depth * 2, body, 0)
        state["1", p] = [
            push(sum_c.at[p, 0], got_a.at[p], along_x),
            push(sum_c.at[p, 1], got_b.at[p], along_y),
        ]

    def piece_1(p):
        wait_recv(state["1", p])

        def side_a(zz, w):
            at = 2 * w + x
            return add(own[p, zz, at, low, :], got_c[p, zz, at, low, :]) + got_a[p, zz, w].astype(F32)

        def side_b(zz, w):
            at = 2 * y + w
            return add(own[p, zz, at, high, :], got_c[p, zz, at, high, :]) + got_b[p, zz, w].astype(F32)

        def body(zz, carry):
            sum_a[p, zz] = side_a(zz, 1 - y).astype(BF)
            sum_b[p, zz] = side_b(zz, 1 - x).astype(BF)
            keep_a[p, zz] = side_a(zz, y)
            keep_b[p, zz] = side_b(zz, x)
            return carry

        lax.fori_loop(0, depth, body, 0)
        state["2", p] = [
            push(sum_a.at[p], got_a2.at[p], along_y),
            push(sum_b.at[p], got_b2.at[p], along_x),
        ]

    def piece_2(p):
        wait_recv(state["2", p])

        def body(zz, carry):
            total_a = keep_a[p, zz] + got_a2[p, zz].astype(F32)
            total_b = keep_b[p, zz] + got_b2[p, zz].astype(F32)
            sum_z[p, zz, low, :] = total_a.astype(BF)
            sum_z[p, zz, high, :] = total_b.astype(BF)
            return carry

        lax.fori_loop(0, depth, body, 0)
        keep_z[p, low, :] = keep_a[p, z] + got_a2[p, z].astype(F32)
        keep_z[p, high, :] = keep_b[p, z] + got_b2[p, z].astype(F32)
        state["z", p] = [
            push(sum_z.at[p, lax.rem(z + d, depth)], got_z.at[p, d - 1], along_z[d - 1])
            for d in range(1, depth)
        ]

    def piece_z(p):
        wait_recv(state["z", p])
        total = keep_z[p]
        for d in range(depth - 1):
            total = total + got_z[p, d].astype(F32)
        grads[(p // 2 + 1) % 3, :, pl.ds((p % 2) * cols, cols)] = total

    def extra_c():
        e_load[0].wait()
        wait_recv(e_first)

        def body(i, carry):
            zz, yx = i // 4, i % 4
            e_sum[zz, yx // 2, yx % 2] = e_own[zz, yx] + e_got[zz, yx]
            return carry

        lax.fori_loop(0, depth * 4, body, 0)
        state["ez"] = [
            push(e_sum.at[lax.rem(z + d, depth)], e_gotz.at[d - 1], along_z[d - 1])
            for d in range(1, depth)
        ]

    def extra_1():
        wait_recv(state["ez"])

        def body(i, carry):
            yy, xx = i // 2, i % 2
            total = e_sum[z, yy, xx]
            for d in range(depth - 1):
                total = total + e_gotz[d, yy, xx]
            e_sum1[yy, xx] = total
            return carry

        lax.fori_loop(0, 4, body, 0)
        state["e1"] = [push(e_sum1.at[:, 1 - x], e_got1, along_x)]

    def extra_2():
        wait_recv(state["e1"])

        def body(yy, carry):
            e_sum2[yy] = e_sum1[yy, x] + e_got1[yy]
            return carry

        lax.fori_loop(0, 2, body, 0)
        state["e2"] = [push(e_sum2.at[1 - y], e_got2, along_y)]

    def extra_z():
        wait_recv(state["e2"])
        e_all[z, y] = e_sum2[y] + e_got2[...]
        state["gz"] = [push(e_all.at[z, y], e_all.at[z, y], there) for there in along_z]

    def extra_gather_y():
        wait_recv(state["gz"])
        state["gy"] = [push(e_all.at[:, y], e_all.at[:, y], along_y)]

    def extra_gather_x():
        wait_recv(state["gy"])
        e_rows[x, c] = e_all[:, :, pl.ds(extra_keep, e_rows.shape[4]), :]
        state["gx"] = [push(e_rows.at[x, c], e_rows.at[x, c], along_x)]

    def extra_gather_c():
        wait_recv(state["gx"])
        state["gc"] = [push(e_rows.at[:, c], e_rows.at[:, c], core)]

    stages = [piece_c, piece_1, piece_2, piece_z]
    small = {0: extra_c, 3: extra_1, 4: extra_2, 5: extra_z, 6: extra_gather_y}
    small |= {7: extra_gather_x, 8: extra_gather_c}
    piece_core(0)
    piece_core(1)
    for turn in range(9):
        for stage in range(4):
            if 0 <= turn - stage < 6:
                stages[stage](turn - stage)
            if stage == 0 and turn + 2 < 6:
                piece_core(turn + 2)
        if turn in small:
            small[turn]()
    shares_out[...] = e_all[:, :, pl.ds(0, extra_keep), :]
    wait_recv(state["gc"])
    rows_out[...] = e_rows[...]
    for copy in sent:
        copy.wait_send()


def reduce_all(g_query, g_keyval, g_out, g_up, g_down, extra, peers):
    depth = peers // 2
    size, width = g_up.shape[2], g_up.shape[3]
    half = size // 2
    e_rows_all, kp = extra.shape[1], extra.shape[2]
    keep = e_rows_all - 8
    sources = (
        [
            g_up.reshape(depth // 2, 4, 2, 2, size, width),
            g_down.reshape(depth // 2, 4, 2, 2, size, width),
        ]
        + [
            g_query.reshape(4, 2, size, width),
            g_keyval.reshape(2, 4, 2, size, width),
            g_out.reshape(4, 2, size, width),
        ]
        + [extra.reshape(depth, 4, 2, e_rows_all, kp)]
    )
    n_src = len(sources)
    cols = width // 2
    messages = 1 + 8 + 2 * depth + 6 * (4 + depth - 1) + 2 + 2 * (depth - 1) + 3
    loads = 1 + 8 + 2 * depth
    any_spec = pl.BlockSpec(memory_space=pl.ANY)
    vmem = pl.BlockSpec(memory_space=pltpu.VMEM)
    scratch = [
        pltpu.VMEM((6, depth, 4, size, cols), BF),
        pltpu.VMEM((6, depth, 4, size, cols), BF),
        pltpu.VMEM((6, 2, depth, 2, half, cols), BF),
        pltpu.VMEM((6, depth, 2, half, cols), BF),
        pltpu.VMEM((6, depth, 2, half, cols), BF),
        pltpu.VMEM((6, depth, half, cols), BF),
        pltpu.VMEM((6, depth, half, cols), BF),
        pltpu.VMEM((6, depth, half, cols), BF),
        pltpu.VMEM((6, depth, half, cols), BF),
        pltpu.VMEM((6, depth, size, cols), BF),
        pltpu.VMEM((6, depth - 1, size, cols), BF),
        pltpu.VMEM((6, depth, half, cols), F32),
        pltpu.VMEM((6, depth, half, cols), F32),
        pltpu.VMEM((6, size, cols), F32),
        pltpu.VMEM((depth, 4, e_rows_all, kp), F32),
        pltpu.VMEM((depth, 4, e_rows_all, kp), F32),
        pltpu.VMEM((depth, 2, 2, e_rows_all, kp), F32),
        pltpu.VMEM((2, e_rows_all, kp), F32),
        pltpu.VMEM((2, 2, e_rows_all, kp), F32),
        pltpu.VMEM((e_rows_all, kp), F32),
        pltpu.VMEM((2, e_rows_all, kp), F32),
        pltpu.VMEM((depth - 1, 2, 2, e_rows_all, kp), F32),
        pltpu.VMEM((depth, 2, e_rows_all, kp), F32),
        pltpu.VMEM((2, 2, depth, 2, 8, kp), F32),
        pltpu.SemaphoreType.DMA((messages,)),
        pltpu.SemaphoreType.DMA((messages,)),
        pltpu.SemaphoreType.DMA((loads,)),
    ]
    return pl.pallas_call(
        functools.partial(reduce_body, depth, half, n_src, keep),
        in_specs=[any_spec] * n_src,
        out_specs=[vmem] * 3,
        out_shape=[
            jax.ShapeDtypeStruct((3, size, width), F32),
            jax.ShapeDtypeStruct((depth, 2, keep, kp), F32),
            jax.ShapeDtypeStruct((2, 2, depth, 2, 8, kp), F32),
        ],
        scratch_shapes=scratch,
        compiler_params=pltpu.CompilerParams(
            collective_id=1, has_side_effects=True, vmem_limit_bytes=VMEM_LIMIT
        ),
        name="reduce_all",
    )(*sources)


def gather_body(depth, half, band_ref, proj_ref, out_ref, pout_ref, send, recv, local):
    seq, mine = lax.axis_index("seq"), lax.axis_index("own")
    z, y, x, c = seq // 2, seq % 2, mine // 2, mine % 2
    core = (seq, 2 * x + (1 - c))
    along_x = (seq, 2 * (1 - x) + c)
    along_y = (2 * z + (1 - y), mine)
    order = [1, 3, 2]
    along_z = [(2 * lax.rem(z + d, depth) + y, mine) for d in order]
    barrier = pltpu.get_barrier_semaphore()
    partners = [core, along_x, along_y] + along_z
    for partner in partners:
        pl.semaphore_signal(barrier, inc=1, device_id=partner, device_id_type=MESH_ID)
    pl.semaphore_wait(barrier, len(partners))

    sent = []

    def push(src, dst, partner):
        at = len(sent)
        copy = pltpu.make_async_remote_copy(
            src_ref=src,
            dst_ref=dst,
            send_sem=send.at[at],
            recv_sem=recv.at[at],
            device_id=partner,
            device_id_type=MESH_ID,
        )
        copy.start()
        sent.append(copy)
        return copy

    keep = pltpu.make_async_copy(band_ref, out_ref.at[z, y, x, c], local.at[0])
    keep.start()
    keep_p = pltpu.make_async_copy(proj_ref, pout_ref.at[x, c], local.at[1])
    keep_p.start()
    mine_at = out_ref.at[z, y, x, c]
    from_z = [push(band_ref, mine_at, there) for there in along_z]
    from_x = [push(band_ref, mine_at, along_x)]
    from_y = [push(band_ref, mine_at, along_y)]
    proj_x = push(proj_ref, pout_ref.at[x, c], along_x)
    last = [push(band_ref, mine_at, core), push(proj_ref, pout_ref.at[x, c], core)]
    planes = [z]
    for k in range(depth - 1):
        from_z[k].wait_recv()
        plane = lax.rem(z + depth - order[k], depth)
        planes.append(plane)
        slab = out_ref.at[plane, y, x, c]
        from_x.append(push(slab, slab, along_x))
        from_y.append(push(slab, slab, along_y))
        last.append(push(slab, slab, core))
    low, high = pl.ds(0, half), pl.ds(half, half)
    cross = []
    for k in range(depth):
        plane = planes[k]
        from_x[k].wait_recv()
        slab = out_ref.at[plane, y, 1 - x, c]
        part = out_ref.at[plane, y, 1 - x, c, low, :]
        cross_y = push(part, part, along_y)
        last.append(push(slab, slab, core))
        from_y[k].wait_recv()
        slab = out_ref.at[plane, 1 - y, x, c]
        part = out_ref.at[plane, 1 - y, x, c, high, :]
        cross.append((cross_y, push(part, part, along_x)))
        last.append(push(slab, slab, core))
        if k == 0:
            proj_x.wait_recv()
            slab = pout_ref.at[1 - x, c]
            last.append(push(slab, slab, core))
    for k in range(depth):
        for copy in cross[k]:
            copy.wait_recv()
        slab = out_ref.at[planes[k], 1 - y, 1 - x, c]
        last.append(push(slab, slab, core))
    for copy in last:
        copy.wait_recv()
    keep.wait()
    keep_p.wait()
    for copy in sent:
        copy.wait_send()


def gather_bands(band, proj, peers):
    depth = peers // 2
    size, width = band.shape
    messages = (depth - 1) + 3 + 2 + 3 * (depth - 1) + 4 * depth + 1 + depth
    vmem = pl.BlockSpec(memory_space=pltpu.VMEM)
    return pl.pallas_call(
        functools.partial(gather_body, depth, size // 2),
        in_specs=[vmem] * 2,
        out_specs=[vmem] * 2,
        out_shape=[
            jax.ShapeDtypeStruct((depth, 2, 2, 2, size, width), BF),
            jax.ShapeDtypeStruct((2, 2) + proj.shape, BF),
        ],
        scratch_shapes=[
            pltpu.SemaphoreType.DMA((messages,)),
            pltpu.SemaphoreType.DMA((messages,)),
            pltpu.SemaphoreType.DMA((2,)),
        ],
        compiler_params=pltpu.CompilerParams(
            collective_id=2, has_side_effects=True, vmem_limit_bytes=VMEM_LIMIT
        ),
        cost_estimate=cost(1e9, 90e6),
        name="gather_bands",
    )(band, proj)


def shampoo(grad, left, right, root_left, root_right, weight):
    new_left = decay * left + (1.0 - decay) * jnp.einsum(
        "tij,tkj->tik", grad, grad, precision=highest
    )
    new_right = decay * right + (1.0 - decay) * jnp.einsum(
        "tji,tjk->tik", grad, grad, precision=highest
    )
    inner = jnp.einsum("tij,tjk->tik", grad, root_right, precision=highest)
    step = jnp.einsum("tij,tjk->tik", root_left, inner, precision=highest)
    return (new_left, new_right, weight - rate_matrix * step)


def exact(a, b, left, right):
    return lax.dot_general(
        a, b, (((left,), (right,)), ((), ())), precision=highest, preferred_element_type=F32
    )


def step_body(bands, *refs):
    band_ref, tiles, proj_ref, blocks = refs[0], refs[1:6], refs[6], refs[7:12]
    rows_ref, norm_ref, second_ref = refs[12:15]
    owned_ref, new_tiles, new_blocks = refs[15], refs[16:19], refs[19:22]
    grad_ref, second_new_ref, norm_new_ref, rms_ref = refs[22:]
    at = pl.program_id(0)
    size, kp = tiles[0].shape[1], proj_ref.shape[-1]

    def update(grad, state, new, t):
        left, right, root_left, root_right, weight = (ref[t] for ref in state)
        new[0][t] = decay * left + (1.0 - decay) * exact(grad, grad, 1, 1)
        new[1][t] = decay * right + (1.0 - decay) * exact(grad, grad, 0, 0)
        new[2][t] = weight - rate_matrix * exact(root_left, exact(grad, root_right, 1, 0), 1, 0)

    @pl.when(at < bands)
    def _():
        for t in range(tiles[0].shape[0]):
            grad = band_ref[0, :, pl.ds(t * size, size)]
            owned_ref[t] = grad
            update(grad, tiles, new_tiles, t)

    @pl.when(at >= bands)
    def _():
        update(proj_ref[0], blocks, new_blocks, 0)

    @pl.when(at == bands)
    def _():
        depth = rows_ref.shape[2]

        def row(r):
            return rows_ref[r // 2 % 2, r % 2, r // 8 % depth, r // 4 % 2, pl.ds(0, 1), :]

        per = norm_ref.shape[1] // kp
        for i in range(4):
            grad = jnp.concatenate([row(per * i + j) for j in range(per)], axis=1)
            grad_ref[pl.ds(i, 1), :] = grad
            second = decay * second_ref[pl.ds(i, 1), :] + (1.0 - decay) * grad * grad
            second_new_ref[pl.ds(i, 1), :] = second
            norm_new_ref[pl.ds(i, 1), :] = norm_ref[pl.ds(i, 1), :] - rate_norm * grad * lax.rsqrt(second)
        count = jnp.sum(row(6 * per), axis=1, keepdims=True)
        for i in range(2):
            square = row(4 * per + per * i)
            for j in range(1, per):
                square = square + row(4 * per + per * i + j)
            total = jnp.sum(square, axis=1, keepdims=True)
            ratio = jnp.sqrt(total / (count * norm_ref.shape[1]))
            rms_ref[pl.ds(i, 1), :] = jnp.broadcast_to(ratio, (1, rms_ref.shape[1]))


def step_all(bands, tiles, proj_grad, blocks, rows, norm_params, norm_stat):
    count, size, width = bands.shape
    each, kp = width // size, proj_grad.shape[-1]
    n_blocks = proj_grad.shape[0]
    tile = lambda: vspec((each, size, size), lambda i: (jnp.minimum(i, count - 1), 0, 0))
    block = lambda: vspec((1, kp, kp), lambda i: (jnp.maximum(i - count, 0), 0, 0))
    whole = lambda a: vspec(a.shape, lambda i: (0,) * len(a.shape))
    like = lambda a: jax.ShapeDtypeStruct(a.shape, F32)
    rms = jax.ShapeDtypeStruct((2, 128), F32)
    return pl.pallas_call(
        functools.partial(step_body, count),
        grid=(count + n_blocks,),
        in_specs=[vspec((1, size, width), lambda i: (jnp.minimum(i, count - 1), 0, 0))]
        + [tile() for _ in range(5)]
        + [block() for _ in range(6)]
        + [whole(rows), whole(norm_params), whole(norm_stat)],
        out_specs=[tile() for _ in range(4)]
        + [block() for _ in range(3)]
        + [whole(norm_params)] * 3
        + [whole(rms)],
        out_shape=[like(tiles[0])] * 4 + [like(proj_grad)] * 3 + [like(norm_params)] * 3 + [rms],
        compiler_params=params(),
        cost_estimate=cost(1e9, 20e6),
        name="step_all",
    )(bands, *tiles, proj_grad, *blocks, rows, norm_params, norm_stat)


def to_matrix(tiles, rows, cols):
    size = tiles.shape[-1]
    return (
        tiles.reshape(rows // size, cols // size, size, size)
        .transpose(0, 2, 1, 3)
        .reshape(rows, cols)
    )


def to_bands(tiles, cols):
    count, size, _ = tiles.shape
    return to_matrix(tiles, count * size * size // cols, cols)


def from_bands(bands, size):
    rows, cols = bands.shape
    return (
        bands.reshape(rows // size, size, cols // size, size)
        .transpose(0, 2, 1, 3)
        .reshape(-1, size, size)
    )


def gather_weights(weights, projection, att_dev, width, both, fused, peers):
    size = weights.shape[-1]
    low = weights.astype(BF)
    groups, chunks = width // size, FF // width
    if banded(weights.shape[0], att_dev, width, size):
        ffn = lax.all_gather(to_bands(low[att_dev:], width), both, axis=0, tiled=True)
        band = to_bands(low[:att_dev], width)
        if fused:
            att, proj = gather_bands(band, projection.astype(BF), peers)
            att, proj = att.reshape(-1, width), proj.reshape(-1, projection.shape[1])
        else:
            att = lax.all_gather(band, both, axis=0, tiled=True)
            proj = lax.all_gather(projection.astype(BF), "own", axis=0, tiled=True)
        return att, ffn.reshape(2 * groups, chunks, size, width), proj
    per_dev = weights.shape[0]
    proj = lax.all_gather(projection.astype(BF), "own", axis=0, tiled=True)
    grid = lax.all_gather(low, both, axis=0, tiled=True).reshape(-1, per_dev, size, size)
    att = to_bands(grid[:, :att_dev].reshape(-1, size, size), width)
    tiles = grid[:, att_dev:].reshape(-1, size, size)
    half = tiles.shape[0] // 2
    w_up = to_matrix(tiles[:half], width, FF).reshape(groups, size, chunks, width)
    w_down = to_matrix(tiles[half:], FF, width).reshape(groups, chunks, size, width)
    return att, jnp.concatenate([w_up.transpose(0, 2, 1, 3), w_down], axis=0), proj


def banded(per_dev, att_dev, width, size):
    wide = width // size
    return att_dev % wide == 0 and (per_dev - att_dev) % wide == 0


def scatter_weight_grads(g_att, g_up, g_down, per_dev, att_dev, both):
    size, width = g_up.shape[2], g_up.shape[3]
    if banded(per_dev, att_dev, width, size):
        ffn = jnp.concatenate([g_up.reshape(-1, width), g_down], axis=0)
        ffn = lax.psum_scatter(ffn, both, scatter_dimension=0, tiled=True)
        att = lax.psum_scatter(g_att, both, scatter_dimension=0, tiled=True)
        return jnp.concatenate([from_bands(att, size), from_bands(ffn, size)], axis=0)
    up = g_up.transpose(0, 2, 1, 3).reshape(width, -1)
    att = from_bands(g_att, size)
    ffn = jnp.concatenate([from_bands(up, size), from_bands(g_down, size)], axis=0)
    stacked = jnp.concatenate(
        [
            att.reshape(-1, att_dev, size, size),
            ffn.reshape(-1, per_dev - att_dev, size, size),
        ],
        axis=1,
    ).reshape(-1, size, size)
    return lax.psum_scatter(stacked, both, scatter_dimension=0, tiled=True)


def per_device(
    tokens,
    cotangent,
    lengths,
    offsets,
    valid_count,
    weights,
    stat_left,
    stat_right,
    root_left,
    root_right,
    projection,
    projection_left,
    projection_right,
    projection_root_left,
    projection_root_right,
    norm_params,
    norm_stat,
):
    both = ("seq", "own")
    size = weights.shape[-1]
    width = tokens.shape[-1]
    rows_here = tokens.shape[1]
    head = width // HEADS
    kp = projection.shape[1]
    blocks = rows_here // SHORT
    peers = lax.axis_size("seq")
    devices = peers * lax.axis_size("own")
    per_dev = weights.shape[0]
    att_dev = 4 * (width // size) ** 2 // devices
    x = tokens[0]
    swap = [(i, i ^ 1) for i in range(peers)]
    peer_x = lax.ppermute(x, "seq", swap)
    own_size = lax.axis_size("own")
    fused = own_size == 4 and peers == 8 and banded(per_dev, att_dev, width, size)
    w_att, w_ffn, proj_all = gather_weights(
        weights, projection, att_dev, width, both, fused, peers
    )

    places, table, coef_back = tables(lengths, offsets, valid_count, blocks, rows_here)

    def proj_rows(at):
        col, n = places[0, at : at + blocks], places[1, at : at + blocks]
        rows = jnp.stack(
            [lax.dynamic_slice_in_dim(proj_all, col[b], SHORT, 0) for b in range(blocks)]
        )
        keep = lax.broadcasted_iota(jnp.int32, (blocks, SHORT, 1), 1) < n[:, None, None]
        return jnp.where(keep, rows, jnp.zeros((), BF))

    e_own = proj_rows(0)
    e_peer = proj_rows(blocks)
    n_own = places[1, :blocks]

    if fused:
        query, keyval, summary, mixed, first_sum, row_sums = forward(
            table, places, x, peer_x, w_att, e_own, e_peer, head, peers
        )
    else:
        query, keyval, part_own = project(x, w_att, e_own.transpose(0, 2, 1), True)
        (part_peer,) = project(peer_x, w_att, e_peer.transpose(0, 2, 1), False)

        def unit_sum(flag):
            total = flag[0] * part_own[0]
            for b in range(1, blocks):
                total = total + flag[b] * part_own[b]
            for b in range(blocks):
                total = total + flag[blocks + b] * part_peer[b]
            return total

        head_sum, tail_sum = unit_sum(table[0]), unit_sum(table[1])
        from_left = lax.ppermute(tail_sum, "seq", [(i, i + 2) for i in range(peers - 2)])
        from_right = lax.ppermute(head_sum, "seq", [(i + 2, i) for i in range(peers - 2)])
        summary = jnp.stack(
            [
                (
                    table[2, b] * head_sum
                    + table[3, b] * from_left
                    + table[4, b] * tail_sum
                    + table[5, b] * from_right
                    + table[6, b] * part_own[b]
                ).astype(BF)
                for b in range(blocks)
            ]
        )
        mixed, first_sum, row_sums = attend(n_own, query, summary, w_att, x, head)
    (
        result,
        hidden,
        grad_up,
        grad_down,
        first_low,
        grad_first,
        grad_branch,
        grad_mix,
        norm_terms,
    ) = feed(first_sum, w_ffn, w_att, cotangent[0], norm_params, 256)
    grad_query, grad_parts = attend_back(query, summary, grad_mix, head)

    g_head = coef_back[0, 0] * grad_parts[0]
    g_tail = coef_back[-1, 0] * grad_parts[0]
    for b in range(1, blocks):
        g_head = g_head + coef_back[0, b] * grad_parts[b]
        g_tail = g_tail + coef_back[-1, b] * grad_parts[b]
    low_head, low_tail = g_head.astype(BF), g_tail.astype(BF)
    far_parts = []
    for far in (1, 2):
        far_parts.append(lax.ppermute(low_tail, "seq", [(i, i + far) for i in range(peers - far)]))
        far_parts.append(lax.ppermute(low_head, "seq", [(i + far, i) for i in range(peers - far)]))
    gtype = BF if fused else F32
    g_up = outer_up(first_low, grad_up, size, gtype)
    g_down = outer_rows(hidden, grad_down, gtype, "outer_down")
    g_out = outer_rows(mixed, grad_branch, gtype, "outer_out")
    g_query = outer_rows(x, grad_query, gtype, "outer_query")
    grad_keyval, grad_proj, grad_input = back(
        coef_back,
        places,
        e_own,
        keyval,
        grad_parts,
        far_parts,
        grad_query,
        w_att,
        grad_first,
        proj_all.shape[0],
    )
    g_keyval = outer_rows(x, grad_keyval, gtype, "outer_keyval")
    part_rows = projection.shape[0]
    valid_here = jnp.sum(n_own).astype(F32)
    extra = jnp.concatenate(
        [
            norm_terms.reshape(-1, kp),
            row_sums.reshape(-1, kp),
            jnp.full((1, kp), 1.0 / kp, F32) * valid_here,
        ],
        axis=0,
    )
    n_norm = 4 * width // kp
    n_row = 2 * width // kp
    if fused:
        extra = jnp.pad(extra, ((0, devices - extra.shape[0]), (0, 0)))[:, None, :]
        extra = jnp.pad(extra, ((0, 0), (0, 7), (0, 0)))
        shares = grad_proj.reshape(own_size, peers, part_rows // peers, kp).swapaxes(0, 1)
        shares = shares.reshape(devices, part_rows // peers, kp)
        banded_grads, proj_parts, rows = reduce_all(
            g_query, g_keyval, g_out, g_up, g_down, jnp.concatenate([shares, extra], axis=1), peers
        )
        (
            owned,
            left_new,
            right_new,
            weights_new,
            proj_left_new,
            proj_right_new,
            proj_blocks,
            norm_grad,
            stat_new,
            norm_new,
            rms,
        ) = step_all(
            banded_grads,
            [stat_left, stat_right, root_left, root_right, weights],
            proj_parts.reshape(-1, kp, kp),
            [
                projection_left,
                projection_right,
                projection_root_left,
                projection_root_right,
                projection.reshape(-1, kp, kp),
            ],
            rows,
            norm_params,
            norm_stat,
        )
        proj_grad = proj_parts.reshape(part_rows, kp)
        residual_rms = rms[:, 0]
    else:
        owned = scatter_weight_grads(
            jnp.concatenate([g_query, g_keyval, g_out], axis=0), g_up, g_down, per_dev, att_dev, both
        )
        packed = jnp.concatenate([grad_proj, extra], axis=0)
        packed = lax.psum(jnp.pad(packed, ((0, -packed.shape[0] % 16), (0, 0))), both)
        proj_grad = lax.dynamic_slice_in_dim(
            packed, lax.axis_index("own") * part_rows, part_rows, 0
        )
        totals = packed[grad_proj.shape[0] :]
        norm_grad = totals[:n_norm].reshape(4, width)
        row_total = totals[n_norm : n_norm + n_row].reshape(2, width).sum(axis=1)
        valid_total = totals[n_norm + n_row].sum()
        residual_rms = jnp.sqrt(row_total / (valid_total * width))
        left_new, right_new, weights_new = shampoo(
            owned, stat_left, stat_right, root_left, root_right, weights
        )
        proj_left_new, proj_right_new, proj_blocks = shampoo(
            proj_grad.reshape(-1, kp, kp),
            projection_left,
            projection_right,
            projection_root_left,
            projection_root_right,
            projection.reshape(-1, kp, kp),
        )
        stat_new = decay * norm_stat + (1.0 - decay) * norm_grad * norm_grad
        norm_new = norm_params - rate_norm * norm_grad * lax.rsqrt(stat_new)
    return (
        result[None],
        grad_input[None],
        owned,
        left_new,
        right_new,
        weights_new,
        proj_grad,
        proj_left_new,
        proj_right_new,
        proj_blocks.reshape(part_rows, kp),
        norm_grad,
        stat_new,
        norm_new,
        residual_rms,
    )


def solution(mesh):
    pack = P("own", "seq", None)
    table = P("own", None)
    tile = P(("seq", "own"), None, None)
    proj = P("own", None, None)
    return jax.shard_map(
        per_device,
        mesh=mesh,
        in_specs=(pack, pack, table, table, table)
        + (tile,) * 5
        + (table, proj, proj, proj, proj, P(), P()),
        out_specs=(pack, pack) + (tile,) * 4 + (table, proj, proj, table, P(), P(), P(), P()),
        check_vma=False,
    )
```

```python
import functools
import math

import jax
import jax.numpy as jnp
from jax import lax
from jax.experimental import pallas as pl
from jax.experimental.pallas import tpu as pltpu
from jax.sharding import PartitionSpec as P

HEADS = 12
FF = 3072
SHORT = 512
BF = jnp.bfloat16
F32 = jnp.float32

eps_norm = 1e-05
decay = 0.5
rate_matrix = 0.2
rate_norm = 0.2
highest = lax.Precision.HIGHEST
VMEM_LIMIT = 60 * 1024 * 1024
MESH_ID = pl.DeviceIdType.MESH


def dot(a, b):
    return lax.dot_general(a, b, (((1,), (0,)), ((), ())), preferred_element_type=F32)


def dot_t(a, b):
    return lax.dot_general(a, b, (((1,), (1,)), ((), ())), preferred_element_type=F32)


def dot_l(a, b):
    return lax.dot_general(a, b, (((0,), (0,)), ((), ())), preferred_element_type=F32)


def vspec(shape, index_map, once=False):
    if once:
        return pl.BlockSpec(shape, index_map, pipeline_mode=pl.Buffered(1))
    return pl.BlockSpec(shape, index_map)


def params():
    return pltpu.CompilerParams(
        dimension_semantics=("arbitrary",), vmem_limit_bytes=VMEM_LIMIT
    )


def cost(flops, nbytes, trans=0):
    return pl.CostEstimate(flops=int(flops), bytes_accessed=int(nbytes), transcendentals=int(trans))


def tables_body(blocks, rows_here, l_ref, o_ref, v_ref, i_ref, f_ref, b_ref):
    seq = lax.axis_index("seq")
    side = seq % 2
    row_start = seq * rows_here
    row_end = row_start + rows_here
    unit_start = (seq - side) * rows_here
    peer_start = (seq + 1 - 2 * side) * rows_here
    flag = lambda cond: jnp.where(cond, 1.0, 0.0).astype(F32)

    def locate(row):
        def body(i, carry):
            at, start, end, off, count = carry
            stop = at + l_ref[0, i]
            inside = jnp.logical_and(row >= at, row < stop)
            pick = lambda new, old: jnp.where(inside, new, old)
            return (
                stop,
                pick(at, start),
                pick(stop, end),
                pick(o_ref[0, i], off),
                pick(v_ref[0, i], count),
            )

        zero = jnp.int32(0)
        return lax.fori_loop(0, l_ref.shape[1], body, (zero,) * 5)[1:]

    starts, ends = [], []
    for k in range(2 * blocks):
        row = row_start + SHORT * k if k < blocks else peer_start + SHORT * (k - blocks)
        start, end, off, count = locate(row)
        starts.append(start)
        ends.append(end)
        i_ref[0, k] = off + row - start
        i_ref[1, k] = jnp.clip(count - (row - start), 0, SHORT)
    first = jnp.where(side == 0, starts[0], starts[blocks])
    last = jnp.where(side == 0, starts[-1], starts[blocks - 1])
    last_end = jnp.where(side == 0, ends[-1], ends[blocks - 1])
    head_cross = flag(first < unit_start)
    tail_cross = flag(last_end > unit_start + 2 * rows_here)
    for k in range(2 * blocks):
        is_head, is_tail = flag(starts[k] == first), flag(starts[k] == last)
        pick_tail = (1.0 - is_head) * is_tail
        f_ref[0, k] = is_head
        f_ref[1, k] = is_tail
        f_ref[2, k] = is_head
        f_ref[3, k] = is_head * head_cross
        f_ref[4, k] = pick_tail
        f_ref[5, k] = pick_tail * tail_cross
        f_ref[6, k] = (1.0 - is_head) * (1.0 - is_tail)
    own_last, own_end = starts[blocks - 1], ends[blocks - 1]
    for k in range(blocks):
        at_head, at_tail = flag(starts[k] == starts[0]), flag(starts[k] == own_last)
        for other in range(blocks):
            b_ref[k, other] = flag(starts[k] == starts[other])
        for far in range(2):
            reach = far * rows_here
            b_ref[k, blocks + 2 * far] = at_head * flag(starts[0] < row_start - reach)
            b_ref[k, blocks + 2 * far + 1] = at_tail * flag(own_end > row_end + reach)


def tables(lengths, offsets, valid_count, blocks, rows_here):
    smem = pl.BlockSpec(memory_space=pltpu.SMEM)
    return pl.pallas_call(
        functools.partial(tables_body, blocks, rows_here),
        in_specs=[smem] * 3,
        out_specs=[smem] * 3,
        out_shape=[
            jax.ShapeDtypeStruct((2, 2 * blocks), jnp.int32),
            jax.ShapeDtypeStruct((7, 2 * blocks), F32),
            jax.ShapeDtypeStruct((blocks, blocks + 4), F32),
        ],
        name="tables",
    )(lengths, offsets, valid_count)


def project_body(width, with_query, x_ref, w_ref, e_ref, *outs):
    x = x_ref[...]
    if with_query:
        q_ref, kv_ref, p_ref = outs
        q_ref[...] = dot(x, w_ref[pl.ds(0, width), :]).astype(BF)
    else:
        (p_ref,) = outs
    e = e_ref[0]
    for part in range(2):
        kv = dot(x, w_ref[pl.ds((1 + part) * width, width), :]).astype(BF)
        if with_query:
            kv_ref[:, pl.ds(part * width, width)] = kv
        p_ref[0, :, pl.ds(part * width, width)] = dot(e, kv)


def project(x, w_att, e_t, with_query):
    rows, width = x.shape
    blocks, kp, short = e_t.shape
    out_shape = [jax.ShapeDtypeStruct((blocks, kp, 2 * width), F32)]
    out_specs = [vspec((1, kp, 2 * width), lambda i: (i, 0, 0))]
    if with_query:
        out_shape = [
            jax.ShapeDtypeStruct((rows, width), BF),
            jax.ShapeDtypeStruct((rows, 2 * width), BF),
        ] + out_shape
        out_specs = [
            vspec((short, width), lambda i: (i, 0)),
            vspec((short, 2 * width), lambda i: (i, 0)),
        ] + out_specs
    return pl.pallas_call(
        functools.partial(project_body, width, with_query),
        grid=(blocks,),
        in_specs=[
            vspec((short, width), lambda i: (i, 0)),
            vspec((3 * width, width), lambda i: (0, 0), True),
            vspec((1, kp, short), lambda i: (i, 0, 0)),
        ],
        out_specs=out_specs,
        out_shape=out_shape,
        compiler_params=params(),
        cost_estimate=cost(2 * rows * width * width * 3, 12e6),
        name="project" if with_query else "project_peer",
    )(x, w_att, e_t)


def head_pair(ref_slice, low_lane):
    zero = jnp.zeros_like(ref_slice)
    return jnp.concatenate(
        [jnp.where(low_lane, ref_slice, zero), jnp.where(low_lane, zero, ref_slice)], axis=0
    )


def softmax_pair(scores, kp):
    parts = []
    for half in range(2):
        s = scores[:, half * kp : (half + 1) * kp]
        top = jnp.max(s, axis=-1, keepdims=True)
        e = jnp.exp(s - top)
        parts.append(e * (1.0 / jnp.sum(e, axis=-1, keepdims=True)))
    return parts


def attend_body(width, head, kp, n_ref, q_ref, s_ref, w_ref, x_ref, mix_ref, sum_ref, stat_ref):
    pairs = width // (2 * head)
    step = pl.program_id(0)
    scale = head ** (-0.5)
    low_lane = lax.broadcasted_iota(jnp.int32, (kp, 2 * head), 1) < head
    for j in range(pairs):
        cols = pl.ds(j * 2 * head, 2 * head)
        keys = head_pair(s_ref[0, :, cols], low_lane)
        values = head_pair(s_ref[0, :, pl.ds(width + j * 2 * head, 2 * head)], low_lane)
        scores = dot_t(q_ref[:, cols], keys) * scale
        prob = jnp.concatenate(softmax_pair(scores, kp), axis=1).astype(BF)
        mix_ref[:, cols] = dot(prob, values).astype(BF)
    branch = dot(mix_ref[...], w_ref[...])
    first = x_ref[...].astype(F32) + branch
    sum_ref[...] = first
    rows = q_ref.shape[0]
    keep = (lax.broadcasted_iota(jnp.int32, (rows, 1), 0) < n_ref[step]).astype(F32)
    sums = jnp.concatenate(
        [
            jnp.sum(keep * first * first, axis=0, keepdims=True),
            jnp.sum(keep * branch * branch, axis=0, keepdims=True),
        ],
        axis=0,
    )

    @pl.when(step == 0)
    def _():
        stat_ref[...] = sums

    @pl.when(step > 0)
    def _():
        stat_ref[...] += sums


def attend(n_valid, q, summary, w_att, x, head):
    rows, width = q.shape
    blocks, kp, _ = summary.shape
    short = rows // blocks
    return pl.pallas_call(
        functools.partial(attend_body, width, head, kp),
        grid_spec=pltpu.PrefetchScalarGridSpec(
            num_scalar_prefetch=1,
            grid=(blocks,),
            in_specs=[
                vspec((short, width), lambda i, n: (i, 0)),
                vspec((1, kp, 2 * width), lambda i, n: (i, 0, 0)),
                vspec((width, width), lambda i, n: (3, 0), True),
                vspec((short, width), lambda i, n: (i, 0)),
            ],
            out_specs=[
                vspec((short, width), lambda i, n: (i, 0)),
                vspec((short, width), lambda i, n: (i, 0)),
                vspec((2, width), lambda i, n: (0, 0)),
            ],
        ),
        out_shape=[
            jax.ShapeDtypeStruct((rows, width), BF),
            jax.ShapeDtypeStruct((rows, width), F32),
            jax.ShapeDtypeStruct((2, width), F32),
        ],
        compiler_params=params(),
        cost_estimate=cost(2 * rows * width * (width + 4 * kp), 10e6, rows * kp * 12),
        name="attend",
    )(n_valid, q, summary, w_att, x)


def forward_body(
    depth, head, c_ref, n_ref, x_ref, px_ref, w_ref, e_ref, pe_ref, *refs
):
    q_ref, kv_ref, s_ref, mix_ref, sum_ref, stat_ref, part, unit, got, send, recv = refs
    blocks, short, kp = e_ref.shape
    width = x_ref.shape[1]
    seq, mine = lax.axis_index("seq"), lax.axis_index("own")
    z, y = seq // 2, seq % 2
    along_y = (2 * z + (1 - y), mine)
    after = (2 * lax.rem(z + 1, depth) + y, mine)
    before = (2 * lax.rem(z + depth - 1, depth) + y, mine)
    has_left, has_right = z > 0, z < depth - 1
    shared = kp * 5 // 16
    direct = kp - 2 * shared
    barrier = pltpu.get_barrier_semaphore()
    pl.semaphore_signal(barrier, inc=1, device_id=along_y, device_id_type=MESH_ID)

    @pl.when(has_left)
    def _():
        pl.semaphore_signal(barrier, inc=1, device_id=before, device_id_type=MESH_ID)

    @pl.when(has_right)
    def _():
        pl.semaphore_signal(barrier, inc=1, device_id=after, device_id_type=MESH_ID)

    pl.semaphore_wait(barrier, 1 + jnp.minimum(z, 1) + jnp.minimum(depth - 1 - z, 1))

    @pl.when(jnp.logical_not(has_left))
    def _():
        got[0] = jnp.zeros_like(got[0])

    @pl.when(jnp.logical_not(has_right))
    def _():
        got[1] = jnp.zeros_like(got[1])

    def copy(at, src, dst, there):
        return pltpu.make_async_remote_copy(
            src_ref=src,
            dst_ref=dst,
            send_sem=send.at[at],
            recv_sem=recv.at[at],
            device_id=there,
            device_id_type=MESH_ID,
        )

    every = pl.ds(0, direct)
    single = pl.ds(pl.multiple_of(direct + shared * y, 8), shared)
    moves, hands = {}, {}
    for kind in range(2):
        cols = pl.ds(kind * width, width)
        for side in range(2):
            there = (after, before)[side]
            at = (kind * 2 + side) * 3
            moves[kind, side] = [
                copy(at, unit.at[side, every, cols], got.at[side, every, cols], there),
                copy(at + 1, unit.at[side, single, cols], got.at[side, single, cols], there),
            ]
            hands[kind, side] = copy(
                at + 2, got.at[side, single, cols], got.at[side, single, cols], along_y
            )
    can_send = (has_right, has_left)
    can_get = (has_left, has_right)

    for kind in range(2):
        cols = pl.ds(kind * width, width)
        weight = pl.ds((1 + kind) * width, width)

        def own_block(b, carry):
            rows = pl.ds(pl.multiple_of(b * short, short), short)
            kv = dot(x_ref[rows, :], w_ref[weight, :]).astype(BF)
            kv_ref[rows, cols] = kv
            total = dot_l(e_ref[b], kv)
            part[b, :, cols] = total

            @pl.when(b == 0)
            def _():
                for side in range(2):
                    unit[side, :, cols] = c_ref[1 - side, b] * total

            @pl.when(b > 0)
            def _():
                for side in range(2):
                    unit[side, :, cols] += c_ref[1 - side, b] * total

            return carry

        def peer_block(b, carry):
            rows = pl.ds(pl.multiple_of(b * short, short), short)
            kv = dot(px_ref[rows, :], w_ref[weight, :]).astype(BF)
            total = dot_l(pe_ref[b], kv)
            for side in range(2):
                unit[side, :, cols] += c_ref[1 - side, blocks + b] * total
            return carry

        lax.fori_loop(0, blocks, own_block, 0)
        lax.fori_loop(0, blocks, peer_block, 0)
        for side in range(2):

            @pl.when(can_send[side])
            def _():
                for move in moves[kind, side]:
                    move.start()

    def query_block(b, carry):
        rows = pl.ds(pl.multiple_of(b * short, short), short)
        q_ref[rows, :] = dot(x_ref[rows, :], w_ref[pl.ds(0, width), :]).astype(BF)
        return carry

    lax.fori_loop(0, blocks, query_block, 0)
    for kind in range(2):
        for side in range(2):

            @pl.when(can_get[side])
            def _():
                moves[kind, side][1].wait_recv()
                hands[kind, side].start()

    for kind in range(2):
        for side in range(2):

            @pl.when(can_get[side])
            def _():
                moves[kind, side][0].wait_recv()
                hands[kind, side].wait_recv()

    slab = 64

    def combine(i, carry):
        b, at = i // (kp // slab), i % (kp // slab)
        rows = pl.ds(pl.multiple_of(at * slab, slab), slab)
        total = c_ref[2, b] * unit[1, rows, :] + c_ref[3, b] * got[0, rows, :]
        total = total + c_ref[4, b] * unit[0, rows, :] + c_ref[5, b] * got[1, rows, :]
        s_ref[b, rows, :] = (total + c_ref[6, b] * part[b, rows, :]).astype(BF)
        return carry

    lax.fori_loop(0, blocks * (kp // slab), combine, 0)
    pairs = width // (2 * head)
    scale = head ** (-0.5)
    low_lane = lax.broadcasted_iota(jnp.int32, (kp, 2 * head), 1) < head

    def attend_block(b, carry):
        rows = pl.ds(pl.multiple_of(b * short, short), short)
        def pair(j):
            cols = pl.ds(pl.multiple_of(j * 2 * head, 2 * head), 2 * head)
            vcols = pl.ds(pl.multiple_of(width + j * 2 * head, 2 * head), 2 * head)
            keys = head_pair(s_ref[b, :, cols], low_lane)
            values = head_pair(s_ref[b, :, vcols], low_lane)
            scores = dot_t(q_ref[rows, cols], keys) * scale
            prob = jnp.concatenate(softmax_pair(scores, kp), axis=1).astype(BF)
            mix_ref[rows, cols] = dot(prob, values).astype(BF)

        def two(i, inner):
            pair(2 * i)
            pair(2 * i + 1)
            return inner

        lax.fori_loop(0, pairs // 2, two, 0)
        branch = dot(mix_ref[rows, :], w_ref[pl.ds(3 * width, width), :])
        first = x_ref[rows, :].astype(F32) + branch
        sum_ref[rows, :] = first
        keep = (lax.broadcasted_iota(jnp.int32, (short, 1), 0) < n_ref[1, b]).astype(F32)
        stat_ref[...] += jnp.concatenate(
            [
                jnp.sum(keep * first * first, axis=0, keepdims=True),
                jnp.sum(keep * branch * branch, axis=0, keepdims=True),
            ],
            axis=0,
        )
        return carry

    stat_ref[...] = jnp.zeros_like(stat_ref)
    lax.fori_loop(0, blocks, attend_block, 0)
    for kind in range(2):
        for side in range(2):

            @pl.when(can_send[side])
            def _():
                for move in moves[kind, side]:
                    move.wait_send()

            @pl.when(can_get[side])
            def _():
                hands[kind, side].wait_send()


def forward(coef, n_valid, x, peer_x, w_att, e_own, e_peer, head, peers):
    rows, width = x.shape
    blocks, short, kp = e_own.shape
    vmem = pl.BlockSpec(memory_space=pltpu.VMEM)
    smem = pl.BlockSpec(memory_space=pltpu.SMEM)
    return pl.pallas_call(
        functools.partial(forward_body, peers // 2, head),
        in_specs=[smem] * 2 + [vmem] * 5,
        out_specs=[vmem] * 6,
        out_shape=[
            jax.ShapeDtypeStruct((rows, width), BF),
            jax.ShapeDtypeStruct((rows, 2 * width), BF),
            jax.ShapeDtypeStruct((blocks, kp, 2 * width), BF),
            jax.ShapeDtypeStruct((rows, width), BF),
            jax.ShapeDtypeStruct((rows, width), F32),
            jax.ShapeDtypeStruct((2, width), F32),
        ],
        scratch_shapes=[
            pltpu.VMEM((blocks, kp, 2 * width), F32),
            pltpu.VMEM((2, kp, 2 * width), F32),
            pltpu.VMEM((2, kp, 2 * width), F32),
            pltpu.SemaphoreType.DMA((12,)),
            pltpu.SemaphoreType.DMA((12,)),
        ],
        compiler_params=pltpu.CompilerParams(
            collective_id=3, has_side_effects=True, vmem_limit_bytes=VMEM_LIMIT
        ),
        cost_estimate=cost(2 * rows * width * width * 8, 200e6, rows * kp * 12),
        name="forward",
    )(coef, n_valid, x, peer_x, w_att, e_own, e_peer)


def normalize(values):
    mean = jnp.mean(values, axis=-1, keepdims=True)
    centered = values - mean
    inverse = lax.rsqrt(jnp.mean(centered * centered, axis=-1, keepdims=True) + eps_norm)
    return centered * inverse, inverse


def norm_back(grad_out, normed, inverse, gain):
    scaled = grad_out * gain
    return inverse * (
        scaled
        - jnp.mean(scaled, axis=-1, keepdims=True)
        - normed * jnp.mean(scaled * normed, axis=-1, keepdims=True)
    )


def feed_body(
    chunks,
    first_ref,
    w1_ref,
    w2_ref,
    wo_ref,
    cot_ref,
    np_ref,
    out_ref,
    hid_ref,
    up_ref,
    down_ref,
    flow_ref,
    dfirst_ref,
    dbranch_ref,
    dmix_ref,
    ng_ref,
    slope_ref,
):
    step = pl.program_id(0)
    rows, width = first_ref.shape
    deep = w2_ref.shape[0] // chunks
    down_rows = lambda c: w2_ref[pl.ds(c * deep, deep)].reshape(width, width)
    normed_one, inverse_one = normalize(first_ref[...])
    first_norm = normed_one * np_ref[0:1, :] + np_ref[1:2, :]
    first_low = first_norm.astype(BF)
    flow_ref[...] = first_low
    second = first_norm
    for c in range(chunks):
        cols = pl.ds(c * width, width)
        u = dot(first_low, w1_ref[:, c].reshape(width, width))
        cumulative = 0.5 * (1.0 + lax.erf(u * (1.0 / math.sqrt(2.0))))
        density = jnp.exp(-0.5 * u * u) * (1.0 / math.sqrt(2.0 * math.pi))
        slope_ref[:, cols] = cumulative + u * density
        hidden = (u * cumulative).astype(BF)
        hid_ref[:, cols] = hidden
        second = second + dot(hidden, down_rows(c))
    normed_two, inverse_two = normalize(second)
    out_ref[...] = (normed_two * np_ref[2:3, :] + np_ref[3:4, :]).astype(BF)
    grad_out = cot_ref[...].astype(F32)
    gain_two = jnp.sum(grad_out * normed_two, axis=0, keepdims=True)
    shift_two = jnp.sum(grad_out, axis=0, keepdims=True)
    grad_second = norm_back(grad_out, normed_two, inverse_two, np_ref[2:3, :])
    down = grad_second.astype(BF)
    down_ref[...] = down
    grad_first_norm = grad_second
    for c in range(chunks):
        cols = pl.ds(c * width, width)
        grad_hidden = dot_t(down, down_rows(c))
        up = (grad_hidden * slope_ref[:, cols]).astype(BF)
        up_ref[:, cols] = up
        grad_first_norm = grad_first_norm + dot_t(up, w1_ref[:, c].reshape(width, width))
    gain_one = jnp.sum(grad_first_norm * normed_one, axis=0, keepdims=True)
    shift_one = jnp.sum(grad_first_norm, axis=0, keepdims=True)
    grad_first = norm_back(grad_first_norm, normed_one, inverse_one, np_ref[0:1, :])
    dfirst_ref[...] = grad_first
    grad_branch = grad_first.astype(BF)
    dbranch_ref[...] = grad_branch
    dmix_ref[...] = dot_t(grad_branch, wo_ref[...]).astype(BF)
    sums = jnp.concatenate([gain_one, shift_one, gain_two, shift_two], axis=0)

    @pl.when(step == 0)
    def _():
        ng_ref[...] = sums

    @pl.when(step > 0)
    def _():
        ng_ref[...] += sums


def feed(first_sum, w_ffn, w_att, cotangent, norm_params, tile):
    rows, width = first_sum.shape
    groups, chunks, size, _ = w_ffn.shape
    groups = groups // 2
    ff = chunks * width
    row = lambda i: (i, 0)
    return pl.pallas_call(
        functools.partial(feed_body, chunks),
        grid=(rows // tile,),
        in_specs=[
            vspec((tile, width), row),
            vspec((groups, chunks, size, width), lambda i: (0, 0, 0, 0), True),
            vspec((groups, chunks, size, width), lambda i: (1, 0, 0, 0), True),
            vspec((width, width), lambda i: (3, 0), True),
            vspec((tile, width), row),
            vspec(norm_params.shape, lambda i: (0, 0)),
        ],
        out_specs=[
            vspec((tile, width), row),
            vspec((tile, ff), row),
            vspec((tile, ff), row),
            vspec((tile, width), row),
            vspec((tile, width), row),
            vspec((tile, width), row),
            vspec((tile, width), row),
            vspec((tile, width), row),
            vspec((4, width), lambda i: (0, 0)),
        ],
        out_shape=[
            jax.ShapeDtypeStruct((rows, width), BF),
            jax.ShapeDtypeStruct((rows, ff), BF),
            jax.ShapeDtypeStruct((rows, ff), BF),
            jax.ShapeDtypeStruct((rows, width), BF),
            jax.ShapeDtypeStruct((rows, width), BF),
            jax.ShapeDtypeStruct((rows, width), F32),
            jax.ShapeDtypeStruct((rows, width), BF),
            jax.ShapeDtypeStruct((rows, width), BF),
            jax.ShapeDtypeStruct((4, width), F32),
        ],
        scratch_shapes=[pltpu.VMEM((tile, ff), F32)],
        compiler_params=params(),
        cost_estimate=cost(2 * rows * width * ff * 4, 30e6, rows * ff * 2),
        name="feed",
    )(first_sum, w_ffn, w_ffn, w_att, cotangent, norm_params)


def attend_back_body(width, head, kp, c_ref, q_ref, s_ref, g_ref, dq_ref, ds_ref, head_ref, tail_ref, acc_ref):
    step = pl.program_id(0)
    last = pl.num_programs(0) - 1
    scale = head ** (-0.5)
    low_lane = lax.broadcasted_iota(jnp.int32, (kp, 2 * head), 1) < head

    def pair(j):
        cols = pl.ds(pl.multiple_of(j * 2 * head, 2 * head), 2 * head)
        vcols = pl.ds(pl.multiple_of(width + j * 2 * head, 2 * head), 2 * head)
        keys = head_pair(s_ref[0, :, cols], low_lane)
        values = head_pair(s_ref[0, :, vcols], low_lane)
        q = q_ref[:, cols]
        g = g_ref[:, cols]
        prob = softmax_pair(dot_t(q, keys) * scale, kp)
        grad_prob = dot_t(g, values)
        low_parts = []
        for half in range(2):
            p = prob[half]
            d = grad_prob[:, half * kp : (half + 1) * kp]
            low_parts.append((p * (d - jnp.sum(p * d, axis=-1, keepdims=True))).astype(BF))
        grad_scores = jnp.concatenate(low_parts, axis=1)
        prob_low = jnp.concatenate(prob, axis=1).astype(BF)
        dq_ref[:, cols] = (dot(grad_scores, keys) * scale).astype(BF)
        dk = dot_l(grad_scores, q) * scale
        dv = dot_l(prob_low, g)
        for at, both in ((cols, dk), (vcols, dv)):
            value = jnp.where(low_lane, both[:kp], both[kp:])
            ds_ref[0, :, at] = value
            for side, row, low_ref in ((0, 0, head_ref), (1, last, tail_ref)):
                before = jnp.where(step > 0, acc_ref[side, :, at], 0.0)
                total = before + c_ref[row, step] * value
                acc_ref[side, :, at] = total
                low_ref[:, at] = total.astype(BF)

    def two(i, carry):
        pair(2 * i)
        pair(2 * i + 1)
        return carry

    lax.fori_loop(0, width // (4 * head), two, 0)


def attend_back(coef, q, summary, grad_mix, head):
    rows, width = q.shape
    blocks, kp, _ = summary.shape
    short = rows // blocks
    row = lambda i, *_: (i, 0)
    lead = lambda i, *_: (i, 0, 0)
    return pl.pallas_call(
        functools.partial(attend_back_body, width, head, kp),
        grid_spec=pltpu.PrefetchScalarGridSpec(
            num_scalar_prefetch=1,
            grid=(blocks,),
            in_specs=[
                vspec((short, width), row),
                vspec((1, kp, 2 * width), lead),
                vspec((short, width), row),
            ],
            out_specs=[
                vspec((short, width), row),
                vspec((1, kp, 2 * width), lead),
                vspec((kp, 2 * width), lambda i, *_: (0, 0)),
                vspec((kp, 2 * width), lambda i, *_: (0, 0)),
            ],
            scratch_shapes=[pltpu.VMEM((2, kp, 2 * width), F32)],
        ),
        out_shape=[
            jax.ShapeDtypeStruct((rows, width), BF),
            jax.ShapeDtypeStruct((blocks, kp, 2 * width), F32),
            jax.ShapeDtypeStruct((kp, 2 * width), BF),
            jax.ShapeDtypeStruct((kp, 2 * width), BF),
        ],
        compiler_params=params(),
        cost_estimate=cost(2 * rows * width * 8 * kp, 10e6, rows * kp * 12),
        name="attend_back",
    )(coef, q, summary, grad_mix)


def outer_body(split, l_ref, r_ref, o_ref):
    value = dot_l(l_ref[...], r_ref[...])
    o_ref[...] = value.reshape(o_ref.shape).astype(o_ref.dtype)


def outer_up(first_low, grad_up, size, dtype):
    rows, width = first_low.shape
    chunks = grad_up.shape[1] // width
    groups = width // size
    return pl.pallas_call(
        functools.partial(outer_body, True),
        grid=(chunks,),
        in_specs=[
            vspec((rows, width), lambda i: (0, 0), True),
            vspec((rows, width), lambda i: (0, i)),
        ],
        out_specs=vspec((groups, 1, size, width), lambda i: (0, i, 0, 0)),
        out_shape=jax.ShapeDtypeStruct((groups, chunks, size, width), dtype),
        compiler_params=params(),
        cost_estimate=cost(2 * rows * width * width * chunks, 20e6),
        name="outer_up",
    )(first_low, grad_up)


def outer_rows(left, right, dtype, name):
    rows, width = right.shape[0], min(left.shape[1], right.shape[1])
    tall, wide = left.shape[1] // width, right.shape[1] // width
    moving = lambda n: (lambda i: (0, i)) if n > 1 else (lambda i: (0, 0))
    return pl.pallas_call(
        functools.partial(outer_body, False),
        grid=(tall * wide,),
        in_specs=[
            vspec((rows, width), moving(tall), tall == 1),
            vspec((rows, width), moving(wide), wide == 1),
        ],
        out_specs=vspec((width, width), lambda i: (i, 0)),
        out_shape=jax.ShapeDtypeStruct((tall * wide * width, width), dtype),
        compiler_params=params(),
        cost_estimate=cost(2 * rows * width * width * tall * wide, 20e6),
        name=name,
    )(left, right)


def back_body(
    width, blocks, c_ref, n_ref, e_ref, kv_ref, p_ref, *refs
):
    far_refs = refs[:4]
    dq_ref, w_ref, df_ref, dkv_ref, gp_ref, gi_ref = refs[4:]
    step = pl.program_id(0)
    short, kp = e_ref.shape[1], e_ref.shape[2]
    total = c_ref[step, 0] * p_ref[0]
    for other in range(1, blocks):
        total = total + c_ref[step, other] * p_ref[other]
    for k in range(4):
        total = total + c_ref[step, blocks + k] * far_refs[k][...].astype(F32)
    summary = total.astype(BF)
    dkv = dot(e_ref[0], summary).astype(BF)
    dkv_ref[...] = dkv
    keep = lax.broadcasted_iota(jnp.int32, (short, 1), 0) < n_ref[1, step]
    grad_e = jnp.where(keep, dot_t(kv_ref[...], summary), 0.0)
    column = n_ref[0, step]
    at = pl.multiple_of(jnp.minimum((column // 8) * 8, gp_ref.shape[0] - short - 8), 8)
    moved = pltpu.roll(
        jnp.concatenate([grad_e, jnp.zeros((8, kp), F32)], axis=0), column - at, 0
    )

    @pl.when(step == 0)
    def _():
        gp_ref[...] = jnp.zeros_like(gp_ref)

    gp_ref[pl.ds(at, short + 8), :] += moved
    gi_ref[...] = (
        df_ref[...]
        + dot_t(dq_ref[...], w_ref[pl.ds(0, width), :])
        + dot_t(dkv[:, :width], w_ref[pl.ds(width, width), :])
        + dot_t(dkv[:, width:], w_ref[pl.ds(2 * width, width), :])
    )


def back(coef, places, e_rows, kv, grad_parts, far_parts, dq, w_att, grad_first, positions):
    rows, width = dq.shape
    blocks, short, kp = e_rows.shape
    row = lambda i, *_: (i, 0)
    lead = lambda i, *_: (i, 0, 0)
    fixed = lambda i, *_: (0, 0)
    return pl.pallas_call(
        functools.partial(back_body, width, blocks),
        grid_spec=pltpu.PrefetchScalarGridSpec(
            num_scalar_prefetch=2,
            grid=(blocks,),
            in_specs=[
                vspec((1, short, kp), lead),
                vspec((short, 2 * width), row),
                vspec(grad_parts.shape, lambda i, *_: (0, 0, 0), True),
            ]
            + [vspec((kp, 2 * width), fixed, True)] * 4
            + [
                vspec((short, width), row),
                vspec((3 * width, width), fixed, True),
                vspec((short, width), row),
            ],
            out_specs=[
                vspec((short, 2 * width), row),
                vspec((positions, kp), fixed),
                vspec((short, width), row),
            ],
        ),
        out_shape=[
            jax.ShapeDtypeStruct((rows, 2 * width), BF),
            jax.ShapeDtypeStruct((positions, kp), F32),
            jax.ShapeDtypeStruct((rows, width), F32),
        ],
        compiler_params=params(),
        cost_estimate=cost(2 * rows * width * (3 * width + 4 * kp), 20e6),
        name="back",
    )(coef, places, e_rows, kv, grad_parts, *far_parts, dq, w_att, grad_first)


def reduce_body(depth, half, n_src, extra_keep, *refs):
    sources = refs[:n_src]
    grads, shares_out, rows_out = refs[n_src : n_src + 3]
    (own, got_c, sum_c, got_a, got_b, sum_a, sum_b, got_a2, got_b2, sum_z, got_z) = refs[
        n_src + 3 : n_src + 14
    ]
    keep_a, keep_b, keep_z = refs[n_src + 14 : n_src + 17]
    (e_own, e_got, e_sum, e_got1, e_sum1, e_got2, e_sum2, e_gotz, e_all, e_rows) = refs[
        n_src + 17 : n_src + 27
    ]
    send, recv, local = refs[n_src + 27 :]
    seq, mine = lax.axis_index("seq"), lax.axis_index("own")
    z, y, x, c = seq // 2, seq % 2, mine // 2, mine % 2
    core = (seq, 2 * x + (1 - c))
    along_x = (seq, 2 * (1 - x) + c)
    along_y = (2 * z + (1 - y), mine)
    along_z = [(2 * lax.rem(z + d, depth) + y, mine) for d in range(1, depth)]
    barrier = pltpu.get_barrier_semaphore()
    partners = [core, along_x, along_y] + along_z
    for partner in partners:
        pl.semaphore_signal(barrier, inc=1, device_id=partner, device_id_type=MESH_ID)
    pl.semaphore_wait(barrier, len(partners))

    sent = []

    def push(src, dst, partner):
        at = len(sent)
        copy = pltpu.make_async_remote_copy(
            src_ref=src,
            dst_ref=dst,
            send_sem=send.at[at],
            recv_sem=recv.at[at],
            device_id=partner,
            device_id_type=MESH_ID,
        )
        copy.start()
        sent.append(copy)
        return copy

    up, down, g_query, g_keyval, g_out, extra = sources
    bands = [g_query, g_keyval.at[0], g_keyval.at[1], g_out]
    half_z = depth // 2
    cols = own.shape[-1]
    loads = []

    def load(src, dst):
        copy = pltpu.make_async_copy(src, dst, local.at[len(loads)])
        copy.start()
        loads.append(copy)
        return copy

    e_first = [push(extra.at[:, :, 1 - c], e_got, core)]
    e_load = [load(extra.at[:, :, c], e_own)]
    piece_first, piece_load = [], []

    def piece_core(p):
        at, part = p // 2, pl.ds((p % 2) * cols, cols)
        if at < 2:
            first = [
                push(up.at[:, :, 1 - c, at, :, part], got_c.at[p, pl.ds(0, half_z)], core),
                push(down.at[:, :, 1 - c, at, :, part], got_c.at[p, pl.ds(half_z, half_z)], core),
            ]
            kept = [
                load(up.at[:, :, c, at, :, part], own.at[p, pl.ds(0, half_z)]),
                load(down.at[:, :, c, at, :, part], own.at[p, pl.ds(half_z, half_z)]),
            ]
        else:
            first = [
                push(bands[m].at[:, 1 - c, :, part], got_c.at[p, m], core) for m in range(depth)
            ]
            kept = [load(bands[m].at[:, c, :, part], own.at[p, m]) for m in range(depth)]
        piece_first.append(first)
        piece_load.append(kept)

    state = {}

    def wait_recv(copies):
        for copy in copies:
            copy.wait_recv()

    low, high = pl.ds(0, half), pl.ds(half, half)

    def add(a, b):
        return a.astype(F32) + b.astype(F32)

    def piece_c(p):
        for copy in piece_load[p]:
            copy.wait()
        wait_recv(piece_first[p])

        def body(i, carry):
            zz, w = i // 2, i % 2
            to_x, to_y = 2 * w + 1 - x, 2 * (1 - y) + w
            sum_c[p, 0, zz, w] = add(own[p, zz, to_x, low, :], got_c[p, zz, to_x, low, :]).astype(BF)
            sum_c[p, 1, zz, w] = add(own[p, zz, to_y, high, :], got_c[p, zz, to_y, high, :]).astype(BF)
            return carry

        lax.fori_loop(0, depth * 2, body, 0)
        state["1", p] = [
            push(sum_c.at[p, 0], got_a.at[p], along_x),
            push(sum_c.at[p, 1], got_b.at[p], along_y),
        ]

    def piece_1(p):
        wait_recv(state["1", p])

        def side_a(zz, w):
            at = 2 * w + x
            return add(own[p, zz, at, low, :], got_c[p, zz, at, low, :]) + got_a[p, zz, w].astype(F32)

        def side_b(zz, w):
            at = 2 * y + w
            return add(own[p, zz, at, high, :], got_c[p, zz, at, high, :]) + got_b[p, zz, w].astype(F32)

        def body(zz, carry):
            sum_a[p, zz] = side_a(zz, 1 - y).astype(BF)
            sum_b[p, zz] = side_b(zz, 1 - x).astype(BF)
            keep_a[p, zz] = side_a(zz, y)
            keep_b[p, zz] = side_b(zz, x)
            return carry

        lax.fori_loop(0, depth, body, 0)
        state["2", p] = [
            push(sum_a.at[p], got_a2.at[p], along_y),
            push(sum_b.at[p], got_b2.at[p], along_x),
        ]

    def piece_2(p):
        wait_recv(state["2", p])

        def body(zz, carry):
            total_a = keep_a[p, zz] + got_a2[p, zz].astype(F32)
            total_b = keep_b[p, zz] + got_b2[p, zz].astype(F32)
            sum_z[p, zz, low, :] = total_a.astype(BF)
            sum_z[p, zz, high, :] = total_b.astype(BF)
            return carry

        lax.fori_loop(0, depth, body, 0)
        keep_z[p, low, :] = keep_a[p, z] + got_a2[p, z].astype(F32)
        keep_z[p, high, :] = keep_b[p, z] + got_b2[p, z].astype(F32)
        state["z", p] = [
            push(sum_z.at[p, lax.rem(z + d, depth)], got_z.at[p, d - 1], along_z[d - 1])
            for d in range(1, depth)
        ]

    def piece_z(p):
        wait_recv(state["z", p])
        total = keep_z[p]
        for d in range(depth - 1):
            total = total + got_z[p, d].astype(F32)
        grads[(p // 2 + 1) % 3, :, pl.ds((p % 2) * cols, cols)] = total

    def extra_c():
        e_load[0].wait()
        wait_recv(e_first)

        def body(i, carry):
            zz, yx = i // 4, i % 4
            e_sum[zz, yx // 2, yx % 2] = e_own[zz, yx] + e_got[zz, yx]
            return carry

        lax.fori_loop(0, depth * 4, body, 0)
        state["ez"] = [
            push(e_sum.at[lax.rem(z + d, depth)], e_gotz.at[d - 1], along_z[d - 1])
            for d in range(1, depth)
        ]

    def extra_1():
        wait_recv(state["ez"])

        def body(i, carry):
            yy, xx = i // 2, i % 2
            total = e_sum[z, yy, xx]
            for d in range(depth - 1):
                total = total + e_gotz[d, yy, xx]
            e_sum1[yy, xx] = total
            return carry

        lax.fori_loop(0, 4, body, 0)
        state["e1"] = [push(e_sum1.at[:, 1 - x], e_got1, along_x)]

    def extra_2():
        wait_recv(state["e1"])

        def body(yy, carry):
            e_sum2[yy] = e_sum1[yy, x] + e_got1[yy]
            return carry

        lax.fori_loop(0, 2, body, 0)
        state["e2"] = [push(e_sum2.at[1 - y], e_got2, along_y)]

    def extra_z():
        wait_recv(state["e2"])
        e_all[z, y] = e_sum2[y] + e_got2[...]
        state["gz"] = [push(e_all.at[z, y], e_all.at[z, y], there) for there in along_z]

    def extra_gather_y():
        wait_recv(state["gz"])
        state["gy"] = [push(e_all.at[:, y], e_all.at[:, y], along_y)]

    def extra_gather_x():
        wait_recv(state["gy"])
        e_rows[x, c] = e_all[:, :, pl.ds(extra_keep, e_rows.shape[4]), :]
        state["gx"] = [push(e_rows.at[x, c], e_rows.at[x, c], along_x)]

    def extra_gather_c():
        wait_recv(state["gx"])
        state["gc"] = [push(e_rows.at[:, c], e_rows.at[:, c], core)]

    stages = [piece_c, piece_1, piece_2, piece_z]
    small = {0: extra_c, 3: extra_1, 4: extra_2, 5: extra_z, 6: extra_gather_y}
    small |= {7: extra_gather_x, 8: extra_gather_c}
    piece_core(0)
    piece_core(1)
    for turn in range(9):
        for stage in range(4):
            if 0 <= turn - stage < 6:
                stages[stage](turn - stage)
            if stage == 0 and turn + 2 < 6:
                piece_core(turn + 2)
        if turn in small:
            small[turn]()
    shares_out[...] = e_all[:, :, pl.ds(0, extra_keep), :]
    wait_recv(state["gc"])
    rows_out[...] = e_rows[...]
    for copy in sent:
        copy.wait_send()


def reduce_all(g_query, g_keyval, g_out, g_up, g_down, extra, peers):
    depth = peers // 2
    size, width = g_up.shape[2], g_up.shape[3]
    half = size // 2
    e_rows_all, kp = extra.shape[1], extra.shape[2]
    keep = e_rows_all - 8
    sources = (
        [
            g_up.reshape(depth // 2, 4, 2, 2, size, width),
            g_down.reshape(depth // 2, 4, 2, 2, size, width),
        ]
        + [
            g_query.reshape(4, 2, size, width),
            g_keyval.reshape(2, 4, 2, size, width),
            g_out.reshape(4, 2, size, width),
        ]
        + [extra.reshape(depth, 4, 2, e_rows_all, kp)]
    )
    n_src = len(sources)
    cols = width // 2
    messages = 1 + 8 + 2 * depth + 6 * (4 + depth - 1) + 2 + 2 * (depth - 1) + 3
    loads = 1 + 8 + 2 * depth
    any_spec = pl.BlockSpec(memory_space=pl.ANY)
    vmem = pl.BlockSpec(memory_space=pltpu.VMEM)
    scratch = [
        pltpu.VMEM((6, depth, 4, size, cols), BF),
        pltpu.VMEM((6, depth, 4, size, cols), BF),
        pltpu.VMEM((6, 2, depth, 2, half, cols), BF),
        pltpu.VMEM((6, depth, 2, half, cols), BF),
        pltpu.VMEM((6, depth, 2, half, cols), BF),
        pltpu.VMEM((6, depth, half, cols), BF),
        pltpu.VMEM((6, depth, half, cols), BF),
        pltpu.VMEM((6, depth, half, cols), BF),
        pltpu.VMEM((6, depth, half, cols), BF),
        pltpu.VMEM((6, depth, size, cols), BF),
        pltpu.VMEM((6, depth - 1, size, cols), BF),
        pltpu.VMEM((6, depth, half, cols), F32),
        pltpu.VMEM((6, depth, half, cols), F32),
        pltpu.VMEM((6, size, cols), F32),
        pltpu.VMEM((depth, 4, e_rows_all, kp), F32),
        pltpu.VMEM((depth, 4, e_rows_all, kp), F32),
        pltpu.VMEM((depth, 2, 2, e_rows_all, kp), F32),
        pltpu.VMEM((2, e_rows_all, kp), F32),
        pltpu.VMEM((2, 2, e_rows_all, kp), F32),
        pltpu.VMEM((e_rows_all, kp), F32),
        pltpu.VMEM((2, e_rows_all, kp), F32),
        pltpu.VMEM((depth - 1, 2, 2, e_rows_all, kp), F32),
        pltpu.VMEM((depth, 2, e_rows_all, kp), F32),
        pltpu.VMEM((2, 2, depth, 2, 8, kp), F32),
        pltpu.SemaphoreType.DMA((messages,)),
        pltpu.SemaphoreType.DMA((messages,)),
        pltpu.SemaphoreType.DMA((loads,)),
    ]
    return pl.pallas_call(
        functools.partial(reduce_body, depth, half, n_src, keep),
        in_specs=[any_spec] * n_src,
        out_specs=[vmem] * 3,
        out_shape=[
            jax.ShapeDtypeStruct((3, size, width), F32),
            jax.ShapeDtypeStruct((depth, 2, keep, kp), F32),
            jax.ShapeDtypeStruct((2, 2, depth, 2, 8, kp), F32),
        ],
        scratch_shapes=scratch,
        compiler_params=pltpu.CompilerParams(
            collective_id=1, has_side_effects=True, vmem_limit_bytes=VMEM_LIMIT
        ),
        name="reduce_all",
    )(*sources)


def gather_body(depth, half, band_ref, proj_ref, out_ref, pout_ref, send, recv, local):
    seq, mine = lax.axis_index("seq"), lax.axis_index("own")
    z, y, x, c = seq // 2, seq % 2, mine // 2, mine % 2
    core = (seq, 2 * x + (1 - c))
    along_x = (seq, 2 * (1 - x) + c)
    along_y = (2 * z + (1 - y), mine)
    order = [1, 3, 2]
    along_z = [(2 * lax.rem(z + d, depth) + y, mine) for d in order]
    barrier = pltpu.get_barrier_semaphore()
    partners = [core, along_x, along_y] + along_z
    for partner in partners:
        pl.semaphore_signal(barrier, inc=1, device_id=partner, device_id_type=MESH_ID)
    pl.semaphore_wait(barrier, len(partners))

    sent = []

    def push(src, dst, partner):
        at = len(sent)
        copy = pltpu.make_async_remote_copy(
            src_ref=src,
            dst_ref=dst,
            send_sem=send.at[at],
            recv_sem=recv.at[at],
            device_id=partner,
            device_id_type=MESH_ID,
        )
        copy.start()
        sent.append(copy)
        return copy

    keep = pltpu.make_async_copy(band_ref, out_ref.at[z, y, x, c], local.at[0])
    keep.start()
    keep_p = pltpu.make_async_copy(proj_ref, pout_ref.at[x, c], local.at[1])
    keep_p.start()
    mine_at = out_ref.at[z, y, x, c]
    from_z = [push(band_ref, mine_at, there) for there in along_z]
    from_x = [push(band_ref, mine_at, along_x)]
    from_y = [push(band_ref, mine_at, along_y)]
    proj_x = push(proj_ref, pout_ref.at[x, c], along_x)
    last = [push(band_ref, mine_at, core), push(proj_ref, pout_ref.at[x, c], core)]
    planes = [z]
    for k in range(depth - 1):
        from_z[k].wait_recv()
        plane = lax.rem(z + depth - order[k], depth)
        planes.append(plane)
        slab = out_ref.at[plane, y, x, c]
        from_x.append(push(slab, slab, along_x))
        from_y.append(push(slab, slab, along_y))
        last.append(push(slab, slab, core))
    low, high = pl.ds(0, half), pl.ds(half, half)
    cross = []
    for k in range(depth):
        plane = planes[k]
        from_x[k].wait_recv()
        slab = out_ref.at[plane, y, 1 - x, c]
        part = out_ref.at[plane, y, 1 - x, c, low, :]
        cross_y = push(part, part, along_y)
        last.append(push(slab, slab, core))
        from_y[k].wait_recv()
        slab = out_ref.at[plane, 1 - y, x, c]
        part = out_ref.at[plane, 1 - y, x, c, high, :]
        cross.append((cross_y, push(part, part, along_x)))
        last.append(push(slab, slab, core))
        if k == 0:
            proj_x.wait_recv()
            slab = pout_ref.at[1 - x, c]
            last.append(push(slab, slab, core))
    for k in range(depth):
        for copy in cross[k]:
            copy.wait_recv()
        slab = out_ref.at[planes[k], 1 - y, 1 - x, c]
        last.append(push(slab, slab, core))
    for copy in last:
        copy.wait_recv()
    keep.wait()
    keep_p.wait()
    for copy in sent:
        copy.wait_send()


def gather_bands(band, proj, peers):
    depth = peers // 2
    size, width = band.shape
    messages = (depth - 1) + 3 + 2 + 3 * (depth - 1) + 4 * depth + 1 + depth
    vmem = pl.BlockSpec(memory_space=pltpu.VMEM)
    return pl.pallas_call(
        functools.partial(gather_body, depth, size // 2),
        in_specs=[vmem] * 2,
        out_specs=[vmem] * 2,
        out_shape=[
            jax.ShapeDtypeStruct((depth, 2, 2, 2, size, width), BF),
            jax.ShapeDtypeStruct((2, 2) + proj.shape, BF),
        ],
        scratch_shapes=[
            pltpu.SemaphoreType.DMA((messages,)),
            pltpu.SemaphoreType.DMA((messages,)),
            pltpu.SemaphoreType.DMA((2,)),
        ],
        compiler_params=pltpu.CompilerParams(
            collective_id=2, has_side_effects=True, vmem_limit_bytes=VMEM_LIMIT
        ),
        cost_estimate=cost(1e9, 90e6),
        name="gather_bands",
    )(band, proj)


def shampoo(grad, left, right, root_left, root_right, weight):
    new_left = decay * left + (1.0 - decay) * jnp.einsum(
        "tij,tkj->tik", grad, grad, precision=highest
    )
    new_right = decay * right + (1.0 - decay) * jnp.einsum(
        "tji,tjk->tik", grad, grad, precision=highest
    )
    inner = jnp.einsum("tij,tjk->tik", grad, root_right, precision=highest)
    step = jnp.einsum("tij,tjk->tik", root_left, inner, precision=highest)
    return (new_left, new_right, weight - rate_matrix * step)


def exact(a, b, left, right):
    return lax.dot_general(
        a, b, (((left,), (right,)), ((), ())), precision=highest, preferred_element_type=F32
    )


def step_body(bands, *refs):
    band_ref, tiles, proj_ref, blocks = refs[0], refs[1:6], refs[6], refs[7:12]
    rows_ref, norm_ref, second_ref = refs[12:15]
    owned_ref, new_tiles, new_blocks = refs[15], refs[16:19], refs[19:22]
    grad_ref, second_new_ref, norm_new_ref, rms_ref = refs[22:]
    at = pl.program_id(0)
    size, kp = tiles[0].shape[1], proj_ref.shape[-1]

    def update(grad, state, new, t):
        left, right, root_left, root_right, weight = (ref[t] for ref in state)
        new[0][t] = decay * left + (1.0 - decay) * exact(grad, grad, 1, 1)
        new[1][t] = decay * right + (1.0 - decay) * exact(grad, grad, 0, 0)
        new[2][t] = weight - rate_matrix * exact(root_left, exact(grad, root_right, 1, 0), 1, 0)

    @pl.when(at < bands)
    def _():
        def four(i, carry):
            part = band_ref[0, :, pl.ds(pl.multiple_of(i * 4 * size, 128), 4 * size)]
            for t in range(4):
                grad = part[:, t * size : (t + 1) * size]
                owned_ref[4 * i + t] = grad
                update(grad, tiles, new_tiles, 4 * i + t)
            return carry

        lax.fori_loop(0, tiles[0].shape[0] // 4, four, 0)

    @pl.when(at >= bands)
    def _():
        update(proj_ref[0], blocks, new_blocks, 0)

    @pl.when(at == bands)
    def _():
        depth = rows_ref.shape[2]

        def row(r):
            return rows_ref[r // 2 % 2, r % 2, r // 8 % depth, r // 4 % 2, pl.ds(0, 1), :]

        per = norm_ref.shape[1] // kp
        for i in range(4):
            grad = jnp.concatenate([row(per * i + j) for j in range(per)], axis=1)
            grad_ref[pl.ds(i, 1), :] = grad
            second = decay * second_ref[pl.ds(i, 1), :] + (1.0 - decay) * grad * grad
            second_new_ref[pl.ds(i, 1), :] = second
            norm_new_ref[pl.ds(i, 1), :] = norm_ref[pl.ds(i, 1), :] - rate_norm * grad * lax.rsqrt(second)
        count = jnp.sum(row(6 * per), axis=1, keepdims=True)
        for i in range(2):
            square = row(4 * per + per * i)
            for j in range(1, per):
                square = square + row(4 * per + per * i + j)
            total = jnp.sum(square, axis=1, keepdims=True)
            ratio = jnp.sqrt(total / (count * norm_ref.shape[1]))
            rms_ref[pl.ds(i, 1), :] = jnp.broadcast_to(ratio, (1, rms_ref.shape[1]))


def step_all(bands, tiles, proj_grad, blocks, rows, norm_params, norm_stat):
    count, size, width = bands.shape
    each, kp = width // size, proj_grad.shape[-1]
    n_blocks = proj_grad.shape[0]
    tile = lambda: vspec((each, size, size), lambda i: (jnp.minimum(i, count - 1), 0, 0))
    block = lambda: vspec((1, kp, kp), lambda i: (jnp.maximum(i - count, 0), 0, 0))
    whole = lambda a: vspec(a.shape, lambda i: (0,) * len(a.shape))
    like = lambda a: jax.ShapeDtypeStruct(a.shape, F32)
    rms = jax.ShapeDtypeStruct((2, 128), F32)
    return pl.pallas_call(
        functools.partial(step_body, count),
        grid=(count + n_blocks,),
        in_specs=[vspec((1, size, width), lambda i: (jnp.minimum(i, count - 1), 0, 0))]
        + [tile() for _ in range(5)]
        + [block() for _ in range(6)]
        + [whole(rows), whole(norm_params), whole(norm_stat)],
        out_specs=[tile() for _ in range(4)]
        + [block() for _ in range(3)]
        + [whole(norm_params)] * 3
        + [whole(rms)],
        out_shape=[like(tiles[0])] * 4 + [like(proj_grad)] * 3 + [like(norm_params)] * 3 + [rms],
        compiler_params=params(),
        cost_estimate=cost(1e9, 20e6),
        name="step_all",
    )(bands, *tiles, proj_grad, *blocks, rows, norm_params, norm_stat)


def to_matrix(tiles, rows, cols):
    size = tiles.shape[-1]
    return (
        tiles.reshape(rows // size, cols // size, size, size)
        .transpose(0, 2, 1, 3)
        .reshape(rows, cols)
    )


def to_bands(tiles, cols):
    count, size, _ = tiles.shape
    return to_matrix(tiles, count * size * size // cols, cols)


def from_bands(bands, size):
    rows, cols = bands.shape
    return (
        bands.reshape(rows // size, size, cols // size, size)
        .transpose(0, 2, 1, 3)
        .reshape(-1, size, size)
    )


def bands_body(w_ref, p_ref, att_ref, ffn_ref, proj_ref):
    count, size, _ = w_ref.shape
    wide = att_ref.shape[1] // size
    near = att_ref.shape[0] // size
    for k in range(count):
        at, cols = k // wide, pl.ds(k % wide * size, size)
        tile = w_ref[k].astype(BF)
        if at < near:
            att_ref[pl.ds(at * size, size), cols] = tile
        else:
            ffn_ref[pl.ds((at - near) * size, size), cols] = tile
    proj_ref[...] = p_ref[...].astype(BF)


def make_bands(weights, projection, att_dev, width):
    per_dev, size, _ = weights.shape
    near = att_dev * size // width * size
    return pl.pallas_call(
        bands_body,
        out_shape=[
            jax.ShapeDtypeStruct((near, width), BF),
            jax.ShapeDtypeStruct((per_dev * size // width * size - near, width), BF),
            jax.ShapeDtypeStruct(projection.shape, BF),
        ],
        compiler_params=pltpu.CompilerParams(vmem_limit_bytes=VMEM_LIMIT),
        name="make_bands",
    )(weights, projection)


def gather_weights(weights, projection, att_dev, width, both, fused, peers):
    size = weights.shape[-1]
    low = weights.astype(BF)
    groups, chunks = width // size, FF // width
    if banded(weights.shape[0], att_dev, width, size):
        band, far, proj_low = make_bands(weights, projection, att_dev, width)
        ffn = lax.all_gather(far, both, axis=0, tiled=True)
        if fused:
            att, proj = gather_bands(band, proj_low, peers)
            att, proj = att.reshape(-1, width), proj.reshape(-1, projection.shape[1])
        else:
            att = lax.all_gather(band, both, axis=0, tiled=True)
            proj = lax.all_gather(proj_low, "own", axis=0, tiled=True)
        return att, ffn.reshape(2 * groups, chunks, size, width), proj
    per_dev = weights.shape[0]
    proj = lax.all_gather(projection.astype(BF), "own", axis=0, tiled=True)
    grid = lax.all_gather(low, both, axis=0, tiled=True).reshape(-1, per_dev, size, size)
    att = to_bands(grid[:, :att_dev].reshape(-1, size, size), width)
    tiles = grid[:, att_dev:].reshape(-1, size, size)
    half = tiles.shape[0] // 2
    w_up = to_matrix(tiles[:half], width, FF).reshape(groups, size, chunks, width)
    w_down = to_matrix(tiles[half:], FF, width).reshape(groups, chunks, size, width)
    return att, jnp.concatenate([w_up.transpose(0, 2, 1, 3), w_down], axis=0), proj


def banded(per_dev, att_dev, width, size):
    wide = width // size
    return att_dev % wide == 0 and (per_dev - att_dev) % wide == 0


def scatter_weight_grads(g_att, g_up, g_down, per_dev, att_dev, both):
    size, width = g_up.shape[2], g_up.shape[3]
    if banded(per_dev, att_dev, width, size):
        ffn = jnp.concatenate([g_up.reshape(-1, width), g_down], axis=0)
        ffn = lax.psum_scatter(ffn, both, scatter_dimension=0, tiled=True)
        att = lax.psum_scatter(g_att, both, scatter_dimension=0, tiled=True)
        return jnp.concatenate([from_bands(att, size), from_bands(ffn, size)], axis=0)
    up = g_up.transpose(0, 2, 1, 3).reshape(width, -1)
    att = from_bands(g_att, size)
    ffn = jnp.concatenate([from_bands(up, size), from_bands(g_down, size)], axis=0)
    stacked = jnp.concatenate(
        [
            att.reshape(-1, att_dev, size, size),
            ffn.reshape(-1, per_dev - att_dev, size, size),
        ],
        axis=1,
    ).reshape(-1, size, size)
    return lax.psum_scatter(stacked, both, scatter_dimension=0, tiled=True)


def per_device(
    tokens,
    cotangent,
    lengths,
    offsets,
    valid_count,
    weights,
    stat_left,
    stat_right,
    root_left,
    root_right,
    projection,
    projection_left,
    projection_right,
    projection_root_left,
    projection_root_right,
    norm_params,
    norm_stat,
):
    both = ("seq", "own")
    size = weights.shape[-1]
    width = tokens.shape[-1]
    rows_here = tokens.shape[1]
    head = width // HEADS
    kp = projection.shape[1]
    blocks = rows_here // SHORT
    peers = lax.axis_size("seq")
    devices = peers * lax.axis_size("own")
    per_dev = weights.shape[0]
    att_dev = 4 * (width // size) ** 2 // devices
    x = tokens[0]
    swap = [(i, i ^ 1) for i in range(peers)]
    peer_x = lax.ppermute(x, "seq", swap)
    own_size = lax.axis_size("own")
    fused = own_size == 4 and peers == 8 and banded(per_dev, att_dev, width, size)
    w_att, w_ffn, proj_all = gather_weights(
        weights, projection, att_dev, width, both, fused, peers
    )

    places, table, coef_back = tables(lengths, offsets, valid_count, blocks, rows_here)

    def proj_rows(at):
        col, n = places[0, at : at + blocks], places[1, at : at + blocks]
        rows = jnp.stack(
            [lax.dynamic_slice_in_dim(proj_all, col[b], SHORT, 0) for b in range(blocks)]
        )
        keep = lax.broadcasted_iota(jnp.int32, (blocks, SHORT, 1), 1) < n[:, None, None]
        return jnp.where(keep, rows, jnp.zeros((), BF))

    e_own = proj_rows(0)
    e_peer = proj_rows(blocks)
    n_own = places[1, :blocks]

    if fused:
        query, keyval, summary, mixed, first_sum, row_sums = forward(
            table, places, x, peer_x, w_att, e_own, e_peer, head, peers
        )
    else:
        query, keyval, part_own = project(x, w_att, e_own.transpose(0, 2, 1), True)
        (part_peer,) = project(peer_x, w_att, e_peer.transpose(0, 2, 1), False)

        def unit_sum(flag):
            total = flag[0] * part_own[0]
            for b in range(1, blocks):
                total = total + flag[b] * part_own[b]
            for b in range(blocks):
                total = total + flag[blocks + b] * part_peer[b]
            return total

        head_sum, tail_sum = unit_sum(table[0]), unit_sum(table[1])
        from_left = lax.ppermute(tail_sum, "seq", [(i, i + 2) for i in range(peers - 2)])
        from_right = lax.ppermute(head_sum, "seq", [(i + 2, i) for i in range(peers - 2)])
        summary = jnp.stack(
            [
                (
                    table[2, b] * head_sum
                    + table[3, b] * from_left
                    + table[4, b] * tail_sum
                    + table[5, b] * from_right
                    + table[6, b] * part_own[b]
                ).astype(BF)
                for b in range(blocks)
            ]
        )
        mixed, first_sum, row_sums = attend(n_own, query, summary, w_att, x, head)
    (
        result,
        hidden,
        grad_up,
        grad_down,
        first_low,
        grad_first,
        grad_branch,
        grad_mix,
        norm_terms,
    ) = feed(first_sum, w_ffn, w_att, cotangent[0], norm_params, 256)
    grad_query, grad_parts, low_head, low_tail = attend_back(
        coef_back, query, summary, grad_mix, head
    )

    far_parts = []
    for far in (1, 2):
        far_parts.append(lax.ppermute(low_tail, "seq", [(i, i + far) for i in range(peers - far)]))
        far_parts.append(lax.ppermute(low_head, "seq", [(i + far, i) for i in range(peers - far)]))
    gtype = BF if fused else F32
    g_up = outer_up(first_low, grad_up, size, gtype)
    g_down = outer_rows(hidden, grad_down, gtype, "outer_down")
    g_out = outer_rows(mixed, grad_branch, gtype, "outer_out")
    g_query = outer_rows(x, grad_query, gtype, "outer_query")
    grad_keyval, grad_proj, grad_input = back(
        coef_back,
        places,
        e_own,
        keyval,
        grad_parts,
        far_parts,
        grad_query,
        w_att,
        grad_first,
        proj_all.shape[0],
    )
    g_keyval = outer_rows(x, grad_keyval, gtype, "outer_keyval")
    part_rows = projection.shape[0]
    valid_here = jnp.sum(n_own).astype(F32)
    extra = jnp.concatenate(
        [
            norm_terms.reshape(-1, kp),
            row_sums.reshape(-1, kp),
            jnp.full((1, kp), 1.0 / kp, F32) * valid_here,
        ],
        axis=0,
    )
    n_norm = 4 * width // kp
    n_row = 2 * width // kp
    if fused:
        extra = jnp.pad(extra, ((0, devices - extra.shape[0]), (0, 0)))[:, None, :]
        extra = jnp.pad(extra, ((0, 0), (0, 7), (0, 0)))
        shares = grad_proj.reshape(own_size, peers, part_rows // peers, kp).swapaxes(0, 1)
        shares = shares.reshape(devices, part_rows // peers, kp)
        banded_grads, proj_parts, rows = reduce_all(
            g_query, g_keyval, g_out, g_up, g_down, jnp.concatenate([shares, extra], axis=1), peers
        )
        (
            owned,
            left_new,
            right_new,
            weights_new,
            proj_left_new,
            proj_right_new,
            proj_blocks,
            norm_grad,
            stat_new,
            norm_new,
            rms,
        ) = step_all(
            banded_grads,
            [stat_left, stat_right, root_left, root_right, weights],
            proj_parts.reshape(-1, kp, kp),
            [
                projection_left,
                projection_right,
                projection_root_left,
                projection_root_right,
                projection.reshape(-1, kp, kp),
            ],
            rows,
            norm_params,
            norm_stat,
        )
        proj_grad = proj_parts.reshape(part_rows, kp)
        residual_rms = rms[:, 0]
    else:
        owned = scatter_weight_grads(
            jnp.concatenate([g_query, g_keyval, g_out], axis=0), g_up, g_down, per_dev, att_dev, both
        )
        packed = jnp.concatenate([grad_proj, extra], axis=0)
        packed = lax.psum(jnp.pad(packed, ((0, -packed.shape[0] % 16), (0, 0))), both)
        proj_grad = lax.dynamic_slice_in_dim(
            packed, lax.axis_index("own") * part_rows, part_rows, 0
        )
        totals = packed[grad_proj.shape[0] :]
        norm_grad = totals[:n_norm].reshape(4, width)
        row_total = totals[n_norm : n_norm + n_row].reshape(2, width).sum(axis=1)
        valid_total = totals[n_norm + n_row].sum()
        residual_rms = jnp.sqrt(row_total / (valid_total * width))
        left_new, right_new, weights_new = shampoo(
            owned, stat_left, stat_right, root_left, root_right, weights
        )
        proj_left_new, proj_right_new, proj_blocks = shampoo(
            proj_grad.reshape(-1, kp, kp),
            projection_left,
            projection_right,
            projection_root_left,
            projection_root_right,
            projection.reshape(-1, kp, kp),
        )
        stat_new = decay * norm_stat + (1.0 - decay) * norm_grad * norm_grad
        norm_new = norm_params - rate_norm * norm_grad * lax.rsqrt(stat_new)
    return (
        result[None],
        grad_input[None],
        owned,
        left_new,
        right_new,
        weights_new,
        proj_grad,
        proj_left_new,
        proj_right_new,
        proj_blocks.reshape(part_rows, kp),
        norm_grad,
        stat_new,
        norm_new,
        residual_rms,
    )


def solution(mesh):
    pack = P("own", "seq", None)
    table = P("own", None)
    tile = P(("seq", "own"), None, None)
    proj = P("own", None, None)
    return jax.shard_map(
        per_device,
        mesh=mesh,
        in_specs=(pack, pack, table, table, table)
        + (tile,) * 5
        + (table, proj, proj, proj, proj, P(), P()),
        out_specs=(pack, pack) + (tile,) * 4 + (table, proj, proj, table, P(), P(), P(), P()),
        check_vma=False,
    )
```

```python
import functools
import math

import jax
import jax.numpy as jnp
from jax import lax
from jax.experimental import pallas as pl
from jax.experimental.pallas import tpu as pltpu
from jax.sharding import PartitionSpec as P

HEADS = 12
FF = 3072
SHORT = 512
BF = jnp.bfloat16
F32 = jnp.float32

eps_norm = 1e-05
decay = 0.5
rate_matrix = 0.2
rate_norm = 0.2
highest = lax.Precision.HIGHEST
VMEM_LIMIT = 60 * 1024 * 1024
MESH_ID = pl.DeviceIdType.MESH


def dot(a, b):
    return lax.dot_general(a, b, (((1,), (0,)), ((), ())), preferred_element_type=F32)


def dot_t(a, b):
    return lax.dot_general(a, b, (((1,), (1,)), ((), ())), preferred_element_type=F32)


def dot_l(a, b):
    return lax.dot_general(a, b, (((0,), (0,)), ((), ())), preferred_element_type=F32)


def vspec(shape, index_map, once=False):
    if once:
        return pl.BlockSpec(shape, index_map, pipeline_mode=pl.Buffered(1))
    return pl.BlockSpec(shape, index_map)


def params():
    return pltpu.CompilerParams(
        dimension_semantics=("arbitrary",), vmem_limit_bytes=VMEM_LIMIT
    )


def cost(flops, nbytes, trans=0):
    return pl.CostEstimate(flops=int(flops), bytes_accessed=int(nbytes), transcendentals=int(trans))


def tables_body(blocks, rows_here, l_ref, o_ref, v_ref, i_ref, f_ref, b_ref):
    seq = lax.axis_index("seq")
    side = seq % 2
    row_start = seq * rows_here
    row_end = row_start + rows_here
    unit_start = (seq - side) * rows_here
    peer_start = (seq + 1 - 2 * side) * rows_here
    flag = lambda cond: jnp.where(cond, 1.0, 0.0).astype(F32)

    def locate(row):
        def body(i, carry):
            at, start, end, off, count = carry
            stop = at + l_ref[0, i]
            inside = jnp.logical_and(row >= at, row < stop)
            pick = lambda new, old: jnp.where(inside, new, old)
            return (
                stop,
                pick(at, start),
                pick(stop, end),
                pick(o_ref[0, i], off),
                pick(v_ref[0, i], count),
            )

        zero = jnp.int32(0)
        return lax.fori_loop(0, l_ref.shape[1], body, (zero,) * 5)[1:]

    starts, ends = [], []
    for k in range(2 * blocks):
        row = row_start + SHORT * k if k < blocks else peer_start + SHORT * (k - blocks)
        start, end, off, count = locate(row)
        starts.append(start)
        ends.append(end)
        i_ref[0, k] = off + row - start
        i_ref[1, k] = jnp.clip(count - (row - start), 0, SHORT)
    first = jnp.where(side == 0, starts[0], starts[blocks])
    last = jnp.where(side == 0, starts[-1], starts[blocks - 1])
    last_end = jnp.where(side == 0, ends[-1], ends[blocks - 1])
    head_cross = flag(first < unit_start)
    tail_cross = flag(last_end > unit_start + 2 * rows_here)
    for k in range(2 * blocks):
        is_head, is_tail = flag(starts[k] == first), flag(starts[k] == last)
        pick_tail = (1.0 - is_head) * is_tail
        f_ref[0, k] = is_head
        f_ref[1, k] = is_tail
        f_ref[2, k] = is_head
        f_ref[3, k] = is_head * head_cross
        f_ref[4, k] = pick_tail
        f_ref[5, k] = pick_tail * tail_cross
        f_ref[6, k] = (1.0 - is_head) * (1.0 - is_tail)
    own_last, own_end = starts[blocks - 1], ends[blocks - 1]
    for k in range(blocks):
        at_head, at_tail = flag(starts[k] == starts[0]), flag(starts[k] == own_last)
        for other in range(blocks):
            b_ref[k, other] = flag(starts[k] == starts[other])
        for far in range(2):
            reach = far * rows_here
            b_ref[k, blocks + 2 * far] = at_head * flag(starts[0] < row_start - reach)
            b_ref[k, blocks + 2 * far + 1] = at_tail * flag(own_end > row_end + reach)


def tables(lengths, offsets, valid_count, blocks, rows_here):
    smem = pl.BlockSpec(memory_space=pltpu.SMEM)
    return pl.pallas_call(
        functools.partial(tables_body, blocks, rows_here),
        in_specs=[smem] * 3,
        out_specs=[smem] * 3,
        out_shape=[
            jax.ShapeDtypeStruct((2, 2 * blocks), jnp.int32),
            jax.ShapeDtypeStruct((7, 2 * blocks), F32),
            jax.ShapeDtypeStruct((blocks, blocks + 4), F32),
        ],
        name="tables",
    )(lengths, offsets, valid_count)


def project_body(width, with_query, x_ref, w_ref, e_ref, *outs):
    x = x_ref[...]
    if with_query:
        q_ref, kv_ref, p_ref = outs
        q_ref[...] = dot(x, w_ref[pl.ds(0, width), :]).astype(BF)
    else:
        (p_ref,) = outs
    e = e_ref[0]
    for part in range(2):
        kv = dot(x, w_ref[pl.ds((1 + part) * width, width), :]).astype(BF)
        if with_query:
            kv_ref[:, pl.ds(part * width, width)] = kv
        p_ref[0, :, pl.ds(part * width, width)] = dot(e, kv)


def project(x, w_att, e_t, with_query):
    rows, width = x.shape
    blocks, kp, short = e_t.shape
    out_shape = [jax.ShapeDtypeStruct((blocks, kp, 2 * width), F32)]
    out_specs = [vspec((1, kp, 2 * width), lambda i: (i, 0, 0))]
    if with_query:
        out_shape = [
            jax.ShapeDtypeStruct((rows, width), BF),
            jax.ShapeDtypeStruct((rows, 2 * width), BF),
        ] + out_shape
        out_specs = [
            vspec((short, width), lambda i: (i, 0)),
            vspec((short, 2 * width), lambda i: (i, 0)),
        ] + out_specs
    return pl.pallas_call(
        functools.partial(project_body, width, with_query),
        grid=(blocks,),
        in_specs=[
            vspec((short, width), lambda i: (i, 0)),
            vspec((3 * width, width), lambda i: (0, 0), True),
            vspec((1, kp, short), lambda i: (i, 0, 0)),
        ],
        out_specs=out_specs,
        out_shape=out_shape,
        compiler_params=params(),
        cost_estimate=cost(2 * rows * width * width * 3, 12e6),
        name="project" if with_query else "project_peer",
    )(x, w_att, e_t)


def head_pair(ref_slice, low_lane):
    zero = jnp.zeros_like(ref_slice)
    return jnp.concatenate(
        [jnp.where(low_lane, ref_slice, zero), jnp.where(low_lane, zero, ref_slice)], axis=0
    )


def softmax_pair(scores, kp):
    parts = []
    for half in range(2):
        s = scores[:, half * kp : (half + 1) * kp]
        top = jnp.max(s, axis=-1, keepdims=True)
        e = jnp.exp(s - top)
        parts.append(e * (1.0 / jnp.sum(e, axis=-1, keepdims=True)))
    return parts


def attend_body(width, head, kp, n_ref, q_ref, s_ref, w_ref, x_ref, mix_ref, sum_ref, stat_ref):
    pairs = width // (2 * head)
    step = pl.program_id(0)
    scale = head ** (-0.5)
    low_lane = lax.broadcasted_iota(jnp.int32, (kp, 2 * head), 1) < head
    for j in range(pairs):
        cols = pl.ds(j * 2 * head, 2 * head)
        keys = head_pair(s_ref[0, :, cols], low_lane)
        values = head_pair(s_ref[0, :, pl.ds(width + j * 2 * head, 2 * head)], low_lane)
        scores = dot_t(q_ref[:, cols], keys) * scale
        prob = jnp.concatenate(softmax_pair(scores, kp), axis=1).astype(BF)
        mix_ref[:, cols] = dot(prob, values).astype(BF)
    branch = dot(mix_ref[...], w_ref[...])
    first = x_ref[...].astype(F32) + branch
    sum_ref[...] = first
    rows = q_ref.shape[0]
    keep = (lax.broadcasted_iota(jnp.int32, (rows, 1), 0) < n_ref[step]).astype(F32)
    sums = jnp.concatenate(
        [
            jnp.sum(keep * first * first, axis=0, keepdims=True),
            jnp.sum(keep * branch * branch, axis=0, keepdims=True),
        ],
        axis=0,
    )

    @pl.when(step == 0)
    def _():
        stat_ref[...] = sums

    @pl.when(step > 0)
    def _():
        stat_ref[...] += sums


def attend(n_valid, q, summary, w_att, x, head):
    rows, width = q.shape
    blocks, kp, _ = summary.shape
    short = rows // blocks
    return pl.pallas_call(
        functools.partial(attend_body, width, head, kp),
        grid_spec=pltpu.PrefetchScalarGridSpec(
            num_scalar_prefetch=1,
            grid=(blocks,),
            in_specs=[
                vspec((short, width), lambda i, n: (i, 0)),
                vspec((1, kp, 2 * width), lambda i, n: (i, 0, 0)),
                vspec((width, width), lambda i, n: (3, 0), True),
                vspec((short, width), lambda i, n: (i, 0)),
            ],
            out_specs=[
                vspec((short, width), lambda i, n: (i, 0)),
                vspec((short, width), lambda i, n: (i, 0)),
                vspec((2, width), lambda i, n: (0, 0)),
            ],
        ),
        out_shape=[
            jax.ShapeDtypeStruct((rows, width), BF),
            jax.ShapeDtypeStruct((rows, width), F32),
            jax.ShapeDtypeStruct((2, width), F32),
        ],
        compiler_params=params(),
        cost_estimate=cost(2 * rows * width * (width + 4 * kp), 10e6, rows * kp * 12),
        name="attend",
    )(n_valid, q, summary, w_att, x)


def forward_body(
    depth, head, c_ref, n_ref, x_ref, px_ref, w_ref, e_ref, pe_ref, *refs
):
    q_ref, kv_ref, s_ref, mix_ref, sum_ref, stat_ref, part, unit, got, send, recv = refs
    blocks, short, kp = e_ref.shape
    width = x_ref.shape[1]
    seq, mine = lax.axis_index("seq"), lax.axis_index("own")
    z, y = seq // 2, seq % 2
    along_y = (2 * z + (1 - y), mine)
    after = (2 * lax.rem(z + 1, depth) + y, mine)
    before = (2 * lax.rem(z + depth - 1, depth) + y, mine)
    has_left, has_right = z > 0, z < depth - 1
    shared = kp * 5 // 16
    direct = kp - 2 * shared
    barrier = pltpu.get_barrier_semaphore()
    pl.semaphore_signal(barrier, inc=1, device_id=along_y, device_id_type=MESH_ID)

    @pl.when(has_left)
    def _():
        pl.semaphore_signal(barrier, inc=1, device_id=before, device_id_type=MESH_ID)

    @pl.when(has_right)
    def _():
        pl.semaphore_signal(barrier, inc=1, device_id=after, device_id_type=MESH_ID)

    pl.semaphore_wait(barrier, 1 + jnp.minimum(z, 1) + jnp.minimum(depth - 1 - z, 1))

    @pl.when(jnp.logical_not(has_left))
    def _():
        got[0] = jnp.zeros_like(got[0])

    @pl.when(jnp.logical_not(has_right))
    def _():
        got[1] = jnp.zeros_like(got[1])

    def copy(at, src, dst, there):
        return pltpu.make_async_remote_copy(
            src_ref=src,
            dst_ref=dst,
            send_sem=send.at[at],
            recv_sem=recv.at[at],
            device_id=there,
            device_id_type=MESH_ID,
        )

    every = pl.ds(0, direct)
    single = pl.ds(pl.multiple_of(direct + shared * y, 8), shared)
    moves, hands = {}, {}
    for kind in range(2):
        cols = pl.ds(kind * width, width)
        for side in range(2):
            there = (after, before)[side]
            at = (kind * 2 + side) * 3
            moves[kind, side] = [
                copy(at, unit.at[side, every, cols], got.at[side, every, cols], there),
                copy(at + 1, unit.at[side, single, cols], got.at[side, single, cols], there),
            ]
            hands[kind, side] = copy(
                at + 2, got.at[side, single, cols], got.at[side, single, cols], along_y
            )
    can_send = (has_right, has_left)
    can_get = (has_left, has_right)

    for kind in range(2):
        cols = pl.ds(kind * width, width)
        weight = pl.ds((1 + kind) * width, width)

        def own_block(b, carry):
            rows = pl.ds(pl.multiple_of(b * short, short), short)
            kv = dot(x_ref[rows, :], w_ref[weight, :]).astype(BF)
            kv_ref[rows, cols] = kv
            total = dot_l(e_ref[b], kv)
            part[b, :, cols] = total

            @pl.when(b == 0)
            def _():
                for side in range(2):
                    unit[side, :, cols] = c_ref[1 - side, b] * total

            @pl.when(b > 0)
            def _():
                for side in range(2):
                    unit[side, :, cols] += c_ref[1 - side, b] * total

            return carry

        def peer_block(b, carry):
            rows = pl.ds(pl.multiple_of(b * short, short), short)
            kv = dot(px_ref[rows, :], w_ref[weight, :]).astype(BF)
            total = dot_l(pe_ref[b], kv)
            for side in range(2):
                unit[side, :, cols] += c_ref[1 - side, blocks + b] * total
            return carry

        lax.fori_loop(0, blocks, own_block, 0)
        lax.fori_loop(0, blocks, peer_block, 0)
        for side in range(2):

            @pl.when(can_send[side])
            def _():
                for move in moves[kind, side]:
                    move.start()

    def query_block(b, carry):
        rows = pl.ds(pl.multiple_of(b * short, short), short)
        q_ref[rows, :] = dot(x_ref[rows, :], w_ref[pl.ds(0, width), :]).astype(BF)
        return carry

    lax.fori_loop(0, blocks, query_block, 0)
    for kind in range(2):
        for side in range(2):

            @pl.when(can_get[side])
            def _():
                moves[kind, side][1].wait_recv()
                hands[kind, side].start()

    for kind in range(2):
        for side in range(2):

            @pl.when(can_get[side])
            def _():
                moves[kind, side][0].wait_recv()
                hands[kind, side].wait_recv()

    slab = 64

    def combine(i, carry):
        b, at = i // (kp // slab), i % (kp // slab)
        rows = pl.ds(pl.multiple_of(at * slab, slab), slab)
        total = c_ref[2, b] * unit[1, rows, :] + c_ref[3, b] * got[0, rows, :]
        total = total + c_ref[4, b] * unit[0, rows, :] + c_ref[5, b] * got[1, rows, :]
        s_ref[b, rows, :] = (total + c_ref[6, b] * part[b, rows, :]).astype(BF)
        return carry

    lax.fori_loop(0, blocks * (kp // slab), combine, 0)
    pairs = width // (2 * head)
    scale = head ** (-0.5)
    low_lane = lax.broadcasted_iota(jnp.int32, (kp, 2 * head), 1) < head

    def attend_block(b, carry):
        rows = pl.ds(pl.multiple_of(b * short, short), short)
        def pair(j):
            cols = pl.ds(pl.multiple_of(j * 2 * head, 2 * head), 2 * head)
            vcols = pl.ds(pl.multiple_of(width + j * 2 * head, 2 * head), 2 * head)
            keys = head_pair(s_ref[b, :, cols], low_lane)
            values = head_pair(s_ref[b, :, vcols], low_lane)
            scores = dot_t(q_ref[rows, cols], keys) * scale
            prob = jnp.concatenate(softmax_pair(scores, kp), axis=1).astype(BF)
            mix_ref[rows, cols] = dot(prob, values).astype(BF)

        def two(i, inner):
            pair(2 * i)
            pair(2 * i + 1)
            return inner

        lax.fori_loop(0, pairs // 2, two, 0)
        branch = dot(mix_ref[rows, :], w_ref[pl.ds(3 * width, width), :])
        first = x_ref[rows, :].astype(F32) + branch
        sum_ref[rows, :] = first
        keep = (lax.broadcasted_iota(jnp.int32, (short, 1), 0) < n_ref[1, b]).astype(F32)
        here = lax.broadcasted_iota(jnp.int32, (1, width), 1) == 0
        stat_ref[...] += jnp.concatenate(
            [
                jnp.sum(keep * first * first, axis=0, keepdims=True),
                jnp.sum(keep * branch * branch, axis=0, keepdims=True),
                jnp.where(here, n_ref[1, b].astype(F32), 0.0),
            ],
            axis=0,
        )
        return carry

    stat_ref[...] = jnp.zeros_like(stat_ref)
    lax.fori_loop(0, blocks, attend_block, 0)
    for kind in range(2):
        for side in range(2):

            @pl.when(can_send[side])
            def _():
                for move in moves[kind, side]:
                    move.wait_send()

            @pl.when(can_get[side])
            def _():
                hands[kind, side].wait_send()


def forward(coef, n_valid, x, peer_x, w_att, e_own, e_peer, head, peers):
    rows, width = x.shape
    blocks, short, kp = e_own.shape
    vmem = pl.BlockSpec(memory_space=pltpu.VMEM)
    smem = pl.BlockSpec(memory_space=pltpu.SMEM)
    return pl.pallas_call(
        functools.partial(forward_body, peers // 2, head),
        in_specs=[smem] * 2 + [vmem] * 5,
        out_specs=[vmem] * 6,
        out_shape=[
            jax.ShapeDtypeStruct((rows, width), BF),
            jax.ShapeDtypeStruct((rows, 2 * width), BF),
            jax.ShapeDtypeStruct((blocks, kp, 2 * width), BF),
            jax.ShapeDtypeStruct((rows, width), BF),
            jax.ShapeDtypeStruct((rows, width), F32),
            jax.ShapeDtypeStruct((3, width), F32),
        ],
        scratch_shapes=[
            pltpu.VMEM((blocks, kp, 2 * width), F32),
            pltpu.VMEM((2, kp, 2 * width), F32),
            pltpu.VMEM((2, kp, 2 * width), F32),
            pltpu.SemaphoreType.DMA((12,)),
            pltpu.SemaphoreType.DMA((12,)),
        ],
        compiler_params=pltpu.CompilerParams(
            collective_id=3, has_side_effects=True, vmem_limit_bytes=VMEM_LIMIT
        ),
        cost_estimate=cost(2 * rows * width * width * 8, 200e6, rows * kp * 12),
        name="forward",
    )(coef, n_valid, x, peer_x, w_att, e_own, e_peer)


def normalize(values):
    mean = jnp.mean(values, axis=-1, keepdims=True)
    centered = values - mean
    inverse = lax.rsqrt(jnp.mean(centered * centered, axis=-1, keepdims=True) + eps_norm)
    return centered * inverse, inverse


def norm_back(grad_out, normed, inverse, gain):
    scaled = grad_out * gain
    return inverse * (
        scaled
        - jnp.mean(scaled, axis=-1, keepdims=True)
        - normed * jnp.mean(scaled * normed, axis=-1, keepdims=True)
    )


def feed_body(
    chunks,
    first_ref,
    w1_ref,
    w2_ref,
    wo_ref,
    cot_ref,
    np_ref,
    out_ref,
    hid_ref,
    up_ref,
    down_ref,
    flow_ref,
    dfirst_ref,
    dbranch_ref,
    dmix_ref,
    ng_ref,
    slope_ref,
):
    step = pl.program_id(0)
    rows, width = first_ref.shape
    deep = w2_ref.shape[0] // chunks
    down_rows = lambda c: w2_ref[pl.ds(c * deep, deep)].reshape(width, width)
    normed_one, inverse_one = normalize(first_ref[...])
    first_norm = normed_one * np_ref[0:1, :] + np_ref[1:2, :]
    first_low = first_norm.astype(BF)
    flow_ref[...] = first_low
    second = first_norm
    for c in range(chunks):
        cols = pl.ds(c * width, width)
        u = dot(first_low, w1_ref[:, c].reshape(width, width))
        cumulative = 0.5 * (1.0 + lax.erf(u * (1.0 / math.sqrt(2.0))))
        density = jnp.exp(-0.5 * u * u) * (1.0 / math.sqrt(2.0 * math.pi))
        slope_ref[:, cols] = cumulative + u * density
        hidden = (u * cumulative).astype(BF)
        hid_ref[:, cols] = hidden
        second = second + dot(hidden, down_rows(c))
    normed_two, inverse_two = normalize(second)
    out_ref[...] = (normed_two * np_ref[2:3, :] + np_ref[3:4, :]).astype(BF)
    grad_out = cot_ref[...].astype(F32)
    gain_two = jnp.sum(grad_out * normed_two, axis=0, keepdims=True)
    shift_two = jnp.sum(grad_out, axis=0, keepdims=True)
    grad_second = norm_back(grad_out, normed_two, inverse_two, np_ref[2:3, :])
    down = grad_second.astype(BF)
    down_ref[...] = down
    grad_first_norm = grad_second
    for c in range(chunks):
        cols = pl.ds(c * width, width)
        grad_hidden = dot_t(down, down_rows(c))
        up = (grad_hidden * slope_ref[:, cols]).astype(BF)
        up_ref[:, cols] = up
        grad_first_norm = grad_first_norm + dot_t(up, w1_ref[:, c].reshape(width, width))
    gain_one = jnp.sum(grad_first_norm * normed_one, axis=0, keepdims=True)
    shift_one = jnp.sum(grad_first_norm, axis=0, keepdims=True)
    grad_first = norm_back(grad_first_norm, normed_one, inverse_one, np_ref[0:1, :])
    dfirst_ref[...] = grad_first
    grad_branch = grad_first.astype(BF)
    dbranch_ref[...] = grad_branch
    dmix_ref[...] = dot_t(grad_branch, wo_ref[...]).astype(BF)
    sums = jnp.concatenate([gain_one, shift_one, gain_two, shift_two], axis=0)

    @pl.when(step == 0)
    def _():
        ng_ref[...] = sums

    @pl.when(step > 0)
    def _():
        ng_ref[...] += sums


def feed(first_sum, w_ffn, w_att, cotangent, norm_params, tile):
    rows, width = first_sum.shape
    groups, chunks, size, _ = w_ffn.shape
    groups = groups // 2
    ff = chunks * width
    row = lambda i: (i, 0)
    return pl.pallas_call(
        functools.partial(feed_body, chunks),
        grid=(rows // tile,),
        in_specs=[
            vspec((tile, width), row),
            vspec((groups, chunks, size, width), lambda i: (0, 0, 0, 0), True),
            vspec((groups, chunks, size, width), lambda i: (1, 0, 0, 0), True),
            vspec((width, width), lambda i: (3, 0), True),
            vspec((tile, width), row),
            vspec(norm_params.shape, lambda i: (0, 0)),
        ],
        out_specs=[
            vspec((tile, width), row),
            vspec((tile, ff), row),
            vspec((tile, ff), row),
            vspec((tile, width), row),
            vspec((tile, width), row),
            vspec((tile, width), row),
            vspec((tile, width), row),
            vspec((tile, width), row),
            vspec((4, width), lambda i: (0, 0)),
        ],
        out_shape=[
            jax.ShapeDtypeStruct((rows, width), BF),
            jax.ShapeDtypeStruct((rows, ff), BF),
            jax.ShapeDtypeStruct((rows, ff), BF),
            jax.ShapeDtypeStruct((rows, width), BF),
            jax.ShapeDtypeStruct((rows, width), BF),
            jax.ShapeDtypeStruct((rows, width), F32),
            jax.ShapeDtypeStruct((rows, width), BF),
            jax.ShapeDtypeStruct((rows, width), BF),
            jax.ShapeDtypeStruct((4, width), F32),
        ],
        scratch_shapes=[pltpu.VMEM((tile, ff), F32)],
        compiler_params=params(),
        cost_estimate=cost(2 * rows * width * ff * 4, 30e6, rows * ff * 2),
        name="feed",
    )(first_sum, w_ffn, w_ffn, w_att, cotangent, norm_params)


def pair_back(key_cols, value_cols, q, g, head, low_lane):
    kp = key_cols.shape[0]
    scale = head ** (-0.5)
    keys, values = head_pair(key_cols, low_lane), head_pair(value_cols, low_lane)
    prob = softmax_pair(dot_t(q, keys) * scale, kp)
    grad_prob = dot_t(g, values)
    low_parts = []
    for half in range(2):
        p = prob[half]
        d = grad_prob[:, half * kp : (half + 1) * kp]
        low_parts.append((p * (d - jnp.sum(p * d, axis=-1, keepdims=True))).astype(BF))
    grad_scores = jnp.concatenate(low_parts, axis=1)
    prob_low = jnp.concatenate(prob, axis=1).astype(BF)
    grad_q = (dot(grad_scores, keys) * scale).astype(BF)
    return grad_q, dot_l(grad_scores, q) * scale, dot_l(prob_low, g)


def attend_back_body(width, head, kp, c_ref, q_ref, s_ref, g_ref, dq_ref, ds_ref, head_ref, tail_ref, acc_ref):
    step = pl.program_id(0)
    last = pl.num_programs(0) - 1
    low_lane = lax.broadcasted_iota(jnp.int32, (kp, 2 * head), 1) < head

    def pair(j):
        cols = pl.ds(pl.multiple_of(j * 2 * head, 2 * head), 2 * head)
        vcols = pl.ds(pl.multiple_of(width + j * 2 * head, 2 * head), 2 * head)
        grads, dk, dv = pair_back(
            s_ref[0, :, cols], s_ref[0, :, vcols], q_ref[:, cols], g_ref[:, cols], head, low_lane
        )
        dq_ref[:, cols] = grads
        for at, both in ((cols, dk), (vcols, dv)):
            value = jnp.where(low_lane, both[:kp], both[kp:])
            ds_ref[0, :, at] = value
            for side, row, low_ref in ((0, 0, head_ref), (1, last, tail_ref)):
                before = jnp.where(step > 0, acc_ref[side, :, at], 0.0)
                total = before + c_ref[row, step] * value
                acc_ref[side, :, at] = total
                low_ref[:, at] = total.astype(BF)

    def two(i, carry):
        pair(2 * i)
        pair(2 * i + 1)
        return carry

    lax.fori_loop(0, width // (4 * head), two, 0)


def attend_back(coef, q, summary, grad_mix, head):
    rows, width = q.shape
    blocks, kp, _ = summary.shape
    short = rows // blocks
    row = lambda i, *_: (i, 0)
    lead = lambda i, *_: (i, 0, 0)
    return pl.pallas_call(
        functools.partial(attend_back_body, width, head, kp),
        grid_spec=pltpu.PrefetchScalarGridSpec(
            num_scalar_prefetch=1,
            grid=(blocks,),
            in_specs=[
                vspec((short, width), row),
                vspec((1, kp, 2 * width), lead),
                vspec((short, width), row),
            ],
            out_specs=[
                vspec((short, width), row),
                vspec((1, kp, 2 * width), lead),
                vspec((kp, 2 * width), lambda i, *_: (0, 0)),
                vspec((kp, 2 * width), lambda i, *_: (0, 0)),
            ],
            scratch_shapes=[pltpu.VMEM((2, kp, 2 * width), F32)],
        ),
        out_shape=[
            jax.ShapeDtypeStruct((rows, width), BF),
            jax.ShapeDtypeStruct((blocks, kp, 2 * width), F32),
            jax.ShapeDtypeStruct((kp, 2 * width), BF),
            jax.ShapeDtypeStruct((kp, 2 * width), BF),
        ],
        compiler_params=params(),
        cost_estimate=cost(2 * rows * width * 8 * kp, 10e6, rows * kp * 12),
        name="attend_back",
    )(coef, q, summary, grad_mix)


def outer_body(split, l_ref, r_ref, o_ref):
    value = dot_l(l_ref[...], r_ref[...])
    o_ref[...] = value.reshape(o_ref.shape).astype(o_ref.dtype)


def outer_up(first_low, grad_up, size, dtype):
    rows, width = first_low.shape
    chunks = grad_up.shape[1] // width
    groups = width // size
    return pl.pallas_call(
        functools.partial(outer_body, True),
        grid=(chunks,),
        in_specs=[
            vspec((rows, width), lambda i: (0, 0), True),
            vspec((rows, width), lambda i: (0, i)),
        ],
        out_specs=vspec((groups, 1, size, width), lambda i: (0, i, 0, 0)),
        out_shape=jax.ShapeDtypeStruct((groups, chunks, size, width), dtype),
        compiler_params=params(),
        cost_estimate=cost(2 * rows * width * width * chunks, 20e6),
        name="outer_up",
    )(first_low, grad_up)


def outer_rows(left, right, dtype, name):
    rows, width = right.shape[0], min(left.shape[1], right.shape[1])
    tall, wide = left.shape[1] // width, right.shape[1] // width
    moving = lambda n: (lambda i: (0, i)) if n > 1 else (lambda i: (0, 0))
    return pl.pallas_call(
        functools.partial(outer_body, False),
        grid=(tall * wide,),
        in_specs=[
            vspec((rows, width), moving(tall), tall == 1),
            vspec((rows, width), moving(wide), wide == 1),
        ],
        out_specs=vspec((width, width), lambda i: (i, 0)),
        out_shape=jax.ShapeDtypeStruct((tall * wide * width, width), dtype),
        compiler_params=params(),
        cost_estimate=cost(2 * rows * width * width * tall * wide, 20e6),
        name=name,
    )(left, right)


def backward_body(peers, head, chunks, c_ref, q_ref, s_ref, g_ref, *refs):
    sources, outs = refs[:7], refs[7:13]
    grad_outs, scratch = refs[13:17], refs[17:]
    dq_ref, ds_ref, far_refs = outs[0], outs[1], outs[2:]
    held, (low_head, low_tail, g_down, g_up, g_out, g_query) = scratch[:7], scratch[7:13]
    send, recv, local = scratch[13:]
    blocks, kp, wide = s_ref.shape
    width = wide // 2
    short = q_ref.shape[0] // blocks
    pairs = width // (2 * head)
    seq, mine = lax.axis_index("seq"), lax.axis_index("own")
    loads = [pltpu.make_async_copy(sources[k], held[k], local.at[k]) for k in range(7)]
    for load in loads:
        load.start()

    def place(d):
        return (lax.rem(seq + peers + d, peers), mine)

    steps = (1, -1, 2, -2)
    inside = lambda d: seq < peers - d if d > 0 else seq >= -d
    can_send = [inside(d) for d in steps]
    can_get = [inside(-d) for d in steps]
    barrier = pltpu.get_barrier_semaphore()
    for k in range(4):

        @pl.when(can_send[k])
        def _():
            pl.semaphore_signal(barrier, inc=1, device_id=place(steps[k]), device_id_type=MESH_ID)

        @pl.when(jnp.logical_not(can_get[k]))
        def _():
            far_refs[k][...] = jnp.zeros_like(far_refs[k])

    pl.semaphore_wait(barrier, jnp.minimum(seq, 2) + jnp.minimum(peers - 1 - seq, 2))
    low_lane = lax.broadcasted_iota(jnp.int32, (kp, 2 * head), 1) < head

    def columns(j):
        at = pl.multiple_of(j * 2 * head, 2 * head)
        return pl.ds(at, 2 * head), pl.ds(pl.multiple_of(width + at, 2 * head), 2 * head)

    def message(j, k, kind):
        low = (low_tail, low_head)[k % 2]
        cols = columns(j)[kind]
        return pltpu.make_async_remote_copy(
            src_ref=low.at[:, cols],
            dst_ref=far_refs[k].at[:, cols],
            send_sem=send.at[j, k, kind],
            recv_sem=recv.at[j, k, kind],
            device_id=place(steps[k]),
            device_id_type=MESH_ID,
        )

    def pair(j, carry):
        cols, vcols = columns(j)
        head_sums, tail_sums = [0.0, 0.0], [0.0, 0.0]
        for b in range(blocks):
            rows = pl.ds(b * short, short)
            grads, dk, dv = pair_back(
                s_ref[b, :, cols], s_ref[b, :, vcols], q_ref[rows, cols], g_ref[rows, cols], head, low_lane
            )
            dq_ref[rows, cols] = grads
            for kind, at, both in ((0, cols, dk), (1, vcols, dv)):
                value = jnp.where(low_lane, both[:kp], both[kp:])
                ds_ref[b, :, at] = value
                head_sums[kind] = head_sums[kind] + c_ref[0, b] * value
                tail_sums[kind] = tail_sums[kind] + c_ref[blocks - 1, b] * value
        for kind, at in ((0, cols), (1, vcols)):
            low_head[:, at] = head_sums[kind].astype(BF)
            low_tail[:, at] = tail_sums[kind].astype(BF)
        for k in range(4):

            @pl.when(can_send[k])
            def _():
                for kind in range(2):
                    message(j, k, kind).start()

        return carry

    lax.fori_loop(0, pairs, pair, 0)
    first_low, grad_up, hidden, grad_down, mixed, grad_branch, x = held
    stores = []

    def store(src, dst):
        copy = pltpu.make_async_copy(src, dst, local.at[7 + len(stores)])
        copy.start()
        stores.append(copy)

    for load in loads:
        load.wait()

    def down_chunk(i, carry):
        at = pl.ds(pl.multiple_of(i * width, width), width)
        g_down[at, :] = dot_l(hidden[:, at], grad_down[...]).astype(BF)
        return carry

    def up_chunk(i, carry):
        at = pl.ds(pl.multiple_of(i * width, width), width)
        value = dot_l(first_low[...], grad_up[:, at]).astype(BF)
        g_up[:, i] = value.reshape(g_up.shape[0], g_up.shape[2], width)
        return carry

    lax.fori_loop(0, chunks, down_chunk, 0)
    store(g_down, grad_outs[0])
    lax.fori_loop(0, chunks, up_chunk, 0)
    store(g_up, grad_outs[1])
    g_out[...] = dot_l(mixed[...], grad_branch[...]).astype(BF)
    store(g_out, grad_outs[2])
    g_query[...] = dot_l(x[...], dq_ref[...]).astype(BF)
    store(g_query, grad_outs[3])

    def finish(j, carry):
        for k in range(4):

            @pl.when(can_get[k])
            def _():
                for kind in range(2):
                    message(j, k, kind).wait_recv()

            @pl.when(can_send[k])
            def _():
                for kind in range(2):
                    message(j, k, kind).wait_send()

        return carry

    lax.fori_loop(0, pairs, finish, 0)
    for copy in stores:
        copy.wait()


def backward(coef, q, summary, grad_mix, operands, head, peers, size):
    rows, width = q.shape
    blocks, kp, _ = summary.shape
    chunks = operands[1].shape[1] // width
    groups = width // size
    vmem, smem = pl.BlockSpec(memory_space=pltpu.VMEM), pl.BlockSpec(memory_space=pltpu.SMEM)
    far = jax.ShapeDtypeStruct((kp, 2 * width), BF)
    products = [(chunks * width, width), (groups, chunks, size, width), (width, width), (width, width)]
    pairs = width // (2 * head)
    return pl.pallas_call(
        functools.partial(backward_body, peers, head, chunks),
        in_specs=[smem] + [vmem] * 3 + [pl.BlockSpec(memory_space=pl.ANY)] * 7,
        out_specs=[vmem] * 6 + [pl.BlockSpec(memory_space=pl.ANY)] * 4,
        out_shape=[
            jax.ShapeDtypeStruct((rows, width), BF),
            jax.ShapeDtypeStruct((blocks, kp, 2 * width), F32),
        ]
        + [far] * 4
        + [jax.ShapeDtypeStruct(shape, BF) for shape in products],
        scratch_shapes=[pltpu.VMEM(a.shape, BF) for a in operands]
        + [pltpu.VMEM(far.shape, BF)] * 2
        + [pltpu.VMEM(shape, BF) for shape in products]
        + [
            pltpu.SemaphoreType.DMA((pairs, 4, 2)),
            pltpu.SemaphoreType.DMA((pairs, 4, 2)),
            pltpu.SemaphoreType.DMA((11,)),
        ],
        compiler_params=pltpu.CompilerParams(
            collective_id=4, has_side_effects=True, vmem_limit_bytes=VMEM_LIMIT
        ),
        cost_estimate=cost(2 * rows * width * (8 * kp + 10 * width), 60e6, rows * kp * 12),
        name="backward",
    )(coef, q, summary, grad_mix, *operands)


def back_body(
    width, blocks, c_ref, n_ref, e_ref, kv_ref, p_ref, *refs
):
    far_refs = refs[:4]
    dq_ref, w_ref, df_ref, dkv_ref, gp_ref, gi_ref = refs[4:]
    step = pl.program_id(0)
    short, kp = e_ref.shape[1], e_ref.shape[2]
    total = c_ref[step, 0] * p_ref[0]
    for other in range(1, blocks):
        total = total + c_ref[step, other] * p_ref[other]
    for k in range(4):
        total = total + c_ref[step, blocks + k] * far_refs[k][...].astype(F32)
    summary = total.astype(BF)
    dkv = dot(e_ref[0], summary).astype(BF)
    dkv_ref[...] = dkv
    keep = lax.broadcasted_iota(jnp.int32, (short, 1), 0) < n_ref[1, step]
    grad_e = jnp.where(keep, dot_t(kv_ref[...], summary), 0.0)
    column = n_ref[0, step]
    at = pl.multiple_of(jnp.minimum((column // 8) * 8, gp_ref.shape[0] - short - 8), 8)
    moved = pltpu.roll(
        jnp.concatenate([grad_e, jnp.zeros((8, kp), F32)], axis=0), column - at, 0
    )

    @pl.when(step == 0)
    def _():
        gp_ref[...] = jnp.zeros_like(gp_ref)

    gp_ref[pl.ds(at, short + 8), :] += moved
    gi_ref[...] = (
        df_ref[...]
        + dot_t(dq_ref[...], w_ref[pl.ds(0, width), :])
        + dot_t(dkv[:, :width], w_ref[pl.ds(width, width), :])
        + dot_t(dkv[:, width:], w_ref[pl.ds(2 * width, width), :])
    )


def back(coef, places, e_rows, kv, grad_parts, far_parts, dq, w_att, grad_first, positions):
    rows, width = dq.shape
    blocks, short, kp = e_rows.shape
    row = lambda i, *_: (i, 0)
    lead = lambda i, *_: (i, 0, 0)
    fixed = lambda i, *_: (0, 0)
    return pl.pallas_call(
        functools.partial(back_body, width, blocks),
        grid_spec=pltpu.PrefetchScalarGridSpec(
            num_scalar_prefetch=2,
            grid=(blocks,),
            in_specs=[
                vspec((1, short, kp), lead),
                vspec((short, 2 * width), row),
                vspec(grad_parts.shape, lambda i, *_: (0, 0, 0), True),
            ]
            + [vspec((kp, 2 * width), fixed, True)] * 4
            + [
                vspec((short, width), row),
                vspec((3 * width, width), fixed, True),
                vspec((short, width), row),
            ],
            out_specs=[
                vspec((short, 2 * width), row),
                vspec((positions, kp), fixed),
                vspec((short, width), row),
            ],
        ),
        out_shape=[
            jax.ShapeDtypeStruct((rows, 2 * width), BF),
            jax.ShapeDtypeStruct((positions, kp), F32),
            jax.ShapeDtypeStruct((rows, width), F32),
        ],
        compiler_params=params(),
        cost_estimate=cost(2 * rows * width * (3 * width + 4 * kp), 20e6),
        name="back",
    )(coef, places, e_rows, kv, grad_parts, *far_parts, dq, w_att, grad_first)


def reduce_body(depth, half, n_src, extra_keep, *refs):
    sources = refs[:n_src]
    grads, shares_out, rows_out = refs[n_src : n_src + 3]
    (own, got_c, sum_c, got_a, got_b, sum_a, sum_b, got_a2, got_b2, sum_z, got_z) = refs[
        n_src + 3 : n_src + 14
    ]
    keep_a, keep_b, keep_z = refs[n_src + 14 : n_src + 17]
    (e_own, e_got, e_sum, e_got1, e_sum1, e_got2, e_sum2, e_gotz, e_all, e_rows) = refs[
        n_src + 17 : n_src + 27
    ]
    send, recv, local = refs[n_src + 27 :]
    seq, mine = lax.axis_index("seq"), lax.axis_index("own")
    z, y, x, c = seq // 2, seq % 2, mine // 2, mine % 2
    core = (seq, 2 * x + (1 - c))
    along_x = (seq, 2 * (1 - x) + c)
    along_y = (2 * z + (1 - y), mine)
    along_z = [(2 * lax.rem(z + d, depth) + y, mine) for d in range(1, depth)]
    barrier = pltpu.get_barrier_semaphore()
    partners = [core, along_x, along_y] + along_z
    for partner in partners:
        pl.semaphore_signal(barrier, inc=1, device_id=partner, device_id_type=MESH_ID)
    pl.semaphore_wait(barrier, len(partners))

    sent = []

    def push(src, dst, partner):
        at = len(sent)
        copy = pltpu.make_async_remote_copy(
            src_ref=src,
            dst_ref=dst,
            send_sem=send.at[at],
            recv_sem=recv.at[at],
            device_id=partner,
            device_id_type=MESH_ID,
        )
        copy.start()
        sent.append(copy)
        return copy

    up, down, g_query, g_keyval, g_out, extra = sources
    bands = [g_query, g_keyval.at[0], g_keyval.at[1], g_out]
    half_z = depth // 2
    cols = own.shape[-1]
    loads = []

    def load(src, dst):
        copy = pltpu.make_async_copy(src, dst, local.at[len(loads)])
        copy.start()
        loads.append(copy)
        return copy

    e_first = [push(extra.at[:, :, 1 - c], e_got, core)]
    e_load = [load(extra.at[:, :, c], e_own)]
    piece_first, piece_load = [], []

    def piece_core(p):
        at, part = p // 2, pl.ds((p % 2) * cols, cols)
        if at < 2:
            first = [
                push(up.at[:, :, 1 - c, at, :, part], got_c.at[p, pl.ds(0, half_z)], core),
                push(down.at[:, :, 1 - c, at, :, part], got_c.at[p, pl.ds(half_z, half_z)], core),
            ]
            kept = [
                load(up.at[:, :, c, at, :, part], own.at[p, pl.ds(0, half_z)]),
                load(down.at[:, :, c, at, :, part], own.at[p, pl.ds(half_z, half_z)]),
            ]
        else:
            first = [
                push(bands[m].at[:, 1 - c, :, part], got_c.at[p, m], core) for m in range(depth)
            ]
            kept = [load(bands[m].at[:, c, :, part], own.at[p, m]) for m in range(depth)]
        piece_first.append(first)
        piece_load.append(kept)

    state = {}

    def wait_recv(copies):
        for copy in copies:
            copy.wait_recv()

    low, high = pl.ds(0, half), pl.ds(half, half)

    def add(a, b):
        return a.astype(F32) + b.astype(F32)

    def piece_c(p):
        for copy in piece_load[p]:
            copy.wait()
        wait_recv(piece_first[p])

        def body(i, carry):
            zz, w = i // 2, i % 2
            to_x, to_y = 2 * w + 1 - x, 2 * (1 - y) + w
            sum_c[p, 0, zz, w] = add(own[p, zz, to_x, low, :], got_c[p, zz, to_x, low, :]).astype(BF)
            sum_c[p, 1, zz, w] = add(own[p, zz, to_y, high, :], got_c[p, zz, to_y, high, :]).astype(BF)
            return carry

        lax.fori_loop(0, depth * 2, body, 0)
        state["1", p] = [
            push(sum_c.at[p, 0], got_a.at[p], along_x),
            push(sum_c.at[p, 1], got_b.at[p], along_y),
        ]

    def piece_1(p):
        wait_recv(state["1", p])

        def side_a(zz, w):
            at = 2 * w + x
            return add(own[p, zz, at, low, :], got_c[p, zz, at, low, :]) + got_a[p, zz, w].astype(F32)

        def side_b(zz, w):
            at = 2 * y + w
            return add(own[p, zz, at, high, :], got_c[p, zz, at, high, :]) + got_b[p, zz, w].astype(F32)

        def body(zz, carry):
            sum_a[p, zz] = side_a(zz, 1 - y).astype(BF)
            sum_b[p, zz] = side_b(zz, 1 - x).astype(BF)
            keep_a[p, zz] = side_a(zz, y)
            keep_b[p, zz] = side_b(zz, x)
            return carry

        lax.fori_loop(0, depth, body, 0)
        state["2", p] = [
            push(sum_a.at[p], got_a2.at[p], along_y),
            push(sum_b.at[p], got_b2.at[p], along_x),
        ]

    def piece_2(p):
        wait_recv(state["2", p])

        def body(zz, carry):
            total_a = keep_a[p, zz] + got_a2[p, zz].astype(F32)
            total_b = keep_b[p, zz] + got_b2[p, zz].astype(F32)
            sum_z[p, zz, low, :] = total_a.astype(BF)
            sum_z[p, zz, high, :] = total_b.astype(BF)
            return carry

        lax.fori_loop(0, depth, body, 0)
        keep_z[p, low, :] = keep_a[p, z] + got_a2[p, z].astype(F32)
        keep_z[p, high, :] = keep_b[p, z] + got_b2[p, z].astype(F32)
        state["z", p] = [
            push(sum_z.at[p, lax.rem(z + d, depth)], got_z.at[p, d - 1], along_z[d - 1])
            for d in range(1, depth)
        ]

    def piece_z(p):
        wait_recv(state["z", p])
        total = keep_z[p]
        for d in range(depth - 1):
            total = total + got_z[p, d].astype(F32)
        grads[(p // 2 + 1) % 3, :, pl.ds((p % 2) * cols, cols)] = total

    def extra_c():
        e_load[0].wait()
        wait_recv(e_first)

        def body(i, carry):
            zz, yx = i // 4, i % 4
            e_sum[zz, yx // 2, yx % 2] = e_own[zz, yx] + e_got[zz, yx]
            return carry

        lax.fori_loop(0, depth * 4, body, 0)
        state["ez"] = [
            push(e_sum.at[lax.rem(z + d, depth)], e_gotz.at[d - 1], along_z[d - 1])
            for d in range(1, depth)
        ]

    def extra_1():
        wait_recv(state["ez"])

        def body(i, carry):
            yy, xx = i // 2, i % 2
            total = e_sum[z, yy, xx]
            for d in range(depth - 1):
                total = total + e_gotz[d, yy, xx]
            e_sum1[yy, xx] = total
            return carry

        lax.fori_loop(0, 4, body, 0)
        state["e1"] = [push(e_sum1.at[:, 1 - x], e_got1, along_x)]

    def extra_2():
        wait_recv(state["e1"])

        def body(yy, carry):
            e_sum2[yy] = e_sum1[yy, x] + e_got1[yy]
            return carry

        lax.fori_loop(0, 2, body, 0)
        state["e2"] = [push(e_sum2.at[1 - y], e_got2, along_y)]

    def extra_z():
        wait_recv(state["e2"])
        e_all[z, y] = e_sum2[y] + e_got2[...]
        state["gz"] = [push(e_all.at[z, y], e_all.at[z, y], there) for there in along_z]

    def extra_gather_y():
        wait_recv(state["gz"])
        state["gy"] = [push(e_all.at[:, y], e_all.at[:, y], along_y)]

    def extra_gather_x():
        wait_recv(state["gy"])
        e_rows[x, c] = e_all[:, :, pl.ds(extra_keep, e_rows.shape[4]), :]
        state["gx"] = [push(e_rows.at[x, c], e_rows.at[x, c], along_x)]

    def extra_gather_c():
        wait_recv(state["gx"])
        state["gc"] = [push(e_rows.at[:, c], e_rows.at[:, c], core)]

    stages = [piece_c, piece_1, piece_2, piece_z]
    small = {0: extra_c, 3: extra_1, 4: extra_2, 5: extra_z, 6: extra_gather_y}
    small |= {7: extra_gather_x, 8: extra_gather_c}
    piece_core(0)
    piece_core(1)
    for turn in range(9):
        for stage in range(4):
            if 0 <= turn - stage < 6:
                stages[stage](turn - stage)
            if stage == 0 and turn + 2 < 6:
                piece_core(turn + 2)
        if turn in small:
            small[turn]()
    shares_out[...] = e_all[:, :, pl.ds(0, extra_keep), :]
    wait_recv(state["gc"])
    rows_out[...] = e_rows[...]
    for copy in sent:
        copy.wait_send()


def reduce_all(g_query, g_keyval, g_out, g_up, g_down, extra, peers):
    depth = peers // 2
    size, width = g_up.shape[2], g_up.shape[3]
    half = size // 2
    e_rows_all, kp = extra.shape[1], extra.shape[2]
    keep = e_rows_all - 8
    sources = (
        [
            g_up.reshape(depth // 2, 4, 2, 2, size, width),
            g_down.reshape(depth // 2, 4, 2, 2, size, width),
        ]
        + [
            g_query.reshape(4, 2, size, width),
            g_keyval.reshape(2, 4, 2, size, width),
            g_out.reshape(4, 2, size, width),
        ]
        + [extra.reshape(depth, 4, 2, e_rows_all, kp)]
    )
    n_src = len(sources)
    cols = width // 2
    messages = 1 + 8 + 2 * depth + 6 * (4 + depth - 1) + 2 + 2 * (depth - 1) + 3
    loads = 1 + 8 + 2 * depth
    any_spec = pl.BlockSpec(memory_space=pl.ANY)
    vmem = pl.BlockSpec(memory_space=pltpu.VMEM)
    scratch = [
        pltpu.VMEM((6, depth, 4, size, cols), BF),
        pltpu.VMEM((6, depth, 4, size, cols), BF),
        pltpu.VMEM((6, 2, depth, 2, half, cols), BF),
        pltpu.VMEM((6, depth, 2, half, cols), BF),
        pltpu.VMEM((6, depth, 2, half, cols), BF),
        pltpu.VMEM((6, depth, half, cols), BF),
        pltpu.VMEM((6, depth, half, cols), BF),
        pltpu.VMEM((6, depth, half, cols), BF),
        pltpu.VMEM((6, depth, half, cols), BF),
        pltpu.VMEM((6, depth, size, cols), BF),
        pltpu.VMEM((6, depth - 1, size, cols), BF),
        pltpu.VMEM((6, depth, half, cols), F32),
        pltpu.VMEM((6, depth, half, cols), F32),
        pltpu.VMEM((6, size, cols), F32),
        pltpu.VMEM((depth, 4, e_rows_all, kp), F32),
        pltpu.VMEM((depth, 4, e_rows_all, kp), F32),
        pltpu.VMEM((depth, 2, 2, e_rows_all, kp), F32),
        pltpu.VMEM((2, e_rows_all, kp), F32),
        pltpu.VMEM((2, 2, e_rows_all, kp), F32),
        pltpu.VMEM((e_rows_all, kp), F32),
        pltpu.VMEM((2, e_rows_all, kp), F32),
        pltpu.VMEM((depth - 1, 2, 2, e_rows_all, kp), F32),
        pltpu.VMEM((depth, 2, e_rows_all, kp), F32),
        pltpu.VMEM((2, 2, depth, 2, 8, kp), F32),
        pltpu.SemaphoreType.DMA((messages,)),
        pltpu.SemaphoreType.DMA((messages,)),
        pltpu.SemaphoreType.DMA((loads,)),
    ]
    return pl.pallas_call(
        functools.partial(reduce_body, depth, half, n_src, keep),
        in_specs=[any_spec] * n_src,
        out_specs=[vmem] * 3,
        out_shape=[
            jax.ShapeDtypeStruct((3, size, width), F32),
            jax.ShapeDtypeStruct((depth, 2, keep, kp), F32),
            jax.ShapeDtypeStruct((2, 2, depth, 2, 8, kp), F32),
        ],
        scratch_shapes=scratch,
        compiler_params=pltpu.CompilerParams(
            collective_id=1, has_side_effects=True, vmem_limit_bytes=VMEM_LIMIT
        ),
        name="reduce_all",
    )(*sources)


def gather_body(depth, half, band_ref, proj_ref, out_ref, pout_ref, send, recv, local):
    seq, mine = lax.axis_index("seq"), lax.axis_index("own")
    z, y, x, c = seq // 2, seq % 2, mine // 2, mine % 2
    core = (seq, 2 * x + (1 - c))
    along_x = (seq, 2 * (1 - x) + c)
    along_y = (2 * z + (1 - y), mine)
    order = [1, 3, 2]
    along_z = [(2 * lax.rem(z + d, depth) + y, mine) for d in order]
    barrier = pltpu.get_barrier_semaphore()
    partners = [core, along_x, along_y] + along_z
    for partner in partners:
        pl.semaphore_signal(barrier, inc=1, device_id=partner, device_id_type=MESH_ID)
    pl.semaphore_wait(barrier, len(partners))

    sent = []

    def push(src, dst, partner):
        at = len(sent)
        copy = pltpu.make_async_remote_copy(
            src_ref=src,
            dst_ref=dst,
            send_sem=send.at[at],
            recv_sem=recv.at[at],
            device_id=partner,
            device_id_type=MESH_ID,
        )
        copy.start()
        sent.append(copy)
        return copy

    keep = pltpu.make_async_copy(band_ref, out_ref.at[z, y, x, c], local.at[0])
    keep.start()
    keep_p = pltpu.make_async_copy(proj_ref, pout_ref.at[x, c], local.at[1])
    keep_p.start()
    mine_at = out_ref.at[z, y, x, c]
    from_z = [push(band_ref, mine_at, there) for there in along_z]
    from_x = [push(band_ref, mine_at, along_x)]
    from_y = [push(band_ref, mine_at, along_y)]
    proj_x = push(proj_ref, pout_ref.at[x, c], along_x)
    last = [push(band_ref, mine_at, core), push(proj_ref, pout_ref.at[x, c], core)]
    planes = [z]
    for k in range(depth - 1):
        from_z[k].wait_recv()
        plane = lax.rem(z + depth - order[k], depth)
        planes.append(plane)
        slab = out_ref.at[plane, y, x, c]
        from_x.append(push(slab, slab, along_x))
        from_y.append(push(slab, slab, along_y))
        last.append(push(slab, slab, core))
    low, high = pl.ds(0, half), pl.ds(half, half)
    cross = []
    for k in range(depth):
        plane = planes[k]
        from_x[k].wait_recv()
        slab = out_ref.at[plane, y, 1 - x, c]
        part = out_ref.at[plane, y, 1 - x, c, low, :]
        cross_y = push(part, part, along_y)
        last.append(push(slab, slab, core))
        from_y[k].wait_recv()
        slab = out_ref.at[plane, 1 - y, x, c]
        part = out_ref.at[plane, 1 - y, x, c, high, :]
        cross.append((cross_y, push(part, part, along_x)))
        last.append(push(slab, slab, core))
        if k == 0:
            proj_x.wait_recv()
            slab = pout_ref.at[1 - x, c]
            last.append(push(slab, slab, core))
    for k in range(depth):
        for copy in cross[k]:
            copy.wait_recv()
        slab = out_ref.at[planes[k], 1 - y, 1 - x, c]
        last.append(push(slab, slab, core))
    for copy in last:
        copy.wait_recv()
    keep.wait()
    keep_p.wait()
    for copy in sent:
        copy.wait_send()


def gather_bands(band, proj, peers):
    depth = peers // 2
    size, width = band.shape
    messages = (depth - 1) + 3 + 2 + 3 * (depth - 1) + 4 * depth + 1 + depth
    vmem = pl.BlockSpec(memory_space=pltpu.VMEM)
    return pl.pallas_call(
        functools.partial(gather_body, depth, size // 2),
        in_specs=[vmem] * 2,
        out_specs=[vmem] * 2,
        out_shape=[
            jax.ShapeDtypeStruct((depth, 2, 2, 2, size, width), BF),
            jax.ShapeDtypeStruct((2, 2) + proj.shape, BF),
        ],
        scratch_shapes=[
            pltpu.SemaphoreType.DMA((messages,)),
            pltpu.SemaphoreType.DMA((messages,)),
            pltpu.SemaphoreType.DMA((2,)),
        ],
        compiler_params=pltpu.CompilerParams(
            collective_id=2, has_side_effects=True, vmem_limit_bytes=VMEM_LIMIT
        ),
        cost_estimate=cost(1e9, 90e6),
        name="gather_bands",
    )(band, proj)


def shampoo(grad, left, right, root_left, root_right, weight):
    new_left = decay * left + (1.0 - decay) * jnp.einsum(
        "tij,tkj->tik", grad, grad, precision=highest
    )
    new_right = decay * right + (1.0 - decay) * jnp.einsum(
        "tji,tjk->tik", grad, grad, precision=highest
    )
    inner = jnp.einsum("tij,tjk->tik", grad, root_right, precision=highest)
    step = jnp.einsum("tij,tjk->tik", root_left, inner, precision=highest)
    return (new_left, new_right, weight - rate_matrix * step)


def exact(a, b, left, right):
    return lax.dot_general(
        a, b, (((left,), (right,)), ((), ())), precision=highest, preferred_element_type=F32
    )


def step_body(bands, *refs):
    band_ref, tiles, proj_ref, blocks = refs[0], refs[1:6], refs[6], refs[7:12]
    rows_ref, norm_ref, second_ref = refs[12:15]
    owned_ref, new_tiles, new_blocks = refs[15], refs[16:19], refs[19:22]
    grad_ref, second_new_ref, norm_new_ref, rms_ref = refs[22:]
    at = pl.program_id(0)
    size, kp = tiles[0].shape[1], proj_ref.shape[-1]

    def update(grad, state, new, t):
        left, right, root_left, root_right, weight = (ref[t] for ref in state)
        new[0][t] = decay * left + (1.0 - decay) * exact(grad, grad, 1, 1)
        new[1][t] = decay * right + (1.0 - decay) * exact(grad, grad, 0, 0)
        new[2][t] = weight - rate_matrix * exact(root_left, exact(grad, root_right, 1, 0), 1, 0)

    @pl.when(at < bands)
    def _():
        def four(i, carry):
            part = band_ref[0, :, pl.ds(pl.multiple_of(i * 4 * size, 128), 4 * size)]
            for t in range(4):
                grad = part[:, t * size : (t + 1) * size]
                owned_ref[4 * i + t] = grad
                update(grad, tiles, new_tiles, 4 * i + t)
            return carry

        lax.fori_loop(0, tiles[0].shape[0] // 4, four, 0)

    @pl.when(at >= bands)
    def _():
        update(proj_ref[0], blocks, new_blocks, 0)

    @pl.when(at == bands)
    def _():
        depth = rows_ref.shape[2]

        def row(r):
            return rows_ref[r // 2 % 2, r % 2, r // 8 % depth, r // 4 % 2, pl.ds(0, 1), :]

        per = norm_ref.shape[1] // kp
        for i in range(4):
            grad = jnp.concatenate([row(per * i + j) for j in range(per)], axis=1)
            grad_ref[pl.ds(i, 1), :] = grad
            second = decay * second_ref[pl.ds(i, 1), :] + (1.0 - decay) * grad * grad
            second_new_ref[pl.ds(i, 1), :] = second
            norm_new_ref[pl.ds(i, 1), :] = norm_ref[pl.ds(i, 1), :] - rate_norm * grad * lax.rsqrt(second)
        count = jnp.sum(sum(row(6 * per + j) for j in range(per)), axis=1, keepdims=True)
        for i in range(2):
            square = row(4 * per + per * i)
            for j in range(1, per):
                square = square + row(4 * per + per * i + j)
            total = jnp.sum(square, axis=1, keepdims=True)
            ratio = jnp.sqrt(total / (count * norm_ref.shape[1]))
            rms_ref[pl.ds(i, 1), :] = jnp.broadcast_to(ratio, (1, rms_ref.shape[1]))


def step_all(bands, tiles, proj_grad, blocks, rows, norm_params, norm_stat):
    count, size, width = bands.shape
    each, kp = width // size, proj_grad.shape[-1]
    n_blocks = proj_grad.shape[0]
    tile = lambda: vspec((each, size, size), lambda i: (jnp.minimum(i, count - 1), 0, 0))
    block = lambda: vspec((1, kp, kp), lambda i: (jnp.maximum(i - count, 0), 0, 0))
    whole = lambda a: vspec(a.shape, lambda i: (0,) * len(a.shape))
    like = lambda a: jax.ShapeDtypeStruct(a.shape, F32)
    rms = jax.ShapeDtypeStruct((2, 128), F32)
    return pl.pallas_call(
        functools.partial(step_body, count),
        grid=(count + n_blocks,),
        in_specs=[vspec((1, size, width), lambda i: (jnp.minimum(i, count - 1), 0, 0))]
        + [tile() for _ in range(5)]
        + [block() for _ in range(6)]
        + [whole(rows), whole(norm_params), whole(norm_stat)],
        out_specs=[tile() for _ in range(4)]
        + [block() for _ in range(3)]
        + [whole(norm_params)] * 3
        + [whole(rms)],
        out_shape=[like(tiles[0])] * 4 + [like(proj_grad)] * 3 + [like(norm_params)] * 3 + [rms],
        compiler_params=params(),
        cost_estimate=cost(1e9, 20e6),
        name="step_all",
    )(bands, *tiles, proj_grad, *blocks, rows, norm_params, norm_stat)


def to_matrix(tiles, rows, cols):
    size = tiles.shape[-1]
    return (
        tiles.reshape(rows // size, cols // size, size, size)
        .transpose(0, 2, 1, 3)
        .reshape(rows, cols)
    )


def to_bands(tiles, cols):
    count, size, _ = tiles.shape
    return to_matrix(tiles, count * size * size // cols, cols)


def from_bands(bands, size):
    rows, cols = bands.shape
    return (
        bands.reshape(rows // size, size, cols // size, size)
        .transpose(0, 2, 1, 3)
        .reshape(-1, size, size)
    )


def bands_body(w_ref, p_ref, att_ref, ffn_ref, proj_ref):
    count, size, _ = w_ref.shape
    wide = att_ref.shape[1] // size
    near = att_ref.shape[0] // size
    for k in range(count):
        at, cols = k // wide, pl.ds(k % wide * size, size)
        tile = w_ref[k].astype(BF)
        if at < near:
            att_ref[pl.ds(at * size, size), cols] = tile
        else:
            ffn_ref[pl.ds((at - near) * size, size), cols] = tile
    proj_ref[...] = p_ref[...].astype(BF)


def make_bands(weights, projection, att_dev, width):
    per_dev, size, _ = weights.shape
    near = att_dev * size // width * size
    return pl.pallas_call(
        bands_body,
        out_shape=[
            jax.ShapeDtypeStruct((near, width), BF),
            jax.ShapeDtypeStruct((per_dev * size // width * size - near, width), BF),
            jax.ShapeDtypeStruct(projection.shape, BF),
        ],
        compiler_params=pltpu.CompilerParams(vmem_limit_bytes=VMEM_LIMIT),
        name="make_bands",
    )(weights, projection)


def gather_weights(weights, projection, att_dev, width, both, fused, peers):
    size = weights.shape[-1]
    low = weights.astype(BF)
    groups, chunks = width // size, FF // width
    if banded(weights.shape[0], att_dev, width, size):
        band, far, proj_low = make_bands(weights, projection, att_dev, width)
        ffn = lax.all_gather(far, both, axis=0, tiled=True)
        if fused:
            att, proj = gather_bands(band, proj_low, peers)
            att, proj = att.reshape(-1, width), proj.reshape(-1, projection.shape[1])
        else:
            att = lax.all_gather(band, both, axis=0, tiled=True)
            proj = lax.all_gather(proj_low, "own", axis=0, tiled=True)
        return att, ffn.reshape(2 * groups, chunks, size, width), proj
    per_dev = weights.shape[0]
    proj = lax.all_gather(projection.astype(BF), "own", axis=0, tiled=True)
    grid = lax.all_gather(low, both, axis=0, tiled=True).reshape(-1, per_dev, size, size)
    att = to_bands(grid[:, :att_dev].reshape(-1, size, size), width)
    tiles = grid[:, att_dev:].reshape(-1, size, size)
    half = tiles.shape[0] // 2
    w_up = to_matrix(tiles[:half], width, FF).reshape(groups, size, chunks, width)
    w_down = to_matrix(tiles[half:], FF, width).reshape(groups, chunks, size, width)
    return att, jnp.concatenate([w_up.transpose(0, 2, 1, 3), w_down], axis=0), proj


def banded(per_dev, att_dev, width, size):
    wide = width // size
    return att_dev % wide == 0 and (per_dev - att_dev) % wide == 0


def scatter_weight_grads(g_att, g_up, g_down, per_dev, att_dev, both):
    size, width = g_up.shape[2], g_up.shape[3]
    if banded(per_dev, att_dev, width, size):
        ffn = jnp.concatenate([g_up.reshape(-1, width), g_down], axis=0)
        ffn = lax.psum_scatter(ffn, both, scatter_dimension=0, tiled=True)
        att = lax.psum_scatter(g_att, both, scatter_dimension=0, tiled=True)
        return jnp.concatenate([from_bands(att, size), from_bands(ffn, size)], axis=0)
    up = g_up.transpose(0, 2, 1, 3).reshape(width, -1)
    att = from_bands(g_att, size)
    ffn = jnp.concatenate([from_bands(up, size), from_bands(g_down, size)], axis=0)
    stacked = jnp.concatenate(
        [
            att.reshape(-1, att_dev, size, size),
            ffn.reshape(-1, per_dev - att_dev, size, size),
        ],
        axis=1,
    ).reshape(-1, size, size)
    return lax.psum_scatter(stacked, both, scatter_dimension=0, tiled=True)


def per_device(
    tokens,
    cotangent,
    lengths,
    offsets,
    valid_count,
    weights,
    stat_left,
    stat_right,
    root_left,
    root_right,
    projection,
    projection_left,
    projection_right,
    projection_root_left,
    projection_root_right,
    norm_params,
    norm_stat,
):
    both = ("seq", "own")
    size = weights.shape[-1]
    width = tokens.shape[-1]
    rows_here = tokens.shape[1]
    head = width // HEADS
    kp = projection.shape[1]
    blocks = rows_here // SHORT
    peers = lax.axis_size("seq")
    devices = peers * lax.axis_size("own")
    per_dev = weights.shape[0]
    att_dev = 4 * (width // size) ** 2 // devices
    x = tokens[0]
    swap = [(i, i ^ 1) for i in range(peers)]
    peer_x = lax.ppermute(x, "seq", swap)
    own_size = lax.axis_size("own")
    fused = own_size == 4 and peers == 8 and banded(per_dev, att_dev, width, size)
    w_att, w_ffn, proj_all = gather_weights(
        weights, projection, att_dev, width, both, fused, peers
    )

    places, table, coef_back = tables(lengths, offsets, valid_count, blocks, rows_here)

    def proj_rows(at):
        col, n = places[0, at : at + blocks], places[1, at : at + blocks]
        rows = jnp.stack(
            [lax.dynamic_slice_in_dim(proj_all, col[b], SHORT, 0) for b in range(blocks)]
        )
        keep = lax.broadcasted_iota(jnp.int32, (blocks, SHORT, 1), 1) < n[:, None, None]
        return jnp.where(keep, rows, jnp.zeros((), BF))

    e_own = proj_rows(0)
    e_peer = proj_rows(blocks)
    n_own = places[1, :blocks]

    if fused:
        query, keyval, summary, mixed, first_sum, row_sums = forward(
            table, places, x, peer_x, w_att, e_own, e_peer, head, peers
        )
    else:
        query, keyval, part_own = project(x, w_att, e_own.transpose(0, 2, 1), True)
        (part_peer,) = project(peer_x, w_att, e_peer.transpose(0, 2, 1), False)

        def unit_sum(flag):
            total = flag[0] * part_own[0]
            for b in range(1, blocks):
                total = total + flag[b] * part_own[b]
            for b in range(blocks):
                total = total + flag[blocks + b] * part_peer[b]
            return total

        head_sum, tail_sum = unit_sum(table[0]), unit_sum(table[1])
        from_left = lax.ppermute(tail_sum, "seq", [(i, i + 2) for i in range(peers - 2)])
        from_right = lax.ppermute(head_sum, "seq", [(i + 2, i) for i in range(peers - 2)])
        summary = jnp.stack(
            [
                (
                    table[2, b] * head_sum
                    + table[3, b] * from_left
                    + table[4, b] * tail_sum
                    + table[5, b] * from_right
                    + table[6, b] * part_own[b]
                ).astype(BF)
                for b in range(blocks)
            ]
        )
        mixed, first_sum, row_sums = attend(n_own, query, summary, w_att, x, head)
    (
        result,
        hidden,
        grad_up,
        grad_down,
        first_low,
        grad_first,
        grad_branch,
        grad_mix,
        norm_terms,
    ) = feed(first_sum, w_ffn, w_att, cotangent[0], norm_params, 256)
    gtype = BF if fused else F32
    if fused:
        operands = [first_low, grad_up, hidden, grad_down, mixed, grad_branch, x]
        grad_query, grad_parts, *far_parts, g_down, g_up, g_out, g_query = backward(
            coef_back, query, summary, grad_mix, operands, head, peers, size
        )
    else:
        grad_query, grad_parts, low_head, low_tail = attend_back(
            coef_back, query, summary, grad_mix, head
        )
        far_parts = []
        for far in (1, 2):
            onward = [(i, i + far) for i in range(peers - far)]
            far_parts.append(lax.ppermute(low_tail, "seq", onward))
            far_parts.append(lax.ppermute(low_head, "seq", [(j, i) for i, j in onward]))
        g_up = outer_up(first_low, grad_up, size, gtype)
        g_down = outer_rows(hidden, grad_down, gtype, "outer_down")
        g_out = outer_rows(mixed, grad_branch, gtype, "outer_out")
        g_query = outer_rows(x, grad_query, gtype, "outer_query")
    grad_keyval, grad_proj, grad_input = back(
        coef_back,
        places,
        e_own,
        keyval,
        grad_parts,
        far_parts,
        grad_query,
        w_att,
        grad_first,
        proj_all.shape[0],
    )
    g_keyval = outer_rows(x, grad_keyval, gtype, "outer_keyval")
    part_rows = projection.shape[0]
    if not fused:
        valid_here = jnp.sum(n_own).astype(F32)
        here = lax.broadcasted_iota(jnp.int32, (1, width), 1) == 0
        row_sums = jnp.concatenate([row_sums, jnp.where(here, valid_here, 0.0)], axis=0)
    extra = jnp.concatenate([norm_terms.reshape(-1, kp), row_sums.reshape(-1, kp)], axis=0)
    n_norm = 4 * width // kp
    n_row = 2 * width // kp
    if fused:
        extra = jnp.pad(extra, ((0, devices - extra.shape[0]), (0, 0)))[:, None, :]
        extra = jnp.pad(extra, ((0, 0), (0, 7), (0, 0)))
        shares = grad_proj.reshape(own_size, peers, part_rows // peers, kp).swapaxes(0, 1)
        shares = shares.reshape(devices, part_rows // peers, kp)
        banded_grads, proj_parts, rows = reduce_all(
            g_query, g_keyval, g_out, g_up, g_down, jnp.concatenate([shares, extra], axis=1), peers
        )
        (
            owned,
            left_new,
            right_new,
            weights_new,
            proj_left_new,
            proj_right_new,
            proj_blocks,
            norm_grad,
            stat_new,
            norm_new,
            rms,
        ) = step_all(
            banded_grads,
            [stat_left, stat_right, root_left, root_right, weights],
            proj_parts.reshape(-1, kp, kp),
            [
                projection_left,
                projection_right,
                projection_root_left,
                projection_root_right,
                projection.reshape(-1, kp, kp),
            ],
            rows,
            norm_params,
            norm_stat,
        )
        proj_grad = proj_parts.reshape(part_rows, kp)
        residual_rms = rms[:, 0]
    else:
        owned = scatter_weight_grads(
            jnp.concatenate([g_query, g_keyval, g_out], axis=0), g_up, g_down, per_dev, att_dev, both
        )
        packed = jnp.concatenate([grad_proj, extra], axis=0)
        packed = lax.psum(jnp.pad(packed, ((0, -packed.shape[0] % 16), (0, 0))), both)
        proj_grad = lax.dynamic_slice_in_dim(
            packed, lax.axis_index("own") * part_rows, part_rows, 0
        )
        totals = packed[grad_proj.shape[0] :]
        norm_grad = totals[:n_norm].reshape(4, width)
        row_total = totals[n_norm : n_norm + n_row].reshape(2, width).sum(axis=1)
        valid_total = totals[n_norm + n_row : n_norm + n_row + width // kp].sum()
        residual_rms = jnp.sqrt(row_total / (valid_total * width))
        left_new, right_new, weights_new = shampoo(
            owned, stat_left, stat_right, root_left, root_right, weights
        )
        proj_left_new, proj_right_new, proj_blocks = shampoo(
            proj_grad.reshape(-1, kp, kp),
            projection_left,
            projection_right,
            projection_root_left,
            projection_root_right,
            projection.reshape(-1, kp, kp),
        )
        stat_new = decay * norm_stat + (1.0 - decay) * norm_grad * norm_grad
        norm_new = norm_params - rate_norm * norm_grad * lax.rsqrt(stat_new)
    return (
        result[None],
        grad_input[None],
        owned,
        left_new,
        right_new,
        weights_new,
        proj_grad,
        proj_left_new,
        proj_right_new,
        proj_blocks.reshape(part_rows, kp),
        norm_grad,
        stat_new,
        norm_new,
        residual_rms,
    )


def solution(mesh):
    pack = P("own", "seq", None)
    table = P("own", None)
    tile = P(("seq", "own"), None, None)
    proj = P("own", None, None)
    return jax.shard_map(
        per_device,
        mesh=mesh,
        in_specs=(pack, pack, table, table, table)
        + (tile,) * 5
        + (table, proj, proj, proj, proj, P(), P()),
        out_specs=(pack, pack) + (tile,) * 4 + (table, proj, proj, table, P(), P(), P(), P()),
        check_vma=False,
    )
```

```python
import functools
import math

import jax
import jax.numpy as jnp
from jax import lax
from jax.experimental import pallas as pl
from jax.experimental.pallas import tpu as pltpu
from jax.sharding import PartitionSpec as P

HEADS = 12
FF = 3072
SHORT = 512
BF = jnp.bfloat16
F32 = jnp.float32

eps_norm = 1e-05
decay = 0.5
rate_matrix = 0.2
rate_norm = 0.2
highest = lax.Precision.HIGHEST
VMEM_LIMIT = 60 * 1024 * 1024
MESH_ID = pl.DeviceIdType.MESH


def dot(a, b):
    return lax.dot_general(a, b, (((1,), (0,)), ((), ())), preferred_element_type=F32)


def dot_t(a, b):
    return lax.dot_general(a, b, (((1,), (1,)), ((), ())), preferred_element_type=F32)


def dot_l(a, b):
    return lax.dot_general(a, b, (((0,), (0,)), ((), ())), preferred_element_type=F32)


def vspec(shape, index_map, once=False):
    if once:
        return pl.BlockSpec(shape, index_map, pipeline_mode=pl.Buffered(1))
    return pl.BlockSpec(shape, index_map)


def params():
    return pltpu.CompilerParams(
        dimension_semantics=("arbitrary",), vmem_limit_bytes=VMEM_LIMIT
    )


def cost(flops, nbytes, trans=0):
    return pl.CostEstimate(flops=int(flops), bytes_accessed=int(nbytes), transcendentals=int(trans))


def tables_body(blocks, rows_here, l_ref, o_ref, v_ref, i_ref, f_ref, b_ref):
    seq = lax.axis_index("seq")
    side = seq % 2
    row_start = seq * rows_here
    row_end = row_start + rows_here
    unit_start = (seq - side) * rows_here
    peer_start = (seq + 1 - 2 * side) * rows_here
    flag = lambda cond: jnp.where(cond, 1.0, 0.0).astype(F32)

    def locate(row):
        def body(i, carry):
            at, start, end, off, count = carry
            stop = at + l_ref[0, i]
            inside = jnp.logical_and(row >= at, row < stop)
            pick = lambda new, old: jnp.where(inside, new, old)
            return (
                stop,
                pick(at, start),
                pick(stop, end),
                pick(o_ref[0, i], off),
                pick(v_ref[0, i], count),
            )

        zero = jnp.int32(0)
        return lax.fori_loop(0, l_ref.shape[1], body, (zero,) * 5)[1:]

    starts, ends = [], []
    for k in range(2 * blocks):
        row = row_start + SHORT * k if k < blocks else peer_start + SHORT * (k - blocks)
        start, end, off, count = locate(row)
        starts.append(start)
        ends.append(end)
        i_ref[0, k] = off + row - start
        i_ref[1, k] = jnp.clip(count - (row - start), 0, SHORT)
    first = jnp.where(side == 0, starts[0], starts[blocks])
    last = jnp.where(side == 0, starts[-1], starts[blocks - 1])
    last_end = jnp.where(side == 0, ends[-1], ends[blocks - 1])
    head_cross = flag(first < unit_start)
    tail_cross = flag(last_end > unit_start + 2 * rows_here)
    for k in range(2 * blocks):
        is_head, is_tail = flag(starts[k] == first), flag(starts[k] == last)
        pick_tail = (1.0 - is_head) * is_tail
        f_ref[0, k] = is_head
        f_ref[1, k] = is_tail
        f_ref[2, k] = is_head
        f_ref[3, k] = is_head * head_cross
        f_ref[4, k] = pick_tail
        f_ref[5, k] = pick_tail * tail_cross
        f_ref[6, k] = (1.0 - is_head) * (1.0 - is_tail)
    own_last, own_end = starts[blocks - 1], ends[blocks - 1]
    for k in range(blocks):
        at_head, at_tail = flag(starts[k] == starts[0]), flag(starts[k] == own_last)
        for other in range(blocks):
            b_ref[k, other] = flag(starts[k] == starts[other])
        for far in range(2):
            reach = far * rows_here
            b_ref[k, blocks + 2 * far] = at_head * flag(starts[0] < row_start - reach)
            b_ref[k, blocks + 2 * far + 1] = at_tail * flag(own_end > row_end + reach)


def tables(lengths, offsets, valid_count, blocks, rows_here):
    smem = pl.BlockSpec(memory_space=pltpu.SMEM)
    return pl.pallas_call(
        functools.partial(tables_body, blocks, rows_here),
        in_specs=[smem] * 3,
        out_specs=[smem] * 3,
        out_shape=[
            jax.ShapeDtypeStruct((2, 2 * blocks), jnp.int32),
            jax.ShapeDtypeStruct((7, 2 * blocks), F32),
            jax.ShapeDtypeStruct((blocks, blocks + 4), F32),
        ],
        name="tables",
    )(lengths, offsets, valid_count)


def pick_body(places_ref, proj_ref, own_ref, peer_ref):
    blocks, short, kp = own_ref.shape
    span = short + 16
    keep = lax.broadcasted_iota(jnp.int32, (short, 1), 0)
    for first, out in ((0, own_ref), (blocks, peer_ref)):

        def block(b, carry):
            column = places_ref[0, first + b]
            at = jnp.clip((column // 16) * 16, 0, proj_ref.shape[0] - span)
            rows = proj_ref[pl.ds(pl.multiple_of(at, 16), span), :].astype(F32)
            rows = pltpu.roll(rows, lax.rem(span + at - column, span), 0)[:short]
            out[b] = jnp.where(keep < places_ref[1, first + b], rows, 0.0).astype(BF)
            return carry

        lax.fori_loop(0, blocks, block, 0)


def pick_rows(places, proj_all, blocks):
    vmem, smem = pl.BlockSpec(memory_space=pltpu.VMEM), pl.BlockSpec(memory_space=pltpu.SMEM)
    shape = jax.ShapeDtypeStruct((blocks, SHORT, proj_all.shape[1]), BF)
    return pl.pallas_call(
        pick_body,
        in_specs=[smem, vmem],
        out_specs=[vmem] * 2,
        out_shape=[shape] * 2,
        compiler_params=pltpu.CompilerParams(vmem_limit_bytes=VMEM_LIMIT),
        name="pick_rows",
    )(places, proj_all)


def project_body(width, with_query, x_ref, w_ref, e_ref, *outs):
    x = x_ref[...]
    if with_query:
        q_ref, kv_ref, p_ref = outs
        q_ref[...] = dot(x, w_ref[pl.ds(0, width), :]).astype(BF)
    else:
        (p_ref,) = outs
    e = e_ref[0]
    for part in range(2):
        kv = dot(x, w_ref[pl.ds((1 + part) * width, width), :]).astype(BF)
        if with_query:
            kv_ref[:, pl.ds(part * width, width)] = kv
        p_ref[0, :, pl.ds(part * width, width)] = dot(e, kv)


def project(x, w_att, e_t, with_query):
    rows, width = x.shape
    blocks, kp, short = e_t.shape
    out_shape = [jax.ShapeDtypeStruct((blocks, kp, 2 * width), F32)]
    out_specs = [vspec((1, kp, 2 * width), lambda i: (i, 0, 0))]
    if with_query:
        out_shape = [
            jax.ShapeDtypeStruct((rows, width), BF),
            jax.ShapeDtypeStruct((rows, 2 * width), BF),
        ] + out_shape
        out_specs = [
            vspec((short, width), lambda i: (i, 0)),
            vspec((short, 2 * width), lambda i: (i, 0)),
        ] + out_specs
    return pl.pallas_call(
        functools.partial(project_body, width, with_query),
        grid=(blocks,),
        in_specs=[
            vspec((short, width), lambda i: (i, 0)),
            vspec((3 * width, width), lambda i: (0, 0), True),
            vspec((1, kp, short), lambda i: (i, 0, 0)),
        ],
        out_specs=out_specs,
        out_shape=out_shape,
        compiler_params=params(),
        cost_estimate=cost(2 * rows * width * width * 3, 12e6),
        name="project" if with_query else "project_peer",
    )(x, w_att, e_t)


def head_pair(ref_slice, low_lane):
    zero = jnp.zeros_like(ref_slice)
    return jnp.concatenate(
        [jnp.where(low_lane, ref_slice, zero), jnp.where(low_lane, zero, ref_slice)], axis=0
    )


def softmax_pair(scores, kp):
    parts = []
    for half in range(2):
        s = scores[:, half * kp : (half + 1) * kp]
        top = jnp.max(s, axis=-1, keepdims=True)
        e = jnp.exp(s - top)
        parts.append(e * (1.0 / jnp.sum(e, axis=-1, keepdims=True)))
    return parts


def attend_body(width, head, kp, n_ref, q_ref, s_ref, w_ref, x_ref, mix_ref, sum_ref, stat_ref):
    pairs = width // (2 * head)
    step = pl.program_id(0)
    scale = head ** (-0.5)
    low_lane = lax.broadcasted_iota(jnp.int32, (kp, 2 * head), 1) < head
    for j in range(pairs):
        cols = pl.ds(j * 2 * head, 2 * head)
        keys = head_pair(s_ref[0, :, cols], low_lane)
        values = head_pair(s_ref[0, :, pl.ds(width + j * 2 * head, 2 * head)], low_lane)
        scores = dot_t(q_ref[:, cols], keys) * scale
        prob = jnp.concatenate(softmax_pair(scores, kp), axis=1).astype(BF)
        mix_ref[:, cols] = dot(prob, values).astype(BF)
    branch = dot(mix_ref[...], w_ref[...])
    first = x_ref[...].astype(F32) + branch
    sum_ref[...] = first
    rows = q_ref.shape[0]
    keep = (lax.broadcasted_iota(jnp.int32, (rows, 1), 0) < n_ref[step]).astype(F32)
    sums = jnp.concatenate(
        [
            jnp.sum(keep * first * first, axis=0, keepdims=True),
            jnp.sum(keep * branch * branch, axis=0, keepdims=True),
        ],
        axis=0,
    )

    @pl.when(step == 0)
    def _():
        stat_ref[...] = sums

    @pl.when(step > 0)
    def _():
        stat_ref[...] += sums


def attend(n_valid, q, summary, w_att, x, head):
    rows, width = q.shape
    blocks, kp, _ = summary.shape
    short = rows // blocks
    return pl.pallas_call(
        functools.partial(attend_body, width, head, kp),
        grid_spec=pltpu.PrefetchScalarGridSpec(
            num_scalar_prefetch=1,
            grid=(blocks,),
            in_specs=[
                vspec((short, width), lambda i, n: (i, 0)),
                vspec((1, kp, 2 * width), lambda i, n: (i, 0, 0)),
                vspec((width, width), lambda i, n: (3, 0), True),
                vspec((short, width), lambda i, n: (i, 0)),
            ],
            out_specs=[
                vspec((short, width), lambda i, n: (i, 0)),
                vspec((short, width), lambda i, n: (i, 0)),
                vspec((2, width), lambda i, n: (0, 0)),
            ],
        ),
        out_shape=[
            jax.ShapeDtypeStruct((rows, width), BF),
            jax.ShapeDtypeStruct((rows, width), F32),
            jax.ShapeDtypeStruct((2, width), F32),
        ],
        compiler_params=params(),
        cost_estimate=cost(2 * rows * width * (width + 4 * kp), 10e6, rows * kp * 12),
        name="attend",
    )(n_valid, q, summary, w_att, x)


def forward_body(
    depth, head, c_ref, n_ref, x_ref, px_ref, w_ref, e_ref, pe_ref, *refs
):
    q_ref, kv_ref, s_ref, mix_ref, sum_ref, stat_ref, part, unit, got, send, recv = refs
    blocks, short, kp = e_ref.shape
    width = x_ref.shape[1]
    seq, mine = lax.axis_index("seq"), lax.axis_index("own")
    z, y = seq // 2, seq % 2
    along_y = (2 * z + (1 - y), mine)
    after = (2 * lax.rem(z + 1, depth) + y, mine)
    before = (2 * lax.rem(z + depth - 1, depth) + y, mine)
    has_left, has_right = z > 0, z < depth - 1
    shared = kp * 5 // 16
    direct = kp - 2 * shared
    barrier = pltpu.get_barrier_semaphore()
    pl.semaphore_signal(barrier, inc=1, device_id=along_y, device_id_type=MESH_ID)

    @pl.when(has_left)
    def _():
        pl.semaphore_signal(barrier, inc=1, device_id=before, device_id_type=MESH_ID)

    @pl.when(has_right)
    def _():
        pl.semaphore_signal(barrier, inc=1, device_id=after, device_id_type=MESH_ID)

    pl.semaphore_wait(barrier, 1 + jnp.minimum(z, 1) + jnp.minimum(depth - 1 - z, 1))

    @pl.when(jnp.logical_not(has_left))
    def _():
        got[0] = jnp.zeros_like(got[0])

    @pl.when(jnp.logical_not(has_right))
    def _():
        got[1] = jnp.zeros_like(got[1])

    def copy(at, src, dst, there):
        return pltpu.make_async_remote_copy(
            src_ref=src,
            dst_ref=dst,
            send_sem=send.at[at],
            recv_sem=recv.at[at],
            device_id=there,
            device_id_type=MESH_ID,
        )

    every = pl.ds(0, direct)
    single = pl.ds(pl.multiple_of(direct + shared * y, 8), shared)
    moves, hands = {}, {}
    for kind in range(2):
        cols = pl.ds(kind * width, width)
        for side in range(2):
            there = (after, before)[side]
            at = (kind * 2 + side) * 3
            moves[kind, side] = [
                copy(at, unit.at[side, every, cols], got.at[side, every, cols], there),
                copy(at + 1, unit.at[side, single, cols], got.at[side, single, cols], there),
            ]
            hands[kind, side] = copy(
                at + 2, got.at[side, single, cols], got.at[side, single, cols], along_y
            )
    can_send = (has_right, has_left)
    can_get = (has_left, has_right)

    for kind in range(2):
        cols = pl.ds(kind * width, width)
        weight = pl.ds((1 + kind) * width, width)

        def own_block(b, carry):
            rows = pl.ds(pl.multiple_of(b * short, short), short)
            kv = dot(x_ref[rows, :], w_ref[weight, :]).astype(BF)
            kv_ref[rows, cols] = kv
            total = dot_l(e_ref[b], kv)
            part[b, :, cols] = total

            @pl.when(b == 0)
            def _():
                for side in range(2):
                    unit[side, :, cols] = c_ref[1 - side, b] * total

            @pl.when(b > 0)
            def _():
                for side in range(2):
                    unit[side, :, cols] += c_ref[1 - side, b] * total

            return carry

        def peer_block(b, carry):
            rows = pl.ds(pl.multiple_of(b * short, short), short)
            kv = dot(px_ref[rows, :], w_ref[weight, :]).astype(BF)
            total = dot_l(pe_ref[b], kv)
            for side in range(2):
                unit[side, :, cols] += c_ref[1 - side, blocks + b] * total
            return carry

        lax.fori_loop(0, blocks, own_block, 0)
        lax.fori_loop(0, blocks, peer_block, 0)
        for side in range(2):

            @pl.when(can_send[side])
            def _():
                for move in moves[kind, side]:
                    move.start()

    def query_block(b, carry):
        rows = pl.ds(pl.multiple_of(b * short, short), short)
        q_ref[rows, :] = dot(x_ref[rows, :], w_ref[pl.ds(0, width), :]).astype(BF)
        return carry

    lax.fori_loop(0, blocks, query_block, 0)
    for kind in range(2):
        for side in range(2):

            @pl.when(can_get[side])
            def _():
                moves[kind, side][1].wait_recv()
                hands[kind, side].start()

    for kind in range(2):
        for side in range(2):

            @pl.when(can_get[side])
            def _():
                moves[kind, side][0].wait_recv()
                hands[kind, side].wait_recv()

    slab = 64

    def combine(i, carry):
        b, at = i // (kp // slab), i % (kp // slab)
        rows = pl.ds(pl.multiple_of(at * slab, slab), slab)
        total = c_ref[2, b] * unit[1, rows, :] + c_ref[3, b] * got[0, rows, :]
        total = total + c_ref[4, b] * unit[0, rows, :] + c_ref[5, b] * got[1, rows, :]
        s_ref[b, rows, :] = (total + c_ref[6, b] * part[b, rows, :]).astype(BF)
        return carry

    lax.fori_loop(0, blocks * (kp // slab), combine, 0)
    pairs = width // (2 * head)
    scale = head ** (-0.5)
    low_lane = lax.broadcasted_iota(jnp.int32, (kp, 2 * head), 1) < head

    def attend_block(b, carry):
        rows = pl.ds(pl.multiple_of(b * short, short), short)
        def pair(j):
            cols = pl.ds(pl.multiple_of(j * 2 * head, 2 * head), 2 * head)
            vcols = pl.ds(pl.multiple_of(width + j * 2 * head, 2 * head), 2 * head)
            keys = head_pair(s_ref[b, :, cols], low_lane)
            values = head_pair(s_ref[b, :, vcols], low_lane)
            scores = dot_t(q_ref[rows, cols], keys) * scale
            prob = jnp.concatenate(softmax_pair(scores, kp), axis=1).astype(BF)
            mix_ref[rows, cols] = dot(prob, values).astype(BF)

        def two(i, inner):
            pair(2 * i)
            pair(2 * i + 1)
            return inner

        lax.fori_loop(0, pairs // 2, two, 0)
        branch = dot(mix_ref[rows, :], w_ref[pl.ds(3 * width, width), :])
        first = x_ref[rows, :].astype(F32) + branch
        sum_ref[rows, :] = first
        keep = (lax.broadcasted_iota(jnp.int32, (short, 1), 0) < n_ref[1, b]).astype(F32)
        here = lax.broadcasted_iota(jnp.int32, (1, width), 1) == 0
        stat_ref[...] += jnp.concatenate(
            [
                jnp.sum(keep * first * first, axis=0, keepdims=True),
                jnp.sum(keep * branch * branch, axis=0, keepdims=True),
                jnp.where(here, n_ref[1, b].astype(F32), 0.0),
            ],
            axis=0,
        )
        return carry

    stat_ref[...] = jnp.zeros_like(stat_ref)
    lax.fori_loop(0, blocks, attend_block, 0)
    for kind in range(2):
        for side in range(2):

            @pl.when(can_send[side])
            def _():
                for move in moves[kind, side]:
                    move.wait_send()

            @pl.when(can_get[side])
            def _():
                hands[kind, side].wait_send()


def forward(coef, n_valid, x, peer_x, w_att, e_own, e_peer, head, peers):
    rows, width = x.shape
    blocks, short, kp = e_own.shape
    vmem = pl.BlockSpec(memory_space=pltpu.VMEM)
    smem = pl.BlockSpec(memory_space=pltpu.SMEM)
    return pl.pallas_call(
        functools.partial(forward_body, peers // 2, head),
        in_specs=[smem] * 2 + [vmem] * 5,
        out_specs=[vmem] * 6,
        out_shape=[
            jax.ShapeDtypeStruct((rows, width), BF),
            jax.ShapeDtypeStruct((rows, 2 * width), BF),
            jax.ShapeDtypeStruct((blocks, kp, 2 * width), BF),
            jax.ShapeDtypeStruct((rows, width), BF),
            jax.ShapeDtypeStruct((rows, width), F32),
            jax.ShapeDtypeStruct((3, width), F32),
        ],
        scratch_shapes=[
            pltpu.VMEM((blocks, kp, 2 * width), F32),
            pltpu.VMEM((2, kp, 2 * width), F32),
            pltpu.VMEM((2, kp, 2 * width), F32),
            pltpu.SemaphoreType.DMA((12,)),
            pltpu.SemaphoreType.DMA((12,)),
        ],
        compiler_params=pltpu.CompilerParams(
            collective_id=3, has_side_effects=True, vmem_limit_bytes=VMEM_LIMIT
        ),
        cost_estimate=cost(2 * rows * width * width * 8, 200e6, rows * kp * 12),
        name="forward",
    )(coef, n_valid, x, peer_x, w_att, e_own, e_peer)


def normalize(values):
    mean = jnp.mean(values, axis=-1, keepdims=True)
    centered = values - mean
    inverse = lax.rsqrt(jnp.mean(centered * centered, axis=-1, keepdims=True) + eps_norm)
    return centered * inverse, inverse


def norm_back(grad_out, normed, inverse, gain):
    scaled = grad_out * gain
    return inverse * (
        scaled
        - jnp.mean(scaled, axis=-1, keepdims=True)
        - normed * jnp.mean(scaled * normed, axis=-1, keepdims=True)
    )


def feed_body(
    chunks,
    first_ref,
    w1_ref,
    w2_ref,
    wo_ref,
    cot_ref,
    np_ref,
    out_ref,
    hid_ref,
    up_ref,
    down_ref,
    flow_ref,
    dfirst_ref,
    dbranch_ref,
    dmix_ref,
    ng_ref,
    slope_ref,
):
    step = pl.program_id(0)
    rows, width = first_ref.shape
    deep = w2_ref.shape[0] // chunks
    down_rows = lambda c: w2_ref[pl.ds(c * deep, deep)].reshape(width, width)
    normed_one, inverse_one = normalize(first_ref[...])
    first_norm = normed_one * np_ref[0:1, :] + np_ref[1:2, :]
    first_low = first_norm.astype(BF)
    flow_ref[...] = first_low
    second = first_norm
    for c in range(chunks):
        cols = pl.ds(c * width, width)
        u = dot(first_low, w1_ref[:, c].reshape(width, width))
        cumulative = 0.5 * (1.0 + lax.erf(u * (1.0 / math.sqrt(2.0))))
        density = jnp.exp(-0.5 * u * u) * (1.0 / math.sqrt(2.0 * math.pi))
        slope_ref[:, cols] = cumulative + u * density
        hidden = (u * cumulative).astype(BF)
        hid_ref[:, cols] = hidden
        second = second + dot(hidden, down_rows(c))
    normed_two, inverse_two = normalize(second)
    out_ref[...] = (normed_two * np_ref[2:3, :] + np_ref[3:4, :]).astype(BF)
    grad_out = cot_ref[...].astype(F32)
    gain_two = jnp.sum(grad_out * normed_two, axis=0, keepdims=True)
    shift_two = jnp.sum(grad_out, axis=0, keepdims=True)
    grad_second = norm_back(grad_out, normed_two, inverse_two, np_ref[2:3, :])
    down = grad_second.astype(BF)
    down_ref[...] = down
    grad_first_norm = grad_second
    for c in range(chunks):
        cols = pl.ds(c * width, width)
        grad_hidden = dot_t(down, down_rows(c))
        up = (grad_hidden * slope_ref[:, cols]).astype(BF)
        up_ref[:, cols] = up
        grad_first_norm = grad_first_norm + dot_t(up, w1_ref[:, c].reshape(width, width))
    gain_one = jnp.sum(grad_first_norm * normed_one, axis=0, keepdims=True)
    shift_one = jnp.sum(grad_first_norm, axis=0, keepdims=True)
    grad_first = norm_back(grad_first_norm, normed_one, inverse_one, np_ref[0:1, :])
    dfirst_ref[...] = grad_first
    grad_branch = grad_first.astype(BF)
    dbranch_ref[...] = grad_branch
    dmix_ref[...] = dot_t(grad_branch, wo_ref[...]).astype(BF)
    sums = jnp.concatenate([gain_one, shift_one, gain_two, shift_two], axis=0)

    @pl.when(step == 0)
    def _():
        ng_ref[...] = sums

    @pl.when(step > 0)
    def _():
        ng_ref[...] += sums


def feed(first_sum, w_ffn, w_att, cotangent, norm_params, tile):
    rows, width = first_sum.shape
    groups, chunks, size, _ = w_ffn.shape
    groups = groups // 2
    ff = chunks * width
    row = lambda i: (i, 0)
    return pl.pallas_call(
        functools.partial(feed_body, chunks),
        grid=(rows // tile,),
        in_specs=[
            vspec((tile, width), row),
            vspec((groups, chunks, size, width), lambda i: (0, 0, 0, 0), True),
            vspec((groups, chunks, size, width), lambda i: (1, 0, 0, 0), True),
            vspec((width, width), lambda i: (3, 0), True),
            vspec((tile, width), row),
            vspec(norm_params.shape, lambda i: (0, 0)),
        ],
        out_specs=[
            vspec((tile, width), row),
            vspec((tile, ff), row),
            vspec((tile, ff), row),
            vspec((tile, width), row),
            vspec((tile, width), row),
            vspec((tile, width), row),
            vspec((tile, width), row),
            vspec((tile, width), row),
            vspec((4, width), lambda i: (0, 0)),
        ],
        out_shape=[
            jax.ShapeDtypeStruct((rows, width), BF),
            jax.ShapeDtypeStruct((rows, ff), BF),
            jax.ShapeDtypeStruct((rows, ff), BF),
            jax.ShapeDtypeStruct((rows, width), BF),
            jax.ShapeDtypeStruct((rows, width), BF),
            jax.ShapeDtypeStruct((rows, width), F32),
            jax.ShapeDtypeStruct((rows, width), BF),
            jax.ShapeDtypeStruct((rows, width), BF),
            jax.ShapeDtypeStruct((4, width), F32),
        ],
        scratch_shapes=[pltpu.VMEM((tile, ff), F32)],
        compiler_params=params(),
        cost_estimate=cost(2 * rows * width * ff * 4, 30e6, rows * ff * 2),
        name="feed",
    )(first_sum, w_ffn, w_ffn, w_att, cotangent, norm_params)


def pair_back(key_cols, value_cols, q, g, head, low_lane):
    kp = key_cols.shape[0]
    scale = head ** (-0.5)
    keys, values = head_pair(key_cols, low_lane), head_pair(value_cols, low_lane)
    prob = softmax_pair(dot_t(q, keys) * scale, kp)
    grad_prob = dot_t(g, values)
    low_parts = []
    for half in range(2):
        p = prob[half]
        d = grad_prob[:, half * kp : (half + 1) * kp]
        low_parts.append((p * (d - jnp.sum(p * d, axis=-1, keepdims=True))).astype(BF))
    grad_scores = jnp.concatenate(low_parts, axis=1)
    prob_low = jnp.concatenate(prob, axis=1).astype(BF)
    grad_q = (dot(grad_scores, keys) * scale).astype(BF)
    return grad_q, dot_l(grad_scores, q) * scale, dot_l(prob_low, g)


def attend_back_body(width, head, kp, c_ref, q_ref, s_ref, g_ref, dq_ref, ds_ref, head_ref, tail_ref, acc_ref):
    step = pl.program_id(0)
    last = pl.num_programs(0) - 1
    low_lane = lax.broadcasted_iota(jnp.int32, (kp, 2 * head), 1) < head

    def pair(j):
        cols = pl.ds(pl.multiple_of(j * 2 * head, 2 * head), 2 * head)
        vcols = pl.ds(pl.multiple_of(width + j * 2 * head, 2 * head), 2 * head)
        grads, dk, dv = pair_back(
            s_ref[0, :, cols], s_ref[0, :, vcols], q_ref[:, cols], g_ref[:, cols], head, low_lane
        )
        dq_ref[:, cols] = grads
        for at, both in ((cols, dk), (vcols, dv)):
            value = jnp.where(low_lane, both[:kp], both[kp:])
            ds_ref[0, :, at] = value
            for side, row, low_ref in ((0, 0, head_ref), (1, last, tail_ref)):
                before = jnp.where(step > 0, acc_ref[side, :, at], 0.0)
                total = before + c_ref[row, step] * value
                acc_ref[side, :, at] = total
                low_ref[:, at] = total.astype(BF)

    def two(i, carry):
        pair(2 * i)
        pair(2 * i + 1)
        return carry

    lax.fori_loop(0, width // (4 * head), two, 0)


def attend_back(coef, q, summary, grad_mix, head):
    rows, width = q.shape
    blocks, kp, _ = summary.shape
    short = rows // blocks
    row = lambda i, *_: (i, 0)
    lead = lambda i, *_: (i, 0, 0)
    return pl.pallas_call(
        functools.partial(attend_back_body, width, head, kp),
        grid_spec=pltpu.PrefetchScalarGridSpec(
            num_scalar_prefetch=1,
            grid=(blocks,),
            in_specs=[
                vspec((short, width), row),
                vspec((1, kp, 2 * width), lead),
                vspec((short, width), row),
            ],
            out_specs=[
                vspec((short, width), row),
                vspec((1, kp, 2 * width), lead),
                vspec((kp, 2 * width), lambda i, *_: (0, 0)),
                vspec((kp, 2 * width), lambda i, *_: (0, 0)),
            ],
            scratch_shapes=[pltpu.VMEM((2, kp, 2 * width), F32)],
        ),
        out_shape=[
            jax.ShapeDtypeStruct((rows, width), BF),
            jax.ShapeDtypeStruct((blocks, kp, 2 * width), F32),
            jax.ShapeDtypeStruct((kp, 2 * width), BF),
            jax.ShapeDtypeStruct((kp, 2 * width), BF),
        ],
        compiler_params=params(),
        cost_estimate=cost(2 * rows * width * 8 * kp, 10e6, rows * kp * 12),
        name="attend_back",
    )(coef, q, summary, grad_mix)


def outer_body(split, l_ref, r_ref, o_ref):
    value = dot_l(l_ref[...], r_ref[...])
    o_ref[...] = value.reshape(o_ref.shape).astype(o_ref.dtype)


def outer_up(first_low, grad_up, size, dtype):
    rows, width = first_low.shape
    chunks = grad_up.shape[1] // width
    groups = width // size
    return pl.pallas_call(
        functools.partial(outer_body, True),
        grid=(chunks,),
        in_specs=[
            vspec((rows, width), lambda i: (0, 0), True),
            vspec((rows, width), lambda i: (0, i)),
        ],
        out_specs=vspec((groups, 1, size, width), lambda i: (0, i, 0, 0)),
        out_shape=jax.ShapeDtypeStruct((groups, chunks, size, width), dtype),
        compiler_params=params(),
        cost_estimate=cost(2 * rows * width * width * chunks, 20e6),
        name="outer_up",
    )(first_low, grad_up)


def outer_rows(left, right, dtype, name):
    rows, width = right.shape[0], min(left.shape[1], right.shape[1])
    tall, wide = left.shape[1] // width, right.shape[1] // width
    moving = lambda n: (lambda i: (0, i)) if n > 1 else (lambda i: (0, 0))
    return pl.pallas_call(
        functools.partial(outer_body, False),
        grid=(tall * wide,),
        in_specs=[
            vspec((rows, width), moving(tall), tall == 1),
            vspec((rows, width), moving(wide), wide == 1),
        ],
        out_specs=vspec((width, width), lambda i: (i, 0)),
        out_shape=jax.ShapeDtypeStruct((tall * wide * width, width), dtype),
        compiler_params=params(),
        cost_estimate=cost(2 * rows * width * width * tall * wide, 20e6),
        name=name,
    )(left, right)


def backward_body(peers, head, chunks, c_ref, q_ref, s_ref, g_ref, *refs):
    sources, outs = refs[:7], refs[7:13]
    grad_outs, scratch = refs[13:17], refs[17:]
    dq_ref, ds_ref, far_refs = outs[0], outs[1], outs[2:]
    held, (low_head, low_tail, g_down, g_up, g_out, g_query) = scratch[:7], scratch[7:13]
    send, recv, local = scratch[13:]
    blocks, kp, wide = s_ref.shape
    width = wide // 2
    short = q_ref.shape[0] // blocks
    pairs = width // (2 * head)
    seq, mine = lax.axis_index("seq"), lax.axis_index("own")
    loads = [pltpu.make_async_copy(sources[k], held[k], local.at[k]) for k in range(7)]
    for load in loads:
        load.start()

    def place(d):
        return (lax.rem(seq + peers + d, peers), mine)

    steps = (1, -1, 2, -2)
    inside = lambda d: seq < peers - d if d > 0 else seq >= -d
    can_send = [inside(d) for d in steps]
    can_get = [inside(-d) for d in steps]
    barrier = pltpu.get_barrier_semaphore()
    for k in range(4):

        @pl.when(can_send[k])
        def _():
            pl.semaphore_signal(barrier, inc=1, device_id=place(steps[k]), device_id_type=MESH_ID)

        @pl.when(jnp.logical_not(can_get[k]))
        def _():
            far_refs[k][...] = jnp.zeros_like(far_refs[k])

    pl.semaphore_wait(barrier, jnp.minimum(seq, 2) + jnp.minimum(peers - 1 - seq, 2))
    low_lane = lax.broadcasted_iota(jnp.int32, (kp, 2 * head), 1) < head

    def columns(j):
        at = pl.multiple_of(j * 2 * head, 2 * head)
        return pl.ds(at, 2 * head), pl.ds(pl.multiple_of(width + at, 2 * head), 2 * head)

    def message(j, k, kind):
        low = (low_tail, low_head)[k % 2]
        cols = columns(j)[kind]
        return pltpu.make_async_remote_copy(
            src_ref=low.at[:, cols],
            dst_ref=far_refs[k].at[:, cols],
            send_sem=send.at[j, k, kind],
            recv_sem=recv.at[j, k, kind],
            device_id=place(steps[k]),
            device_id_type=MESH_ID,
        )

    def pair(j, carry):
        cols, vcols = columns(j)
        head_sums, tail_sums = [0.0, 0.0], [0.0, 0.0]
        for b in range(blocks):
            rows = pl.ds(b * short, short)
            grads, dk, dv = pair_back(
                s_ref[b, :, cols], s_ref[b, :, vcols], q_ref[rows, cols], g_ref[rows, cols], head, low_lane
            )
            dq_ref[rows, cols] = grads
            for kind, at, both in ((0, cols, dk), (1, vcols, dv)):
                value = jnp.where(low_lane, both[:kp], both[kp:])
                ds_ref[b, :, at] = value
                head_sums[kind] = head_sums[kind] + c_ref[0, b] * value
                tail_sums[kind] = tail_sums[kind] + c_ref[blocks - 1, b] * value
        for kind, at in ((0, cols), (1, vcols)):
            low_head[:, at] = head_sums[kind].astype(BF)
            low_tail[:, at] = tail_sums[kind].astype(BF)
        for k in range(4):

            @pl.when(can_send[k])
            def _():
                for kind in range(2):
                    message(j, k, kind).start()

        return carry

    lax.fori_loop(0, pairs, pair, 0)
    first_low, grad_up, hidden, grad_down, mixed, grad_branch, x = held
    stores = []

    def store(src, dst):
        copy = pltpu.make_async_copy(src, dst, local.at[7 + len(stores)])
        copy.start()
        stores.append(copy)

    for load in loads:
        load.wait()

    def down_chunk(i, carry):
        at = pl.ds(pl.multiple_of(i * width, width), width)
        g_down[at, :] = dot_l(hidden[:, at], grad_down[...]).astype(BF)
        return carry

    def up_chunk(i, carry):
        at = pl.ds(pl.multiple_of(i * width, width), width)
        value = dot_l(first_low[...], grad_up[:, at]).astype(BF)
        g_up[:, i] = value.reshape(g_up.shape[0], g_up.shape[2], width)
        return carry

    lax.fori_loop(0, chunks, down_chunk, 0)
    store(g_down, grad_outs[0])
    lax.fori_loop(0, chunks, up_chunk, 0)
    store(g_up, grad_outs[1])
    g_out[...] = dot_l(mixed[...], grad_branch[...]).astype(BF)
    store(g_out, grad_outs[2])
    g_query[...] = dot_l(x[...], dq_ref[...]).astype(BF)
    store(g_query, grad_outs[3])

    def finish(j, carry):
        for k in range(4):

            @pl.when(can_get[k])
            def _():
                for kind in range(2):
                    message(j, k, kind).wait_recv()

            @pl.when(can_send[k])
            def _():
                for kind in range(2):
                    message(j, k, kind).wait_send()

        return carry

    lax.fori_loop(0, pairs, finish, 0)
    for copy in stores:
        copy.wait()


def backward(coef, q, summary, grad_mix, operands, head, peers, size):
    rows, width = q.shape
    blocks, kp, _ = summary.shape
    chunks = operands[1].shape[1] // width
    groups = width // size
    vmem, smem = pl.BlockSpec(memory_space=pltpu.VMEM), pl.BlockSpec(memory_space=pltpu.SMEM)
    far = jax.ShapeDtypeStruct((kp, 2 * width), BF)
    products = [(chunks * width, width), (groups, chunks, size, width), (width, width), (width, width)]
    pairs = width // (2 * head)
    return pl.pallas_call(
        functools.partial(backward_body, peers, head, chunks),
        in_specs=[smem] + [vmem] * 3 + [pl.BlockSpec(memory_space=pl.ANY)] * 7,
        out_specs=[vmem] * 6 + [pl.BlockSpec(memory_space=pl.ANY)] * 4,
        out_shape=[
            jax.ShapeDtypeStruct((rows, width), BF),
            jax.ShapeDtypeStruct((blocks, kp, 2 * width), F32),
        ]
        + [far] * 4
        + [jax.ShapeDtypeStruct(shape, BF) for shape in products],
        scratch_shapes=[pltpu.VMEM(a.shape, BF) for a in operands]
        + [pltpu.VMEM(far.shape, BF)] * 2
        + [pltpu.VMEM(shape, BF) for shape in products]
        + [
            pltpu.SemaphoreType.DMA((pairs, 4, 2)),
            pltpu.SemaphoreType.DMA((pairs, 4, 2)),
            pltpu.SemaphoreType.DMA((11,)),
        ],
        compiler_params=pltpu.CompilerParams(
            collective_id=4, has_side_effects=True, vmem_limit_bytes=VMEM_LIMIT
        ),
        cost_estimate=cost(2 * rows * width * (8 * kp + 10 * width), 60e6, rows * kp * 12),
        name="backward",
    )(coef, q, summary, grad_mix, *operands)


def back_body(
    width, blocks, c_ref, n_ref, e_ref, kv_ref, p_ref, *refs
):
    far_refs = refs[:4]
    dq_ref, w_ref, df_ref, dkv_ref, gp_ref, gi_ref = refs[4:]
    step = pl.program_id(0)
    short, kp = e_ref.shape[1], e_ref.shape[2]
    total = c_ref[step, 0] * p_ref[0]
    for other in range(1, blocks):
        total = total + c_ref[step, other] * p_ref[other]
    for k in range(4):
        total = total + c_ref[step, blocks + k] * far_refs[k][...].astype(F32)
    summary = total.astype(BF)
    dkv = dot(e_ref[0], summary).astype(BF)
    dkv_ref[...] = dkv
    keep = lax.broadcasted_iota(jnp.int32, (short, 1), 0) < n_ref[1, step]
    grad_e = jnp.where(keep, dot_t(kv_ref[...], summary), 0.0)
    column = n_ref[0, step]
    at = pl.multiple_of(jnp.minimum((column // 8) * 8, gp_ref.shape[0] - short - 8), 8)
    moved = pltpu.roll(
        jnp.concatenate([grad_e, jnp.zeros((8, kp), F32)], axis=0), column - at, 0
    )

    @pl.when(step == 0)
    def _():
        gp_ref[...] = jnp.zeros_like(gp_ref)

    gp_ref[pl.ds(at, short + 8), :] += moved
    gi_ref[...] = (
        df_ref[...]
        + dot_t(dq_ref[...], w_ref[pl.ds(0, width), :])
        + dot_t(dkv[:, :width], w_ref[pl.ds(width, width), :])
        + dot_t(dkv[:, width:], w_ref[pl.ds(2 * width, width), :])
    )


def back(coef, places, e_rows, kv, grad_parts, far_parts, dq, w_att, grad_first, positions):
    rows, width = dq.shape
    blocks, short, kp = e_rows.shape
    row = lambda i, *_: (i, 0)
    lead = lambda i, *_: (i, 0, 0)
    fixed = lambda i, *_: (0, 0)
    return pl.pallas_call(
        functools.partial(back_body, width, blocks),
        grid_spec=pltpu.PrefetchScalarGridSpec(
            num_scalar_prefetch=2,
            grid=(blocks,),
            in_specs=[
                vspec((1, short, kp), lead),
                vspec((short, 2 * width), row),
                vspec(grad_parts.shape, lambda i, *_: (0, 0, 0), True),
            ]
            + [vspec((kp, 2 * width), fixed, True)] * 4
            + [
                vspec((short, width), row),
                vspec((3 * width, width), fixed, True),
                vspec((short, width), row),
            ],
            out_specs=[
                vspec((short, 2 * width), row),
                vspec((positions, kp), fixed),
                vspec((short, width), row),
            ],
        ),
        out_shape=[
            jax.ShapeDtypeStruct((rows, 2 * width), BF),
            jax.ShapeDtypeStruct((positions, kp), F32),
            jax.ShapeDtypeStruct((rows, width), F32),
        ],
        compiler_params=params(),
        cost_estimate=cost(2 * rows * width * (3 * width + 4 * kp), 20e6),
        name="back",
    )(coef, places, e_rows, kv, grad_parts, *far_parts, dq, w_att, grad_first)


def reduce_body(depth, half, n_src, extra_keep, *refs):
    sources = refs[:n_src]
    grads, shares_out, rows_out = refs[n_src : n_src + 3]
    (own, got_c, sum_c, got_a, got_b, sum_a, sum_b, got_a2, got_b2, sum_z, got_z) = refs[
        n_src + 3 : n_src + 14
    ]
    keep_a, keep_b, keep_z = refs[n_src + 14 : n_src + 17]
    (e_own, e_got, e_sum, e_got1, e_sum1, e_got2, e_sum2, e_gotz, e_all, e_rows) = refs[
        n_src + 17 : n_src + 27
    ]
    send, recv, local = refs[n_src + 27 :]
    seq, mine = lax.axis_index("seq"), lax.axis_index("own")
    z, y, x, c = seq // 2, seq % 2, mine // 2, mine % 2
    core = (seq, 2 * x + (1 - c))
    along_x = (seq, 2 * (1 - x) + c)
    along_y = (2 * z + (1 - y), mine)
    along_z = [(2 * lax.rem(z + d, depth) + y, mine) for d in range(1, depth)]
    barrier = pltpu.get_barrier_semaphore()
    partners = [core, along_x, along_y] + along_z
    for partner in partners:
        pl.semaphore_signal(barrier, inc=1, device_id=partner, device_id_type=MESH_ID)
    pl.semaphore_wait(barrier, len(partners))

    sent = []

    def push(src, dst, partner):
        at = len(sent)
        copy = pltpu.make_async_remote_copy(
            src_ref=src,
            dst_ref=dst,
            send_sem=send.at[at],
            recv_sem=recv.at[at],
            device_id=partner,
            device_id_type=MESH_ID,
        )
        copy.start()
        sent.append(copy)
        return copy

    up, down, g_query, g_keyval, g_out, extra = sources
    bands = [g_query, g_keyval.at[0], g_keyval.at[1], g_out]
    half_z = depth // 2
    cols = own.shape[-1]
    loads = []

    def load(src, dst):
        copy = pltpu.make_async_copy(src, dst, local.at[len(loads)])
        copy.start()
        loads.append(copy)
        return copy

    e_first = [push(extra.at[:, :, 1 - c], e_got, core)]
    e_load = [load(extra.at[:, :, c], e_own)]
    piece_first, piece_load = [], []

    def piece_core(p):
        at, part = p // 2, pl.ds((p % 2) * cols, cols)
        if at < 2:
            first = [
                push(up.at[:, :, 1 - c, at, :, part], got_c.at[p, pl.ds(0, half_z)], core),
                push(down.at[:, :, 1 - c, at, :, part], got_c.at[p, pl.ds(half_z, half_z)], core),
            ]
            kept = [
                load(up.at[:, :, c, at, :, part], own.at[p, pl.ds(0, half_z)]),
                load(down.at[:, :, c, at, :, part], own.at[p, pl.ds(half_z, half_z)]),
            ]
        else:
            first = [
                push(bands[m].at[:, 1 - c, :, part], got_c.at[p, m], core) for m in range(depth)
            ]
            kept = [load(bands[m].at[:, c, :, part], own.at[p, m]) for m in range(depth)]
        piece_first.append(first)
        piece_load.append(kept)

    state = {}

    def wait_recv(copies):
        for copy in copies:
            copy.wait_recv()

    low, high = pl.ds(0, half), pl.ds(half, half)

    def add(a, b):
        return a.astype(F32) + b.astype(F32)

    def piece_c(p):
        for copy in piece_load[p]:
            copy.wait()
        wait_recv(piece_first[p])

        def body(i, carry):
            zz, w = i // 2, i % 2
            to_x, to_y = 2 * w + 1 - x, 2 * (1 - y) + w
            sum_c[p, 0, zz, w] = add(own[p, zz, to_x, low, :], got_c[p, zz, to_x, low, :]).astype(BF)
            sum_c[p, 1, zz, w] = add(own[p, zz, to_y, high, :], got_c[p, zz, to_y, high, :]).astype(BF)
            return carry

        lax.fori_loop(0, depth * 2, body, 0)
        state["1", p] = [
            push(sum_c.at[p, 0], got_a.at[p], along_x),
            push(sum_c.at[p, 1], got_b.at[p], along_y),
        ]

    def piece_1(p):
        wait_recv(state["1", p])

        def side_a(zz, w):
            at = 2 * w + x
            return add(own[p, zz, at, low, :], got_c[p, zz, at, low, :]) + got_a[p, zz, w].astype(F32)

        def side_b(zz, w):
            at = 2 * y + w
            return add(own[p, zz, at, high, :], got_c[p, zz, at, high, :]) + got_b[p, zz, w].astype(F32)

        def body(zz, carry):
            sum_a[p, zz] = side_a(zz, 1 - y).astype(BF)
            sum_b[p, zz] = side_b(zz, 1 - x).astype(BF)
            keep_a[p, zz] = side_a(zz, y)
            keep_b[p, zz] = side_b(zz, x)
            return carry

        lax.fori_loop(0, depth, body, 0)
        state["2", p] = [
            push(sum_a.at[p], got_a2.at[p], along_y),
            push(sum_b.at[p], got_b2.at[p], along_x),
        ]

    def piece_2(p):
        wait_recv(state["2", p])

        def body(zz, carry):
            total_a = keep_a[p, zz] + got_a2[p, zz].astype(F32)
            total_b = keep_b[p, zz] + got_b2[p, zz].astype(F32)
            sum_z[p, zz, low, :] = total_a.astype(BF)
            sum_z[p, zz, high, :] = total_b.astype(BF)
            return carry

        lax.fori_loop(0, depth, body, 0)
        keep_z[p, low, :] = keep_a[p, z] + got_a2[p, z].astype(F32)
        keep_z[p, high, :] = keep_b[p, z] + got_b2[p, z].astype(F32)
        state["z", p] = [
            push(sum_z.at[p, lax.rem(z + d, depth)], got_z.at[p, d - 1], along_z[d - 1])
            for d in range(1, depth)
        ]

    def piece_z(p):
        wait_recv(state["z", p])
        total = keep_z[p]
        for d in range(depth - 1):
            total = total + got_z[p, d].astype(F32)
        grads[(p // 2 + 1) % 3, :, pl.ds((p % 2) * cols, cols)] = total

    def extra_c():
        e_load[0].wait()
        wait_recv(e_first)

        def body(i, carry):
            zz, yx = i // 4, i % 4
            e_sum[zz, yx // 2, yx % 2] = e_own[zz, yx] + e_got[zz, yx]
            return carry

        lax.fori_loop(0, depth * 4, body, 0)
        state["ez"] = [
            push(e_sum.at[lax.rem(z + d, depth)], e_gotz.at[d - 1], along_z[d - 1])
            for d in range(1, depth)
        ]

    def extra_1():
        wait_recv(state["ez"])

        def body(i, carry):
            yy, xx = i // 2, i % 2
            total = e_sum[z, yy, xx]
            for d in range(depth - 1):
                total = total + e_gotz[d, yy, xx]
            e_sum1[yy, xx] = total
            return carry

        lax.fori_loop(0, 4, body, 0)
        state["e1"] = [push(e_sum1.at[:, 1 - x], e_got1, along_x)]

    def extra_2():
        wait_recv(state["e1"])

        def body(yy, carry):
            e_sum2[yy] = e_sum1[yy, x] + e_got1[yy]
            return carry

        lax.fori_loop(0, 2, body, 0)
        state["e2"] = [push(e_sum2.at[1 - y], e_got2, along_y)]

    def extra_z():
        wait_recv(state["e2"])
        e_all[z, y] = e_sum2[y] + e_got2[...]
        state["gz"] = [push(e_all.at[z, y], e_all.at[z, y], there) for there in along_z]

    def extra_gather_y():
        wait_recv(state["gz"])
        state["gy"] = [push(e_all.at[:, y], e_all.at[:, y], along_y)]

    def extra_gather_x():
        wait_recv(state["gy"])
        e_rows[x, c] = e_all[:, :, pl.ds(extra_keep, e_rows.shape[4]), :]
        state["gx"] = [push(e_rows.at[x, c], e_rows.at[x, c], along_x)]

    def extra_gather_c():
        wait_recv(state["gx"])
        state["gc"] = [push(e_rows.at[:, c], e_rows.at[:, c], core)]

    stages = [piece_c, piece_1, piece_2, piece_z]
    small = {0: extra_c, 3: extra_1, 4: extra_2, 5: extra_z, 6: extra_gather_y}
    small |= {7: extra_gather_x, 8: extra_gather_c}
    piece_core(0)
    piece_core(1)
    for turn in range(9):
        for stage in range(4):
            if 0 <= turn - stage < 6:
                stages[stage](turn - stage)
            if stage == 0 and turn + 2 < 6:
                piece_core(turn + 2)
        if turn in small:
            small[turn]()
    shares_out[...] = e_all[:, :, pl.ds(0, extra_keep), :]
    wait_recv(state["gc"])
    rows_out[...] = e_rows[...]
    for copy in sent:
        copy.wait_send()


def reduce_all(g_query, g_keyval, g_out, g_up, g_down, extra, peers):
    depth = peers // 2
    size, width = g_up.shape[2], g_up.shape[3]
    half = size // 2
    e_rows_all, kp = extra.shape[1], extra.shape[2]
    keep = e_rows_all - 8
    sources = (
        [
            g_up.reshape(depth // 2, 4, 2, 2, size, width),
            g_down.reshape(depth // 2, 4, 2, 2, size, width),
        ]
        + [
            g_query.reshape(4, 2, size, width),
            g_keyval.reshape(2, 4, 2, size, width),
            g_out.reshape(4, 2, size, width),
        ]
        + [extra.reshape(depth, 4, 2, e_rows_all, kp)]
    )
    n_src = len(sources)
    cols = width // 2
    messages = 1 + 8 + 2 * depth + 6 * (4 + depth - 1) + 2 + 2 * (depth - 1) + 3
    loads = 1 + 8 + 2 * depth
    any_spec = pl.BlockSpec(memory_space=pl.ANY)
    vmem = pl.BlockSpec(memory_space=pltpu.VMEM)
    scratch = [
        pltpu.VMEM((6, depth, 4, size, cols), BF),
        pltpu.VMEM((6, depth, 4, size, cols), BF),
        pltpu.VMEM((6, 2, depth, 2, half, cols), BF),
        pltpu.VMEM((6, depth, 2, half, cols), BF),
        pltpu.VMEM((6, depth, 2, half, cols), BF),
        pltpu.VMEM((6, depth, half, cols), BF),
        pltpu.VMEM((6, depth, half, cols), BF),
        pltpu.VMEM((6, depth, half, cols), BF),
        pltpu.VMEM((6, depth, half, cols), BF),
        pltpu.VMEM((6, depth, size, cols), BF),
        pltpu.VMEM((6, depth - 1, size, cols), BF),
        pltpu.VMEM((6, depth, half, cols), F32),
        pltpu.VMEM((6, depth, half, cols), F32),
        pltpu.VMEM((6, size, cols), F32),
        pltpu.VMEM((depth, 4, e_rows_all, kp), F32),
        pltpu.VMEM((depth, 4, e_rows_all, kp), F32),
        pltpu.VMEM((depth, 2, 2, e_rows_all, kp), F32),
        pltpu.VMEM((2, e_rows_all, kp), F32),
        pltpu.VMEM((2, 2, e_rows_all, kp), F32),
        pltpu.VMEM((e_rows_all, kp), F32),
        pltpu.VMEM((2, e_rows_all, kp), F32),
        pltpu.VMEM((depth - 1, 2, 2, e_rows_all, kp), F32),
        pltpu.VMEM((depth, 2, e_rows_all, kp), F32),
        pltpu.VMEM((2, 2, depth, 2, 8, kp), F32),
        pltpu.SemaphoreType.DMA((messages,)),
        pltpu.SemaphoreType.DMA((messages,)),
        pltpu.SemaphoreType.DMA((loads,)),
    ]
    return pl.pallas_call(
        functools.partial(reduce_body, depth, half, n_src, keep),
        in_specs=[any_spec] * n_src,
        out_specs=[vmem] * 3,
        out_shape=[
            jax.ShapeDtypeStruct((3, size, width), F32),
            jax.ShapeDtypeStruct((depth, 2, keep, kp), F32),
            jax.ShapeDtypeStruct((2, 2, depth, 2, 8, kp), F32),
        ],
        scratch_shapes=scratch,
        compiler_params=pltpu.CompilerParams(
            collective_id=1, has_side_effects=True, vmem_limit_bytes=VMEM_LIMIT
        ),
        name="reduce_all",
    )(*sources)


def gather_body(depth, half, band_ref, proj_ref, out_ref, pout_ref, send, recv, local):
    seq, mine = lax.axis_index("seq"), lax.axis_index("own")
    z, y, x, c = seq // 2, seq % 2, mine // 2, mine % 2
    core = (seq, 2 * x + (1 - c))
    along_x = (seq, 2 * (1 - x) + c)
    along_y = (2 * z + (1 - y), mine)
    order = [1, 3, 2]
    along_z = [(2 * lax.rem(z + d, depth) + y, mine) for d in order]
    barrier = pltpu.get_barrier_semaphore()
    partners = [core, along_x, along_y] + along_z
    for partner in partners:
        pl.semaphore_signal(barrier, inc=1, device_id=partner, device_id_type=MESH_ID)
    pl.semaphore_wait(barrier, len(partners))

    sent = []

    def push(src, dst, partner):
        at = len(sent)
        copy = pltpu.make_async_remote_copy(
            src_ref=src,
            dst_ref=dst,
            send_sem=send.at[at],
            recv_sem=recv.at[at],
            device_id=partner,
            device_id_type=MESH_ID,
        )
        copy.start()
        sent.append(copy)
        return copy

    keep = pltpu.make_async_copy(band_ref, out_ref.at[z, y, x, c], local.at[0])
    keep.start()
    keep_p = pltpu.make_async_copy(proj_ref, pout_ref.at[x, c], local.at[1])
    keep_p.start()
    mine_at = out_ref.at[z, y, x, c]
    from_z = [push(band_ref, mine_at, there) for there in along_z]
    from_x = [push(band_ref, mine_at, along_x)]
    from_y = [push(band_ref, mine_at, along_y)]
    proj_x = push(proj_ref, pout_ref.at[x, c], along_x)
    last = [push(band_ref, mine_at, core), push(proj_ref, pout_ref.at[x, c], core)]
    planes = [z]
    for k in range(depth - 1):
        from_z[k].wait_recv()
        plane = lax.rem(z + depth - order[k], depth)
        planes.append(plane)
        slab = out_ref.at[plane, y, x, c]
        from_x.append(push(slab, slab, along_x))
        from_y.append(push(slab, slab, along_y))
        last.append(push(slab, slab, core))
    low, high = pl.ds(0, half), pl.ds(half, half)
    cross = []
    for k in range(depth):
        plane = planes[k]
        from_x[k].wait_recv()
        slab = out_ref.at[plane, y, 1 - x, c]
        part = out_ref.at[plane, y, 1 - x, c, low, :]
        cross_y = push(part, part, along_y)
        last.append(push(slab, slab, core))
        from_y[k].wait_recv()
        slab = out_ref.at[plane, 1 - y, x, c]
        part = out_ref.at[plane, 1 - y, x, c, high, :]
        cross.append((cross_y, push(part, part, along_x)))
        last.append(push(slab, slab, core))
        if k == 0:
            proj_x.wait_recv()
            slab = pout_ref.at[1 - x, c]
            last.append(push(slab, slab, core))
    for k in range(depth):
        for copy in cross[k]:
            copy.wait_recv()
        slab = out_ref.at[planes[k], 1 - y, 1 - x, c]
        last.append(push(slab, slab, core))
    for copy in last:
        copy.wait_recv()
    keep.wait()
    keep_p.wait()
    for copy in sent:
        copy.wait_send()


def gather_bands(band, proj, peers):
    depth = peers // 2
    size, width = band.shape
    messages = (depth - 1) + 3 + 2 + 3 * (depth - 1) + 4 * depth + 1 + depth
    vmem = pl.BlockSpec(memory_space=pltpu.VMEM)
    return pl.pallas_call(
        functools.partial(gather_body, depth, size // 2),
        in_specs=[vmem] * 2,
        out_specs=[vmem] * 2,
        out_shape=[
            jax.ShapeDtypeStruct((depth, 2, 2, 2, size, width), BF),
            jax.ShapeDtypeStruct((2, 2) + proj.shape, BF),
        ],
        scratch_shapes=[
            pltpu.SemaphoreType.DMA((messages,)),
            pltpu.SemaphoreType.DMA((messages,)),
            pltpu.SemaphoreType.DMA((2,)),
        ],
        compiler_params=pltpu.CompilerParams(
            collective_id=2, has_side_effects=True, vmem_limit_bytes=VMEM_LIMIT
        ),
        cost_estimate=cost(1e9, 90e6),
        name="gather_bands",
    )(band, proj)


def shampoo(grad, left, right, root_left, root_right, weight):
    new_left = decay * left + (1.0 - decay) * jnp.einsum(
        "tij,tkj->tik", grad, grad, precision=highest
    )
    new_right = decay * right + (1.0 - decay) * jnp.einsum(
        "tji,tjk->tik", grad, grad, precision=highest
    )
    inner = jnp.einsum("tij,tjk->tik", grad, root_right, precision=highest)
    step = jnp.einsum("tij,tjk->tik", root_left, inner, precision=highest)
    return (new_left, new_right, weight - rate_matrix * step)


def exact(a, b, left, right):
    return lax.dot_general(
        a, b, (((left,), (right,)), ((), ())), precision=highest, preferred_element_type=F32
    )


def step_body(bands, *refs):
    band_ref, tiles, proj_ref, blocks = refs[0], refs[1:6], refs[6], refs[7:12]
    rows_ref, norm_ref, second_ref = refs[12:15]
    owned_ref, new_tiles, new_blocks = refs[15], refs[16:19], refs[19:22]
    grad_ref, second_new_ref, norm_new_ref, rms_ref = refs[22:]
    at = pl.program_id(0)
    size, kp = tiles[0].shape[1], proj_ref.shape[-1]

    def update(grad, state, new, t):
        left, right, root_left, root_right, weight = (ref[t] for ref in state)
        new[0][t] = decay * left + (1.0 - decay) * exact(grad, grad, 1, 1)
        new[1][t] = decay * right + (1.0 - decay) * exact(grad, grad, 0, 0)
        new[2][t] = weight - rate_matrix * exact(root_left, exact(grad, root_right, 1, 0), 1, 0)

    @pl.when(at < bands)
    def _():
        def four(i, carry):
            part = band_ref[0, :, pl.ds(pl.multiple_of(i * 4 * size, 128), 4 * size)]
            for t in range(4):
                grad = part[:, t * size : (t + 1) * size]
                owned_ref[4 * i + t] = grad
                update(grad, tiles, new_tiles, 4 * i + t)
            return carry

        lax.fori_loop(0, tiles[0].shape[0] // 4, four, 0)

    @pl.when(at >= bands)
    def _():
        update(proj_ref[0], blocks, new_blocks, 0)

    @pl.when(at == bands)
    def _():
        depth = rows_ref.shape[2]

        def row(r):
            return rows_ref[r // 2 % 2, r % 2, r // 8 % depth, r // 4 % 2, pl.ds(0, 1), :]

        per = norm_ref.shape[1] // kp
        for i in range(4):
            grad = jnp.concatenate([row(per * i + j) for j in range(per)], axis=1)
            grad_ref[pl.ds(i, 1), :] = grad
            second = decay * second_ref[pl.ds(i, 1), :] + (1.0 - decay) * grad * grad
            second_new_ref[pl.ds(i, 1), :] = second
            norm_new_ref[pl.ds(i, 1), :] = norm_ref[pl.ds(i, 1), :] - rate_norm * grad * lax.rsqrt(second)
        count = jnp.sum(sum(row(6 * per + j) for j in range(per)), axis=1, keepdims=True)
        for i in range(2):
            square = row(4 * per + per * i)
            for j in range(1, per):
                square = square + row(4 * per + per * i + j)
            total = jnp.sum(square, axis=1, keepdims=True)
            ratio = jnp.sqrt(total / (count * norm_ref.shape[1]))
            rms_ref[i] = jnp.sum(ratio)


def step_all(bands, tiles, proj_grad, blocks, rows, norm_params, norm_stat):
    count, size, width = bands.shape
    each, kp = width // size, proj_grad.shape[-1]
    n_blocks = proj_grad.shape[0]
    tile = lambda: vspec((each, size, size), lambda i: (jnp.minimum(i, count - 1), 0, 0))
    block = lambda: vspec((1, kp, kp), lambda i: (jnp.maximum(i - count, 0), 0, 0))
    whole = lambda a: vspec(a.shape, lambda i: (0,) * len(a.shape))
    like = lambda a: jax.ShapeDtypeStruct(a.shape, F32)
    rms = jax.ShapeDtypeStruct((2,), F32)
    return pl.pallas_call(
        functools.partial(step_body, count),
        grid=(count + n_blocks,),
        in_specs=[vspec((1, size, width), lambda i: (jnp.minimum(i, count - 1), 0, 0))]
        + [tile() for _ in range(5)]
        + [block() for _ in range(6)]
        + [whole(rows), whole(norm_params), whole(norm_stat)],
        out_specs=[tile() for _ in range(4)]
        + [block() for _ in range(3)]
        + [whole(norm_params)] * 3
        + [pl.BlockSpec(memory_space=pltpu.SMEM)],
        out_shape=[like(tiles[0])] * 4 + [like(proj_grad)] * 3 + [like(norm_params)] * 3 + [rms],
        compiler_params=params(),
        cost_estimate=cost(1e9, 20e6),
        name="step_all",
    )(bands, *tiles, proj_grad, *blocks, rows, norm_params, norm_stat)


def to_matrix(tiles, rows, cols):
    size = tiles.shape[-1]
    return (
        tiles.reshape(rows // size, cols // size, size, size)
        .transpose(0, 2, 1, 3)
        .reshape(rows, cols)
    )


def to_bands(tiles, cols):
    count, size, _ = tiles.shape
    return to_matrix(tiles, count * size * size // cols, cols)


def from_bands(bands, size):
    rows, cols = bands.shape
    return (
        bands.reshape(rows // size, size, cols // size, size)
        .transpose(0, 2, 1, 3)
        .reshape(-1, size, size)
    )


def bands_body(w_ref, p_ref, att_ref, ffn_ref, proj_ref):
    count, size, _ = w_ref.shape
    wide = att_ref.shape[1] // size
    near = att_ref.shape[0] // size
    for k in range(count):
        at, cols = k // wide, pl.ds(k % wide * size, size)
        tile = w_ref[k].astype(BF)
        if at < near:
            att_ref[pl.ds(at * size, size), cols] = tile
        else:
            ffn_ref[pl.ds((at - near) * size, size), cols] = tile
    proj_ref[...] = p_ref[...].astype(BF)


def make_bands(weights, projection, att_dev, width):
    per_dev, size, _ = weights.shape
    near = att_dev * size // width * size
    return pl.pallas_call(
        bands_body,
        out_shape=[
            jax.ShapeDtypeStruct((near, width), BF),
            jax.ShapeDtypeStruct((per_dev * size // width * size - near, width), BF),
            jax.ShapeDtypeStruct(projection.shape, BF),
        ],
        compiler_params=pltpu.CompilerParams(vmem_limit_bytes=VMEM_LIMIT),
        name="make_bands",
    )(weights, projection)


def gather_weights(weights, projection, att_dev, width, both, fused, peers):
    size = weights.shape[-1]
    low = weights.astype(BF)
    groups, chunks = width // size, FF // width
    if banded(weights.shape[0], att_dev, width, size):
        band, far, proj_low = make_bands(weights, projection, att_dev, width)
        ffn = lax.all_gather(far, both, axis=0, tiled=True)
        if fused:
            att, proj = gather_bands(band, proj_low, peers)
            att, proj = att.reshape(-1, width), proj.reshape(-1, projection.shape[1])
        else:
            att = lax.all_gather(band, both, axis=0, tiled=True)
            proj = lax.all_gather(proj_low, "own", axis=0, tiled=True)
        return att, ffn.reshape(2 * groups, chunks, size, width), proj
    per_dev = weights.shape[0]
    proj = lax.all_gather(projection.astype(BF), "own", axis=0, tiled=True)
    grid = lax.all_gather(low, both, axis=0, tiled=True).reshape(-1, per_dev, size, size)
    att = to_bands(grid[:, :att_dev].reshape(-1, size, size), width)
    tiles = grid[:, att_dev:].reshape(-1, size, size)
    half = tiles.shape[0] // 2
    w_up = to_matrix(tiles[:half], width, FF).reshape(groups, size, chunks, width)
    w_down = to_matrix(tiles[half:], FF, width).reshape(groups, chunks, size, width)
    return att, jnp.concatenate([w_up.transpose(0, 2, 1, 3), w_down], axis=0), proj


def banded(per_dev, att_dev, width, size):
    wide = width // size
    return att_dev % wide == 0 and (per_dev - att_dev) % wide == 0


def scatter_weight_grads(g_att, g_up, g_down, per_dev, att_dev, both):
    size, width = g_up.shape[2], g_up.shape[3]
    if banded(per_dev, att_dev, width, size):
        ffn = jnp.concatenate([g_up.reshape(-1, width), g_down], axis=0)
        ffn = lax.psum_scatter(ffn, both, scatter_dimension=0, tiled=True)
        att = lax.psum_scatter(g_att, both, scatter_dimension=0, tiled=True)
        return jnp.concatenate([from_bands(att, size), from_bands(ffn, size)], axis=0)
    up = g_up.transpose(0, 2, 1, 3).reshape(width, -1)
    att = from_bands(g_att, size)
    ffn = jnp.concatenate([from_bands(up, size), from_bands(g_down, size)], axis=0)
    stacked = jnp.concatenate(
        [
            att.reshape(-1, att_dev, size, size),
            ffn.reshape(-1, per_dev - att_dev, size, size),
        ],
        axis=1,
    ).reshape(-1, size, size)
    return lax.psum_scatter(stacked, both, scatter_dimension=0, tiled=True)


def per_device(
    tokens,
    cotangent,
    lengths,
    offsets,
    valid_count,
    weights,
    stat_left,
    stat_right,
    root_left,
    root_right,
    projection,
    projection_left,
    projection_right,
    projection_root_left,
    projection_root_right,
    norm_params,
    norm_stat,
):
    both = ("seq", "own")
    size = weights.shape[-1]
    width = tokens.shape[-1]
    rows_here = tokens.shape[1]
    head = width // HEADS
    kp = projection.shape[1]
    blocks = rows_here // SHORT
    peers = lax.axis_size("seq")
    devices = peers * lax.axis_size("own")
    per_dev = weights.shape[0]
    att_dev = 4 * (width // size) ** 2 // devices
    x = tokens[0]
    swap = [(i, i ^ 1) for i in range(peers)]
    peer_x = lax.ppermute(x, "seq", swap)
    own_size = lax.axis_size("own")
    fused = own_size == 4 and peers == 8 and banded(per_dev, att_dev, width, size)
    w_att, w_ffn, proj_all = gather_weights(
        weights, projection, att_dev, width, both, fused, peers
    )

    places, table, coef_back = tables(lengths, offsets, valid_count, blocks, rows_here)

    e_own, e_peer = pick_rows(places, proj_all, blocks)
    n_own = places[1, :blocks]

    if fused:
        query, keyval, summary, mixed, first_sum, row_sums = forward(
            table, places, x, peer_x, w_att, e_own, e_peer, head, peers
        )
    else:
        query, keyval, part_own = project(x, w_att, e_own.transpose(0, 2, 1), True)
        (part_peer,) = project(peer_x, w_att, e_peer.transpose(0, 2, 1), False)

        def unit_sum(flag):
            total = flag[0] * part_own[0]
            for b in range(1, blocks):
                total = total + flag[b] * part_own[b]
            for b in range(blocks):
                total = total + flag[blocks + b] * part_peer[b]
            return total

        head_sum, tail_sum = unit_sum(table[0]), unit_sum(table[1])
        from_left = lax.ppermute(tail_sum, "seq", [(i, i + 2) for i in range(peers - 2)])
        from_right = lax.ppermute(head_sum, "seq", [(i + 2, i) for i in range(peers - 2)])
        summary = jnp.stack(
            [
                (
                    table[2, b] * head_sum
                    + table[3, b] * from_left
                    + table[4, b] * tail_sum
                    + table[5, b] * from_right
                    + table[6, b] * part_own[b]
                ).astype(BF)
                for b in range(blocks)
            ]
        )
        mixed, first_sum, row_sums = attend(n_own, query, summary, w_att, x, head)
    (
        result,
        hidden,
        grad_up,
        grad_down,
        first_low,
        grad_first,
        grad_branch,
        grad_mix,
        norm_terms,
    ) = feed(first_sum, w_ffn, w_att, cotangent[0], norm_params, 256)
    gtype = BF if fused else F32
    if fused:
        operands = [first_low, grad_up, hidden, grad_down, mixed, grad_branch, x]
        grad_query, grad_parts, *far_parts, g_down, g_up, g_out, g_query = backward(
            coef_back, query, summary, grad_mix, operands, head, peers, size
        )
    else:
        grad_query, grad_parts, low_head, low_tail = attend_back(
            coef_back, query, summary, grad_mix, head
        )
        far_parts = []
        for far in (1, 2):
            onward = [(i, i + far) for i in range(peers - far)]
            far_parts.append(lax.ppermute(low_tail, "seq", onward))
            far_parts.append(lax.ppermute(low_head, "seq", [(j, i) for i, j in onward]))
        g_up = outer_up(first_low, grad_up, size, gtype)
        g_down = outer_rows(hidden, grad_down, gtype, "outer_down")
        g_out = outer_rows(mixed, grad_branch, gtype, "outer_out")
        g_query = outer_rows(x, grad_query, gtype, "outer_query")
    grad_keyval, grad_proj, grad_input = back(
        coef_back,
        places,
        e_own,
        keyval,
        grad_parts,
        far_parts,
        grad_query,
        w_att,
        grad_first,
        proj_all.shape[0],
    )
    g_keyval = outer_rows(x, grad_keyval, gtype, "outer_keyval")
    part_rows = projection.shape[0]
    if not fused:
        valid_here = jnp.sum(n_own).astype(F32)
        here = lax.broadcasted_iota(jnp.int32, (1, width), 1) == 0
        row_sums = jnp.concatenate([row_sums, jnp.where(here, valid_here, 0.0)], axis=0)
    extra = jnp.concatenate([norm_terms.reshape(-1, kp), row_sums.reshape(-1, kp)], axis=0)
    n_norm = 4 * width // kp
    n_row = 2 * width // kp
    if fused:
        extra = jnp.pad(extra, ((0, devices - extra.shape[0]), (0, 0)))[:, None, :]
        extra = jnp.pad(extra, ((0, 0), (0, 7), (0, 0)))
        shares = grad_proj.reshape(own_size, peers, part_rows // peers, kp).swapaxes(0, 1)
        shares = shares.reshape(devices, part_rows // peers, kp)
        banded_grads, proj_parts, rows = reduce_all(
            g_query, g_keyval, g_out, g_up, g_down, jnp.concatenate([shares, extra], axis=1), peers
        )
        (
            owned,
            left_new,
            right_new,
            weights_new,
            proj_left_new,
            proj_right_new,
            proj_blocks,
            norm_grad,
            stat_new,
            norm_new,
            residual_rms,
        ) = step_all(
            banded_grads,
            [stat_left, stat_right, root_left, root_right, weights],
            proj_parts.reshape(-1, kp, kp),
            [
                projection_left,
                projection_right,
                projection_root_left,
                projection_root_right,
                projection.reshape(-1, kp, kp),
            ],
            rows,
            norm_params,
            norm_stat,
        )
        proj_grad = proj_parts.reshape(part_rows, kp)
    else:
        owned = scatter_weight_grads(
            jnp.concatenate([g_query, g_keyval, g_out], axis=0), g_up, g_down, per_dev, att_dev, both
        )
        packed = jnp.concatenate([grad_proj, extra], axis=0)
        packed = lax.psum(jnp.pad(packed, ((0, -packed.shape[0] % 16), (0, 0))), both)
        proj_grad = lax.dynamic_slice_in_dim(
            packed, lax.axis_index("own") * part_rows, part_rows, 0
        )
        totals = packed[grad_proj.shape[0] :]
        norm_grad = totals[:n_norm].reshape(4, width)
        row_total = totals[n_norm : n_norm + n_row].reshape(2, width).sum(axis=1)
        valid_total = totals[n_norm + n_row : n_norm + n_row + width // kp].sum()
        residual_rms = jnp.sqrt(row_total / (valid_total * width))
        left_new, right_new, weights_new = shampoo(
            owned, stat_left, stat_right, root_left, root_right, weights
        )
        proj_left_new, proj_right_new, proj_blocks = shampoo(
            proj_grad.reshape(-1, kp, kp),
            projection_left,
            projection_right,
            projection_root_left,
            projection_root_right,
            projection.reshape(-1, kp, kp),
        )
        stat_new = decay * norm_stat + (1.0 - decay) * norm_grad * norm_grad
        norm_new = norm_params - rate_norm * norm_grad * lax.rsqrt(stat_new)
    return (
        result[None],
        grad_input[None],
        owned,
        left_new,
        right_new,
        weights_new,
        proj_grad,
        proj_left_new,
        proj_right_new,
        proj_blocks.reshape(part_rows, kp),
        norm_grad,
        stat_new,
        norm_new,
        residual_rms,
    )


def solution(mesh):
    pack = P("own", "seq", None)
    table = P("own", None)
    tile = P(("seq", "own"), None, None)
    proj = P("own", None, None)
    return jax.shard_map(
        per_device,
        mesh=mesh,
        in_specs=(pack, pack, table, table, table)
        + (tile,) * 5
        + (table, proj, proj, proj, proj, P(), P()),
        out_specs=(pack, pack) + (tile,) * 4 + (table, proj, proj, table, P(), P(), P(), P()),
        check_vma=False,
    )
```

```python
import functools
import math

import jax
import jax.numpy as jnp
from jax import lax
from jax.experimental import pallas as pl
from jax.experimental.pallas import tpu as pltpu
from jax.sharding import PartitionSpec as P

HEADS = 12
FF = 3072
SHORT = 512
BF = jnp.bfloat16
F32 = jnp.float32

eps_norm = 1e-05
decay = 0.5
rate_matrix = 0.2
rate_norm = 0.2
highest = lax.Precision.HIGHEST
VMEM_LIMIT = 60 * 1024 * 1024
MESH_ID = pl.DeviceIdType.MESH


def dot(a, b):
    return lax.dot_general(a, b, (((1,), (0,)), ((), ())), preferred_element_type=F32)


def dot_t(a, b):
    return lax.dot_general(a, b, (((1,), (1,)), ((), ())), preferred_element_type=F32)


def dot_l(a, b):
    return lax.dot_general(a, b, (((0,), (0,)), ((), ())), preferred_element_type=F32)


def vspec(shape, index_map, once=False):
    if once:
        return pl.BlockSpec(shape, index_map, pipeline_mode=pl.Buffered(1))
    return pl.BlockSpec(shape, index_map)


def params():
    return pltpu.CompilerParams(
        dimension_semantics=("arbitrary",), vmem_limit_bytes=VMEM_LIMIT
    )


def cost(flops, nbytes, trans=0):
    return pl.CostEstimate(flops=int(flops), bytes_accessed=int(nbytes), transcendentals=int(trans))


def tables_body(blocks, rows_here, l_ref, o_ref, v_ref, i_ref, f_ref, b_ref):
    seq = lax.axis_index("seq")
    side = seq % 2
    row_start = seq * rows_here
    row_end = row_start + rows_here
    unit_start = (seq - side) * rows_here
    peer_start = (seq + 1 - 2 * side) * rows_here
    flag = lambda cond: jnp.where(cond, 1.0, 0.0).astype(F32)

    def locate(row):
        def body(i, carry):
            at, start, end, off, count = carry
            stop = at + l_ref[0, i]
            inside = jnp.logical_and(row >= at, row < stop)
            pick = lambda new, old: jnp.where(inside, new, old)
            return (
                stop,
                pick(at, start),
                pick(stop, end),
                pick(o_ref[0, i], off),
                pick(v_ref[0, i], count),
            )

        zero = jnp.int32(0)
        return lax.fori_loop(0, l_ref.shape[1], body, (zero,) * 5)[1:]

    starts, ends = [], []
    for k in range(2 * blocks):
        row = row_start + SHORT * k if k < blocks else peer_start + SHORT * (k - blocks)
        start, end, off, count = locate(row)
        starts.append(start)
        ends.append(end)
        i_ref[0, k] = off + row - start
        i_ref[1, k] = jnp.clip(count - (row - start), 0, SHORT)
    first = jnp.where(side == 0, starts[0], starts[blocks])
    last = jnp.where(side == 0, starts[-1], starts[blocks - 1])
    last_end = jnp.where(side == 0, ends[-1], ends[blocks - 1])
    head_cross = flag(first < unit_start)
    tail_cross = flag(last_end > unit_start + 2 * rows_here)
    for k in range(2 * blocks):
        is_head, is_tail = flag(starts[k] == first), flag(starts[k] == last)
        pick_tail = (1.0 - is_head) * is_tail
        f_ref[0, k] = is_head
        f_ref[1, k] = is_tail
        f_ref[2, k] = is_head
        f_ref[3, k] = is_head * head_cross
        f_ref[4, k] = pick_tail
        f_ref[5, k] = pick_tail * tail_cross
        f_ref[6, k] = (1.0 - is_head) * (1.0 - is_tail)
    own_last, own_end = starts[blocks - 1], ends[blocks - 1]
    for k in range(blocks):
        at_head, at_tail = flag(starts[k] == starts[0]), flag(starts[k] == own_last)
        for other in range(blocks):
            b_ref[k, other] = flag(starts[k] == starts[other])
        for far in range(2):
            reach = far * rows_here
            b_ref[k, blocks + 2 * far] = at_head * flag(starts[0] < row_start - reach)
            b_ref[k, blocks + 2 * far + 1] = at_tail * flag(own_end > row_end + reach)


def tables(lengths, offsets, valid_count, blocks, rows_here):
    smem = pl.BlockSpec(memory_space=pltpu.SMEM)
    return pl.pallas_call(
        functools.partial(tables_body, blocks, rows_here),
        in_specs=[smem] * 3,
        out_specs=[smem] * 3,
        out_shape=[
            jax.ShapeDtypeStruct((2, 2 * blocks), jnp.int32),
            jax.ShapeDtypeStruct((7, 2 * blocks), F32),
            jax.ShapeDtypeStruct((blocks, blocks + 4), F32),
        ],
        name="tables",
    )(lengths, offsets, valid_count)


def pick_body(places_ref, proj_ref, own_ref, peer_ref):
    blocks, short, kp = own_ref.shape
    span = short + 16
    keep = lax.broadcasted_iota(jnp.int32, (short, 1), 0)
    for first, out in ((0, own_ref), (blocks, peer_ref)):

        def block(b, carry):
            column = places_ref[0, first + b]
            at = jnp.clip((column // 16) * 16, 0, proj_ref.shape[0] - span)
            rows = proj_ref[pl.ds(pl.multiple_of(at, 16), span), :].astype(F32)
            rows = pltpu.roll(rows, lax.rem(span + at - column, span), 0)[:short]
            out[b] = jnp.where(keep < places_ref[1, first + b], rows, 0.0).astype(BF)
            return carry

        lax.fori_loop(0, blocks, block, 0)


def pick_rows(places, proj_all, blocks):
    vmem, smem = pl.BlockSpec(memory_space=pltpu.VMEM), pl.BlockSpec(memory_space=pltpu.SMEM)
    shape = jax.ShapeDtypeStruct((blocks, SHORT, proj_all.shape[1]), BF)
    return pl.pallas_call(
        pick_body,
        in_specs=[smem, vmem],
        out_specs=[vmem] * 2,
        out_shape=[shape] * 2,
        compiler_params=pltpu.CompilerParams(vmem_limit_bytes=VMEM_LIMIT),
        name="pick_rows",
    )(places, proj_all)


def project_body(width, with_query, x_ref, w_ref, e_ref, *outs):
    x = x_ref[...]
    if with_query:
        q_ref, kv_ref, p_ref = outs
        q_ref[...] = dot(x, w_ref[pl.ds(0, width), :]).astype(BF)
    else:
        (p_ref,) = outs
    e = e_ref[0]
    for part in range(2):
        kv = dot(x, w_ref[pl.ds((1 + part) * width, width), :]).astype(BF)
        if with_query:
            kv_ref[:, pl.ds(part * width, width)] = kv
        p_ref[0, :, pl.ds(part * width, width)] = dot(e, kv)


def project(x, w_att, e_t, with_query):
    rows, width = x.shape
    blocks, kp, short = e_t.shape
    out_shape = [jax.ShapeDtypeStruct((blocks, kp, 2 * width), F32)]
    out_specs = [vspec((1, kp, 2 * width), lambda i: (i, 0, 0))]
    if with_query:
        out_shape = [
            jax.ShapeDtypeStruct((rows, width), BF),
            jax.ShapeDtypeStruct((rows, 2 * width), BF),
        ] + out_shape
        out_specs = [
            vspec((short, width), lambda i: (i, 0)),
            vspec((short, 2 * width), lambda i: (i, 0)),
        ] + out_specs
    return pl.pallas_call(
        functools.partial(project_body, width, with_query),
        grid=(blocks,),
        in_specs=[
            vspec((short, width), lambda i: (i, 0)),
            vspec((3 * width, width), lambda i: (0, 0), True),
            vspec((1, kp, short), lambda i: (i, 0, 0)),
        ],
        out_specs=out_specs,
        out_shape=out_shape,
        compiler_params=params(),
        cost_estimate=cost(2 * rows * width * width * 3, 12e6),
        name="project" if with_query else "project_peer",
    )(x, w_att, e_t)


def head_pair(ref_slice, low_lane):
    zero = jnp.zeros_like(ref_slice)
    return jnp.concatenate(
        [jnp.where(low_lane, ref_slice, zero), jnp.where(low_lane, zero, ref_slice)], axis=0
    )


def softmax_pair(scores, kp):
    parts = []
    for half in range(2):
        s = scores[:, half * kp : (half + 1) * kp]
        top = jnp.max(s, axis=-1, keepdims=True)
        e = jnp.exp(s - top)
        parts.append(e * (1.0 / jnp.sum(e, axis=-1, keepdims=True)))
    return parts


def attend_body(width, head, kp, n_ref, q_ref, s_ref, w_ref, x_ref, mix_ref, sum_ref, stat_ref):
    pairs = width // (2 * head)
    step = pl.program_id(0)
    scale = head ** (-0.5)
    low_lane = lax.broadcasted_iota(jnp.int32, (kp, 2 * head), 1) < head
    for j in range(pairs):
        cols = pl.ds(j * 2 * head, 2 * head)
        keys = head_pair(s_ref[0, :, cols], low_lane)
        values = head_pair(s_ref[0, :, pl.ds(width + j * 2 * head, 2 * head)], low_lane)
        scores = dot_t(q_ref[:, cols], keys) * scale
        prob = jnp.concatenate(softmax_pair(scores, kp), axis=1).astype(BF)
        mix_ref[:, cols] = dot(prob, values).astype(BF)
    branch = dot(mix_ref[...], w_ref[...])
    first = x_ref[...].astype(F32) + branch
    sum_ref[...] = first
    rows = q_ref.shape[0]
    keep = (lax.broadcasted_iota(jnp.int32, (rows, 1), 0) < n_ref[step]).astype(F32)
    sums = jnp.concatenate(
        [
            jnp.sum(keep * first * first, axis=0, keepdims=True),
            jnp.sum(keep * branch * branch, axis=0, keepdims=True),
        ],
        axis=0,
    )

    @pl.when(step == 0)
    def _():
        stat_ref[...] = sums

    @pl.when(step > 0)
    def _():
        stat_ref[...] += sums


def attend(n_valid, q, summary, w_att, x, head):
    rows, width = q.shape
    blocks, kp, _ = summary.shape
    short = rows // blocks
    return pl.pallas_call(
        functools.partial(attend_body, width, head, kp),
        grid_spec=pltpu.PrefetchScalarGridSpec(
            num_scalar_prefetch=1,
            grid=(blocks,),
            in_specs=[
                vspec((short, width), lambda i, n: (i, 0)),
                vspec((1, kp, 2 * width), lambda i, n: (i, 0, 0)),
                vspec((width, width), lambda i, n: (3, 0), True),
                vspec((short, width), lambda i, n: (i, 0)),
            ],
            out_specs=[
                vspec((short, width), lambda i, n: (i, 0)),
                vspec((short, width), lambda i, n: (i, 0)),
                vspec((2, width), lambda i, n: (0, 0)),
            ],
        ),
        out_shape=[
            jax.ShapeDtypeStruct((rows, width), BF),
            jax.ShapeDtypeStruct((rows, width), F32),
            jax.ShapeDtypeStruct((2, width), F32),
        ],
        compiler_params=params(),
        cost_estimate=cost(2 * rows * width * (width + 4 * kp), 10e6, rows * kp * 12),
        name="attend",
    )(n_valid, q, summary, w_att, x)


def forward_body(
    depth, head, c_ref, n_ref, x_ref, px_ref, w_ref, e_ref, pe_ref, *refs
):
    q_ref, kv_ref, s_ref, mix_ref, sum_ref, stat_ref, part, unit, got, send, recv = refs
    blocks, short, kp = e_ref.shape
    width = x_ref.shape[1]
    seq, mine = lax.axis_index("seq"), lax.axis_index("own")
    z, y = seq // 2, seq % 2
    along_y = (2 * z + (1 - y), mine)
    after = (2 * lax.rem(z + 1, depth) + y, mine)
    before = (2 * lax.rem(z + depth - 1, depth) + y, mine)
    has_left, has_right = z > 0, z < depth - 1
    shared = kp * 5 // 16
    direct = kp - 2 * shared
    barrier = pltpu.get_barrier_semaphore()
    pl.semaphore_signal(barrier, inc=1, device_id=along_y, device_id_type=MESH_ID)

    @pl.when(has_left)
    def _():
        pl.semaphore_signal(barrier, inc=1, device_id=before, device_id_type=MESH_ID)

    @pl.when(has_right)
    def _():
        pl.semaphore_signal(barrier, inc=1, device_id=after, device_id_type=MESH_ID)

    pl.semaphore_wait(barrier, 1 + jnp.minimum(z, 1) + jnp.minimum(depth - 1 - z, 1))

    @pl.when(jnp.logical_not(has_left))
    def _():
        got[0] = jnp.zeros_like(got[0])

    @pl.when(jnp.logical_not(has_right))
    def _():
        got[1] = jnp.zeros_like(got[1])

    def copy(at, src, dst, there):
        return pltpu.make_async_remote_copy(
            src_ref=src,
            dst_ref=dst,
            send_sem=send.at[at],
            recv_sem=recv.at[at],
            device_id=there,
            device_id_type=MESH_ID,
        )

    every = pl.ds(0, direct)
    single = pl.ds(pl.multiple_of(direct + shared * y, 8), shared)
    moves, hands = {}, {}
    for kind in range(2):
        cols = pl.ds(kind * width, width)
        for side in range(2):
            there = (after, before)[side]
            at = (kind * 2 + side) * 3
            moves[kind, side] = [
                copy(at, unit.at[side, every, cols], got.at[side, every, cols], there),
                copy(at + 1, unit.at[side, single, cols], got.at[side, single, cols], there),
            ]
            hands[kind, side] = copy(
                at + 2, got.at[side, single, cols], got.at[side, single, cols], along_y
            )
    can_send = (has_right, has_left)
    can_get = (has_left, has_right)

    for kind in range(2):
        cols = pl.ds(kind * width, width)
        weight = pl.ds((1 + kind) * width, width)

        def own_block(b, carry):
            rows = pl.ds(pl.multiple_of(b * short, short), short)
            kv = dot(x_ref[rows, :], w_ref[weight, :]).astype(BF)
            kv_ref[rows, cols] = kv
            total = dot_l(e_ref[b], kv)
            part[b, :, cols] = total

            @pl.when(b == 0)
            def _():
                for side in range(2):
                    unit[side, :, cols] = c_ref[1 - side, b] * total

            @pl.when(b > 0)
            def _():
                for side in range(2):
                    unit[side, :, cols] += c_ref[1 - side, b] * total

            return carry

        def peer_block(b, carry):
            rows = pl.ds(pl.multiple_of(b * short, short), short)
            kv = dot(px_ref[rows, :], w_ref[weight, :]).astype(BF)
            total = dot_l(pe_ref[b], kv)
            for side in range(2):
                unit[side, :, cols] += c_ref[1 - side, blocks + b] * total
            return carry

        lax.fori_loop(0, blocks, own_block, 0)
        lax.fori_loop(0, blocks, peer_block, 0)
        for side in range(2):

            @pl.when(can_send[side])
            def _():
                for move in moves[kind, side]:
                    move.start()

    def query_block(b, carry):
        rows = pl.ds(pl.multiple_of(b * short, short), short)
        q_ref[rows, :] = dot(x_ref[rows, :], w_ref[pl.ds(0, width), :]).astype(BF)
        return carry

    lax.fori_loop(0, blocks, query_block, 0)
    for kind in range(2):
        for side in range(2):

            @pl.when(can_get[side])
            def _():
                moves[kind, side][1].wait_recv()
                hands[kind, side].start()

    for kind in range(2):
        for side in range(2):

            @pl.when(can_get[side])
            def _():
                moves[kind, side][0].wait_recv()
                hands[kind, side].wait_recv()

    slab = 64

    def combine(i, carry):
        b, at = i // (kp // slab), i % (kp // slab)
        rows = pl.ds(pl.multiple_of(at * slab, slab), slab)
        total = c_ref[2, b] * unit[1, rows, :] + c_ref[3, b] * got[0, rows, :]
        total = total + c_ref[4, b] * unit[0, rows, :] + c_ref[5, b] * got[1, rows, :]
        s_ref[b, rows, :] = (total + c_ref[6, b] * part[b, rows, :]).astype(BF)
        return carry

    lax.fori_loop(0, blocks * (kp // slab), combine, 0)
    pairs = width // (2 * head)
    scale = head ** (-0.5)
    low_lane = lax.broadcasted_iota(jnp.int32, (kp, 2 * head), 1) < head

    def attend_block(b, carry):
        rows = pl.ds(pl.multiple_of(b * short, short), short)
        def pair(j):
            cols = pl.ds(pl.multiple_of(j * 2 * head, 2 * head), 2 * head)
            vcols = pl.ds(pl.multiple_of(width + j * 2 * head, 2 * head), 2 * head)
            keys = head_pair(s_ref[b, :, cols], low_lane)
            values = head_pair(s_ref[b, :, vcols], low_lane)
            scores = dot_t(q_ref[rows, cols], keys) * scale
            prob = jnp.concatenate(softmax_pair(scores, kp), axis=1).astype(BF)
            mix_ref[rows, cols] = dot(prob, values).astype(BF)

        def two(i, inner):
            pair(2 * i)
            pair(2 * i + 1)
            return inner

        lax.fori_loop(0, pairs // 2, two, 0)
        branch = dot(mix_ref[rows, :], w_ref[pl.ds(3 * width, width), :])
        first = x_ref[rows, :].astype(F32) + branch
        sum_ref[rows, :] = first
        keep = (lax.broadcasted_iota(jnp.int32, (short, 1), 0) < n_ref[1, b]).astype(F32)
        here = lax.broadcasted_iota(jnp.int32, (1, width), 1) == 0
        stat_ref[...] += jnp.concatenate(
            [
                jnp.sum(keep * first * first, axis=0, keepdims=True),
                jnp.sum(keep * branch * branch, axis=0, keepdims=True),
                jnp.where(here, n_ref[1, b].astype(F32), 0.0),
            ],
            axis=0,
        )
        return carry

    stat_ref[...] = jnp.zeros_like(stat_ref)
    lax.fori_loop(0, blocks, attend_block, 0)
    for kind in range(2):
        for side in range(2):

            @pl.when(can_send[side])
            def _():
                for move in moves[kind, side]:
                    move.wait_send()

            @pl.when(can_get[side])
            def _():
                hands[kind, side].wait_send()


def forward(coef, n_valid, x, peer_x, w_att, e_own, e_peer, head, peers):
    rows, width = x.shape
    blocks, short, kp = e_own.shape
    vmem = pl.BlockSpec(memory_space=pltpu.VMEM)
    smem = pl.BlockSpec(memory_space=pltpu.SMEM)
    return pl.pallas_call(
        functools.partial(forward_body, peers // 2, head),
        in_specs=[smem] * 2 + [vmem] * 5,
        out_specs=[vmem] * 6,
        out_shape=[
            jax.ShapeDtypeStruct((rows, width), BF),
            jax.ShapeDtypeStruct((rows, 2 * width), BF),
            jax.ShapeDtypeStruct((blocks, kp, 2 * width), BF),
            jax.ShapeDtypeStruct((rows, width), BF),
            jax.ShapeDtypeStruct((rows, width), F32),
            jax.ShapeDtypeStruct((3, width), F32),
        ],
        scratch_shapes=[
            pltpu.VMEM((blocks, kp, 2 * width), F32),
            pltpu.VMEM((2, kp, 2 * width), F32),
            pltpu.VMEM((2, kp, 2 * width), F32),
            pltpu.SemaphoreType.DMA((12,)),
            pltpu.SemaphoreType.DMA((12,)),
        ],
        compiler_params=pltpu.CompilerParams(
            collective_id=3, has_side_effects=True, vmem_limit_bytes=VMEM_LIMIT
        ),
        cost_estimate=cost(2 * rows * width * width * 8, 200e6, rows * kp * 12),
        name="forward",
    )(coef, n_valid, x, peer_x, w_att, e_own, e_peer)


def normalize(values):
    mean = jnp.mean(values, axis=-1, keepdims=True)
    centered = values - mean
    inverse = lax.rsqrt(jnp.mean(centered * centered, axis=-1, keepdims=True) + eps_norm)
    return centered * inverse, inverse


def norm_back(grad_out, normed, inverse, gain):
    scaled = grad_out * gain
    return inverse * (
        scaled
        - jnp.mean(scaled, axis=-1, keepdims=True)
        - normed * jnp.mean(scaled * normed, axis=-1, keepdims=True)
    )


def feed_body(
    chunks,
    first_ref,
    w1_ref,
    w2_ref,
    wo_ref,
    cot_ref,
    np_ref,
    out_ref,
    hid_ref,
    up_ref,
    down_ref,
    flow_ref,
    dfirst_ref,
    dbranch_ref,
    dmix_ref,
    ng_ref,
    slope_ref,
):
    step = pl.program_id(0)
    rows, width = first_ref.shape
    deep = w2_ref.shape[0] // chunks
    down_rows = lambda c: w2_ref[pl.ds(c * deep, deep)].reshape(width, width)
    normed_one, inverse_one = normalize(first_ref[...])
    first_norm = normed_one * np_ref[0:1, :] + np_ref[1:2, :]
    first_low = first_norm.astype(BF)
    flow_ref[...] = first_low
    second = first_norm
    for c in range(chunks):
        cols = pl.ds(c * width, width)
        u = dot(first_low, w1_ref[:, c].reshape(width, width))
        cumulative = 0.5 * (1.0 + lax.erf(u * (1.0 / math.sqrt(2.0))))
        density = jnp.exp(-0.5 * u * u) * (1.0 / math.sqrt(2.0 * math.pi))
        slope_ref[:, cols] = cumulative + u * density
        hidden = (u * cumulative).astype(BF)
        hid_ref[:, cols] = hidden
        second = second + dot(hidden, down_rows(c))
    normed_two, inverse_two = normalize(second)
    out_ref[...] = (normed_two * np_ref[2:3, :] + np_ref[3:4, :]).astype(BF)
    grad_out = cot_ref[...].astype(F32)
    gain_two = jnp.sum(grad_out * normed_two, axis=0, keepdims=True)
    shift_two = jnp.sum(grad_out, axis=0, keepdims=True)
    grad_second = norm_back(grad_out, normed_two, inverse_two, np_ref[2:3, :])
    down = grad_second.astype(BF)
    down_ref[...] = down
    grad_first_norm = grad_second
    for c in range(chunks):
        cols = pl.ds(c * width, width)
        grad_hidden = dot_t(down, down_rows(c))
        up = (grad_hidden * slope_ref[:, cols]).astype(BF)
        up_ref[:, cols] = up
        grad_first_norm = grad_first_norm + dot_t(up, w1_ref[:, c].reshape(width, width))
    gain_one = jnp.sum(grad_first_norm * normed_one, axis=0, keepdims=True)
    shift_one = jnp.sum(grad_first_norm, axis=0, keepdims=True)
    grad_first = norm_back(grad_first_norm, normed_one, inverse_one, np_ref[0:1, :])
    dfirst_ref[...] = grad_first
    grad_branch = grad_first.astype(BF)
    dbranch_ref[...] = grad_branch
    dmix_ref[...] = dot_t(grad_branch, wo_ref[...]).astype(BF)
    sums = jnp.concatenate([gain_one, shift_one, gain_two, shift_two], axis=0)

    @pl.when(step == 0)
    def _():
        ng_ref[...] = sums

    @pl.when(step > 0)
    def _():
        ng_ref[...] += sums


def feed(first_sum, w_ffn, w_att, cotangent, norm_params, tile):
    rows, width = first_sum.shape
    groups, chunks, size, _ = w_ffn.shape
    groups = groups // 2
    ff = chunks * width
    row = lambda i: (i, 0)
    return pl.pallas_call(
        functools.partial(feed_body, chunks),
        grid=(rows // tile,),
        in_specs=[
            vspec((tile, width), row),
            vspec((groups, chunks, size, width), lambda i: (0, 0, 0, 0), True),
            vspec((groups, chunks, size, width), lambda i: (1, 0, 0, 0), True),
            vspec((width, width), lambda i: (3, 0), True),
            vspec((tile, width), row),
            vspec(norm_params.shape, lambda i: (0, 0)),
        ],
        out_specs=[
            vspec((tile, width), row),
            vspec((tile, ff), row),
            vspec((tile, ff), row),
            vspec((tile, width), row),
            vspec((tile, width), row),
            vspec((tile, width), row),
            vspec((tile, width), row),
            vspec((tile, width), row),
            vspec((4, width), lambda i: (0, 0)),
        ],
        out_shape=[
            jax.ShapeDtypeStruct((rows, width), BF),
            jax.ShapeDtypeStruct((rows, ff), BF),
            jax.ShapeDtypeStruct((rows, ff), BF),
            jax.ShapeDtypeStruct((rows, width), BF),
            jax.ShapeDtypeStruct((rows, width), BF),
            jax.ShapeDtypeStruct((rows, width), F32),
            jax.ShapeDtypeStruct((rows, width), BF),
            jax.ShapeDtypeStruct((rows, width), BF),
            jax.ShapeDtypeStruct((4, width), F32),
        ],
        scratch_shapes=[pltpu.VMEM((tile, ff), F32)],
        compiler_params=params(),
        cost_estimate=cost(2 * rows * width * ff * 4, 30e6, rows * ff * 2),
        name="feed",
    )(first_sum, w_ffn, w_ffn, w_att, cotangent, norm_params)


def pair_back(key_cols, value_cols, q, g, head, low_lane):
    kp = key_cols.shape[0]
    scale = head ** (-0.5)
    keys, values = head_pair(key_cols, low_lane), head_pair(value_cols, low_lane)
    prob = softmax_pair(dot_t(q, keys) * scale, kp)
    grad_prob = dot_t(g, values)
    low_parts = []
    for half in range(2):
        p = prob[half]
        d = grad_prob[:, half * kp : (half + 1) * kp]
        low_parts.append((p * (d - jnp.sum(p * d, axis=-1, keepdims=True))).astype(BF))
    grad_scores = jnp.concatenate(low_parts, axis=1)
    prob_low = jnp.concatenate(prob, axis=1).astype(BF)
    grad_q = (dot(grad_scores, keys) * scale).astype(BF)
    return grad_q, dot_l(grad_scores, q) * scale, dot_l(prob_low, g)


def attend_back_body(width, head, kp, c_ref, q_ref, s_ref, g_ref, dq_ref, ds_ref, head_ref, tail_ref, acc_ref):
    step = pl.program_id(0)
    last = pl.num_programs(0) - 1
    low_lane = lax.broadcasted_iota(jnp.int32, (kp, 2 * head), 1) < head

    def pair(j):
        cols = pl.ds(pl.multiple_of(j * 2 * head, 2 * head), 2 * head)
        vcols = pl.ds(pl.multiple_of(width + j * 2 * head, 2 * head), 2 * head)
        grads, dk, dv = pair_back(
            s_ref[0, :, cols], s_ref[0, :, vcols], q_ref[:, cols], g_ref[:, cols], head, low_lane
        )
        dq_ref[:, cols] = grads
        for at, both in ((cols, dk), (vcols, dv)):
            value = jnp.where(low_lane, both[:kp], both[kp:])
            ds_ref[0, :, at] = value
            for side, row, low_ref in ((0, 0, head_ref), (1, last, tail_ref)):
                before = jnp.where(step > 0, acc_ref[side, :, at], 0.0)
                total = before + c_ref[row, step] * value
                acc_ref[side, :, at] = total
                low_ref[:, at] = total.astype(BF)

    def two(i, carry):
        pair(2 * i)
        pair(2 * i + 1)
        return carry

    lax.fori_loop(0, width // (4 * head), two, 0)


def attend_back(coef, q, summary, grad_mix, head):
    rows, width = q.shape
    blocks, kp, _ = summary.shape
    short = rows // blocks
    row = lambda i, *_: (i, 0)
    lead = lambda i, *_: (i, 0, 0)
    return pl.pallas_call(
        functools.partial(attend_back_body, width, head, kp),
        grid_spec=pltpu.PrefetchScalarGridSpec(
            num_scalar_prefetch=1,
            grid=(blocks,),
            in_specs=[
                vspec((short, width), row),
                vspec((1, kp, 2 * width), lead),
                vspec((short, width), row),
            ],
            out_specs=[
                vspec((short, width), row),
                vspec((1, kp, 2 * width), lead),
                vspec((kp, 2 * width), lambda i, *_: (0, 0)),
                vspec((kp, 2 * width), lambda i, *_: (0, 0)),
            ],
            scratch_shapes=[pltpu.VMEM((2, kp, 2 * width), F32)],
        ),
        out_shape=[
            jax.ShapeDtypeStruct((rows, width), BF),
            jax.ShapeDtypeStruct((blocks, kp, 2 * width), F32),
            jax.ShapeDtypeStruct((kp, 2 * width), BF),
            jax.ShapeDtypeStruct((kp, 2 * width), BF),
        ],
        compiler_params=params(),
        cost_estimate=cost(2 * rows * width * 8 * kp, 10e6, rows * kp * 12),
        name="attend_back",
    )(coef, q, summary, grad_mix)


def outer_body(split, l_ref, r_ref, o_ref):
    value = dot_l(l_ref[...], r_ref[...])
    o_ref[...] = value.reshape(o_ref.shape).astype(o_ref.dtype)


def outer_up(first_low, grad_up, size, dtype):
    rows, width = first_low.shape
    chunks = grad_up.shape[1] // width
    groups = width // size
    return pl.pallas_call(
        functools.partial(outer_body, True),
        grid=(chunks,),
        in_specs=[
            vspec((rows, width), lambda i: (0, 0), True),
            vspec((rows, width), lambda i: (0, i)),
        ],
        out_specs=vspec((groups, 1, size, width), lambda i: (0, i, 0, 0)),
        out_shape=jax.ShapeDtypeStruct((groups, chunks, size, width), dtype),
        compiler_params=params(),
        cost_estimate=cost(2 * rows * width * width * chunks, 20e6),
        name="outer_up",
    )(first_low, grad_up)


def outer_rows(left, right, dtype, name):
    rows, width = right.shape[0], min(left.shape[1], right.shape[1])
    tall, wide = left.shape[1] // width, right.shape[1] // width
    moving = lambda n: (lambda i: (0, i)) if n > 1 else (lambda i: (0, 0))
    return pl.pallas_call(
        functools.partial(outer_body, False),
        grid=(tall * wide,),
        in_specs=[
            vspec((rows, width), moving(tall), tall == 1),
            vspec((rows, width), moving(wide), wide == 1),
        ],
        out_specs=vspec((width, width), lambda i: (i, 0)),
        out_shape=jax.ShapeDtypeStruct((tall * wide * width, width), dtype),
        compiler_params=params(),
        cost_estimate=cost(2 * rows * width * width * tall * wide, 20e6),
        name=name,
    )(left, right)


def backward_body(peers, head, chunks, c_ref, q_ref, s_ref, g_ref, *refs):
    sources, outs = refs[:7], refs[7:13]
    grad_outs, scratch = refs[13:17], refs[17:]
    dq_ref, ds_ref, far_refs = outs[0], outs[1], outs[2:]
    held, (low_head, low_tail, g_down, g_up, g_out, g_query) = scratch[:7], scratch[7:13]
    send, recv, local = scratch[13:]
    blocks, kp, wide = s_ref.shape
    width = wide // 2
    short = q_ref.shape[0] // blocks
    pairs = width // (2 * head)
    seq, mine = lax.axis_index("seq"), lax.axis_index("own")
    loads = [pltpu.make_async_copy(sources[k], held[k], local.at[k]) for k in range(7)]
    for load in loads:
        load.start()

    def place(d):
        return (lax.rem(seq + peers + d, peers), mine)

    steps = (1, -1, 2, -2)
    inside = lambda d: seq < peers - d if d > 0 else seq >= -d
    can_send = [inside(d) for d in steps]
    can_get = [inside(-d) for d in steps]
    barrier = pltpu.get_barrier_semaphore()
    for k in range(4):

        @pl.when(can_send[k])
        def _():
            pl.semaphore_signal(barrier, inc=1, device_id=place(steps[k]), device_id_type=MESH_ID)

        @pl.when(jnp.logical_not(can_get[k]))
        def _():
            far_refs[k][...] = jnp.zeros_like(far_refs[k])

    pl.semaphore_wait(barrier, jnp.minimum(seq, 2) + jnp.minimum(peers - 1 - seq, 2))
    low_lane = lax.broadcasted_iota(jnp.int32, (kp, 2 * head), 1) < head

    def columns(j):
        at = pl.multiple_of(j * 2 * head, 2 * head)
        return pl.ds(at, 2 * head), pl.ds(pl.multiple_of(width + at, 2 * head), 2 * head)

    def message(j, k, kind):
        low = (low_tail, low_head)[k % 2]
        cols = columns(j)[kind]
        return pltpu.make_async_remote_copy(
            src_ref=low.at[:, cols],
            dst_ref=far_refs[k].at[:, cols],
            send_sem=send.at[j, k, kind],
            recv_sem=recv.at[j, k, kind],
            device_id=place(steps[k]),
            device_id_type=MESH_ID,
        )

    def pair(j, carry):
        cols, vcols = columns(j)
        head_sums, tail_sums = [0.0, 0.0], [0.0, 0.0]
        for b in range(blocks):
            rows = pl.ds(b * short, short)
            grads, dk, dv = pair_back(
                s_ref[b, :, cols], s_ref[b, :, vcols], q_ref[rows, cols], g_ref[rows, cols], head, low_lane
            )
            dq_ref[rows, cols] = grads
            for kind, at, both in ((0, cols, dk), (1, vcols, dv)):
                value = jnp.where(low_lane, both[:kp], both[kp:])
                ds_ref[b, :, at] = value
                head_sums[kind] = head_sums[kind] + c_ref[0, b] * value
                tail_sums[kind] = tail_sums[kind] + c_ref[blocks - 1, b] * value
        for kind, at in ((0, cols), (1, vcols)):
            low_head[:, at] = head_sums[kind].astype(BF)
            low_tail[:, at] = tail_sums[kind].astype(BF)
        for k in range(4):

            @pl.when(can_send[k])
            def _():
                for kind in range(2):
                    message(j, k, kind).start()

        return carry

    lax.fori_loop(0, pairs, pair, 0)
    first_low, grad_up, hidden, grad_down, mixed, grad_branch, x = held
    stores = []

    def store(src, dst):
        copy = pltpu.make_async_copy(src, dst, local.at[7 + len(stores)])
        copy.start()
        stores.append(copy)

    for load in loads:
        load.wait()

    def down_chunk(i, carry):
        at = pl.ds(pl.multiple_of(i * width, width), width)
        g_down[at, :] = dot_l(hidden[:, at], grad_down[...]).astype(BF)
        return carry

    def up_chunk(i, carry):
        at = pl.ds(pl.multiple_of(i * width, width), width)
        value = dot_l(first_low[...], grad_up[:, at]).astype(BF)
        g_up[:, i] = value.reshape(g_up.shape[0], g_up.shape[2], width)
        return carry

    lax.fori_loop(0, chunks, down_chunk, 0)
    store(g_down, grad_outs[0])
    lax.fori_loop(0, chunks, up_chunk, 0)
    store(g_up, grad_outs[1])
    g_out[...] = dot_l(mixed[...], grad_branch[...]).astype(BF)
    store(g_out, grad_outs[2])
    g_query[...] = dot_l(x[...], dq_ref[...]).astype(BF)
    store(g_query, grad_outs[3])

    def finish(j, carry):
        for k in range(4):

            @pl.when(can_get[k])
            def _():
                for kind in range(2):
                    message(j, k, kind).wait_recv()

            @pl.when(can_send[k])
            def _():
                for kind in range(2):
                    message(j, k, kind).wait_send()

        return carry

    lax.fori_loop(0, pairs, finish, 0)
    for copy in stores:
        copy.wait()


def backward(coef, q, summary, grad_mix, operands, head, peers, size):
    rows, width = q.shape
    blocks, kp, _ = summary.shape
    chunks = operands[1].shape[1] // width
    groups = width // size
    vmem, smem = pl.BlockSpec(memory_space=pltpu.VMEM), pl.BlockSpec(memory_space=pltpu.SMEM)
    far = jax.ShapeDtypeStruct((kp, 2 * width), BF)
    products = [(chunks * width, width), (groups, chunks, size, width), (width, width), (width, width)]
    pairs = width // (2 * head)
    return pl.pallas_call(
        functools.partial(backward_body, peers, head, chunks),
        in_specs=[smem] + [vmem] * 3 + [pl.BlockSpec(memory_space=pl.ANY)] * 7,
        out_specs=[vmem] * 6 + [pl.BlockSpec(memory_space=pl.ANY)] * 4,
        out_shape=[
            jax.ShapeDtypeStruct((rows, width), BF),
            jax.ShapeDtypeStruct((blocks, kp, 2 * width), F32),
        ]
        + [far] * 4
        + [jax.ShapeDtypeStruct(shape, BF) for shape in products],
        scratch_shapes=[pltpu.VMEM(a.shape, BF) for a in operands]
        + [pltpu.VMEM(far.shape, BF)] * 2
        + [pltpu.VMEM(shape, BF) for shape in products]
        + [
            pltpu.SemaphoreType.DMA((pairs, 4, 2)),
            pltpu.SemaphoreType.DMA((pairs, 4, 2)),
            pltpu.SemaphoreType.DMA((11,)),
        ],
        compiler_params=pltpu.CompilerParams(
            collective_id=4, has_side_effects=True, vmem_limit_bytes=VMEM_LIMIT
        ),
        cost_estimate=cost(2 * rows * width * (8 * kp + 10 * width), 60e6, rows * kp * 12),
        name="backward",
    )(coef, q, summary, grad_mix, *operands)


def pack_sums(out_ref, gp_ref, norm_ref, sums_ref):
    depth, _, _, tall, kp = out_ref.shape
    each = tall - 8
    per = norm_ref.shape[1] // kp
    rows = [(norm_ref, i, j) for i in range(4) for j in range(per)]
    rows += [(sums_ref, i, j) for i in range(3) for j in range(per)]
    top = lax.broadcasted_iota(jnp.int32, (8, kp), 0) == 0
    for device in range(8 * depth):
        z, y, x, c = device // 8, device // 4 % 2, device // 2 % 2, device % 2
        at = ((2 * x + c) * 2 * depth + 2 * z + y) * each
        out_ref[z, 2 * y + x, c, pl.ds(0, each), :] = gp_ref[pl.ds(at, each), :]
        if device < len(rows):
            ref, i, j = rows[device]
            line = jnp.where(top, ref[pl.ds(i, 1), pl.ds(j * kp, kp)], 0.0)
        else:
            line = jnp.zeros((8, kp), F32)
        out_ref[z, 2 * y + x, c, pl.ds(each, 8), :] = line


def back_body(width, blocks, packed, c_ref, n_ref, e_ref, kv_ref, p_ref, *refs):
    far_refs = refs[:4]
    dq_ref, w_ref, df_ref = refs[4:7]
    if packed:
        x_ref, norm_ref, sums_ref, gkv_ref, out_ref, gi_ref, gp_ref, acc_ref = refs[7:]
    else:
        dkv_ref, gp_ref, gi_ref = refs[7:]
    step = pl.program_id(0)
    short, kp = e_ref.shape[1], e_ref.shape[2]
    total = c_ref[step, 0] * p_ref[0]
    for other in range(1, blocks):
        total = total + c_ref[step, other] * p_ref[other]
    for k in range(4):
        total = total + c_ref[step, blocks + k] * far_refs[k][...].astype(F32)
    summary = total.astype(BF)
    dkv = dot(e_ref[0], summary).astype(BF)
    keep = lax.broadcasted_iota(jnp.int32, (short, 1), 0) < n_ref[1, step]
    grad_e = jnp.where(keep, dot_t(kv_ref[...], summary), 0.0)
    column = n_ref[0, step]
    at = pl.multiple_of(jnp.minimum((column // 8) * 8, gp_ref.shape[0] - short - 8), 8)
    moved = pltpu.roll(
        jnp.concatenate([grad_e, jnp.zeros((8, kp), F32)], axis=0), column - at, 0
    )

    @pl.when(step == 0)
    def _():
        gp_ref[...] = jnp.zeros_like(gp_ref)

    gp_ref[pl.ds(at, short + 8), :] += moved
    gi_ref[...] = (
        df_ref[...]
        + dot_t(dq_ref[...], w_ref[pl.ds(0, width), :])
        + dot_t(dkv[:, :width], w_ref[pl.ds(width, width), :])
        + dot_t(dkv[:, width:], w_ref[pl.ds(2 * width, width), :])
    )
    if not packed:
        dkv_ref[...] = dkv
        return
    for kind in range(2):
        rows = pl.ds(kind * width, width)
        value = dot_l(x_ref[...], dkv[:, kind * width : (kind + 1) * width])
        value = value + jnp.where(step > 0, acc_ref[rows, :], 0.0)
        acc_ref[rows, :] = value
        gkv_ref[rows, :] = value.astype(BF)

    @pl.when(step == blocks - 1)
    def _():
        pack_sums(out_ref, gp_ref, norm_ref, sums_ref)


def back(coef, places, e_rows, kv, grad_parts, far_parts, dq, w_att, grad_first, positions, small=None, depth=0):
    rows, width = dq.shape
    blocks, short, kp = e_rows.shape
    row = lambda i, *_: (i, 0)
    lead = lambda i, *_: (i, 0, 0)
    fixed = lambda i, *_: (0, 0)
    packed = small is not None
    more_specs, scratch = [], []
    if packed:
        tall = positions // (8 * depth) + 8
        more_specs = [
            vspec((short, width), row),
            vspec(small[1].shape, fixed),
            vspec(small[2].shape, fixed),
        ]
        first_spec, second_spec = (
            vspec((2 * width, width), fixed),
            vspec((depth, 4, 2, tall, kp), lambda i, *_: (0,) * 5),
        )
        first_out = jax.ShapeDtypeStruct((2 * width, width), BF)
        second_out = jax.ShapeDtypeStruct((depth, 4, 2, tall, kp), F32)
        scratch = [pltpu.VMEM((positions, kp), F32), pltpu.VMEM((2 * width, width), F32)]
    else:
        first_spec, second_spec = vspec((short, 2 * width), row), vspec((positions, kp), fixed)
        first_out = jax.ShapeDtypeStruct((rows, 2 * width), BF)
        second_out = jax.ShapeDtypeStruct((positions, kp), F32)
    return pl.pallas_call(
        functools.partial(back_body, width, blocks, packed),
        grid_spec=pltpu.PrefetchScalarGridSpec(
            num_scalar_prefetch=2,
            grid=(blocks,),
            in_specs=[
                vspec((1, short, kp), lead),
                vspec((short, 2 * width), row),
                vspec(grad_parts.shape, lambda i, *_: (0, 0, 0), True),
            ]
            + [vspec((kp, 2 * width), fixed, True)] * 4
            + [
                vspec((short, width), row),
                vspec((3 * width, width), fixed, True),
                vspec((short, width), row),
            ]
            + more_specs,
            out_specs=[first_spec, second_spec, vspec((short, width), row)],
            scratch_shapes=scratch,
        ),
        out_shape=[first_out, second_out, jax.ShapeDtypeStruct((rows, width), F32)],
        compiler_params=params(),
        cost_estimate=cost(2 * rows * width * (3 * width + 4 * kp), 20e6),
        name="back",
    )(coef, places, e_rows, kv, grad_parts, *far_parts, dq, w_att, grad_first, *(small or ()))


def reduce_body(depth, half, n_src, extra_keep, *refs):
    sources = refs[:n_src]
    grads, shares_out, rows_out = refs[n_src : n_src + 3]
    (own, got_c, sum_c, got_a, got_b, sum_a, sum_b, got_a2, got_b2, sum_z, got_z) = refs[
        n_src + 3 : n_src + 14
    ]
    keep_a, keep_b, keep_z = refs[n_src + 14 : n_src + 17]
    (e_own, e_got, e_sum, e_got1, e_sum1, e_got2, e_sum2, e_gotz, e_all, e_rows) = refs[
        n_src + 17 : n_src + 27
    ]
    send, recv, local = refs[n_src + 27 :]
    seq, mine = lax.axis_index("seq"), lax.axis_index("own")
    z, y, x, c = seq // 2, seq % 2, mine // 2, mine % 2
    core = (seq, 2 * x + (1 - c))
    along_x = (seq, 2 * (1 - x) + c)
    along_y = (2 * z + (1 - y), mine)
    along_z = [(2 * lax.rem(z + d, depth) + y, mine) for d in range(1, depth)]
    barrier = pltpu.get_barrier_semaphore()
    partners = [core, along_x, along_y] + along_z
    for partner in partners:
        pl.semaphore_signal(barrier, inc=1, device_id=partner, device_id_type=MESH_ID)
    pl.semaphore_wait(barrier, len(partners))

    sent = []

    def push(src, dst, partner):
        at = len(sent)
        copy = pltpu.make_async_remote_copy(
            src_ref=src,
            dst_ref=dst,
            send_sem=send.at[at],
            recv_sem=recv.at[at],
            device_id=partner,
            device_id_type=MESH_ID,
        )
        copy.start()
        sent.append(copy)
        return copy

    up, down, g_query, g_keyval, g_out, extra = sources
    bands = [g_query, g_keyval.at[0], g_keyval.at[1], g_out]
    half_z = depth // 2
    cols = own.shape[-1]
    loads = []

    def load(src, dst):
        copy = pltpu.make_async_copy(src, dst, local.at[len(loads)])
        copy.start()
        loads.append(copy)
        return copy

    e_first = [push(extra.at[:, :, 1 - c], e_got, core)]
    e_load = [load(extra.at[:, :, c], e_own)]
    piece_first, piece_load = [], []

    def piece_core(p):
        at, part = p // 2, pl.ds((p % 2) * cols, cols)
        if at < 2:
            first = [
                push(up.at[:, :, 1 - c, at, :, part], got_c.at[p, pl.ds(0, half_z)], core),
                push(down.at[:, :, 1 - c, at, :, part], got_c.at[p, pl.ds(half_z, half_z)], core),
            ]
            kept = [
                load(up.at[:, :, c, at, :, part], own.at[p, pl.ds(0, half_z)]),
                load(down.at[:, :, c, at, :, part], own.at[p, pl.ds(half_z, half_z)]),
            ]
        else:
            first = [
                push(bands[m].at[:, 1 - c, :, part], got_c.at[p, m], core) for m in range(depth)
            ]
            kept = [load(bands[m].at[:, c, :, part], own.at[p, m]) for m in range(depth)]
        piece_first.append(first)
        piece_load.append(kept)

    state = {}

    def wait_recv(copies):
        for copy in copies:
            copy.wait_recv()

    low, high = pl.ds(0, half), pl.ds(half, half)

    def add(a, b):
        return a.astype(F32) + b.astype(F32)

    def piece_c(p):
        for copy in piece_load[p]:
            copy.wait()
        wait_recv(piece_first[p])

        def body(i, carry):
            zz, w = i // 2, i % 2
            to_x, to_y = 2 * w + 1 - x, 2 * (1 - y) + w
            sum_c[p, 0, zz, w] = add(own[p, zz, to_x, low, :], got_c[p, zz, to_x, low, :]).astype(BF)
            sum_c[p, 1, zz, w] = add(own[p, zz, to_y, high, :], got_c[p, zz, to_y, high, :]).astype(BF)
            return carry

        lax.fori_loop(0, depth * 2, body, 0)
        state["1", p] = [
            push(sum_c.at[p, 0], got_a.at[p], along_x),
            push(sum_c.at[p, 1], got_b.at[p], along_y),
        ]

    def piece_1(p):
        wait_recv(state["1", p])

        def side_a(zz, w):
            at = 2 * w + x
            return add(own[p, zz, at, low, :], got_c[p, zz, at, low, :]) + got_a[p, zz, w].astype(F32)

        def side_b(zz, w):
            at = 2 * y + w
            return add(own[p, zz, at, high, :], got_c[p, zz, at, high, :]) + got_b[p, zz, w].astype(F32)

        def body(zz, carry):
            sum_a[p, zz] = side_a(zz, 1 - y).astype(BF)
            sum_b[p, zz] = side_b(zz, 1 - x).astype(BF)
            keep_a[p, zz] = side_a(zz, y)
            keep_b[p, zz] = side_b(zz, x)
            return carry

        lax.fori_loop(0, depth, body, 0)
        state["2", p] = [
            push(sum_a.at[p], got_a2.at[p], along_y),
            push(sum_b.at[p], got_b2.at[p], along_x),
        ]

    def piece_2(p):
        wait_recv(state["2", p])

        def body(zz, carry):
            total_a = keep_a[p, zz] + got_a2[p, zz].astype(F32)
            total_b = keep_b[p, zz] + got_b2[p, zz].astype(F32)
            sum_z[p, zz, low, :] = total_a.astype(BF)
            sum_z[p, zz, high, :] = total_b.astype(BF)
            return carry

        lax.fori_loop(0, depth, body, 0)
        keep_z[p, low, :] = keep_a[p, z] + got_a2[p, z].astype(F32)
        keep_z[p, high, :] = keep_b[p, z] + got_b2[p, z].astype(F32)
        state["z", p] = [
            push(sum_z.at[p, lax.rem(z + d, depth)], got_z.at[p, d - 1], along_z[d - 1])
            for d in range(1, depth)
        ]

    def piece_z(p):
        wait_recv(state["z", p])
        total = keep_z[p]
        for d in range(depth - 1):
            total = total + got_z[p, d].astype(F32)
        grads[(p // 2 + 1) % 3, :, pl.ds((p % 2) * cols, cols)] = total

    def extra_c():
        e_load[0].wait()
        wait_recv(e_first)

        def body(i, carry):
            zz, yx = i // 4, i % 4
            e_sum[zz, yx // 2, yx % 2] = e_own[zz, yx] + e_got[zz, yx]
            return carry

        lax.fori_loop(0, depth * 4, body, 0)
        state["ez"] = [
            push(e_sum.at[lax.rem(z + d, depth)], e_gotz.at[d - 1], along_z[d - 1])
            for d in range(1, depth)
        ]

    def extra_1():
        wait_recv(state["ez"])

        def body(i, carry):
            yy, xx = i // 2, i % 2
            total = e_sum[z, yy, xx]
            for d in range(depth - 1):
                total = total + e_gotz[d, yy, xx]
            e_sum1[yy, xx] = total
            return carry

        lax.fori_loop(0, 4, body, 0)
        state["e1"] = [push(e_sum1.at[:, 1 - x], e_got1, along_x)]

    def extra_2():
        wait_recv(state["e1"])

        def body(yy, carry):
            e_sum2[yy] = e_sum1[yy, x] + e_got1[yy]
            return carry

        lax.fori_loop(0, 2, body, 0)
        state["e2"] = [push(e_sum2.at[1 - y], e_got2, along_y)]

    def extra_z():
        wait_recv(state["e2"])
        e_all[z, y] = e_sum2[y] + e_got2[...]
        state["gz"] = [push(e_all.at[z, y], e_all.at[z, y], there) for there in along_z]

    def extra_gather_y():
        wait_recv(state["gz"])
        state["gy"] = [push(e_all.at[:, y], e_all.at[:, y], along_y)]

    def extra_gather_x():
        wait_recv(state["gy"])
        e_rows[x, c] = e_all[:, :, pl.ds(extra_keep, e_rows.shape[4]), :]
        state["gx"] = [push(e_rows.at[x, c], e_rows.at[x, c], along_x)]

    def extra_gather_c():
        wait_recv(state["gx"])
        state["gc"] = [push(e_rows.at[:, c], e_rows.at[:, c], core)]

    stages = [piece_c, piece_1, piece_2, piece_z]
    small = {0: extra_c, 3: extra_1, 4: extra_2, 5: extra_z, 6: extra_gather_y}
    small |= {7: extra_gather_x, 8: extra_gather_c}
    piece_core(0)
    piece_core(1)
    for turn in range(9):
        for stage in range(4):
            if 0 <= turn - stage < 6:
                stages[stage](turn - stage)
            if stage == 0 and turn + 2 < 6:
                piece_core(turn + 2)
        if turn in small:
            small[turn]()
    shares_out[...] = e_all[:, :, pl.ds(0, extra_keep), :]
    wait_recv(state["gc"])
    rows_out[...] = e_rows[...]
    for copy in sent:
        copy.wait_send()


def reduce_all(g_query, g_keyval, g_out, g_up, g_down, extra, peers):
    depth = peers // 2
    size, width = g_up.shape[2], g_up.shape[3]
    half = size // 2
    e_rows_all, kp = extra.shape[-2:]
    keep = e_rows_all - 8
    sources = (
        [
            g_up.reshape(depth // 2, 4, 2, 2, size, width),
            g_down.reshape(depth // 2, 4, 2, 2, size, width),
        ]
        + [
            g_query.reshape(4, 2, size, width),
            g_keyval.reshape(2, 4, 2, size, width),
            g_out.reshape(4, 2, size, width),
        ]
        + [extra]
    )
    n_src = len(sources)
    cols = width // 2
    messages = 1 + 8 + 2 * depth + 6 * (4 + depth - 1) + 2 + 2 * (depth - 1) + 3
    loads = 1 + 8 + 2 * depth
    any_spec = pl.BlockSpec(memory_space=pl.ANY)
    vmem = pl.BlockSpec(memory_space=pltpu.VMEM)
    scratch = [
        pltpu.VMEM((6, depth, 4, size, cols), BF),
        pltpu.VMEM((6, depth, 4, size, cols), BF),
        pltpu.VMEM((6, 2, depth, 2, half, cols), BF),
        pltpu.VMEM((6, depth, 2, half, cols), BF),
        pltpu.VMEM((6, depth, 2, half, cols), BF),
        pltpu.VMEM((6, depth, half, cols), BF),
        pltpu.VMEM((6, depth, half, cols), BF),
        pltpu.VMEM((6, depth, half, cols), BF),
        pltpu.VMEM((6, depth, half, cols), BF),
        pltpu.VMEM((6, depth, size, cols), BF),
        pltpu.VMEM((6, depth - 1, size, cols), BF),
        pltpu.VMEM((6, depth, half, cols), F32),
        pltpu.VMEM((6, depth, half, cols), F32),
        pltpu.VMEM((6, size, cols), F32),
        pltpu.VMEM((depth, 4, e_rows_all, kp), F32),
        pltpu.VMEM((depth, 4, e_rows_all, kp), F32),
        pltpu.VMEM((depth, 2, 2, e_rows_all, kp), F32),
        pltpu.VMEM((2, e_rows_all, kp), F32),
        pltpu.VMEM((2, 2, e_rows_all, kp), F32),
        pltpu.VMEM((e_rows_all, kp), F32),
        pltpu.VMEM((2, e_rows_all, kp), F32),
        pltpu.VMEM((depth - 1, 2, 2, e_rows_all, kp), F32),
        pltpu.VMEM((depth, 2, e_rows_all, kp), F32),
        pltpu.VMEM((2, 2, depth, 2, 8, kp), F32),
        pltpu.SemaphoreType.DMA((messages,)),
        pltpu.SemaphoreType.DMA((messages,)),
        pltpu.SemaphoreType.DMA((loads,)),
    ]
    return pl.pallas_call(
        functools.partial(reduce_body, depth, half, n_src, keep),
        in_specs=[any_spec] * n_src,
        out_specs=[vmem] * 3,
        out_shape=[
            jax.ShapeDtypeStruct((3, size, width), F32),
            jax.ShapeDtypeStruct((depth, 2, keep, kp), F32),
            jax.ShapeDtypeStruct((2, 2, depth, 2, 8, kp), F32),
        ],
        scratch_shapes=scratch,
        compiler_params=pltpu.CompilerParams(
            collective_id=1, has_side_effects=True, vmem_limit_bytes=VMEM_LIMIT
        ),
        name="reduce_all",
    )(*sources)


def gather_body(depth, band_ref, proj_ref, out_ref, pout_ref, send, recv, local):
    seq, mine = lax.axis_index("seq"), lax.axis_index("own")
    z, y, x, c = seq // 2, seq % 2, mine // 2, mine % 2
    core = (seq, 2 * x + (1 - c))
    along_x = (seq, 2 * (1 - x) + c)
    along_y = (2 * z + (1 - y), mine)
    order = [1, 3, 2]
    along_z = [(2 * lax.rem(z + d, depth) + y, mine) for d in order]
    barrier = pltpu.get_barrier_semaphore()
    partners = [core, along_x, along_y] + along_z
    for partner in partners:
        pl.semaphore_signal(barrier, inc=1, device_id=partner, device_id_type=MESH_ID)
    pl.semaphore_wait(barrier, len(partners))

    sent = []

    def push(src, dst, partner):
        at = len(sent)
        copy = pltpu.make_async_remote_copy(
            src_ref=src,
            dst_ref=dst,
            send_sem=send.at[at],
            recv_sem=recv.at[at],
            device_id=partner,
            device_id_type=MESH_ID,
        )
        copy.start()
        sent.append(copy)
        return copy

    keep = pltpu.make_async_copy(band_ref, out_ref.at[z, y, x, c], local.at[0])
    keep.start()
    keep_p = pltpu.make_async_copy(proj_ref, pout_ref.at[x, c], local.at[1])
    keep_p.start()
    mine_at = out_ref.at[z, y, x, c]
    from_z = [push(band_ref, mine_at, there) for there in along_z]
    from_x = [push(band_ref, mine_at, along_x)]
    from_y = [push(band_ref, mine_at, along_y)]
    proj_x = push(proj_ref, pout_ref.at[x, c], along_x)
    last = [push(band_ref, mine_at, core), push(proj_ref, pout_ref.at[x, c], core)]
    planes = [z]
    for k in range(depth - 1):
        from_z[k].wait_recv()
        plane = lax.rem(z + depth - order[k], depth)
        planes.append(plane)
        slab = out_ref.at[plane, y, x, c]
        from_x.append(push(slab, slab, along_x))
        from_y.append(push(slab, slab, along_y))
        last.append(push(slab, slab, core))
    cross = []
    for k in range(depth):
        plane = planes[k]
        from_y[k].wait_recv()
        slab = out_ref.at[plane, 1 - y, x, c]
        cross.append(push(slab, slab, along_x))
        last.append(push(slab, slab, core))
        from_x[k].wait_recv()
        slab = out_ref.at[plane, y, 1 - x, c]
        last.append(push(slab, slab, core))
        if k == 0:
            proj_x.wait_recv()
            slab = pout_ref.at[1 - x, c]
            last.append(push(slab, slab, core))
    for k in range(depth):
        cross[k].wait_recv()
        slab = out_ref.at[planes[k], 1 - y, 1 - x, c]
        last.append(push(slab, slab, core))
    for copy in last:
        copy.wait_recv()
    keep.wait()
    keep_p.wait()
    for copy in sent:
        copy.wait_send()


def gather_bands(band, proj, peers):
    depth = peers // 2
    size, width = band.shape
    messages = (depth - 1) + 3 + 2 + 3 * (depth - 1) + 3 * depth + 1 + depth
    vmem = pl.BlockSpec(memory_space=pltpu.VMEM)
    return pl.pallas_call(
        functools.partial(gather_body, depth),
        in_specs=[vmem] * 2,
        out_specs=[vmem] * 2,
        out_shape=[
            jax.ShapeDtypeStruct((depth, 2, 2, 2, size, width), BF),
            jax.ShapeDtypeStruct((2, 2) + proj.shape, BF),
        ],
        scratch_shapes=[
            pltpu.SemaphoreType.DMA((messages,)),
            pltpu.SemaphoreType.DMA((messages,)),
            pltpu.SemaphoreType.DMA((2,)),
        ],
        compiler_params=pltpu.CompilerParams(
            collective_id=2, has_side_effects=True, vmem_limit_bytes=VMEM_LIMIT
        ),
        cost_estimate=cost(1e9, 90e6),
        name="gather_bands",
    )(band, proj)


def shampoo(grad, left, right, root_left, root_right, weight):
    new_left = decay * left + (1.0 - decay) * jnp.einsum(
        "tij,tkj->tik", grad, grad, precision=highest
    )
    new_right = decay * right + (1.0 - decay) * jnp.einsum(
        "tji,tjk->tik", grad, grad, precision=highest
    )
    inner = jnp.einsum("tij,tjk->tik", grad, root_right, precision=highest)
    step = jnp.einsum("tij,tjk->tik", root_left, inner, precision=highest)
    return (new_left, new_right, weight - rate_matrix * step)


def exact(a, b, left, right):
    return lax.dot_general(
        a, b, (((left,), (right,)), ((), ())), precision=highest, preferred_element_type=F32
    )


def step_body(bands, *refs):
    band_ref, tiles, proj_ref, blocks = refs[0], refs[1:6], refs[6], refs[7:12]
    rows_ref, norm_ref, second_ref = refs[12:15]
    owned_ref, new_tiles, new_blocks = refs[15], refs[16:19], refs[19:22]
    grad_ref, second_new_ref, norm_new_ref, rms_ref = refs[22:]
    at = pl.program_id(0)
    size, kp = tiles[0].shape[1], proj_ref.shape[-1]

    def update(grad, state, new, t):
        left, right, root_left, root_right, weight = (ref[t] for ref in state)
        new[0][t] = decay * left + (1.0 - decay) * exact(grad, grad, 1, 1)
        new[1][t] = decay * right + (1.0 - decay) * exact(grad, grad, 0, 0)
        new[2][t] = weight - rate_matrix * exact(root_left, exact(grad, root_right, 1, 0), 1, 0)

    @pl.when(at < bands)
    def _():
        def four(i, carry):
            part = band_ref[0, :, pl.ds(pl.multiple_of(i * 4 * size, 128), 4 * size)]
            for t in range(4):
                grad = part[:, t * size : (t + 1) * size]
                owned_ref[4 * i + t] = grad
                update(grad, tiles, new_tiles, 4 * i + t)
            return carry

        lax.fori_loop(0, tiles[0].shape[0] // 4, four, 0)

    @pl.when(at >= bands)
    def _():
        update(proj_ref[0], blocks, new_blocks, 0)

    @pl.when(at == bands)
    def _():
        depth = rows_ref.shape[2]

        def row(r):
            return rows_ref[r // 2 % 2, r % 2, r // 8 % depth, r // 4 % 2, pl.ds(0, 1), :]

        per = norm_ref.shape[1] // kp
        for i in range(4):
            grad = jnp.concatenate([row(per * i + j) for j in range(per)], axis=1)
            grad_ref[pl.ds(i, 1), :] = grad
            second = decay * second_ref[pl.ds(i, 1), :] + (1.0 - decay) * grad * grad
            second_new_ref[pl.ds(i, 1), :] = second
            norm_new_ref[pl.ds(i, 1), :] = norm_ref[pl.ds(i, 1), :] - rate_norm * grad * lax.rsqrt(second)
        count = jnp.sum(sum(row(6 * per + j) for j in range(per)), axis=1, keepdims=True)
        for i in range(2):
            square = row(4 * per + per * i)
            for j in range(1, per):
                square = square + row(4 * per + per * i + j)
            total = jnp.sum(square, axis=1, keepdims=True)
            ratio = jnp.sqrt(total / (count * norm_ref.shape[1]))
            rms_ref[i] = jnp.sum(ratio)


def step_all(bands, tiles, proj_grad, blocks, rows, norm_params, norm_stat):
    count, size, width = bands.shape
    each, kp = width // size, proj_grad.shape[-1]
    n_blocks = proj_grad.shape[0]
    tile = lambda: vspec((each, size, size), lambda i: (jnp.minimum(i, count - 1), 0, 0))
    block = lambda: vspec((1, kp, kp), lambda i: (jnp.maximum(i - count, 0), 0, 0))
    whole = lambda a: vspec(a.shape, lambda i: (0,) * len(a.shape))
    like = lambda a: jax.ShapeDtypeStruct(a.shape, F32)
    rms = jax.ShapeDtypeStruct((2,), F32)
    return pl.pallas_call(
        functools.partial(step_body, count),
        grid=(count + n_blocks,),
        in_specs=[vspec((1, size, width), lambda i: (jnp.minimum(i, count - 1), 0, 0))]
        + [tile() for _ in range(5)]
        + [block() for _ in range(6)]
        + [whole(rows), whole(norm_params), whole(norm_stat)],
        out_specs=[tile() for _ in range(4)]
        + [block() for _ in range(3)]
        + [whole(norm_params)] * 3
        + [pl.BlockSpec(memory_space=pltpu.SMEM)],
        out_shape=[like(tiles[0])] * 4 + [like(proj_grad)] * 3 + [like(norm_params)] * 3 + [rms],
        compiler_params=params(),
        cost_estimate=cost(1e9, 20e6),
        name="step_all",
    )(bands, *tiles, proj_grad, *blocks, rows, norm_params, norm_stat)


def to_matrix(tiles, rows, cols):
    size = tiles.shape[-1]
    return (
        tiles.reshape(rows // size, cols // size, size, size)
        .transpose(0, 2, 1, 3)
        .reshape(rows, cols)
    )


def to_bands(tiles, cols):
    count, size, _ = tiles.shape
    return to_matrix(tiles, count * size * size // cols, cols)


def from_bands(bands, size):
    rows, cols = bands.shape
    return (
        bands.reshape(rows // size, size, cols // size, size)
        .transpose(0, 2, 1, 3)
        .reshape(-1, size, size)
    )


def bands_body(w_ref, p_ref, att_ref, ffn_ref, proj_ref):
    count, size, _ = w_ref.shape
    wide = att_ref.shape[1] // size
    near = att_ref.shape[0] // size
    for k in range(count):
        at, cols = k // wide, pl.ds(k % wide * size, size)
        tile = w_ref[k].astype(BF)
        if at < near:
            att_ref[pl.ds(at * size, size), cols] = tile
        else:
            ffn_ref[pl.ds((at - near) * size, size), cols] = tile
    proj_ref[...] = p_ref[...].astype(BF)


def make_bands(weights, projection, att_dev, width):
    per_dev, size, _ = weights.shape
    near = att_dev * size // width * size
    return pl.pallas_call(
        bands_body,
        out_shape=[
            jax.ShapeDtypeStruct((near, width), BF),
            jax.ShapeDtypeStruct((per_dev * size // width * size - near, width), BF),
            jax.ShapeDtypeStruct(projection.shape, BF),
        ],
        compiler_params=pltpu.CompilerParams(vmem_limit_bytes=VMEM_LIMIT),
        name="make_bands",
    )(weights, projection)


def gather_weights(weights, projection, att_dev, width, both, fused, peers):
    size = weights.shape[-1]
    low = weights.astype(BF)
    groups, chunks = width // size, FF // width
    if banded(weights.shape[0], att_dev, width, size):
        band, far, proj_low = make_bands(weights, projection, att_dev, width)
        ffn = lax.all_gather(far, both, axis=0, tiled=True)
        if fused:
            att, proj = gather_bands(band, proj_low, peers)
            att, proj = att.reshape(-1, width), proj.reshape(-1, projection.shape[1])
        else:
            att = lax.all_gather(band, both, axis=0, tiled=True)
            proj = lax.all_gather(proj_low, "own", axis=0, tiled=True)
        return att, ffn.reshape(2 * groups, chunks, size, width), proj
    per_dev = weights.shape[0]
    proj = lax.all_gather(projection.astype(BF), "own", axis=0, tiled=True)
    grid = lax.all_gather(low, both, axis=0, tiled=True).reshape(-1, per_dev, size, size)
    att = to_bands(grid[:, :att_dev].reshape(-1, size, size), width)
    tiles = grid[:, att_dev:].reshape(-1, size, size)
    half = tiles.shape[0] // 2
    w_up = to_matrix(tiles[:half], width, FF).reshape(groups, size, chunks, width)
    w_down = to_matrix(tiles[half:], FF, width).reshape(groups, chunks, size, width)
    return att, jnp.concatenate([w_up.transpose(0, 2, 1, 3), w_down], axis=0), proj


def banded(per_dev, att_dev, width, size):
    wide = width // size
    return att_dev % wide == 0 and (per_dev - att_dev) % wide == 0


def scatter_weight_grads(g_att, g_up, g_down, per_dev, att_dev, both):
    size, width = g_up.shape[2], g_up.shape[3]
    if banded(per_dev, att_dev, width, size):
        ffn = jnp.concatenate([g_up.reshape(-1, width), g_down], axis=0)
        ffn = lax.psum_scatter(ffn, both, scatter_dimension=0, tiled=True)
        att = lax.psum_scatter(g_att, both, scatter_dimension=0, tiled=True)
        return jnp.concatenate([from_bands(att, size), from_bands(ffn, size)], axis=0)
    up = g_up.transpose(0, 2, 1, 3).reshape(width, -1)
    att = from_bands(g_att, size)
    ffn = jnp.concatenate([from_bands(up, size), from_bands(g_down, size)], axis=0)
    stacked = jnp.concatenate(
        [
            att.reshape(-1, att_dev, size, size),
            ffn.reshape(-1, per_dev - att_dev, size, size),
        ],
        axis=1,
    ).reshape(-1, size, size)
    return lax.psum_scatter(stacked, both, scatter_dimension=0, tiled=True)


def per_device(
    tokens,
    cotangent,
    lengths,
    offsets,
    valid_count,
    weights,
    stat_left,
    stat_right,
    root_left,
    root_right,
    projection,
    projection_left,
    projection_right,
    projection_root_left,
    projection_root_right,
    norm_params,
    norm_stat,
):
    both = ("seq", "own")
    size = weights.shape[-1]
    width = tokens.shape[-1]
    rows_here = tokens.shape[1]
    head = width // HEADS
    kp = projection.shape[1]
    blocks = rows_here // SHORT
    peers = lax.axis_size("seq")
    devices = peers * lax.axis_size("own")
    per_dev = weights.shape[0]
    att_dev = 4 * (width // size) ** 2 // devices
    x = tokens[0]
    swap = [(i, i ^ 1) for i in range(peers)]
    peer_x = lax.ppermute(x, "seq", swap)
    own_size = lax.axis_size("own")
    fused = own_size == 4 and peers == 8 and banded(per_dev, att_dev, width, size)
    w_att, w_ffn, proj_all = gather_weights(
        weights, projection, att_dev, width, both, fused, peers
    )

    places, table, coef_back = tables(lengths, offsets, valid_count, blocks, rows_here)

    e_own, e_peer = pick_rows(places, proj_all, blocks)
    n_own = places[1, :blocks]

    if fused:
        query, keyval, summary, mixed, first_sum, row_sums = forward(
            table, places, x, peer_x, w_att, e_own, e_peer, head, peers
        )
    else:
        query, keyval, part_own = project(x, w_att, e_own.transpose(0, 2, 1), True)
        (part_peer,) = project(peer_x, w_att, e_peer.transpose(0, 2, 1), False)

        def unit_sum(flag):
            total = flag[0] * part_own[0]
            for b in range(1, blocks):
                total = total + flag[b] * part_own[b]
            for b in range(blocks):
                total = total + flag[blocks + b] * part_peer[b]
            return total

        head_sum, tail_sum = unit_sum(table[0]), unit_sum(table[1])
        from_left = lax.ppermute(tail_sum, "seq", [(i, i + 2) for i in range(peers - 2)])
        from_right = lax.ppermute(head_sum, "seq", [(i + 2, i) for i in range(peers - 2)])
        summary = jnp.stack(
            [
                (
                    table[2, b] * head_sum
                    + table[3, b] * from_left
                    + table[4, b] * tail_sum
                    + table[5, b] * from_right
                    + table[6, b] * part_own[b]
                ).astype(BF)
                for b in range(blocks)
            ]
        )
        mixed, first_sum, row_sums = attend(n_own, query, summary, w_att, x, head)
    (
        result,
        hidden,
        grad_up,
        grad_down,
        first_low,
        grad_first,
        grad_branch,
        grad_mix,
        norm_terms,
    ) = feed(first_sum, w_ffn, w_att, cotangent[0], norm_params, 256)
    gtype = BF if fused else F32
    if fused:
        operands = [first_low, grad_up, hidden, grad_down, mixed, grad_branch, x]
        grad_query, grad_parts, *far_parts, g_down, g_up, g_out, g_query = backward(
            coef_back, query, summary, grad_mix, operands, head, peers, size
        )
    else:
        grad_query, grad_parts, low_head, low_tail = attend_back(
            coef_back, query, summary, grad_mix, head
        )
        far_parts = []
        for far in (1, 2):
            onward = [(i, i + far) for i in range(peers - far)]
            far_parts.append(lax.ppermute(low_tail, "seq", onward))
            far_parts.append(lax.ppermute(low_head, "seq", [(j, i) for i, j in onward]))
        g_up = outer_up(first_low, grad_up, size, gtype)
        g_down = outer_rows(hidden, grad_down, gtype, "outer_down")
        g_out = outer_rows(mixed, grad_branch, gtype, "outer_out")
        g_query = outer_rows(x, grad_query, gtype, "outer_query")
    part_rows = projection.shape[0]
    back_args = (
        coef_back,
        places,
        e_own,
        keyval,
        grad_parts,
        far_parts,
        grad_query,
        w_att,
        grad_first,
        proj_all.shape[0],
    )
    if fused:
        g_keyval, small_sums, grad_input = back(
            *back_args, (x, norm_terms, row_sums), peers // 2
        )
    else:
        grad_keyval, grad_proj, grad_input = back(*back_args)
        g_keyval = outer_rows(x, grad_keyval, gtype, "outer_keyval")
        valid_here = jnp.sum(n_own).astype(F32)
        here = lax.broadcasted_iota(jnp.int32, (1, width), 1) == 0
        row_sums = jnp.concatenate([row_sums, jnp.where(here, valid_here, 0.0)], axis=0)
        extra = jnp.concatenate([norm_terms.reshape(-1, kp), row_sums.reshape(-1, kp)], axis=0)
    n_norm = 4 * width // kp
    n_row = 2 * width // kp
    if fused:
        banded_grads, proj_parts, rows = reduce_all(
            g_query, g_keyval, g_out, g_up, g_down, small_sums, peers
        )
        (
            owned,
            left_new,
            right_new,
            weights_new,
            proj_left_new,
            proj_right_new,
            proj_blocks,
            norm_grad,
            stat_new,
            norm_new,
            residual_rms,
        ) = step_all(
            banded_grads,
            [stat_left, stat_right, root_left, root_right, weights],
            proj_parts.reshape(-1, kp, kp),
            [
                projection_left,
                projection_right,
                projection_root_left,
                projection_root_right,
                projection.reshape(-1, kp, kp),
            ],
            rows,
            norm_params,
            norm_stat,
        )
        proj_grad = proj_parts.reshape(part_rows, kp)
    else:
        owned = scatter_weight_grads(
            jnp.concatenate([g_query, g_keyval, g_out], axis=0), g_up, g_down, per_dev, att_dev, both
        )
        packed = jnp.concatenate([grad_proj, extra], axis=0)
        packed = lax.psum(jnp.pad(packed, ((0, -packed.shape[0] % 16), (0, 0))), both)
        proj_grad = lax.dynamic_slice_in_dim(
            packed, lax.axis_index("own") * part_rows, part_rows, 0
        )
        totals = packed[grad_proj.shape[0] :]
        norm_grad = totals[:n_norm].reshape(4, width)
        row_total = totals[n_norm : n_norm + n_row].reshape(2, width).sum(axis=1)
        valid_total = totals[n_norm + n_row : n_norm + n_row + width // kp].sum()
        residual_rms = jnp.sqrt(row_total / (valid_total * width))
        left_new, right_new, weights_new = shampoo(
            owned, stat_left, stat_right, root_left, root_right, weights
        )
        proj_left_new, proj_right_new, proj_blocks = shampoo(
            proj_grad.reshape(-1, kp, kp),
            projection_left,
            projection_right,
            projection_root_left,
            projection_root_right,
            projection.reshape(-1, kp, kp),
        )
        stat_new = decay * norm_stat + (1.0 - decay) * norm_grad * norm_grad
        norm_new = norm_params - rate_norm * norm_grad * lax.rsqrt(stat_new)
    return (
        result[None],
        grad_input[None],
        owned,
        left_new,
        right_new,
        weights_new,
        proj_grad,
        proj_left_new,
        proj_right_new,
        proj_blocks.reshape(part_rows, kp),
        norm_grad,
        stat_new,
        norm_new,
        residual_rms,
    )


def solution(mesh):
    pack = P("own", "seq", None)
    table = P("own", None)
    tile = P(("seq", "own"), None, None)
    proj = P("own", None, None)
    return jax.shard_map(
        per_device,
        mesh=mesh,
        in_specs=(pack, pack, table, table, table)
        + (tile,) * 5
        + (table, proj, proj, proj, proj, P(), P()),
        out_specs=(pack, pack) + (tile,) * 4 + (table, proj, proj, table, P(), P(), P(), P()),
        check_vma=False,
    )
```
